32 devices in a mesh: dp: 16 (over z, y, core), mp: 2 (over x).
Axes of the slice: x: 2, y: 2, z: 4, core: 2. Of those that a mesh axis runs over, the one named last changes fastest.
Arguments:
- tokens: bfloat16 [2048, 2048], P('dp', 'mp'), may hold values from -32 to 32
- lengths: int32 [4], replicated, may hold values from 1 to 1536, 2048 in all
- keep_mask: int32 [2048], replicated, may hold values 0 or 1
- routes: int32 [2048, 8], P('dp'), may hold values from 0 to 63, all different within a row; in each aligned block of 128 rows (0 to 127, 128 to 255, ...) at most 32 rows name the same one
- attention_gain: float32 [2048], replicated, may hold values from 0.1 to 1.9
- mixture_gain: float32 [2048], P('mp'), may hold values from 0.1 to 1.9
- query_gain: float32 [128], replicated, may hold values from 0.5 to 8, as said below
- key_gain: float32 [128], replicated, may hold values from 0.5 to 8, as said below
- query_weight: bfloat16 [2048, 2048], P('dp', 'mp'), may hold values from -0.125 to 0.125
- key_weight: bfloat16 [2048, 2048], P('dp', 'mp'), may hold values from -0.125 to 0.125
- value_weight: bfloat16 [2048, 2048], P('dp', 'mp'), may hold values from -0.125 to 0.125
- output_weight: bfloat16 [2048, 2048], P('mp', 'dp'), may hold values from -0.1875 to 0.1875
- router_weight: float32 [2048, 64], P('mp'), may hold values from -0.125 to 0.125
- expert_gate: bfloat16 [16, 2048, 4096], P('dp', None, 'mp'), may hold values from -0.125 to 0.125
- expert_up: bfloat16 [16, 2048, 4096], P('dp', None, 'mp'), may hold values from -0.125 to 0.125
- expert_down: bfloat16 [16, 4096, 2048], P('dp', 'mp'), may hold values from -0.25 to 0.25
Outputs:
- layer_output: bfloat16 [2048, 2048], P('dp', 'mp')
The draws below stay inside these ranges and needn't reach their ends.
Inputs may be any that keep to these rules, and one draw needn't show every extreme that they name: The lengths sum to 2048; exactly one is 1536. `routes`: each row names 8 different experts. Within each aligned block of 128 rows (the rows of one index of dp) no expert is named by more than 32 rows, a bound that some block reaches. `query_gain`: Positive. `key_gain`: Positive.
All inputs are finite; a program needn't handle non-finite values.
Results may differ from the reference program's by a relative error of at most 0.012.
The reference program's roundings to bfloat16 on the way (of `normed_in`, `values`, `attended`, `residual`, `mixed_in`, `hidden` and `expert_out`) count: a program that leaves them out, or rounds other values in their place, can miss the bound.
Values may be sent and summed in bfloat16 or wider, within the bound.
A program may use at most 128 MiB of HBM per device.

```python
import math
import jax
import jax.numpy as jnp
import numpy as np
from jax import lax

D = 2048
HEADS = 16
HEAD_DIM = 128
FF = 1024
EXPERTS = 64
TOPK = 8
REQUESTS = 4
TOK_DEV = 128
TOKENS = 2048
LONG = 1536
CAP = 32
EXP_DEV = 4
SPLIT = 1
N_DP = 16


def draw_tokens(key, part):
    key_base = jax.random.fold_in(key, 101)
    key_cols = jax.random.fold_in(key, 102)
    key_rows = jax.random.fold_in(key, 103)
    ramp = jnp.arange(D, dtype=jnp.float32) / D
    col_scale = 0.6 * jnp.exp(jnp.log(3.0) * ramp) * jnp.exp(jax.random.uniform(key_cols, (D,), jnp.float32, -0.35, 0.35))
    row_scale = jnp.exp(jax.random.uniform(key_rows, (TOKENS, 1), jnp.float32, jnp.log(0.5), jnp.log(2.0)))
    base_vals = jnp.clip(jax.random.normal(key_base, (TOKENS, D), jnp.float32), -5.0, 5.0)
    return (base_vals * row_scale * col_scale[None, :]).astype(jnp.bfloat16)


def draw_query_gain(key, part):
    sub_key = jax.random.fold_in(key, 201)
    gains = jnp.exp(jax.random.uniform(sub_key, (HEAD_DIM,), jnp.float32, jnp.log(1.6), jnp.log(3.2)))
    return gains


def draw_key_gain(key, part):
    sub_key = jax.random.fold_in(key, 202)
    gains = jnp.exp(jax.random.uniform(sub_key, (HEAD_DIM,), jnp.float32, jnp.log(1.6), jnp.log(3.2)))
    return gains


def touch_ends(values, rng, low, largest):
    extent = values.shape
    spot = [jax.random.randint(jax.random.fold_in(rng, axis), (), 0, extent[axis]) for axis in range(len(extent))]
    values = values.at[tuple(spot)].set(low)
    longest = extent.index(max(extent))
    spot[longest] = (spot[longest] + 1) % extent[longest]
    return values.at[tuple(spot)].set(largest)


def spiked(drawn, own_key, source, target, blocks, factor):
    def block_of(dim):
        return (jnp.arange(drawn.shape[dim]) // (drawn.shape[dim] // blocks)).reshape((-1,) + (1,) * (drawn.ndim - 1 - dim))

    one_side = jax.random.permutation(own_key, blocks)[block_of(target)]
    second = (block_of(target) + blocks // 2) % blocks
    return jnp.where((block_of(source) == one_side) | (block_of(source) == second), factor * drawn, drawn)


def block_levels(own_key, extent, split, low, top_value):
    def one(dim, parts):
        draws = jax.random.uniform(jax.random.fold_in(jax.random.fold_in(own_key, 6), dim), (parts,), jnp.float32, low / len(split), top_value / len(split))
        return jnp.repeat(jnp.exp(draws), extent[dim] // parts).reshape((-1,) + (1,) * (len(extent) - dim - 1))

    level = one(*split[0])
    for cut in split[1:]:
        level = level * one(*cut)
    return level


def split_up(number_of, total, reach, skew):
    weights = [(1 << 20) // math.isqrt(rank ** skew) + 1 for rank in range(2, number_of + 1)]
    rest, holding = total - reach - (number_of - 1), [1] * (number_of - 1)
    while rest > 0:
        candidates = [i for i in range(number_of - 1) if holding[i] < reach]
        whole, remaining = sum([weights[i] for i in candidates]), rest
        for i in candidates:
            addition = min(reach - holding[i], max(1, remaining * weights[i] // whole), rest)
            holding[i] = holding[i] + addition
            rest = rest - addition
    return np.array([reach] + holding)


def ragged_sizes(stream_key, count, total, bound, slope):
    if count == 2:
        one = jax.random.randint(stream_key, (), max(1, total - bound), min(bound, total - 1) + 1)
        return jnp.stack([one, total - one])
    sizes = jnp.asarray(split_up(count, total, bound, slope), jnp.int32)
    twos = (count - 1) // 2
    donor, receiver = sizes[1:1 + 2 * twos:2], sizes[2:2 + 2 * twos:2]
    slack = jnp.minimum(donor - 1, bound - receiver)
    moved = jax.random.randint(jax.random.fold_in(stream_key, 1), (twos,), 0, 1 << 20) % (slack + 1)
    sizes = sizes.at[1:1 + 2 * twos:2].set(donor - moved).at[2:2 + 2 * twos:2].set(receiver + moved)
    return sizes[jax.random.permutation(jax.random.fold_in(stream_key, 2), count)]


def assign_block(key, own, number, rows, number_of, top, bound, slope):
    ranking = jax.random.permutation(key, number_of)
    crowded, usual = portions_of(number_of, rows * top, bound, slope, True), portions_of(number_of, rows * top, bound, slope, False)
    places = jnp.arange(number_of)

    def named(sizes, turn):
        used = int((sizes > 0).sum())
        fixed = max(1, used // 4)
        shifted = fixed + (places - fixed + turn * (used - fixed)) % max(1, number_of - fixed)
        return jnp.zeros((number_of,), jnp.int32).at[ranking[jnp.where(places < fixed, places, shifted)]].set(jnp.asarray(sizes, jnp.int32))

    sizes = jnp.where(number % 4 == 0, named(crowded, number // 4), named(usual, number - number // 4 - 1))
    mixed = jax.random.permutation(jax.random.fold_in(own, 3), number_of)
    donor, sink = mixed[0:number_of // 2 * 2:2], mixed[1:number_of // 2 * 2:2]
    slack = jnp.minimum(sizes[donor] - 1, bound - sizes[sink]) // 2
    slack = jnp.where((donor == ranking[0]) | (sink == ranking[0]) | (sizes[sink] == 0), 0, jnp.maximum(slack, 0))
    shifted = jax.random.randint(jax.random.fold_in(own, 4), (number_of // 2,), 0, 1 << 20) % (slack + 1)
    sizes = sizes.at[donor].add(-shifted).at[sink].add(shifted)
    labels = jnp.searchsorted(jnp.cumsum(sizes), jnp.arange(rows * top), side="right").astype(jnp.int32)
    table = labels.reshape(top, rows).T
    table = table[jax.random.permutation(jax.random.fold_in(own, 1), rows)]
    turn = jax.random.randint(jax.random.fold_in(own, 2), (rows, 1), 0, top)
    return jnp.take_along_axis(table, (jnp.arange(top)[None, :] + turn) % top, axis=1)


def portions_of(amount, total, bound, skew, full):
    loads = [(1 << 20) // math.isqrt(rank ** skew) + 1 for rank in range(1, amount + 1)]
    largest = bound if full else min(bound, max(-(-total // amount), total * loads[0] // sum(loads)))
    least = 1 if total - largest >= amount - 1 else 0
    holding, surplus = [largest] + [least] * (amount - 1), total - largest - least * (amount - 1)
    while surplus > 0:
        free = [i for i in range(1, amount) if holding[i] < largest] or [i for i in range(1, amount) if holding[i] < bound]
        pool, budget = sum([loads[i] for i in free]), surplus
        for i in free:
            extra = min(bound - holding[i], max(1, budget * loads[i] // pool), surplus)
            holding[i] = holding[i] + extra
            surplus = surplus - extra
    return np.array(holding)


def bell_draw(key, dims, deviation, bound, pieces=(), kind=jnp.bfloat16):
    loudness = block_levels(key, dims, pieces, -0.22, 0.18) if pieces else 1.0
    array = jax.random.normal(key, dims, jnp.float32) * deviation * loudness
    return jnp.minimum(jnp.maximum(array, -bound), bound).astype(kind)


def heavy_noise(rng, extent, scale, most, cuts, heavy, kind=jnp.bfloat16):
    drawn = scale * jax.random.normal(rng, extent, jnp.float32)
    if cuts:
        drawn = drawn * block_levels(rng, extent, cuts, -0.22, 0.18)
    return jnp.clip(spiked(drawn, jax.random.fold_in(rng, 3), *heavy), -most, most).astype(kind)


def setup_inputs(seed: int = 0) -> dict:
    key_of = jax.random.split(jax.random.key(seed), 17)
    tokens = draw_tokens(jax.random.fold_in(key_of[16], 71), 0)
    lengths = ragged_sizes(key_of[1], REQUESTS, TOKENS, LONG, 2).astype(jnp.int32)
    keep_mask = touch_ends((jax.random.randint(key_of[2], (TOKENS,), 0, 8) < 7).astype(jnp.int32), jax.random.fold_in(key_of[2], 1), 0, 1)
    routes_keys = jax.random.split(jax.random.fold_in(key_of[3], 1), TOKENS // TOK_DEV)
    routes_turns = jax.random.permutation(jax.random.fold_in(key_of[3], 3), TOKENS // TOK_DEV)
    routes = jax.vmap(lambda own, number: assign_block(jax.random.fold_in(key_of[3], 2), own, number, TOK_DEV, EXPERTS, TOPK, CAP, 2))(routes_keys, routes_turns).reshape((TOKENS, TOPK))
    attention_gain = jnp.clip(1.0 + 0.18 * jax.random.normal(key_of[4], (D,), jnp.float32), 0.1, 1.9)
    mixture_gain = jnp.clip(1.0 + 0.18 * jax.random.normal(key_of[5], (D,), jnp.float32), 0.1, 1.9)
    query_gain = draw_query_gain(jax.random.fold_in(key_of[16], 71), 0)
    key_gain = draw_key_gain(jax.random.fold_in(key_of[16], 71), 0)
    query_weight = bell_draw(key_of[8], (D, D), D ** -0.5, 0.125, ((0, 16), (1, 2)))
    key_weight = bell_draw(key_of[9], (D, D), D ** -0.5, 0.125, ((0, 16), (1, 2)))
    value_weight = bell_draw(key_of[10], (D, D), D ** -0.5, 0.125, ((0, 16), (1, 2)))
    output_weight = heavy_noise(key_of[11], (D, D), D ** -0.5, 0.1875, ((0, 2), (1, 16)), (0, 1, 16, 2.0))
    router_weight = bell_draw(key_of[12], (D, EXPERTS), D ** -0.5, 0.125, ((0, 2),), jnp.float32)
    expert_gate = bell_draw(key_of[13], (N_DP, D, EXP_DEV * FF), D ** -0.5, 0.125, ((0, 16), (2, 2)))
    expert_up = bell_draw(key_of[14], (N_DP, D, EXP_DEV * FF), D ** -0.5, 0.125, ((0, 16), (2, 2)))
    expert_down = heavy_noise(key_of[15], (N_DP, EXP_DEV * FF, D), FF ** -0.5, 0.25, ((0, 16), (1, 2)), (1, 2, 2, 2.0))
    return dict(tokens=tokens, lengths=lengths, keep_mask=keep_mask, routes=routes, attention_gain=attention_gain, mixture_gain=mixture_gain, query_gain=query_gain, key_gain=key_gain, query_weight=query_weight, key_weight=key_weight, value_weight=value_weight, output_weight=output_weight, router_weight=router_weight, expert_gate=expert_gate, expert_up=expert_up, expert_down=expert_down)


EPS = 1e-06
ROPE_BASE = 10000.0
NEG = -1e+30

def rope_tables(position):
    halves = HEAD_DIM // 2
    exponent = jnp.arange(halves, dtype=jnp.float32) * (2.0 / HEAD_DIM)
    frequency = jnp.power(jnp.float32(ROPE_BASE), -exponent)
    angle = position.astype(jnp.float32)[:, None] * frequency[None, :]
    cos_table = jnp.cos(angle)
    sin_table = jnp.sin(angle)
    return (jnp.concatenate([cos_table, cos_table], 1), jnp.concatenate([sin_table, sin_table], 1))

def head_prep(projected, head_gain, cos_table, sin_table):
    row_count = projected.shape[0]
    per_head = projected.reshape(row_count, -1, HEAD_DIM)
    normed = per_head * lax.rsqrt(lax.optimization_barrier(jnp.mean(per_head * per_head, axis=2, keepdims=True)) + EPS) * head_gain
    halves = HEAD_DIM // 2
    rotated = jnp.concatenate([-normed[:, :, halves:], normed[:, :, :halves]], 2)
    turned = normed * cos_table[:, None, :] + rotated * sin_table[:, None, :]
    return turned.reshape(row_count, -1).astype(jnp.bfloat16)

def segment_info(lengths, first_row, row_count):
    request_end = jnp.cumsum(lengths).astype(jnp.int32)
    request_start = (request_end - lengths).astype(jnp.int32)
    global_row = (first_row + jnp.arange(row_count, dtype=jnp.int32)).astype(jnp.int32)
    segment = lax.optimization_barrier(jnp.sum((request_end[None, :] <= global_row[:, None]).astype(jnp.int32), axis=1)).astype(jnp.int32)
    chosen = segment[:, None] == jnp.arange(lengths.shape[0], dtype=jnp.int32)[None, :]
    begin = lax.optimization_barrier(jnp.sum(jnp.where(chosen, request_start[None, :], 0), axis=1)).astype(jnp.int32)
    return (segment, (global_row - begin).astype(jnp.int32), global_row)

def reference(tokens, lengths, keep_mask, routes, attention_gain, mixture_gain, query_gain, key_gain, query_weight, key_weight, value_weight, output_weight, router_weight, expert_gate, expert_up, expert_down):
    xfloat = tokens.astype(jnp.float32)
    normed_in = (xfloat * lax.rsqrt(lax.optimization_barrier(jnp.mean(xfloat * xfloat, axis=1, keepdims=True)) + EPS) * attention_gain).astype(jnp.bfloat16)
    segment, position, global_row = segment_info(lengths, 0, TOKENS)
    cos_table, sin_table = rope_tables(position)
    queries = head_prep(jnp.dot(normed_in, query_weight, preferred_element_type=jnp.float32), query_gain, cos_table, sin_table)
    key_heads = head_prep(jnp.dot(normed_in, key_weight, preferred_element_type=jnp.float32), key_gain, cos_table, sin_table)
    value_heads = jnp.dot(normed_in, value_weight, preferred_element_type=jnp.float32).astype(jnp.bfloat16)
    qblock = math.gcd(TOKENS, 512)
    blocks = TOKENS // qblock
    query_blocks = queries.reshape(blocks, qblock, HEADS, HEAD_DIM)
    key_float = key_heads.reshape(TOKENS, HEADS, HEAD_DIM).astype(jnp.float32)
    value_float = value_heads.reshape(TOKENS, HEADS, HEAD_DIM).astype(jnp.float32)
    scale = HEAD_DIM ** (-0.5)

    def attend(packed):
        query_part, query_seg, query_row = packed
        scores = jnp.einsum('thd,shd->hts', query_part.astype(jnp.float32), key_float) * scale
        visible = (query_seg[:, None] == segment[None, :]) & ((keep_mask[None, :] == 1) | (query_row[:, None] == global_row[None, :]))
        masked = jnp.where(visible[None], scores, NEG)
        top_score = lax.optimization_barrier(jnp.max(masked, axis=2, keepdims=True))
        weights = jnp.where(visible[None], jnp.exp(masked - top_score), 0.0)
        totals = lax.optimization_barrier(jnp.sum(weights, axis=2))
        rounded = lax.optimization_barrier(weights.astype(jnp.bfloat16))
        mixed = jnp.einsum('hts,shd->thd', rounded.astype(jnp.float32), value_float)
        return (mixed / totals.T[:, :, None]).reshape(qblock, D).astype(jnp.bfloat16)
    attended = lax.map(attend, (query_blocks, segment.reshape(blocks, qblock), global_row.reshape(blocks, qblock))).reshape(TOKENS, D)
    residual = (xfloat + jnp.dot(attended, output_weight, preferred_element_type=jnp.float32)).astype(jnp.bfloat16)
    hfloat = residual.astype(jnp.float32)
    inverse = lax.rsqrt(lax.optimization_barrier(jnp.mean(hfloat * hfloat, axis=1, keepdims=True)) + EPS)
    scaled = hfloat * mixture_gain
    mixed_in = (scaled * inverse).astype(jnp.bfloat16)
    logits = jnp.dot(scaled, router_weight, precision=lax.Precision.HIGHEST) * inverse
    picked = jnp.take_along_axis(logits, routes, axis=1)
    sigmoid_vals = jax.nn.sigmoid(picked)
    route_weight = sigmoid_vals / lax.optimization_barrier(jnp.sum(sigmoid_vals, axis=1, keepdims=True))
    onehot = lax.optimization_barrier(jnp.sum((routes[:, :, None] == jnp.arange(EXPERTS, dtype=jnp.int32)[None, None, :]).astype(jnp.int32), axis=1)).astype(jnp.int32)
    per_block = onehot.reshape(N_DP, TOK_DEV, EXPERTS)
    before = (jnp.cumsum(per_block, axis=1).astype(jnp.int32) - per_block).reshape(TOKENS, EXPERTS)
    slot = jnp.take_along_axis(before, routes, axis=1).astype(jnp.int32)
    block_id = (jnp.arange(TOKENS, dtype=jnp.int32) // TOK_DEV)[:, None]
    target = (routes * (N_DP * CAP) + block_id * CAP + slot).astype(jnp.int32)
    token_ids = jnp.repeat(jnp.arange(TOKENS, dtype=jnp.int32), TOPK)
    source = jnp.full((EXPERTS * N_DP * CAP,), TOKENS, jnp.int32).at[target.reshape(-1)].set(token_ids)
    padded = jnp.concatenate([mixed_in, jnp.zeros((1, D), jnp.bfloat16)], 0)
    gate_all = expert_gate.reshape(N_DP, D, EXP_DEV, FF).transpose(0, 2, 1, 3).reshape(EXPERTS, D, FF)
    up_all = expert_up.reshape(N_DP, D, EXP_DEV, FF).transpose(0, 2, 1, 3).reshape(EXPERTS, D, FF)
    down_all = expert_down.reshape(EXPERTS, FF, D)
    ff_block = FF // SPLIT

    def expert_ffn(packed):
        row_index, gate_w, up_w, down_w = packed
        inputs = padded[row_index]
        gate_val = jnp.dot(inputs, gate_w, preferred_element_type=jnp.float32)
        up_val = jnp.dot(inputs, up_w, preferred_element_type=jnp.float32)
        hidden = (jax.nn.silu(gate_val) * up_val).astype(jnp.bfloat16)
        row_count = hidden.shape[0]
        partial_value = jnp.einsum('rjf,jfd->rjd', hidden.reshape(row_count, SPLIT, ff_block).astype(jnp.float32), down_w.reshape(SPLIT, ff_block, D).astype(jnp.float32))
        rounded = lax.optimization_barrier(partial_value.astype(jnp.bfloat16))
        return lax.optimization_barrier(jnp.sum(rounded.astype(jnp.float32), axis=1)).astype(jnp.bfloat16)
    expert_out = lax.map(expert_ffn, (source.reshape(EXPERTS, N_DP * CAP), gate_all, up_all, down_all))
    flat = expert_out.reshape(EXPERTS * N_DP * CAP, D)
    gathered = flat[target]
    mixture = lax.optimization_barrier(jnp.sum(gathered.astype(jnp.float32) * route_weight[:, :, None], axis=1))
    return (hfloat + mixture).astype(jnp.bfloat16)
```

```python
import jax
import jax.numpy as jnp
import numpy as np
from jax import lax
from jax.experimental import pallas as pl
from jax.experimental.pallas import tpu as pltpu
from jax.sharding import PartitionSpec as P

D = 2048
HEAD_DIM = 128
FF = 1024
EXPERTS = 64
TOPK = 8
CAP = 32


EPS = 1e-06
ROPE_BASE = 10000.0
NEG = -1e30


def rope_tables(position):
    halves = HEAD_DIM // 2
    exponent = jnp.arange(halves, dtype=jnp.float32) * (2.0 / HEAD_DIM)
    frequency = jnp.power(jnp.float32(ROPE_BASE), -exponent)
    angle = position.astype(jnp.float32)[:, None] * frequency[None, :]
    cos_table = jnp.cos(angle)
    sin_table = jnp.sin(angle)
    return (jnp.concatenate([cos_table, cos_table], 1), jnp.concatenate([sin_table, sin_table], 1))


def head_prep(projected, head_gain, cos_table, sin_table):
    row_count = projected.shape[0]
    per_head = projected.reshape(row_count, -1, HEAD_DIM)
    normed = (
        per_head * lax.rsqrt(jnp.mean(per_head * per_head, axis=2, keepdims=True) + EPS) * head_gain
    )
    halves = HEAD_DIM // 2
    rotated = jnp.concatenate([-normed[:, :, halves:], normed[:, :, :halves]], 2)
    turned = normed * cos_table[:, None, :] + rotated * sin_table[:, None, :]
    return turned.reshape(row_count, -1).astype(jnp.bfloat16)


def segment_info(lengths, global_row):
    count = jnp.arange(lengths.shape[0], dtype=jnp.int32)
    request_end = jnp.sum(jnp.where(count[None, :] <= count[:, None], lengths[None, :], 0), axis=1)
    request_start = request_end - lengths
    segment = jnp.sum((request_end[None, :] <= global_row[:, None]).astype(jnp.int32), axis=1)
    chosen = segment[:, None] == jnp.arange(lengths.shape[0], dtype=jnp.int32)[None, :]
    begin = jnp.sum(jnp.where(chosen, request_start[None, :], 0), axis=1)
    return (segment, global_row - begin)


MESH = pl.DeviceIdType.MESH


def greet_neighbours():
    index = lax.axis_index("dp")
    x = lax.axis_index("mp")
    layers = lax.axis_size("dp") // 4
    z, y = index // 4, (index // 2) % 2
    barrier = pltpu.get_barrier_semaphore()
    across_y, across_x = (index + 2 - 4 * y, x), (index, 1 - x)
    to_twin = (index + 1 - 2 * (index % 2), x)
    for peer in (across_y, across_x, to_twin):
        pl.semaphore_signal(barrier, inc=1, device_id=peer, device_id_type=MESH)
    has_up, has_down = z < layers - 1, z > 0

    @pl.when(has_up)
    def _():
        pl.semaphore_signal(barrier, inc=1, device_id=(index + 4, x), device_id_type=MESH)

    @pl.when(has_down)
    def _():
        pl.semaphore_signal(barrier, inc=1, device_id=(index - 4, x), device_id_type=MESH)

    pl.semaphore_wait(barrier, 3 + has_up.astype(jnp.int32) + has_down.astype(jnp.int32))


def gather_kernel(block_ref, out_ref, *sems):
    greet_neighbours()
    gather_steps(block_ref, out_ref, *sems)


def gather_steps(block_ref, out_ref, local_sem, a_sem, up_sem, down_sem, b_sem, twin_sem, recv_sem):
    index = lax.axis_index("dp")
    x = lax.axis_index("mp")
    layers = lax.axis_size("dp") // 4
    z, y, core = index // 4, (index // 2) % 2, index % 2
    rows, width = block_ref.shape
    to_a = (index + core * (2 - 4 * y), x + (1 - core) * (1 - 2 * x))
    to_b = (index + (1 - core) * (2 - 4 * y), x + core * (1 - 2 * x))
    to_twin = (index + 1 - 2 * core, x)
    to_up, to_down = (index + 4, x), (index - 4, x)

    def place(layer, da, db, which):
        dy = which * da + (1 - which) * db
        dx = (1 - which) * da + which * db
        yy, xx = y + dy * (1 - 2 * y), x + dx * (1 - 2 * x)
        return layer * 4 + yy * 2 + which, xx

    def view(spot):
        return out_ref.at[
            pl.ds(pl.multiple_of(spot[0] * rows, rows), rows),
            pl.ds(pl.multiple_of(spot[1] * width, width), width),
        ]

    def send(spot, sem, device, own=False):
        return pltpu.make_async_remote_copy(
            src_ref=block_ref if own else view(spot),
            dst_ref=view(spot),
            send_sem=sem,
            recv_sem=recv_sem.at[spot[0] * 2 + spot[1]],
            device_id=device,
            device_id_type=MESH,
        )

    def arrive(spot):
        send(spot, local_sem, to_twin).wait_recv()

    has_up, has_down = z < layers - 1, z > 0
    home = place(z, 0, 0, core)
    keep = pltpu.make_async_copy(block_ref, view(home), local_sem)
    first = send(home, a_sem, to_a, True)

    def spread(layer, da, own, act):
        spot = place(layer, da, 0, core)
        slot = layer * 2 + da

        @pl.when((layer <= z) & has_up)
        def _():
            act(send(spot, up_sem.at[slot], to_up, own))

        @pl.when((layer >= z) & has_down)
        def _():
            act(send(spot, down_sem.at[slot], to_down, own))

        act(send(spot, b_sem.at[slot], to_b, own))
        act(send(spot, twin_sem.at[slot * 2], to_twin, own))

    def hand_over(layer, da, act):
        spot = place(layer, da, 1, core)
        act(send(spot, twin_sem.at[(layer * 2 + da) * 2 + 1], to_twin))

    start = lambda copy: copy.start()
    finish = lambda copy: copy.wait_send()
    first.start()
    spread(z, 0, True, start)
    keep.start()
    arrive(place(z, 1, 0, core))
    spread(z, 1, False, start)

    def both(distance, run):
        for da in range(2):
            @pl.when(z >= distance)
            def _():
                run(z - distance, da)

            @pl.when(z + distance < layers)
            def _():
                run(z + distance, da)

    def onward(layer, da):
        arrive(place(layer, da, 0, core))
        spread(layer, da, False, start)

    def across(layer, da):
        arrive(place(layer, da, 1, core))
        hand_over(layer, da, start)

    for distance in range(1, layers):
        both(distance, onward)
        if distance == 1:
            for da in range(2):
                across(z, da)
        else:
            both(distance - 1, across)
    both(layers - 1, across)
    keep.wait()
    first.wait_send()
    for layer in range(layers):
        for da in range(2):
            spread(layer, da, False, finish)
            hand_over(layer, da, finish)
            for db in range(2):
                arrive(place(layer, da, db, 1 - core))


def gather_scratch(dp_count, mp_count, layers):
    dma = pltpu.SemaphoreType.DMA
    return [
        dma,
        dma,
        dma((layers * 2,)),
        dma((layers * 2,)),
        dma((layers * 2,)),
        dma((layers * 4,)),
        dma((dp_count * mp_count,)),
    ]


def gather_blocks(block):
    dp_count, mp_count = lax.axis_size("dp"), lax.axis_size("mp")
    rows, width = block.shape
    if mp_count != 2 or dp_count % 4:
        wide = lax.all_gather(block, "mp", axis=1, tiled=True)
        return lax.all_gather(wide, "dp", axis=0, tiled=True)
    layers = dp_count // 4
    return pl.pallas_call(
        gather_kernel,
        out_shape=jax.ShapeDtypeStruct((dp_count * rows, mp_count * width), block.dtype),
        in_specs=[pl.BlockSpec(memory_space=pl.ANY)],
        out_specs=pl.BlockSpec(memory_space=pl.ANY),
        scratch_shapes=gather_scratch(dp_count, mp_count, layers),
        compiler_params=pltpu.CompilerParams(collective_id=0, has_side_effects=True),
        name="gather_blocks",
    )(block)


def scatter_kernel(
    parts_ref,
    out_ref,
    mine,
    twin,
    cross,
    rise,
    fall,
    last,
    total,
    load_sem,
    twin_send,
    cross_send,
    z_send,
    last_send,
    twin_recv,
    cross_recv,
    rise_recv,
    fall_recv,
    last_recv,
):
    index = lax.axis_index("dp")
    x = lax.axis_index("mp")
    layers = lax.axis_size("dp") // 4
    z, y, core = index // 4, (index // 2) % 2, index % 2
    rows, width = out_ref.shape
    to_a = (index + core * (2 - 4 * y), x + (1 - core) * (1 - 2 * x))
    to_b = (index + (1 - core) * (2 - 4 * y), x + core * (1 - 2 * x))
    to_twin = (index + 1 - 2 * core, x)
    to_up, to_down = (index + 4, x), (index - 4, x)
    has_up, has_down = z < layers - 1, z > 0

    def view(layer, da, db, which):
        dy = which * da + (1 - which) * db
        dx = (1 - which) * da + which * db
        yy, xx = y + dy * (1 - 2 * y), x + dx * (1 - 2 * x)
        row = (layer * 4 + yy * 2 + which) * rows
        return parts_ref.at[
            pl.ds(pl.multiple_of(row, rows), rows),
            pl.ds(pl.multiple_of(xx * width, width), width),
        ]

    def remote(source, target, send_sem, recv_sem, device):
        return pltpu.make_async_remote_copy(
            src_ref=source,
            dst_ref=target,
            send_sem=send_sem,
            recv_sem=recv_sem,
            device_id=device,
            device_id_type=MESH,
        )

    barrier = pltpu.get_barrier_semaphore()
    for peer in (to_a, to_b, to_twin):
        pl.semaphore_signal(barrier, inc=1, device_id=peer, device_id_type=MESH)

    @pl.when(has_up)
    def _():
        pl.semaphore_signal(barrier, inc=1, device_id=to_up, device_id_type=MESH)

    @pl.when(has_down)
    def _():
        pl.semaphore_signal(barrier, inc=1, device_id=to_down, device_id_type=MESH)

    def outward(run):
        for distance in range(layers - 1, 0, -1):
            for da in range(2):
                @pl.when(z + distance < layers)
                def _():
                    run(z + distance, da, True)

                @pl.when(z >= distance)
                def _():
                    run(z - distance, da, False)

    def home(run):
        for da in (1, 0):
            run(z, da, None)

    def load(layer, da, db):
        slot = (layer * 2 + da) * 2 + db
        return pltpu.make_async_copy(view(layer, da, db, core), mine.at[slot], load_sem.at[slot])

    def to_other_core(layer, da, db):
        slot = (layer * 2 + da) * 2 + db
        return remote(
            view(layer, da, db, 1 - core),
            twin.at[slot],
            twin_send.at[slot],
            twin_recv.at[slot],
            to_twin,
        )

    def to_cross(layer, da):
        pair = layer * 2 + da
        return remote(
            mine.at[pair * 2 + 1], cross.at[pair], cross_send.at[pair], cross_recv.at[pair], to_b
        )

    def upward(layer, da):
        pair = layer * 2 + da
        return remote(mine.at[pair * 2], rise.at[pair], z_send.at[pair], rise_recv.at[pair], to_up)

    def downward(layer, da):
        pair = layer * 2 + da
        return remote(
            mine.at[pair * 2], fall.at[pair], z_send.at[pair], fall_recv.at[pair], to_down
        )

    def to_last():
        return remote(mine.at[(z * 2 + 1) * 2], last, last_send, last_recv, to_a)

    def add(target, *sources):
        step = 16

        def body(turn, carry):
            at = pl.ds(pl.multiple_of(turn * step, step), step)
            value = sources[0][at, :].astype(jnp.float32)
            for source in sources[1:]:
                value = value + source[at, :].astype(jnp.float32)
            target[at, :] = value.astype(target.dtype)
            return carry

        lax.fori_loop(0, rows // step, body, 0)

    for db in (1, 0):
        outward(lambda layer, da, up: load(layer, da, db).start())
        home(lambda layer, da, up: load(layer, da, db).start())
    pl.semaphore_wait(barrier, 3 + has_up.astype(jnp.int32) + has_down.astype(jnp.int32))
    for db in (1, 0):
        outward(lambda layer, da, up: to_other_core(layer, da, db).start())
        home(lambda layer, da, up: to_other_core(layer, da, db).start())

    def pair_up(layer, da, up):
        slot = (layer * 2 + da) * 2 + 1
        load(layer, da, 1).wait()
        to_other_core(layer, da, 1).wait_recv()
        add(mine.at[slot], mine.at[slot], twin.at[slot])
        to_cross(layer, da).start()

    outward(pair_up)
    home(pair_up)

    def collect(layer, da, target):
        pair = layer * 2 + da
        load(layer, da, 0).wait()
        to_other_core(layer, da, 0).wait_recv()
        to_cross(layer, da).wait_recv()
        add(target, mine.at[pair * 2], twin.at[pair * 2], cross.at[pair])

    def pass_on(layer, da, up):
        pair = layer * 2 + da
        collect(layer, da, total)
        if up:
            @pl.when(has_down)
            def _():
                upward(layer, da).wait_recv()
                add(total, total, rise.at[pair])
        else:
            @pl.when(has_up)
            def _():
                downward(layer, da).wait_recv()
                add(total, total, fall.at[pair])
        add(mine.at[pair * 2], total)
        (upward if up else downward)(layer, da).start()

    outward(pass_on)

    def settle(layer, da, up):
        pair = layer * 2 + da
        target = total if da else out_ref
        collect(layer, da, target)

        @pl.when(has_down)
        def _():
            upward(layer, da).wait_recv()
            add(target, target, rise.at[pair])

        @pl.when(has_up)
        def _():
            downward(layer, da).wait_recv()
            add(target, target, fall.at[pair])

        if da:
            add(mine.at[pair * 2], total)
            to_last().start()

    home(settle)
    to_last().wait_recv()
    add(out_ref, out_ref, last)

    def finish(layer, da, up):
        to_other_core(layer, da, 0).wait_send()
        to_other_core(layer, da, 1).wait_send()
        to_cross(layer, da).wait_send()
        if up is not None:
            (upward if up else downward)(layer, da).wait_send()

    outward(finish)
    home(finish)
    to_last().wait_send()


def scatter_sum(parts):
    dp_count, mp_count = lax.axis_size("dp"), lax.axis_size("mp")
    rows, width = parts.shape[0] // dp_count, parts.shape[1] // mp_count
    if mp_count != 2 or dp_count % 4:
        halves = lax.psum_scatter(parts, "mp", scatter_dimension=1, tiled=True)
        return lax.psum_scatter(halves, "dp", scatter_dimension=0, tiled=True)
    pairs = dp_count // 2
    dma = pltpu.SemaphoreType.DMA
    block = (rows, width)
    return pl.pallas_call(
        scatter_kernel,
        out_shape=jax.ShapeDtypeStruct(block, jnp.float32),
        in_specs=[pl.BlockSpec(memory_space=pl.ANY)],
        out_specs=pl.BlockSpec(memory_space=pltpu.VMEM),
        scratch_shapes=[
            pltpu.VMEM((2 * pairs,) + block, jnp.bfloat16),
            pltpu.VMEM((2 * pairs,) + block, jnp.bfloat16),
            pltpu.VMEM((pairs,) + block, jnp.bfloat16),
            pltpu.VMEM((pairs,) + block, jnp.bfloat16),
            pltpu.VMEM((pairs,) + block, jnp.bfloat16),
            pltpu.VMEM(block, jnp.bfloat16),
            pltpu.VMEM(block, jnp.float32),
            dma((2 * pairs,)),
            dma((2 * pairs,)),
            dma((pairs,)),
            dma((pairs,)),
            dma,
            dma((2 * pairs,)),
            dma((pairs,)),
            dma((pairs,)),
            dma((pairs,)),
            dma,
        ],
        compiler_params=pltpu.CompilerParams(
            collective_id=1, has_side_effects=True, vmem_limit_bytes=40 * 1024 * 1024
        ),
        name="scatter_sum",
    )(parts.astype(jnp.bfloat16))


def attention(queries, keys, values, query_seg, query_row, key_seg, key_row, keep_mask):
    scale = HEAD_DIM ** (-0.5)
    scores = (
        lax.dot_general(
            queries, keys, (((1,), (1,)), ((), ())), preferred_element_type=jnp.float32
        )
        * scale
    )
    visible = (query_seg[:, None] == key_seg[None, :]) & (
        (keep_mask[None, :] == 1) | (query_row[:, None] == key_row[None, :])
    )
    masked = jnp.where(visible, scores, NEG)
    top = jnp.max(masked, axis=1, keepdims=True)
    weights = jnp.where(visible, jnp.exp(masked - top), 0.0)
    totals = jnp.sum(weights, axis=1, keepdims=True)
    mixed = jnp.dot(weights.astype(jnp.bfloat16), values, preferred_element_type=jnp.float32)
    return (mixed / totals).astype(jnp.bfloat16)


def local_any(
    tokens,
    lengths,
    keep_mask,
    routes,
    attention_gain,
    mixture_gain,
    query_gain,
    key_gain,
    query_weight,
    key_weight,
    value_weight,
    output_weight,
    router_weight,
    expert_gate,
    expert_up,
    expert_down,
):
    tok_rows = tokens.shape[0]
    dp_count = lax.axis_size("dp")
    dp_index = lax.axis_index("dp")
    mp_index = lax.axis_index("mp")
    local_width = query_weight.shape[1]
    local_heads = local_width // HEAD_DIM
    share = dp_count // local_heads
    part = dp_index % share
    total_rows = tok_rows * dp_count

    weight_rows = query_weight.shape[0]
    packed = jnp.stack([query_weight, key_weight, value_weight]).reshape(
        3, weight_rows, local_heads, HEAD_DIM
    )
    packed = packed.transpose(2, 1, 0, 3).reshape(local_heads, weight_rows, 3 * HEAD_DIM)
    packed = jnp.repeat(packed, share, axis=0)
    head_weight = lax.all_to_all(packed, "dp", split_axis=0, concat_axis=0, tiled=True)
    head_weight = head_weight.reshape(dp_count * weight_rows, 3 * HEAD_DIM)

    all_tokens, head_weight, late_weight = lax.optimization_barrier(
        (gather_blocks(tokens), head_weight, output_weight)
    )
    all_output_weight = lax.all_gather(late_weight, "dp", axis=1, tiled=True)
    xfloat = all_tokens.astype(jnp.float32)
    all_in = (
        xfloat * lax.rsqrt(jnp.mean(xfloat * xfloat, axis=1, keepdims=True) + EPS) * attention_gain
    ).astype(jnp.bfloat16)
    all_routes = lax.all_gather(routes, "dp", axis=0, tiled=True)
    all_gain = lax.all_gather(mixture_gain, "mp", axis=0, tiled=True)
    all_router = lax.all_gather(router_weight, "mp", axis=0, tiled=True)

    key_row = jnp.arange(total_rows, dtype=jnp.int32)
    key_seg, key_pos = segment_info(lengths, key_row)
    cos_table, sin_table = rope_tables(key_pos)

    def own(array):
        split = array.reshape((local_heads, share, tok_rows) + array.shape[1:])
        taken = lax.dynamic_index_in_dim(split, part, 1, keepdims=False)
        return taken.reshape((local_heads * tok_rows,) + array.shape[1:])

    projected = jnp.dot(all_in, head_weight, preferred_element_type=jnp.float32)
    queries = head_prep(
        own(projected[:, :HEAD_DIM]), query_gain, own(cos_table), own(sin_table)
    )
    keys = head_prep(projected[:, HEAD_DIM : 2 * HEAD_DIM], key_gain, cos_table, sin_table)
    values = projected[:, 2 * HEAD_DIM :].astype(jnp.bfloat16)
    attended = attention(
        queries, keys, values, own(key_seg), own(key_row), key_seg, key_row, keep_mask
    )
    groups = [[head * share + p for head in range(local_heads)] for p in range(share)]
    attended = lax.all_to_all(
        attended.reshape(local_heads, tok_rows, HEAD_DIM),
        "dp",
        split_axis=0,
        concat_axis=0,
        tiled=True,
        axis_index_groups=groups,
    )
    attended = attended.transpose(1, 0, 2).reshape(tok_rows, local_width)
    partial_out = jnp.dot(attended, all_output_weight, preferred_element_type=jnp.float32)
    summed_out = lax.psum_scatter(partial_out, "mp", scatter_dimension=1, tiled=True)
    residual = (tokens.astype(jnp.float32) + summed_out).astype(jnp.bfloat16)
    all_residual = gather_blocks(residual)
    hfloat = all_residual.astype(jnp.float32)
    inverse = lax.rsqrt(jnp.mean(hfloat * hfloat, axis=1, keepdims=True) + EPS)
    mixed_in = (hfloat * all_gain * inverse).astype(jnp.bfloat16)

    own_rows = lax.dynamic_slice_in_dim(all_residual, dp_index * tok_rows, tok_rows, 0)
    own_float = own_rows.astype(jnp.float32)
    own_inverse = lax.rsqrt(jnp.mean(own_float * own_float, axis=1, keepdims=True) + EPS)
    logits = (
        jnp.dot(own_float * all_gain, all_router, precision=lax.Precision.HIGHEST) * own_inverse
    )

    ids = jnp.arange(tok_rows, dtype=jnp.int32)
    earlier = (ids[:, None] < ids[None, :]).astype(jnp.bfloat16)
    slots = jnp.arange(CAP, dtype=jnp.int32)

    def chosen_slots(named):
        before = jnp.dot(
            named.astype(jnp.bfloat16).reshape(-1, tok_rows),
            earlier,
            preferred_element_type=jnp.float32,
        ).reshape(named.shape)
        place = jnp.where(named, before.astype(jnp.int32), -1)
        return place[:, :, None, :] == slots[None, None, :, None]

    exp_local = EXPERTS // dp_count
    gate_local = expert_gate[0]
    up_local = expert_up[0]
    down_local = expert_down[0]
    unit_count = gate_local.shape[1]
    held = max(1, unit_count // FF)
    units = unit_count // held
    first_expert = (mp_index * unit_count) // FF

    own_experts = dp_index * exp_local + first_expert + jnp.arange(held, dtype=jnp.int32)
    block_routes = all_routes.reshape(dp_count, tok_rows, TOPK)
    here = jnp.any(block_routes[:, None] == own_experts[None, :, None, None], axis=3)
    chosen = chosen_slots(here)
    select = chosen.astype(jnp.bfloat16).reshape(dp_count, held * CAP, tok_rows)
    rows_in = lax.dot_general(
        select,
        mixed_in.reshape(dp_count, tok_rows, D),
        (((2,), (1,)), ((0,), (0,))),
        preferred_element_type=jnp.float32,
    ).astype(jnp.bfloat16)
    rows_in = rows_in.reshape(dp_count, held, CAP, D)
    experts = jnp.arange(EXPERTS, dtype=jnp.int32)
    named = jnp.any(routes[:, :, None] == experts[None, None, :], axis=1)
    sigmoid_vals = jax.nn.sigmoid(logits) * named.astype(jnp.float32)
    route_weight = sigmoid_vals / jnp.sum(sigmoid_vals, axis=1, keepdims=True)
    all_weights = lax.all_gather(route_weight, "dp", axis=0, tiled=True)
    outs = []
    for index in range(held):
        rows = rows_in[:, index].reshape(dp_count * CAP, D)
        low, high = index * units, (index + 1) * units
        gate_val = jnp.dot(rows, gate_local[:, low:high], preferred_element_type=jnp.float32)
        up_val = jnp.dot(rows, up_local[:, low:high], preferred_element_type=jnp.float32)
        hidden = (jax.nn.silu(gate_val) * up_val).astype(jnp.bfloat16)
        out = jnp.dot(hidden, down_local[low:high], preferred_element_type=jnp.float32)
        outs.append(out.astype(jnp.bfloat16).reshape(dp_count, CAP, D))
    first_own = dp_index * exp_local + first_expert
    own_weights = lax.dynamic_slice_in_dim(all_weights, first_own, held, 1)
    own_weights = own_weights.reshape(dp_count, tok_rows, held).transpose(0, 2, 1)
    spread = jnp.where(chosen, own_weights[:, :, None, :], 0.0)
    spread_high = spread.astype(jnp.bfloat16)
    spread_low = (spread - spread_high.astype(jnp.float32)).astype(jnp.bfloat16)
    contract = (((1,), (1,)), ((0,), (0,)))
    both = jnp.concatenate([spread_high, spread_low], 2).reshape(
        dp_count, held * 2 * CAP, tok_rows
    )
    out_rows = jnp.concatenate(sum([[out, out] for out in outs], []), axis=1)
    parts = lax.dot_general(both, out_rows, contract, preferred_element_type=jnp.float32)
    mixture = scatter_sum(parts.reshape(total_rows, D))
    return (residual.astype(jnp.float32) + mixture).astype(jnp.bfloat16)


def row_starts(lengths_ref):
    ends, starts, total = [], [], 0
    for index in range(lengths_ref.shape[0]):
        starts.append(total)
        total = total + lengths_ref[index]
        ends.append(total)
    return ends, starts


def segment_of(row, ends):
    segment = (row >= ends[0]).astype(jnp.int32)
    for end in ends[1:]:
        segment = segment + (row >= end).astype(jnp.int32)
    return segment


def attend_kernel(
    lengths_ref,
    part_ref,
    tokens_ref,
    weight_ref,
    gain_ref,
    query_gain_ref,
    key_gain_ref,
    keep_ref,
    frequency_ref,
    cos_ref,
    sin_ref,
    out_ref,
    held,
    normed,
    keys,
    values,
    queries,
    start_cos,
    start_sin,
    load_sem,
):
    total, width = held.shape
    chunk = normed.shape[0]
    part = part_ref[0]
    rows = chunk // 2

    def load(index):
        at = pl.ds(pl.multiple_of(index * chunk, chunk), chunk)
        return pltpu.make_async_copy(tokens_ref.at[at, :], held.at[at, :], load_sem.at[index])

    for index in range(total // chunk):
        load(index).start()
    ends, starts = row_starts(lengths_ref)
    which = lax.broadcasted_iota(jnp.int32, (8, HEAD_DIM), 0)
    begin = jnp.zeros((8, HEAD_DIM), jnp.int32)
    for index, start in enumerate(starts):
        begin = jnp.where(which == index, start, begin)
    angle = begin.astype(jnp.float32) * frequency_ref[...]
    start_cos[...] = jnp.cos(angle)
    start_sin[...] = jnp.sin(angle)

    def turn(projected, head_gain, row, at):
        square = jnp.mean(projected * projected, axis=1, keepdims=True)
        value = projected * lax.rsqrt(square + EPS) * head_gain
        cos_s, sin_s = start_cos[0:1, :], start_sin[0:1, :]
        for index in range(1, len(starts)):
            past = row >= ends[index - 1]
            cos_s = jnp.where(past, start_cos[index : index + 1, :], cos_s)
            sin_s = jnp.where(past, start_sin[index : index + 1, :], sin_s)
        cos_g, sin_g = cos_ref[at, :], sin_ref[at, :]
        cos_t = cos_g * cos_s + sin_g * sin_s
        sin_t = sin_g * cos_s - cos_g * sin_s
        lane = lax.broadcasted_iota(jnp.int32, value.shape, 1)
        halves = pltpu.roll(value, HEAD_DIM // 2, 1)
        rotated = jnp.where(lane < HEAD_DIM // 2, -halves, halves)
        return (value * cos_t + rotated * sin_t).astype(jnp.bfloat16)

    def project(index, carry):
        load(index).wait()
        at = pl.ds(pl.multiple_of(index * chunk, chunk), chunk)
        x = held[at, :].astype(jnp.float32)
        inverse = lax.rsqrt(jnp.mean(x * x, axis=1, keepdims=True) + EPS)
        normed[...] = (x * inverse * gain_ref[...]).astype(jnp.bfloat16)
        both = jnp.dot(
            normed[...], weight_ref[:, HEAD_DIM:], preferred_element_type=jnp.float32
        )
        row = lax.broadcasted_iota(jnp.int32, (chunk, HEAD_DIM), 0) + index * chunk
        keys[at, :] = turn(both[:, :HEAD_DIM], key_gain_ref[...], row, at)
        values[at, :] = both[:, HEAD_DIM:].astype(jnp.bfloat16)
        mine = normed[pl.ds(pl.multiple_of(part * rows, rows), rows), :]
        asked = jnp.dot(mine, weight_ref[:, :HEAD_DIM], preferred_element_type=jnp.float32)
        first = pl.multiple_of(index * chunk + part * rows, rows)
        row = lax.broadcasted_iota(jnp.int32, (rows, HEAD_DIM), 0) + first
        queries[pl.ds(pl.multiple_of(index * rows, rows), rows), :] = turn(
            asked, query_gain_ref[...], row, pl.ds(first, rows)
        )
        return carry

    lax.fori_loop(0, total // chunk, project, 0)

    key_row = lax.broadcasted_iota(jnp.int32, (1, total), 1)
    key_seg = jnp.where(keep_ref[...] == 1, segment_of(key_row, ends), -1)
    scale = HEAD_DIM ** (-0.5) * 1.4426950408889634

    def attend(index, carry):
        at = pl.ds(pl.multiple_of(index * chunk, chunk), chunk)
        scores = lax.dot_general(
            queries[at, :], keys[...], (((1,), (1,)), ((), ())), preferred_element_type=jnp.float32
        )
        local_row = lax.broadcasted_iota(jnp.int32, (chunk, 1), 0)
        block = index * 2 + (local_row >= rows).astype(jnp.int32)
        row = (
            (block * 2 + part) * rows
            + local_row
            - (local_row >= rows).astype(jnp.int32) * rows
        )
        visible = (segment_of(row, ends) == key_seg) | (row == key_row)
        masked = jnp.where(visible, scores, NEG)
        top = jnp.max(masked, axis=1, keepdims=True)
        weights = jnp.exp2((masked - top) * scale)
        totals = jnp.sum(weights, axis=1, keepdims=True)
        mixed = jnp.dot(
            weights.astype(jnp.bfloat16), values[...], preferred_element_type=jnp.float32
        )
        out_ref[at, :] = (mixed / totals).astype(jnp.bfloat16)
        return carry

    lax.fori_loop(0, total // 2 // chunk, attend, 0)


def attend_local(
    all_tokens, head_weight, lengths, keep_mask, attention_gain, query_gain, key_gain, part
):
    total, width = all_tokens.shape
    halves = HEAD_DIM // 2
    chunk = 256
    exponent = np.arange(halves, dtype=np.float32) * np.float32(2.0 / HEAD_DIM)
    frequency = np.power(np.float32(ROPE_BASE), -exponent).astype(np.float32)
    frequency = np.concatenate([frequency, frequency])[None, :]
    angle = np.arange(total, dtype=np.float32)[:, None] * frequency
    cos_table = np.cos(angle.astype(np.float64)).astype(np.float32)
    sin_table = np.sin(angle.astype(np.float64)).astype(np.float32)
    smem = pl.BlockSpec(memory_space=pltpu.SMEM)
    vmem = pl.BlockSpec(memory_space=pltpu.VMEM)
    return pl.pallas_call(
        attend_kernel,
        out_shape=jax.ShapeDtypeStruct((total // 2, HEAD_DIM), jnp.bfloat16),
        in_specs=[smem, smem, pl.BlockSpec(memory_space=pl.ANY)] + [vmem] * 8,
        out_specs=vmem,
        scratch_shapes=[
            pltpu.VMEM((total, width), jnp.bfloat16),
            pltpu.VMEM((chunk, width), jnp.bfloat16),
            pltpu.VMEM((total, HEAD_DIM), jnp.bfloat16),
            pltpu.VMEM((total, HEAD_DIM), jnp.bfloat16),
            pltpu.VMEM((total // 2, HEAD_DIM), jnp.bfloat16),
            pltpu.VMEM((8, HEAD_DIM), jnp.float32),
            pltpu.VMEM((8, HEAD_DIM), jnp.float32),
            pltpu.SemaphoreType.DMA((total // chunk,)),
        ],
        compiler_params=pltpu.CompilerParams(vmem_limit_bytes=40 * 1024 * 1024),
        name="attend",
    )(
        lengths,
        part,
        all_tokens,
        head_weight,
        attention_gain[None, :],
        query_gain[None, :],
        key_gain[None, :],
        keep_mask[None, :],
        jnp.asarray(frequency),
        jnp.asarray(cos_table),
        jnp.asarray(sin_table),
    )


def experts_kernel(
    first_ref,
    residual_ref,
    router_ref,
    gain_ref,
    routes_ref,
    gate_ref,
    up_ref,
    down_ref,
    out_ref,
    held,
    mixed,
    gate,
    up,
    down,
    rows_in,
    hidden,
    rows_out,
    spread,
    staged,
    load_sem,
    gate_sem,
    up_sem,
    down_sem,
    out_sem,
):
    blocks, tok_rows = routes_ref.shape[0], routes_ref.shape[2]
    held_count = rows_in.shape[0]
    chunk = 2 * tok_rows
    chunks = blocks // 2
    units = hidden.shape[1]
    first = first_ref[0]
    width = held.shape[2]
    tile = 256

    def load(index, slot):
        at = pl.ds(pl.multiple_of(index * chunk, chunk), chunk)
        return pltpu.make_async_copy(residual_ref.at[at, :], held.at[slot], load_sem.at[slot])

    def load_gate(index):
        at = pl.ds(pl.multiple_of(index * units, units), units)
        return pltpu.make_async_copy(gate_ref.at[:, at], gate.at[:, at], gate_sem.at[index])

    def load_up(index):
        at = pl.ds(pl.multiple_of(index * units, units), units)
        return pltpu.make_async_copy(up_ref.at[:, at], up.at[:, at], up_sem.at[index])

    def load_down(index):
        at = pl.ds(pl.multiple_of(index * units, units), units)
        return pltpu.make_async_copy(down_ref.at[at, :], down.at[at, :], down_sem.at[index])

    load(0, 0).start()
    for index in range(held_count):
        load_gate(index).start()
        load_up(index).start()
        load_down(index).start()

    earlier = (
        lax.broadcasted_iota(jnp.int32, (tok_rows, tok_rows), 0)
        < lax.broadcasted_iota(jnp.int32, (tok_rows, tok_rows), 1)
    ).astype(jnp.bfloat16)
    expert_id = lax.broadcasted_iota(jnp.int32, (EXPERTS, tok_rows), 0)
    slot_id = lax.broadcasted_iota(jnp.int32, (CAP, tok_rows), 0)

    def block_slots(block, logits, inverse):
        named_ids = routes_ref[block]
        named = named_ids[0:1, :] == expert_id
        for k in range(1, TOPK):
            named = named | (named_ids[k : k + 1, :] == expert_id)
        logits_t = jnp.transpose(logits * inverse)[:EXPERTS]
        sigmoid = jnp.where(named, 1.0 / (1.0 + jnp.exp(-logits_t)), 0.0)
        route = sigmoid / jnp.sum(sigmoid, axis=0, keepdims=True)
        named_f = named.astype(jnp.float32)
        here, weight = [], []
        for index in range(held_count):
            own = expert_id == first + index
            here.append(jnp.sum(jnp.where(own, named_f, 0.0), axis=0, keepdims=True))
            weight.append(jnp.sum(jnp.where(own, route, 0.0), axis=0, keepdims=True))
        stacked = jnp.concatenate(here + [jnp.zeros((8 - held_count, tok_rows), jnp.float32)], 0)
        before = jnp.dot(
            stacked.astype(jnp.bfloat16), earlier, preferred_element_type=jnp.float32
        )
        place = jnp.where(stacked > 0.5, before.astype(jnp.int32), -1)
        chosen = jnp.concatenate(
            [place[index : index + 1, :] == slot_id for index in range(held_count)], 0
        )
        weights = jnp.concatenate(
            [jnp.broadcast_to(w, (CAP, tok_rows)) for w in weight], 0
        )
        spread_w = jnp.where(chosen, weights, 0.0)
        high = spread_w.astype(jnp.bfloat16)
        low = (spread_w - high.astype(jnp.float32)).astype(jnp.bfloat16)
        return chosen.astype(jnp.float32).astype(jnp.bfloat16), high, low

    def gather(index, carry):
        slot = lax.rem(index, 2)

        @pl.when(index + 1 < chunks)
        def _():
            load(index + 1, 1 - slot).start()

        load(index, slot).wait()
        h = held[slot].astype(jnp.float32)
        inverse = lax.rsqrt(jnp.mean(h * h, axis=1, keepdims=True) + EPS)
        mixed[...] = (h * gain_ref[...] * inverse).astype(jnp.bfloat16)
        logits = jnp.dot(held[slot], router_ref[...], preferred_element_type=jnp.float32)
        logits = logits[:, :128] + logits[:, 128:]
        logits = logits + pltpu.roll(logits, EXPERTS, 1)
        chosen, spreads = [], []
        for half in range(2):
            own = slice(half * tok_rows, (half + 1) * tok_rows)
            pick, high, low = block_slots(index * 2 + half, logits[own], inverse[own])
            chosen.append(pick)
            spreads += [(high, half), (low, half)]
        empty = jnp.zeros_like(chosen[0])
        select = jnp.concatenate(
            [
                jnp.concatenate([chosen[0], empty], 1),
                jnp.concatenate([empty, chosen[1]], 1),
            ],
            0,
        )
        taken = jnp.dot(select, mixed[...], preferred_element_type=jnp.float32).astype(
            jnp.bfloat16
        )
        for half in range(2):
            for expert in range(held_count):
                source = (half * held_count + expert) * CAP
                at = pl.ds(pl.multiple_of((index * 2 + half) * CAP, CAP), CAP)
                rows_in[expert, at, :] = taken[source : source + CAP]
        spread[index] = jnp.concatenate(
            [
                jnp.concatenate([value, empty] if half == 0 else [empty, value], 1)
                for value, half in spreads
            ],
            0,
        )
        return carry

    lax.fori_loop(0, chunks, gather, 0)

    for expert in range(held_count):
        load_gate(expert).wait()
        load_up(expert).wait()

        def widen(turn, carry):
            at = pl.ds(pl.multiple_of(turn * tile, tile), tile)
            wide = pl.ds(pl.multiple_of(expert * units + turn * tile, tile), tile)
            gate_val = jnp.dot(
                rows_in[expert], gate[:, wide], preferred_element_type=jnp.float32
            )
            up_val = jnp.dot(rows_in[expert], up[:, wide], preferred_element_type=jnp.float32)
            silu = gate_val / (1.0 + jnp.exp(-gate_val))
            hidden[:, at] = (silu * up_val).astype(jnp.bfloat16)
            return carry

        lax.fori_loop(0, units // tile, widen, 0)
        load_down(expert).wait()

        def narrow(turn, carry):
            at = pl.ds(pl.multiple_of(turn * tile, tile), tile)
            deep = pl.ds(expert * units, units)
            rows_out[expert, :, at] = jnp.dot(
                hidden[...], down[deep, at], preferred_element_type=jnp.float32
            ).astype(jnp.bfloat16)
            return carry

        lax.fori_loop(0, width // tile, narrow, 0)

    def store(index, slot):
        at = pl.ds(pl.multiple_of(index * chunk, chunk), chunk)
        return pltpu.make_async_copy(staged.at[slot], out_ref.at[at, :], out_sem.at[slot])

    def combine(index, carry):
        slot = lax.rem(index, 2)

        @pl.when(index >= 2)
        def _():
            store(index - 2, slot).wait()

        pieces = []
        for half in range(2):
            at = pl.ds(pl.multiple_of((index * 2 + half) * CAP, CAP), CAP)
            pieces += [rows_out[expert, at, :] for expert in range(held_count)] * 2
        staged[slot] = lax.dot_general(
            spread[index],
            jnp.concatenate(pieces, 0),
            (((0,), (0,)), ((), ())),
            preferred_element_type=jnp.float32,
        ).astype(jnp.bfloat16)
        store(index, slot).start()
        return carry

    lax.fori_loop(0, chunks, combine, 0)
    store(chunks - 2, (chunks - 2) % 2).wait()
    store(chunks - 1, (chunks - 1) % 2).wait()


def experts_local(all_residual, router, gain, all_routes, first, gate, up, down):
    total, width = all_residual.shape
    units = FF
    held_count = gate.shape[1] // FF
    blocks, _, tok_rows = all_routes.shape
    chunk = 2 * tok_rows
    smem = pl.BlockSpec(memory_space=pltpu.SMEM)
    vmem = pl.BlockSpec(memory_space=pltpu.VMEM)
    hbm = pl.BlockSpec(memory_space=pl.ANY)
    dma = pltpu.SemaphoreType.DMA
    return pl.pallas_call(
        experts_kernel,
        out_shape=jax.ShapeDtypeStruct((total, width), jnp.bfloat16),
        in_specs=[smem, hbm, vmem, vmem, vmem, hbm, hbm, hbm],
        out_specs=hbm,
        scratch_shapes=[
            pltpu.VMEM((2, chunk, width), jnp.bfloat16),
            pltpu.VMEM((chunk, width), jnp.bfloat16),
            pltpu.VMEM(gate.shape, jnp.bfloat16),
            pltpu.VMEM(up.shape, jnp.bfloat16),
            pltpu.VMEM(down.shape, jnp.bfloat16),
            pltpu.VMEM((held_count, blocks * CAP, width), jnp.bfloat16),
            pltpu.VMEM((blocks * CAP, units), jnp.bfloat16),
            pltpu.VMEM((held_count, blocks * CAP, width), jnp.bfloat16),
            pltpu.VMEM((blocks // 2, 4 * held_count * CAP, chunk), jnp.bfloat16),
            pltpu.VMEM((2, chunk, width), jnp.bfloat16),
            dma((2,)),
            dma((held_count,)),
            dma((held_count,)),
            dma((held_count,)),
            dma((2,)),
        ],
        compiler_params=pltpu.CompilerParams(vmem_limit_bytes=56 * 1024 * 1024),
        name="experts",
    )(first, all_residual, router, gain, all_routes, gate, up, down)


def exchange_kernel(
    attended_ref,
    weight_ref,
    tokens_ref,
    routes_ref,
    router_ref,
    gain_ref,
    all_ref,
    own_ref,
    all_routes_ref,
    all_router_ref,
    all_gain_ref,
    gathered,
    sent_half,
    got_half,
    residual,
    swap_send,
    swap_recv,
    route_send,
    route_recv,
    pair_send,
    pair_recv,
    local_sem,
    *gather_sems,
):
    index = lax.axis_index("dp")
    x = lax.axis_index("mp")
    dp_count = lax.axis_size("dp")
    heads = attended_ref.shape[0]
    core, chip = index % 2, index // 2
    tok_rows, half = tokens_ref.shape

    barrier = pltpu.get_barrier_semaphore()
    for step in range(1, dp_count):
        peer = lax.rem(index + step, dp_count)
        pl.semaphore_signal(barrier, inc=1, device_id=(peer, x), device_id_type=MESH)
    pl.semaphore_signal(barrier, inc=1, device_id=(index, 1 - x), device_id_type=MESH)
    pl.semaphore_wait(barrier, dp_count)

    def swap(step):
        other = lax.rem(chip + step, heads)
        return pltpu.make_async_remote_copy(
            src_ref=attended_ref.at[other],
            dst_ref=gathered.at[:, pl.ds(pl.multiple_of(chip * HEAD_DIM, HEAD_DIM), HEAD_DIM)],
            send_sem=swap_send.at[step],
            recv_sem=swap_recv.at[step],
            device_id=(other * 2 + core, x),
            device_id_type=MESH,
        )

    def route(step):
        return pltpu.make_async_remote_copy(
            src_ref=routes_ref,
            dst_ref=all_routes_ref.at[index],
            send_sem=route_send.at[step],
            recv_sem=route_recv.at[step],
            device_id=(lax.rem(index + step, dp_count), x),
            device_id_type=MESH,
        )

    def across(source, target, which):
        return pltpu.make_async_remote_copy(
            src_ref=source,
            dst_ref=target,
            send_sem=pair_send.at[which],
            recv_sem=pair_recv.at[which],
            device_id=(index, 1 - x),
            device_id_type=MESH,
        )

    router_copy = across(router_ref, all_router_ref.at[x], 0)
    gain_copy = across(gain_ref, all_gain_ref.at[x], 1)
    half_copy = across(sent_half, got_half, 2)
    for step in range(1, heads):
        swap(step).start()
    keep = [
        pltpu.make_async_copy(
            attended_ref.at[chip],
            gathered.at[:, pl.ds(pl.multiple_of(chip * HEAD_DIM, HEAD_DIM), HEAD_DIM)],
            local_sem.at[0],
        ),
        pltpu.make_async_copy(routes_ref, all_routes_ref.at[index], local_sem.at[1]),
        pltpu.make_async_copy(router_ref, all_router_ref.at[x], local_sem.at[2]),
        pltpu.make_async_copy(gain_ref, all_gain_ref.at[x], local_sem.at[3]),
    ]
    for copy in keep:
        copy.start()
    router_copy.start()
    gain_copy.start()
    for step in range(1, dp_count):
        route(step).start()
    keep[0].wait()
    for step in range(1, heads):
        swap(step).wait_recv()

    tile = 256

    def away(turn, carry):
        at = pl.ds(pl.multiple_of(turn * tile, tile), tile)
        wide = pl.ds(pl.multiple_of((1 - x) * half + turn * tile, tile), tile)
        sent_half[:, at] = jnp.dot(
            gathered[...], weight_ref[:, wide], preferred_element_type=jnp.float32
        )
        return carry

    lax.fori_loop(0, half // tile, away, 0)
    half_copy.start()

    def stay(turn, carry):
        at = pl.ds(pl.multiple_of(turn * tile, tile), tile)
        wide = pl.ds(pl.multiple_of(x * half + turn * tile, tile), tile)
        own_ref[:, at] = tokens_ref[:, at].astype(jnp.float32) + jnp.dot(
            gathered[...], weight_ref[:, wide], preferred_element_type=jnp.float32
        )
        return carry

    lax.fori_loop(0, half // tile, stay, 0)
    half_copy.wait_recv()
    residual[...] = (own_ref[...] + got_half[...]).astype(jnp.bfloat16)
    own_ref[...] = residual[...].astype(jnp.float32)
    gather_steps(residual, all_ref, *gather_sems)

    for copy in keep[1:]:
        copy.wait()
    for step in range(1, heads):
        swap(step).wait_send()
    for copy in (router_copy, gain_copy):
        copy.wait()
    half_copy.wait_send()
    for step in range(1, dp_count):
        route(step).wait()


def exchange(attended, weight, tokens, routes, router, gain):
    dp_count, mp_count = lax.axis_size("dp"), lax.axis_size("mp")
    tok_rows, half = tokens.shape
    heads = attended.shape[0]
    layers = dp_count // 4
    dma = pltpu.SemaphoreType.DMA
    vmem = pl.BlockSpec(memory_space=pltpu.VMEM)
    hbm = pl.BlockSpec(memory_space=pl.ANY)
    shape = jax.ShapeDtypeStruct
    return pl.pallas_call(
        exchange_kernel,
        out_shape=(
            shape((dp_count * tok_rows, mp_count * half), jnp.bfloat16),
            shape((tok_rows, half), jnp.float32),
            shape((dp_count,) + routes.shape, routes.dtype),
            shape((mp_count,) + router.shape, router.dtype),
            shape((mp_count,) + gain.shape, gain.dtype),
        ),
        in_specs=[vmem] * 6,
        out_specs=(hbm, vmem, hbm, hbm, hbm),
        scratch_shapes=[
            pltpu.VMEM((tok_rows, heads * HEAD_DIM), jnp.bfloat16),
            pltpu.VMEM((tok_rows, half), jnp.float32),
            pltpu.VMEM((tok_rows, half), jnp.float32),
            pltpu.VMEM((tok_rows, half), jnp.bfloat16),
            dma((heads,)),
            dma((heads,)),
            dma((dp_count,)),
            dma((dp_count,)),
            dma((3,)),
            dma((3,)),
            dma((4,)),
        ]
        + gather_scratch(dp_count, mp_count, layers),
        compiler_params=pltpu.CompilerParams(
            collective_id=2, has_side_effects=True, vmem_limit_bytes=40 * 1024 * 1024
        ),
        name="exchange",
    )(attended, weight, tokens, routes, router, gain)


def split_three(value):
    high = value.astype(jnp.bfloat16)
    rest = value - high.astype(jnp.float32)
    middle = rest.astype(jnp.bfloat16)
    low = (rest - middle.astype(jnp.float32)).astype(jnp.bfloat16)
    return high, middle, low


def local_paired(
    tokens,
    lengths,
    keep_mask,
    routes,
    attention_gain,
    mixture_gain,
    query_gain,
    key_gain,
    query_weight,
    key_weight,
    value_weight,
    output_weight,
    router_weight,
    expert_gate,
    expert_up,
    expert_down,
):
    tok_rows, half = tokens.shape
    dp_count = lax.axis_size("dp")
    dp_index = lax.axis_index("dp")
    mp_index = lax.axis_index("mp")
    local_heads = query_weight.shape[1] // HEAD_DIM
    share = dp_count // local_heads
    part = (dp_index % share).astype(jnp.int32).reshape(1)

    weight_rows = query_weight.shape[0]
    packed = jnp.stack([query_weight, key_weight, value_weight]).reshape(
        3, weight_rows, local_heads, HEAD_DIM
    )
    packed = packed.transpose(2, 1, 0, 3).reshape(local_heads, weight_rows, 3 * HEAD_DIM)
    packed = jnp.repeat(packed, share, axis=0)
    head_weight = lax.all_to_all(packed, "dp", split_axis=0, concat_axis=0, tiled=True)
    head_weight = head_weight.reshape(dp_count * weight_rows, 3 * HEAD_DIM)
    all_tokens, head_weight, late_weight = lax.optimization_barrier(
        (gather_blocks(tokens), head_weight, output_weight)
    )
    all_output_weight = lax.all_gather(late_weight, "dp", axis=1, tiled=True)
    attended = attend_local(
        all_tokens, head_weight, lengths, keep_mask, attention_gain, query_gain, key_gain, part
    )
    attended = attended.reshape(local_heads, tok_rows, HEAD_DIM)

    parts = split_three(mixture_gain[:, None] * router_weight)
    router = jnp.concatenate(parts + (jnp.zeros_like(parts[0]),), axis=1)
    routes_t = jnp.concatenate(
        [routes.T, jnp.zeros((8, tok_rows), routes.dtype)], 0
    )[: max(8, TOPK)]
    gain = jnp.broadcast_to(mixture_gain[None, :], (8, half))
    all_residual, own, all_routes, all_router, all_gain = exchange(
        attended, all_output_weight, tokens, routes_t, router, gain
    )
    held = expert_gate.shape[2] // FF
    first = (dp_index * (EXPERTS // dp_count) + mp_index * held).astype(jnp.int32).reshape(1)
    parts = experts_local(
        all_residual,
        all_router.reshape(-1, all_router.shape[2]),
        all_gain[:, 0].reshape(1, -1),
        all_routes,
        first,
        expert_gate[0],
        expert_up[0],
        expert_down[0],
    )
    return (own + scatter_sum(parts)).astype(jnp.bfloat16)


def local(*arrays):
    paired = lax.axis_size("mp") == 2 and lax.axis_size("dp") == 16
    return (local_paired if paired else local_any)(*arrays)


def solution(mesh):
    return jax.shard_map(
        local,
        mesh=mesh,
        in_specs=(
            P("dp", "mp"),
            P(),
            P(),
            P("dp", None),
            P(),
            P("mp"),
            P(),
            P(),
            P("dp", "mp"),
            P("dp", "mp"),
            P("dp", "mp"),
            P("mp", "dp"),
            P("mp", None),
            P("dp", None, "mp"),
            P("dp", None, "mp"),
            P("dp", "mp", None),
        ),
        out_specs=P("dp", "mp"),
        check_vma=False,
    )
```

```python
import jax
import jax.numpy as jnp
import numpy as np
from jax import lax
from jax.experimental import pallas as pl
from jax.experimental.pallas import tpu as pltpu
from jax.sharding import PartitionSpec as P

D = 2048
HEAD_DIM = 128
FF = 1024
EXPERTS = 64
TOPK = 8
CAP = 32


EPS = 1e-06
ROPE_BASE = 10000.0
NEG = -1e30


def rope_tables(position):
    halves = HEAD_DIM // 2
    exponent = jnp.arange(halves, dtype=jnp.float32) * (2.0 / HEAD_DIM)
    frequency = jnp.power(jnp.float32(ROPE_BASE), -exponent)
    angle = position.astype(jnp.float32)[:, None] * frequency[None, :]
    cos_table = jnp.cos(angle)
    sin_table = jnp.sin(angle)
    return (jnp.concatenate([cos_table, cos_table], 1), jnp.concatenate([sin_table, sin_table], 1))


def head_prep(projected, head_gain, cos_table, sin_table):
    row_count = projected.shape[0]
    per_head = projected.reshape(row_count, -1, HEAD_DIM)
    normed = (
        per_head * lax.rsqrt(jnp.mean(per_head * per_head, axis=2, keepdims=True) + EPS) * head_gain
    )
    halves = HEAD_DIM // 2
    rotated = jnp.concatenate([-normed[:, :, halves:], normed[:, :, :halves]], 2)
    turned = normed * cos_table[:, None, :] + rotated * sin_table[:, None, :]
    return turned.reshape(row_count, -1).astype(jnp.bfloat16)


def segment_info(lengths, global_row):
    count = jnp.arange(lengths.shape[0], dtype=jnp.int32)
    request_end = jnp.sum(jnp.where(count[None, :] <= count[:, None], lengths[None, :], 0), axis=1)
    request_start = request_end - lengths
    segment = jnp.sum((request_end[None, :] <= global_row[:, None]).astype(jnp.int32), axis=1)
    chosen = segment[:, None] == jnp.arange(lengths.shape[0], dtype=jnp.int32)[None, :]
    begin = jnp.sum(jnp.where(chosen, request_start[None, :], 0), axis=1)
    return (segment, global_row - begin)


MESH = pl.DeviceIdType.MESH


def greet_neighbours():
    index = lax.axis_index("dp")
    x = lax.axis_index("mp")
    layers = lax.axis_size("dp") // 4
    z, y = index // 4, (index // 2) % 2
    barrier = pltpu.get_barrier_semaphore()
    across_y, across_x = (index + 2 - 4 * y, x), (index, 1 - x)
    to_twin = (index + 1 - 2 * (index % 2), x)
    for peer in (across_y, across_x, to_twin):
        pl.semaphore_signal(barrier, inc=1, device_id=peer, device_id_type=MESH)
    has_up, has_down = z < layers - 1, z > 0

    @pl.when(has_up)
    def _():
        pl.semaphore_signal(barrier, inc=1, device_id=(index + 4, x), device_id_type=MESH)

    @pl.when(has_down)
    def _():
        pl.semaphore_signal(barrier, inc=1, device_id=(index - 4, x), device_id_type=MESH)

    pl.semaphore_wait(barrier, 3 + has_up.astype(jnp.int32) + has_down.astype(jnp.int32))


def gather_kernel(block_ref, out_ref, *sems):
    greet_neighbours()
    gather_steps(block_ref, out_ref, *sems)


def gather_steps(block_ref, out_ref, local_sem, a_sem, up_sem, down_sem, b_sem, twin_sem, recv_sem):
    index = lax.axis_index("dp")
    x = lax.axis_index("mp")
    layers = lax.axis_size("dp") // 4
    z, y, core = index // 4, (index // 2) % 2, index % 2
    rows, width = block_ref.shape
    to_a = (index + core * (2 - 4 * y), x + (1 - core) * (1 - 2 * x))
    to_b = (index + (1 - core) * (2 - 4 * y), x + core * (1 - 2 * x))
    to_twin = (index + 1 - 2 * core, x)
    to_up, to_down = (index + 4, x), (index - 4, x)

    def place(layer, da, db, which):
        dy = which * da + (1 - which) * db
        dx = (1 - which) * da + which * db
        yy, xx = y + dy * (1 - 2 * y), x + dx * (1 - 2 * x)
        return layer * 4 + yy * 2 + which, xx

    def view(spot):
        return out_ref.at[
            pl.ds(pl.multiple_of(spot[0] * rows, rows), rows),
            pl.ds(pl.multiple_of(spot[1] * width, width), width),
        ]

    def send(spot, sem, device, own=False):
        return pltpu.make_async_remote_copy(
            src_ref=block_ref if own else view(spot),
            dst_ref=view(spot),
            send_sem=sem,
            recv_sem=recv_sem.at[spot[0] * 2 + spot[1]],
            device_id=device,
            device_id_type=MESH,
        )

    def arrive(spot):
        send(spot, local_sem, to_twin).wait_recv()

    has_up, has_down = z < layers - 1, z > 0
    home = place(z, 0, 0, core)
    keep = pltpu.make_async_copy(block_ref, view(home), local_sem)
    first = send(home, a_sem, to_a, True)

    def spread(layer, da, own, act):
        spot = place(layer, da, 0, core)
        slot = layer * 2 + da

        @pl.when((layer <= z) & has_up)
        def _():
            act(send(spot, up_sem.at[slot], to_up, own))

        @pl.when((layer >= z) & has_down)
        def _():
            act(send(spot, down_sem.at[slot], to_down, own))

        act(send(spot, b_sem.at[slot], to_b, own))
        act(send(spot, twin_sem.at[slot * 2], to_twin, own))

    def hand_over(layer, da, act):
        spot = place(layer, da, 1, core)
        act(send(spot, twin_sem.at[(layer * 2 + da) * 2 + 1], to_twin))

    start = lambda copy: copy.start()
    finish = lambda copy: copy.wait_send()
    first.start()
    spread(z, 0, True, start)
    keep.start()
    arrive(place(z, 1, 0, core))
    spread(z, 1, False, start)

    def both(distance, run):
        for da in range(2):
            @pl.when(z >= distance)
            def _():
                run(z - distance, da)

            @pl.when(z + distance < layers)
            def _():
                run(z + distance, da)

    def onward(layer, da):
        arrive(place(layer, da, 0, core))
        spread(layer, da, False, start)

    def across(layer, da):
        arrive(place(layer, da, 1, core))
        hand_over(layer, da, start)

    for distance in range(1, layers):
        both(distance, onward)
        if distance == 1:
            for da in range(2):
                across(z, da)
        else:
            both(distance - 1, across)
    both(layers - 1, across)
    keep.wait()
    first.wait_send()
    for layer in range(layers):
        for da in range(2):
            spread(layer, da, False, finish)
            hand_over(layer, da, finish)
            for db in range(2):
                arrive(place(layer, da, db, 1 - core))


def gather_scratch(dp_count, mp_count, layers):
    dma = pltpu.SemaphoreType.DMA
    return [
        dma,
        dma,
        dma((layers * 2,)),
        dma((layers * 2,)),
        dma((layers * 2,)),
        dma((layers * 4,)),
        dma((dp_count * mp_count,)),
    ]


def gather_blocks(block):
    dp_count, mp_count = lax.axis_size("dp"), lax.axis_size("mp")
    rows, width = block.shape
    if mp_count != 2 or dp_count % 4:
        wide = lax.all_gather(block, "mp", axis=1, tiled=True)
        return lax.all_gather(wide, "dp", axis=0, tiled=True)
    layers = dp_count // 4
    return pl.pallas_call(
        gather_kernel,
        out_shape=jax.ShapeDtypeStruct((dp_count * rows, mp_count * width), block.dtype),
        in_specs=[pl.BlockSpec(memory_space=pl.ANY)],
        out_specs=pl.BlockSpec(memory_space=pl.ANY),
        scratch_shapes=gather_scratch(dp_count, mp_count, layers),
        compiler_params=pltpu.CompilerParams(collective_id=0, has_side_effects=True),
        name="gather_blocks",
    )(block)


def scatter_kernel(
    parts_ref,
    out_ref,
    mine,
    twin,
    cross,
    rise,
    fall,
    last,
    total,
    load_sem,
    twin_send,
    cross_send,
    z_send,
    last_send,
    twin_recv,
    cross_recv,
    rise_recv,
    fall_recv,
    last_recv,
):
    index = lax.axis_index("dp")
    x = lax.axis_index("mp")
    layers = lax.axis_size("dp") // 4
    z, y, core = index // 4, (index // 2) % 2, index % 2
    rows, width = out_ref.shape
    to_a = (index + core * (2 - 4 * y), x + (1 - core) * (1 - 2 * x))
    to_b = (index + (1 - core) * (2 - 4 * y), x + core * (1 - 2 * x))
    to_twin = (index + 1 - 2 * core, x)
    to_up, to_down = (index + 4, x), (index - 4, x)
    has_up, has_down = z < layers - 1, z > 0

    def view(layer, da, db, which):
        dy = which * da + (1 - which) * db
        dx = (1 - which) * da + which * db
        yy, xx = y + dy * (1 - 2 * y), x + dx * (1 - 2 * x)
        row = (layer * 4 + yy * 2 + which) * rows
        return parts_ref.at[
            pl.ds(pl.multiple_of(row, rows), rows),
            pl.ds(pl.multiple_of(xx * width, width), width),
        ]

    def remote(source, target, send_sem, recv_sem, device):
        return pltpu.make_async_remote_copy(
            src_ref=source,
            dst_ref=target,
            send_sem=send_sem,
            recv_sem=recv_sem,
            device_id=device,
            device_id_type=MESH,
        )

    barrier = pltpu.get_barrier_semaphore()
    for peer in (to_a, to_b, to_twin):
        pl.semaphore_signal(barrier, inc=1, device_id=peer, device_id_type=MESH)

    @pl.when(has_up)
    def _():
        pl.semaphore_signal(barrier, inc=1, device_id=to_up, device_id_type=MESH)

    @pl.when(has_down)
    def _():
        pl.semaphore_signal(barrier, inc=1, device_id=to_down, device_id_type=MESH)

    def outward(run):
        for distance in range(layers - 1, 0, -1):
            for da in range(2):
                @pl.when(z + distance < layers)
                def _():
                    run(z + distance, da, True)

                @pl.when(z >= distance)
                def _():
                    run(z - distance, da, False)

    def home(run):
        for da in (1, 0):
            run(z, da, None)

    def load(layer, da, db):
        slot = (layer * 2 + da) * 2 + db
        return pltpu.make_async_copy(view(layer, da, db, core), mine.at[slot], load_sem.at[slot])

    def to_other_core(layer, da, db):
        slot = (layer * 2 + da) * 2 + db
        return remote(
            view(layer, da, db, 1 - core),
            twin.at[slot],
            twin_send.at[slot],
            twin_recv.at[slot],
            to_twin,
        )

    def to_cross(layer, da):
        pair = layer * 2 + da
        return remote(
            mine.at[pair * 2 + 1], cross.at[pair], cross_send.at[pair], cross_recv.at[pair], to_b
        )

    def upward(layer, da):
        pair = layer * 2 + da
        return remote(mine.at[pair * 2], rise.at[pair], z_send.at[pair], rise_recv.at[pair], to_up)

    def downward(layer, da):
        pair = layer * 2 + da
        return remote(
            mine.at[pair * 2], fall.at[pair], z_send.at[pair], fall_recv.at[pair], to_down
        )

    def to_last():
        return remote(mine.at[(z * 2 + 1) * 2], last, last_send, last_recv, to_a)

    def add(target, *sources):
        step = 16

        def body(turn, carry):
            at = pl.ds(pl.multiple_of(turn * step, step), step)
            value = sources[0][at, :].astype(jnp.float32)
            for source in sources[1:]:
                value = value + source[at, :].astype(jnp.float32)
            target[at, :] = value.astype(target.dtype)
            return carry

        lax.fori_loop(0, rows // step, body, 0)

    for db in (1, 0):
        outward(lambda layer, da, up: load(layer, da, db).start())
        home(lambda layer, da, up: load(layer, da, db).start())
    pl.semaphore_wait(barrier, 3 + has_up.astype(jnp.int32) + has_down.astype(jnp.int32))
    for db in (1, 0):
        outward(lambda layer, da, up: to_other_core(layer, da, db).start())
        home(lambda layer, da, up: to_other_core(layer, da, db).start())

    def pair_up(layer, da, up):
        slot = (layer * 2 + da) * 2 + 1
        load(layer, da, 1).wait()
        to_other_core(layer, da, 1).wait_recv()
        add(mine.at[slot], mine.at[slot], twin.at[slot])
        to_cross(layer, da).start()

    outward(pair_up)
    home(pair_up)

    def collect(layer, da, target):
        pair = layer * 2 + da
        load(layer, da, 0).wait()
        to_other_core(layer, da, 0).wait_recv()
        to_cross(layer, da).wait_recv()
        add(target, mine.at[pair * 2], twin.at[pair * 2], cross.at[pair])

    def pass_on(layer, da, up):
        pair = layer * 2 + da
        collect(layer, da, total)
        if up:
            @pl.when(has_down)
            def _():
                upward(layer, da).wait_recv()
                add(total, total, rise.at[pair])
        else:
            @pl.when(has_up)
            def _():
                downward(layer, da).wait_recv()
                add(total, total, fall.at[pair])
        add(mine.at[pair * 2], total)
        (upward if up else downward)(layer, da).start()

    outward(pass_on)

    def settle(layer, da, up):
        pair = layer * 2 + da
        target = total if da else out_ref
        collect(layer, da, target)

        @pl.when(has_down)
        def _():
            upward(layer, da).wait_recv()
            add(target, target, rise.at[pair])

        @pl.when(has_up)
        def _():
            downward(layer, da).wait_recv()
            add(target, target, fall.at[pair])

        if da:
            add(mine.at[pair * 2], total)
            to_last().start()

    home(settle)
    to_last().wait_recv()
    add(out_ref, out_ref, last)

    def finish(layer, da, up):
        to_other_core(layer, da, 0).wait_send()
        to_other_core(layer, da, 1).wait_send()
        to_cross(layer, da).wait_send()
        if up is not None:
            (upward if up else downward)(layer, da).wait_send()

    outward(finish)
    home(finish)
    to_last().wait_send()


def scatter_sum(parts):
    dp_count, mp_count = lax.axis_size("dp"), lax.axis_size("mp")
    rows, width = parts.shape[0] // dp_count, parts.shape[1] // mp_count
    if mp_count != 2 or dp_count % 4:
        halves = lax.psum_scatter(parts, "mp", scatter_dimension=1, tiled=True)
        return lax.psum_scatter(halves, "dp", scatter_dimension=0, tiled=True)
    pairs = dp_count // 2
    dma = pltpu.SemaphoreType.DMA
    block = (rows, width)
    return pl.pallas_call(
        scatter_kernel,
        out_shape=jax.ShapeDtypeStruct(block, jnp.float32),
        in_specs=[pl.BlockSpec(memory_space=pl.ANY)],
        out_specs=pl.BlockSpec(memory_space=pltpu.VMEM),
        scratch_shapes=[
            pltpu.VMEM((2 * pairs,) + block, jnp.bfloat16),
            pltpu.VMEM((2 * pairs,) + block, jnp.bfloat16),
            pltpu.VMEM((pairs,) + block, jnp.bfloat16),
            pltpu.VMEM((pairs,) + block, jnp.bfloat16),
            pltpu.VMEM((pairs,) + block, jnp.bfloat16),
            pltpu.VMEM(block, jnp.bfloat16),
            pltpu.VMEM(block, jnp.float32),
            dma((2 * pairs,)),
            dma((2 * pairs,)),
            dma((pairs,)),
            dma((pairs,)),
            dma,
            dma((2 * pairs,)),
            dma((pairs,)),
            dma((pairs,)),
            dma((pairs,)),
            dma,
        ],
        compiler_params=pltpu.CompilerParams(
            collective_id=1, has_side_effects=True, vmem_limit_bytes=40 * 1024 * 1024
        ),
        name="scatter_sum",
    )(parts.astype(jnp.bfloat16))


def attention(queries, keys, values, query_seg, query_row, key_seg, key_row, keep_mask):
    scale = HEAD_DIM ** (-0.5)
    scores = (
        lax.dot_general(
            queries, keys, (((1,), (1,)), ((), ())), preferred_element_type=jnp.float32
        )
        * scale
    )
    visible = (query_seg[:, None] == key_seg[None, :]) & (
        (keep_mask[None, :] == 1) | (query_row[:, None] == key_row[None, :])
    )
    masked = jnp.where(visible, scores, NEG)
    top = jnp.max(masked, axis=1, keepdims=True)
    weights = jnp.where(visible, jnp.exp(masked - top), 0.0)
    totals = jnp.sum(weights, axis=1, keepdims=True)
    mixed = jnp.dot(weights.astype(jnp.bfloat16), values, preferred_element_type=jnp.float32)
    return (mixed / totals).astype(jnp.bfloat16)


def local_any(
    tokens,
    lengths,
    keep_mask,
    routes,
    attention_gain,
    mixture_gain,
    query_gain,
    key_gain,
    query_weight,
    key_weight,
    value_weight,
    output_weight,
    router_weight,
    expert_gate,
    expert_up,
    expert_down,
):
    tok_rows = tokens.shape[0]
    dp_count = lax.axis_size("dp")
    dp_index = lax.axis_index("dp")
    mp_index = lax.axis_index("mp")
    local_width = query_weight.shape[1]
    local_heads = local_width // HEAD_DIM
    share = dp_count // local_heads
    part = dp_index % share
    total_rows = tok_rows * dp_count

    weight_rows = query_weight.shape[0]
    packed = jnp.stack([query_weight, key_weight, value_weight]).reshape(
        3, weight_rows, local_heads, HEAD_DIM
    )
    packed = packed.transpose(2, 1, 0, 3).reshape(local_heads, weight_rows, 3 * HEAD_DIM)
    packed = jnp.repeat(packed, share, axis=0)
    head_weight = lax.all_to_all(packed, "dp", split_axis=0, concat_axis=0, tiled=True)
    head_weight = head_weight.reshape(dp_count * weight_rows, 3 * HEAD_DIM)

    all_tokens, head_weight, late_weight = lax.optimization_barrier(
        (gather_blocks(tokens), head_weight, output_weight)
    )
    all_output_weight = lax.all_gather(late_weight, "dp", axis=1, tiled=True)
    xfloat = all_tokens.astype(jnp.float32)
    all_in = (
        xfloat * lax.rsqrt(jnp.mean(xfloat * xfloat, axis=1, keepdims=True) + EPS) * attention_gain
    ).astype(jnp.bfloat16)
    all_routes = lax.all_gather(routes, "dp", axis=0, tiled=True)
    all_gain = lax.all_gather(mixture_gain, "mp", axis=0, tiled=True)
    all_router = lax.all_gather(router_weight, "mp", axis=0, tiled=True)

    key_row = jnp.arange(total_rows, dtype=jnp.int32)
    key_seg, key_pos = segment_info(lengths, key_row)
    cos_table, sin_table = rope_tables(key_pos)

    def own(array):
        split = array.reshape((local_heads, share, tok_rows) + array.shape[1:])
        taken = lax.dynamic_index_in_dim(split, part, 1, keepdims=False)
        return taken.reshape((local_heads * tok_rows,) + array.shape[1:])

    projected = jnp.dot(all_in, head_weight, preferred_element_type=jnp.float32)
    queries = head_prep(
        own(projected[:, :HEAD_DIM]), query_gain, own(cos_table), own(sin_table)
    )
    keys = head_prep(projected[:, HEAD_DIM : 2 * HEAD_DIM], key_gain, cos_table, sin_table)
    values = projected[:, 2 * HEAD_DIM :].astype(jnp.bfloat16)
    attended = attention(
        queries, keys, values, own(key_seg), own(key_row), key_seg, key_row, keep_mask
    )
    groups = [[head * share + p for head in range(local_heads)] for p in range(share)]
    attended = lax.all_to_all(
        attended.reshape(local_heads, tok_rows, HEAD_DIM),
        "dp",
        split_axis=0,
        concat_axis=0,
        tiled=True,
        axis_index_groups=groups,
    )
    attended = attended.transpose(1, 0, 2).reshape(tok_rows, local_width)
    partial_out = jnp.dot(attended, all_output_weight, preferred_element_type=jnp.float32)
    summed_out = lax.psum_scatter(partial_out, "mp", scatter_dimension=1, tiled=True)
    residual = (tokens.astype(jnp.float32) + summed_out).astype(jnp.bfloat16)
    all_residual = gather_blocks(residual)
    hfloat = all_residual.astype(jnp.float32)
    inverse = lax.rsqrt(jnp.mean(hfloat * hfloat, axis=1, keepdims=True) + EPS)
    mixed_in = (hfloat * all_gain * inverse).astype(jnp.bfloat16)

    own_rows = lax.dynamic_slice_in_dim(all_residual, dp_index * tok_rows, tok_rows, 0)
    own_float = own_rows.astype(jnp.float32)
    own_inverse = lax.rsqrt(jnp.mean(own_float * own_float, axis=1, keepdims=True) + EPS)
    logits = (
        jnp.dot(own_float * all_gain, all_router, precision=lax.Precision.HIGHEST) * own_inverse
    )

    ids = jnp.arange(tok_rows, dtype=jnp.int32)
    earlier = (ids[:, None] < ids[None, :]).astype(jnp.bfloat16)
    slots = jnp.arange(CAP, dtype=jnp.int32)

    def chosen_slots(named):
        before = jnp.dot(
            named.astype(jnp.bfloat16).reshape(-1, tok_rows),
            earlier,
            preferred_element_type=jnp.float32,
        ).reshape(named.shape)
        place = jnp.where(named, before.astype(jnp.int32), -1)
        return place[:, :, None, :] == slots[None, None, :, None]

    exp_local = EXPERTS // dp_count
    gate_local = expert_gate[0]
    up_local = expert_up[0]
    down_local = expert_down[0]
    unit_count = gate_local.shape[1]
    held = max(1, unit_count // FF)
    units = unit_count // held
    first_expert = (mp_index * unit_count) // FF

    own_experts = dp_index * exp_local + first_expert + jnp.arange(held, dtype=jnp.int32)
    block_routes = all_routes.reshape(dp_count, tok_rows, TOPK)
    here = jnp.any(block_routes[:, None] == own_experts[None, :, None, None], axis=3)
    chosen = chosen_slots(here)
    select = chosen.astype(jnp.bfloat16).reshape(dp_count, held * CAP, tok_rows)
    rows_in = lax.dot_general(
        select,
        mixed_in.reshape(dp_count, tok_rows, D),
        (((2,), (1,)), ((0,), (0,))),
        preferred_element_type=jnp.float32,
    ).astype(jnp.bfloat16)
    rows_in = rows_in.reshape(dp_count, held, CAP, D)
    experts = jnp.arange(EXPERTS, dtype=jnp.int32)
    named = jnp.any(routes[:, :, None] == experts[None, None, :], axis=1)
    sigmoid_vals = jax.nn.sigmoid(logits) * named.astype(jnp.float32)
    route_weight = sigmoid_vals / jnp.sum(sigmoid_vals, axis=1, keepdims=True)
    all_weights = lax.all_gather(route_weight, "dp", axis=0, tiled=True)
    outs = []
    for index in range(held):
        rows = rows_in[:, index].reshape(dp_count * CAP, D)
        low, high = index * units, (index + 1) * units
        gate_val = jnp.dot(rows, gate_local[:, low:high], preferred_element_type=jnp.float32)
        up_val = jnp.dot(rows, up_local[:, low:high], preferred_element_type=jnp.float32)
        hidden = (jax.nn.silu(gate_val) * up_val).astype(jnp.bfloat16)
        out = jnp.dot(hidden, down_local[low:high], preferred_element_type=jnp.float32)
        outs.append(out.astype(jnp.bfloat16).reshape(dp_count, CAP, D))
    first_own = dp_index * exp_local + first_expert
    own_weights = lax.dynamic_slice_in_dim(all_weights, first_own, held, 1)
    own_weights = own_weights.reshape(dp_count, tok_rows, held).transpose(0, 2, 1)
    spread = jnp.where(chosen, own_weights[:, :, None, :], 0.0)
    spread_high = spread.astype(jnp.bfloat16)
    spread_low = (spread - spread_high.astype(jnp.float32)).astype(jnp.bfloat16)
    contract = (((1,), (1,)), ((0,), (0,)))
    both = jnp.concatenate([spread_high, spread_low], 2).reshape(
        dp_count, held * 2 * CAP, tok_rows
    )
    out_rows = jnp.concatenate(sum([[out, out] for out in outs], []), axis=1)
    parts = lax.dot_general(both, out_rows, contract, preferred_element_type=jnp.float32)
    mixture = scatter_sum(parts.reshape(total_rows, D))
    return (residual.astype(jnp.float32) + mixture).astype(jnp.bfloat16)


def row_starts(lengths_ref):
    ends, starts, total = [], [], 0
    for index in range(lengths_ref.shape[0]):
        starts.append(total)
        total = total + lengths_ref[index]
        ends.append(total)
    return ends, starts


def segment_of(row, ends):
    segment = (row >= ends[0]).astype(jnp.int32)
    for end in ends[1:]:
        segment = segment + (row >= end).astype(jnp.int32)
    return segment


def attend_kernel(
    lengths_ref,
    part_ref,
    tokens_ref,
    weight_ref,
    gain_ref,
    query_gain_ref,
    key_gain_ref,
    keep_ref,
    frequency_ref,
    cos_ref,
    sin_ref,
    out_ref,
    held,
    normed,
    keys,
    values,
    queries,
    start_cos,
    start_sin,
    load_sem,
):
    total, width = held.shape
    chunk = normed.shape[0]
    part = part_ref[0]
    rows = chunk // 2

    def load(index):
        at = pl.ds(pl.multiple_of(index * chunk, chunk), chunk)
        return pltpu.make_async_copy(tokens_ref.at[at, :], held.at[at, :], load_sem.at[index])

    for index in range(total // chunk):
        load(index).start()
    ends, starts = row_starts(lengths_ref)
    which = lax.broadcasted_iota(jnp.int32, (8, HEAD_DIM), 0)
    begin = jnp.zeros((8, HEAD_DIM), jnp.int32)
    for index, start in enumerate(starts):
        begin = jnp.where(which == index, start, begin)
    angle = begin.astype(jnp.float32) * frequency_ref[...]
    start_cos[...] = jnp.cos(angle)
    start_sin[...] = jnp.sin(angle)

    def turn(projected, head_gain, row, at):
        square = jnp.mean(projected * projected, axis=1, keepdims=True)
        value = projected * lax.rsqrt(square + EPS) * head_gain
        cos_s, sin_s = start_cos[0:1, :], start_sin[0:1, :]
        for index in range(1, len(starts)):
            past = row >= ends[index - 1]
            cos_s = jnp.where(past, start_cos[index : index + 1, :], cos_s)
            sin_s = jnp.where(past, start_sin[index : index + 1, :], sin_s)
        cos_g, sin_g = cos_ref[at, :], sin_ref[at, :]
        cos_t = cos_g * cos_s + sin_g * sin_s
        sin_t = sin_g * cos_s - cos_g * sin_s
        lane = lax.broadcasted_iota(jnp.int32, value.shape, 1)
        halves = pltpu.roll(value, HEAD_DIM // 2, 1)
        rotated = jnp.where(lane < HEAD_DIM // 2, -halves, halves)
        return (value * cos_t + rotated * sin_t).astype(jnp.bfloat16)

    def project(index, carry):
        load(index).wait()
        at = pl.ds(pl.multiple_of(index * chunk, chunk), chunk)
        x = held[at, :].astype(jnp.float32)
        inverse = lax.rsqrt(jnp.mean(x * x, axis=1, keepdims=True) + EPS)
        normed[...] = (x * inverse * gain_ref[...]).astype(jnp.bfloat16)
        both = jnp.dot(
            normed[...], weight_ref[:, HEAD_DIM:], preferred_element_type=jnp.float32
        )
        row = lax.broadcasted_iota(jnp.int32, (chunk, HEAD_DIM), 0) + index * chunk
        keys[at, :] = turn(both[:, :HEAD_DIM], key_gain_ref[...], row, at)
        values[at, :] = both[:, HEAD_DIM:].astype(jnp.bfloat16)
        mine = normed[pl.ds(pl.multiple_of(part * rows, rows), rows), :]
        asked = jnp.dot(mine, weight_ref[:, :HEAD_DIM], preferred_element_type=jnp.float32)
        first = pl.multiple_of(index * chunk + part * rows, rows)
        row = lax.broadcasted_iota(jnp.int32, (rows, HEAD_DIM), 0) + first
        queries[pl.ds(pl.multiple_of(index * rows, rows), rows), :] = turn(
            asked, query_gain_ref[...], row, pl.ds(first, rows)
        )
        return carry

    lax.fori_loop(0, total // chunk, project, 0)

    key_row = lax.broadcasted_iota(jnp.int32, (1, total), 1)
    key_seg = jnp.where(keep_ref[...] == 1, segment_of(key_row, ends), -1)
    scale = HEAD_DIM ** (-0.5) * 1.4426950408889634

    def attend(index, carry):
        at = pl.ds(pl.multiple_of(index * chunk, chunk), chunk)
        scores = lax.dot_general(
            queries[at, :], keys[...], (((1,), (1,)), ((), ())), preferred_element_type=jnp.float32
        )
        local_row = lax.broadcasted_iota(jnp.int32, (chunk, 1), 0)
        block = index * 2 + (local_row >= rows).astype(jnp.int32)
        row = (
            (block * 2 + part) * rows
            + local_row
            - (local_row >= rows).astype(jnp.int32) * rows
        )
        visible = (segment_of(row, ends) == key_seg) | (row == key_row)
        masked = jnp.where(visible, scores, NEG)
        top = jnp.max(masked, axis=1, keepdims=True)
        weights = jnp.exp2((masked - top) * scale)
        totals = jnp.sum(weights, axis=1, keepdims=True)
        mixed = jnp.dot(
            weights.astype(jnp.bfloat16), values[...], preferred_element_type=jnp.float32
        )
        out_ref[at, :] = (mixed / totals).astype(jnp.bfloat16)
        return carry

    lax.fori_loop(0, total // 2 // chunk, attend, 0)


def attend_local(
    all_tokens, head_weight, lengths, keep_mask, attention_gain, query_gain, key_gain, part
):
    total, width = all_tokens.shape
    halves = HEAD_DIM // 2
    chunk = 256
    exponent = np.arange(halves, dtype=np.float32) * np.float32(2.0 / HEAD_DIM)
    frequency = np.power(np.float32(ROPE_BASE), -exponent).astype(np.float32)
    frequency = np.concatenate([frequency, frequency])[None, :]
    angle = np.arange(total, dtype=np.float32)[:, None] * frequency
    cos_table = np.cos(angle.astype(np.float64)).astype(np.float32)
    sin_table = np.sin(angle.astype(np.float64)).astype(np.float32)
    smem = pl.BlockSpec(memory_space=pltpu.SMEM)
    vmem = pl.BlockSpec(memory_space=pltpu.VMEM)
    return pl.pallas_call(
        attend_kernel,
        out_shape=jax.ShapeDtypeStruct((total // 2, HEAD_DIM), jnp.bfloat16),
        in_specs=[smem, smem, pl.BlockSpec(memory_space=pl.ANY)] + [vmem] * 8,
        out_specs=vmem,
        scratch_shapes=[
            pltpu.VMEM((total, width), jnp.bfloat16),
            pltpu.VMEM((chunk, width), jnp.bfloat16),
            pltpu.VMEM((total, HEAD_DIM), jnp.bfloat16),
            pltpu.VMEM((total, HEAD_DIM), jnp.bfloat16),
            pltpu.VMEM((total // 2, HEAD_DIM), jnp.bfloat16),
            pltpu.VMEM((8, HEAD_DIM), jnp.float32),
            pltpu.VMEM((8, HEAD_DIM), jnp.float32),
            pltpu.SemaphoreType.DMA((total // chunk,)),
        ],
        compiler_params=pltpu.CompilerParams(vmem_limit_bytes=40 * 1024 * 1024),
        name="attend",
    )(
        lengths,
        part,
        all_tokens,
        head_weight,
        attention_gain[None, :],
        query_gain[None, :],
        key_gain[None, :],
        keep_mask[None, :],
        jnp.asarray(frequency),
        jnp.asarray(cos_table),
        jnp.asarray(sin_table),
    )


def layer_kernel(
    attended_ref,
    weight_ref,
    tokens_ref,
    routes_ref,
    router_ref,
    gain_ref,
    gate_ref,
    up_ref,
    down_ref,
    out_ref,
    gathered,
    sent_half,
    got_half,
    own,
    residual,
    all_routes,
    all_router,
    all_gain,
    held,
    mixed,
    gate,
    up,
    down,
    rows_in,
    hidden,
    wide,
    spread,
    twin,
    cross,
    rise,
    fall,
    last,
    swap_send,
    swap_recv,
    route_send,
    route_recv,
    pair_send,
    pair_recv,
    local_sem,
    gate_sem,
    up_sem,
    down_sem,
    first_sem,
    rise_sem,
    fall_sem,
    b_sem,
    hand_sem,
    block_recv,
    twin_send,
    cross_send,
    z_send,
    last_send,
    twin_recv,
    cross_recv,
    rise_recv,
    fall_recv,
    last_recv,
):
    index = lax.axis_index("dp")
    x = lax.axis_index("mp")
    dp_count = lax.axis_size("dp")
    layers = dp_count // 4
    heads = attended_ref.shape[0]
    core, chip = index % 2, index // 2
    z, y = index // 4, chip % 2
    rows, half = tokens_ref.shape
    width = 2 * half
    tile = 256
    held_count = rows_in.shape[0]
    units = hidden.shape[1]
    first_expert = index * (EXPERTS // dp_count) + x * held_count
    to_a = (index + core * (2 - 4 * y), x + (1 - core) * (1 - 2 * x))
    to_b = (index + (1 - core) * (2 - 4 * y), x + core * (1 - 2 * x))
    to_twin = (index + 1 - 2 * core, x)
    to_up, to_down = (index + 4, x), (index - 4, x)
    has_up, has_down = z < layers - 1, z > 0

    def remote(source, target, send_sem, recv_sem, device):
        return pltpu.make_async_remote_copy(
            src_ref=source,
            dst_ref=target,
            send_sem=send_sem,
            recv_sem=recv_sem,
            device_id=device,
            device_id_type=MESH,
        )

    def tiles(start, step, size):
        return pl.ds(pl.multiple_of(start + step * size, size), size)

    barrier = pltpu.get_barrier_semaphore()
    for step in range(1, dp_count):
        peer = lax.rem(index + step, dp_count)
        pl.semaphore_signal(barrier, inc=1, device_id=(peer, x), device_id_type=MESH)
    pl.semaphore_signal(barrier, inc=1, device_id=(index, 1 - x), device_id_type=MESH)

    load_wide = pltpu.make_async_copy(weight_ref, wide, local_sem.at[4])
    load_wide.start()

    def load_expert(expert):
        columns = tiles(0, expert, units)
        return (
            pltpu.make_async_copy(gate_ref.at[:, columns], gate.at[:, columns], gate_sem.at[expert]),
            pltpu.make_async_copy(up_ref.at[:, columns], up.at[:, columns], up_sem.at[expert]),
            pltpu.make_async_copy(down_ref.at[columns, :], down.at[columns, :], down_sem.at[expert]),
        )

    own_columns = tiles(0, chip, HEAD_DIM)
    own_half = tiles(0, x, half)

    def swap(step):
        other = lax.rem(chip + step, heads)
        return remote(
            attended_ref.at[other],
            gathered.at[:, own_columns],
            swap_send.at[step],
            swap_recv.at[step],
            (other * 2 + core, x),
        )

    def route(step):
        return remote(
            routes_ref,
            all_routes.at[index],
            route_send.at[step],
            route_recv.at[step],
            (lax.rem(index + step, dp_count), x),
        )

    across_x = (index, 1 - x)
    router_copy = remote(
        router_ref, all_router.at[own_half, :], pair_send.at[0], pair_recv.at[0], across_x
    )
    gain_copy = remote(
        gain_ref, all_gain.at[:, own_half], pair_send.at[1], pair_recv.at[1], across_x
    )

    def half_copy(turn):
        at = tiles(0, turn, tile)
        return remote(
            sent_half.at[:, at],
            got_half.at[:, at],
            pair_send.at[2 + turn],
            pair_recv.at[2 + turn],
            across_x,
        )

    keep = [
        pltpu.make_async_copy(
            attended_ref.at[chip], gathered.at[:, own_columns], local_sem.at[0]
        ),
        pltpu.make_async_copy(routes_ref, all_routes.at[index], local_sem.at[1]),
        pltpu.make_async_copy(router_ref, all_router.at[own_half, :], local_sem.at[2]),
        pltpu.make_async_copy(gain_ref, all_gain.at[:, own_half], local_sem.at[3]),
    ]
    for copy in keep:
        copy.start()
    pl.semaphore_wait(barrier, dp_count)
    for step in range(1, heads):
        swap(step).start()
    gain_copy.start()
    router_copy.start()
    for step in range(1, dp_count):
        route(step).start()
    for expert in range(held_count):
        for copy in load_expert(expert):
            copy.start()
    keep[0].wait()
    load_wide.wait()
    for step in range(1, heads):
        swap(step).wait_recv()

    def away(turn, carry):
        sent_half[:, tiles(0, turn, tile)] = jnp.dot(
            gathered[...],
            wide[:, tiles((1 - x) * half, turn, tile)],
            preferred_element_type=jnp.float32,
        )
        half_copy(turn).start()
        return carry

    lax.fori_loop(0, half // tile, away, 0)

    def stay(turn, carry):
        at = tiles(0, turn, tile)
        own[:, at] = tokens_ref[:, at].astype(jnp.float32) + jnp.dot(
            gathered[...],
            wide[:, tiles(x * half, turn, tile)],
            preferred_element_type=jnp.float32,
        )
        return carry

    lax.fori_loop(0, half // tile, stay, 0)

    def settle_tile(turn, carry):
        at = tiles(0, turn, tile)
        half_copy(turn).wait_recv()
        residual[:, at] = (own[:, at] + got_half[:, at]).astype(jnp.bfloat16)
        own[:, at] = residual[:, at].astype(jnp.float32)
        return carry

    lax.fori_loop(0, half // tile, settle_tile, 0)

    def place(layer, da, db, which):
        dy = which * da + (1 - which) * db
        dx = (1 - which) * da + which * db
        yy, xx = y + dy * (1 - 2 * y), x + dx * (1 - 2 * x)
        return layer * 4 + yy * 2 + which, xx

    def view(spot):
        return held.at[tiles(0, spot[0], rows), tiles(0, spot[1], half)]

    def send(spot, sem, device, own_block=False):
        return remote(
            residual if own_block else view(spot),
            view(spot),
            sem,
            block_recv.at[spot[0] * 2 + spot[1]],
            device,
        )

    def arrive(spot):
        send(spot, first_sem.at[1], to_twin).wait_recv()

    home_spot = place(z, 0, 0, core)
    keep_block = pltpu.make_async_copy(residual, view(home_spot), first_sem.at[1])
    first = send(home_spot, first_sem.at[0], to_a, True)

    def spread_out(layer, da, own_block, act):
        spot = place(layer, da, 0, core)
        slot = layer * 2 + da

        @pl.when((layer <= z) & has_up)
        def _():
            act(send(spot, rise_sem.at[slot], to_up, own_block))

        @pl.when((layer >= z) & has_down)
        def _():
            act(send(spot, fall_sem.at[slot], to_down, own_block))

        act(send(spot, b_sem.at[slot], to_b, own_block))
        act(send(spot, hand_sem.at[slot * 2], to_twin, own_block))

    def hand_over(layer, da, act):
        spot = place(layer, da, 1, core)
        act(send(spot, hand_sem.at[(layer * 2 + da) * 2 + 1], to_twin))

    start = lambda copy: copy.start()
    finish = lambda copy: copy.wait_send()

    earlier = (
        lax.broadcasted_iota(jnp.int32, (rows, rows), 0)
        < lax.broadcasted_iota(jnp.int32, (rows, rows), 1)
    ).astype(jnp.bfloat16)
    expert_id = lax.broadcasted_iota(jnp.int32, (EXPERTS, rows), 0)
    slot_id = lax.broadcasted_iota(jnp.int32, (CAP, rows), 0)

    def block_slots(block, logits, inverse):
        named_ids = all_routes[block]
        named = named_ids[0:1, :] == expert_id
        for k in range(1, TOPK):
            named = named | (named_ids[k : k + 1, :] == expert_id)
        logits_t = jnp.transpose(logits * inverse)[:EXPERTS]
        sigmoid = jnp.where(named, 1.0 / (1.0 + jnp.exp(-logits_t)), 0.0)
        route = sigmoid / jnp.sum(sigmoid, axis=0, keepdims=True)
        named_f = named.astype(jnp.float32)
        here, weight = [], []
        for expert in range(held_count):
            own = expert_id == first_expert + expert
            here.append(jnp.sum(jnp.where(own, named_f, 0.0), axis=0, keepdims=True))
            weight.append(jnp.sum(jnp.where(own, route, 0.0), axis=0, keepdims=True))
        stacked = jnp.concatenate(here + [jnp.zeros((8 - held_count, rows), jnp.float32)], 0)
        before = jnp.dot(
            stacked.astype(jnp.bfloat16), earlier, preferred_element_type=jnp.float32
        )
        slot_of = jnp.where(stacked > 0.5, before.astype(jnp.int32), -1)
        chosen = jnp.concatenate(
            [slot_of[expert : expert + 1, :] == slot_id for expert in range(held_count)], 0
        )
        weights = jnp.concatenate(
            [jnp.broadcast_to(w, (CAP, rows)) for w in weight], 0
        )
        spread_w = jnp.where(chosen, weights, 0.0)
        high = spread_w.astype(jnp.bfloat16)
        low = (spread_w - high.astype(jnp.float32)).astype(jnp.bfloat16)
        return chosen.astype(jnp.float32).astype(jnp.bfloat16), high, low

    chunk = 2 * rows

    def take(layer):
        for da in range(2):
            for db in range(2):
                arrive(place(layer, da, db, 1 - core))

        def one(step, carry):
            position = layer * 2 + step
            at = tiles(0, position, chunk)
            h = held[at, :].astype(jnp.float32)
            inverse = lax.rsqrt(jnp.mean(h * h, axis=1, keepdims=True) + EPS)
            mixed[...] = (h * all_gain[0:1, :] * inverse).astype(jnp.bfloat16)
            logits = jnp.dot(held[at, :], all_router[...], preferred_element_type=jnp.float32)
            logits = logits[:, :128] + logits[:, 128:]
            logits = logits + pltpu.roll(logits, EXPERTS, 1)
            chosen, spreads = [], []
            for side in range(2):
                part = slice(side * rows, (side + 1) * rows)
                pick, high, low = block_slots(position * 2 + side, logits[part], inverse[part])
                chosen.append(pick)
                spreads += [(high, side), (low, side)]
            empty = jnp.zeros_like(chosen[0])
            select = jnp.concatenate(
                [
                    jnp.concatenate([chosen[0], empty], 1),
                    jnp.concatenate([empty, chosen[1]], 1),
                ],
                0,
            )
            taken = jnp.dot(select, mixed[...], preferred_element_type=jnp.float32).astype(
                jnp.bfloat16
            )
            for side in range(2):
                for expert in range(held_count):
                    source = (side * held_count + expert) * CAP
                    rows_in[expert, tiles(0, position * 2 + side, CAP), :] = taken[
                        source : source + CAP
                    ]
            spread[position] = jnp.concatenate(
                [
                    jnp.concatenate([value, empty] if side == 0 else [empty, value], 1)
                    for value, side in spreads
                ],
                0,
            )
            return carry

        lax.fori_loop(0, 2, one, 0)

    first.start()
    spread_out(z, 0, True, start)
    keep_block.start()
    arrive(place(z, 1, 0, core))
    spread_out(z, 1, False, start)

    def both(distance, run):
        @pl.when(z >= distance)
        def _():
            run(z - distance)

        @pl.when(z + distance < layers)
        def _():
            run(z + distance)

    def onward(layer):
        for da in range(2):
            arrive(place(layer, da, 0, core))
            spread_out(layer, da, False, start)

    def over(layer):
        for da in range(2):
            arrive(place(layer, da, 1, core))
            hand_over(layer, da, start)

    keep_block.wait()
    for copy in keep[1:]:
        copy.wait()
    gain_copy.wait_recv()
    router_copy.wait_recv()
    for step in range(1, dp_count):
        route(step).wait_recv()
    for distance in range(1, layers):
        both(distance, onward)
        if distance == 1:
            over(z)
            take(z)
        else:
            both(distance - 1, over)
            both(distance - 1, take)
    both(layers - 1, over)
    both(layers - 1, take)

    for expert in range(held_count):
        load_gate, load_up, load_down = load_expert(expert)
        load_gate.wait()
        load_up.wait()

        def widen(turn, carry):
            columns = tiles(expert * units, turn, tile)
            gate_val = jnp.dot(
                rows_in[expert], gate[:, columns], preferred_element_type=jnp.float32
            )
            up_val = jnp.dot(rows_in[expert], up[:, columns], preferred_element_type=jnp.float32)
            silu = gate_val / (1.0 + jnp.exp(-gate_val))
            hidden[:, tiles(0, turn, tile)] = (silu * up_val).astype(jnp.bfloat16)
            return carry

        lax.fori_loop(0, units // tile, widen, 0)
        load_down.wait()
        slots = hidden.shape[0]

        def narrow(turn, carry):
            at = tiles(0, turn, tile)
            wide[expert * slots : (expert + 1) * slots, at] = jnp.dot(
                hidden[...],
                down[expert * units : (expert + 1) * units, at],
                preferred_element_type=jnp.float32,
            ).astype(jnp.bfloat16)
            return carry

        lax.fori_loop(0, width // tile, narrow, 0)

    first.wait_send()
    for turn in range(half // tile):
        half_copy(turn).wait_send()
    total = sent_half

    def sent(layer, carry):
        for da in range(2):
            spread_out(layer, da, False, finish)
            hand_over(layer, da, finish)
        return carry

    lax.fori_loop(0, layers, sent, 0)

    def combine(position):
        pieces = []
        for side in range(2):
            block = position * 2 + side
            pieces += [
                wide[tiles(expert * dp_count * CAP, block, CAP), :] for expert in range(held_count)
            ] * 2
        held[tiles(0, position, chunk), :] = lax.dot_general(
            spread[position],
            jnp.concatenate(pieces, 0),
            (((0,), (0,)), ((), ())),
            preferred_element_type=jnp.float32,
        ).astype(jnp.bfloat16)

    def mine(layer, da, db):
        return view(place(layer, da, db, core))

    def to_other_core(layer, da, db):
        slot = (layer * 2 + da) * 2 + db
        other = 1 - core
        return remote(
            view(place(layer, da, db, other)),
            twin.at[slot],
            twin_send.at[slot],
            twin_recv.at[slot],
            to_twin,
        )

    def to_cross(layer, da):
        pair = layer * 2 + da
        return remote(
            mine(layer, da, 1), cross.at[pair], cross_send.at[pair], cross_recv.at[pair], to_b
        )

    def upward(layer, da):
        pair = layer * 2 + da
        return remote(
            mine(layer, da, 0), rise.at[pair], z_send.at[pair], rise_recv.at[pair], to_up
        )

    def downward(layer, da):
        pair = layer * 2 + da
        return remote(
            mine(layer, da, 0), fall.at[pair], z_send.at[pair], fall_recv.at[pair], to_down
        )

    def to_last():
        return remote(mine(z, 1, 0), last, last_send, last_recv, to_a)

    def add(target, *sources):
        step = 32

        def body(turn, carry):
            at = tiles(0, turn, step)
            value = sources[0][at, :].astype(jnp.float32)
            for source in sources[1:]:
                value = value + source[at, :].astype(jnp.float32)
            target[at, :] = value.astype(target.dtype)
            return carry

        lax.fori_loop(0, rows // step, body, 0)

    inner = ((z == 1) | (z == 2)).astype(jnp.int32)
    below = (z < layers // 2).astype(jnp.int32)

    def ordered(step):
        step = jnp.asarray(step, jnp.int32)
        turned = step + inner * ((step == 2).astype(jnp.int32) - (step == 3).astype(jnp.int32))
        return turned + below * (layers - 1 - 2 * turned)

    def make(step, carry):
        layer = ordered(step)

        def one(side, inner_carry):
            combine(layer * 2 + side)
            return inner_carry

        lax.fori_loop(0, 2, one, 0)
        for db in (1, 0):
            for da in (1, 0):
                to_other_core(layer, da, db).start()
        return carry

    def pair_up(step):
        layer = ordered(step)
        for da in range(2):
            slot = (layer * 2 + da) * 2 + 1
            to_other_core(layer, da, 1).wait_recv()
            add(mine(layer, da, 1), mine(layer, da, 1), twin.at[slot])
            to_cross(layer, da).start()

    def make_and_pair(step, carry):
        make(step, 0)
        pair_up(step - 1)
        return carry

    make(0, 0)
    lax.fori_loop(1, layers, make_and_pair, 0)
    pair_up(layers - 1)

    def collect(layer, da, target):
        pair = layer * 2 + da
        to_other_core(layer, da, 0).wait_recv()
        to_cross(layer, da).wait_recv()
        add(target, mine(layer, da, 0), twin.at[pair * 2], cross.at[pair])

    def pass_on(step, carry):
        layer = ordered(step)
        rising = layer > z
        for da in range(2):
            pair = layer * 2 + da
            collect(layer, da, total)

            @pl.when(rising & has_down)
            def _():
                upward(layer, da).wait_recv()
                add(total, total, rise.at[pair])

            @pl.when(jnp.logical_not(rising) & has_up)
            def _():
                downward(layer, da).wait_recv()
                add(total, total, fall.at[pair])

            add(mine(layer, da, 0), total)

            @pl.when(rising)
            def _():
                upward(layer, da).start()

            @pl.when(jnp.logical_not(rising))
            def _():
                downward(layer, da).start()

        return carry

    lax.fori_loop(0, layers - 1, pass_on, 0)

    for da in (1, 0):
        pair = z * 2 + da
        collect(z, da, total)

        @pl.when(has_down)
        def _():
            upward(z, da).wait_recv()
            add(total, total, rise.at[pair])

        @pl.when(has_up)
        def _():
            downward(z, da).wait_recv()
            add(total, total, fall.at[pair])

        if da:
            add(mine(z, 1, 0), total)
            to_last().start()
    to_last().wait_recv()
    add(out_ref, own, total, last)

    def finish_layer(step, carry):
        layer = ordered(step)
        for da in range(2):
            to_other_core(layer, da, 0).wait_send()
            to_other_core(layer, da, 1).wait_send()
            to_cross(layer, da).wait_send()

            @pl.when(layer != z)
            def _():
                upward(layer, da).wait_send()

        return carry

    lax.fori_loop(0, layers, finish_layer, 0)
    to_last().wait_send()
    for step in range(1, heads):
        swap(step).wait_send()
    gain_copy.wait_send()
    router_copy.wait_send()
    for step in range(1, dp_count):
        route(step).wait_send()


def layer_call(attended, weight, tokens, routes, router, gain, gate, up, down):
    dp_count, mp_count = lax.axis_size("dp"), lax.axis_size("mp")
    rows, half = tokens.shape
    width = mp_count * half
    heads = attended.shape[0]
    layers = dp_count // 4
    pairs = dp_count // 2
    held_count = gate.shape[1] // FF
    dma = pltpu.SemaphoreType.DMA
    vmem = pl.BlockSpec(memory_space=pltpu.VMEM)
    hbm = pl.BlockSpec(memory_space=pltpu.HBM)
    block = (rows, half)
    narrow = jnp.bfloat16
    return pl.pallas_call(
        layer_kernel,
        out_shape=jax.ShapeDtypeStruct(block, narrow),
        in_specs=[vmem, hbm, vmem, vmem, vmem, vmem, hbm, hbm, hbm],
        out_specs=vmem,
        scratch_shapes=[
            pltpu.VMEM((rows, heads * HEAD_DIM), narrow),
            pltpu.VMEM(block, jnp.float32),
            pltpu.VMEM(block, jnp.float32),
            pltpu.VMEM(block, jnp.float32),
            pltpu.VMEM(block, narrow),
            pltpu.VMEM((dp_count,) + routes.shape, routes.dtype),
            pltpu.VMEM((width, router.shape[1]), narrow),
            pltpu.VMEM((gain.shape[0], width), jnp.float32),
            pltpu.VMEM((dp_count * rows, width), narrow),
            pltpu.VMEM((2 * rows, width), narrow),
            pltpu.VMEM(gate.shape, narrow),
            pltpu.VMEM(up.shape, narrow),
            pltpu.VMEM(down.shape, narrow),
            pltpu.VMEM((held_count, dp_count * CAP, width), narrow),
            pltpu.VMEM((dp_count * CAP, FF), narrow),
            pltpu.VMEM(weight.shape, narrow),
            pltpu.VMEM((dp_count // 2, 4 * held_count * CAP, 2 * rows), narrow),
            pltpu.VMEM((2 * pairs,) + block, narrow),
            pltpu.VMEM((pairs,) + block, narrow),
            pltpu.VMEM((pairs,) + block, narrow),
            pltpu.VMEM((pairs,) + block, narrow),
            pltpu.VMEM(block, narrow),
            dma((heads,)),
            dma((heads,)),
            dma((dp_count,)),
            dma((dp_count,)),
            dma((2 + half // 256,)),
            dma((2 + half // 256,)),
            dma((5,)),
            dma((held_count,)),
            dma((held_count,)),
            dma((held_count,)),
            dma((2,)),
            dma((layers * 2,)),
            dma((layers * 2,)),
            dma((layers * 2,)),
            dma((layers * 4,)),
            dma((dp_count * mp_count,)),
            dma((2 * pairs,)),
            dma((pairs,)),
            dma((pairs,)),
            dma,
            dma((2 * pairs,)),
            dma((pairs,)),
            dma((pairs,)),
            dma((pairs,)),
            dma,
        ],
        compiler_params=pltpu.CompilerParams(
            collective_id=2, has_side_effects=True, vmem_limit_bytes=60 * 1024 * 1024
        ),
        name="mixture_layer",
    )(attended, weight, tokens, routes, router, gain, gate, up, down)


def split_three(value):
    high = value.astype(jnp.bfloat16)
    rest = value - high.astype(jnp.float32)
    middle = rest.astype(jnp.bfloat16)
    low = (rest - middle.astype(jnp.float32)).astype(jnp.bfloat16)
    return high, middle, low


def local_paired(
    tokens,
    lengths,
    keep_mask,
    routes,
    attention_gain,
    mixture_gain,
    query_gain,
    key_gain,
    query_weight,
    key_weight,
    value_weight,
    output_weight,
    router_weight,
    expert_gate,
    expert_up,
    expert_down,
):
    tok_rows, half = tokens.shape
    dp_count = lax.axis_size("dp")
    dp_index = lax.axis_index("dp")
    mp_index = lax.axis_index("mp")
    local_heads = query_weight.shape[1] // HEAD_DIM
    share = dp_count // local_heads
    part = (dp_index % share).astype(jnp.int32).reshape(1)

    weight_rows = query_weight.shape[0]
    packed = jnp.stack([query_weight, key_weight, value_weight]).reshape(
        3, weight_rows, local_heads, HEAD_DIM
    )
    packed = packed.transpose(2, 1, 0, 3).reshape(local_heads, weight_rows, 3 * HEAD_DIM)
    packed = jnp.repeat(packed, share, axis=0)
    head_weight = lax.all_to_all(packed, "dp", split_axis=0, concat_axis=0, tiled=True)
    head_weight = head_weight.reshape(dp_count * weight_rows, 3 * HEAD_DIM)
    all_tokens, head_weight, late_weight = lax.optimization_barrier(
        (gather_blocks(tokens), head_weight, output_weight)
    )
    all_output_weight = lax.all_gather(late_weight, "dp", axis=1, tiled=True)
    attended = attend_local(
        all_tokens, head_weight, lengths, keep_mask, attention_gain, query_gain, key_gain, part
    )
    attended = attended.reshape(local_heads, tok_rows, HEAD_DIM)

    parts = split_three(mixture_gain[:, None] * router_weight)
    router = jnp.concatenate(parts + (jnp.zeros_like(parts[0]),), axis=1)
    routes_t = routes.T
    gain = jnp.broadcast_to(mixture_gain[None, :], (8, half))
    return layer_call(
        attended,
        all_output_weight,
        tokens,
        routes_t,
        router,
        gain,
        expert_gate[0],
        expert_up[0],
        expert_down[0],
    )


def local(*arrays):
    paired = lax.axis_size("mp") == 2 and lax.axis_size("dp") == 16
    return (local_paired if paired else local_any)(*arrays)


def solution(mesh):
    return jax.shard_map(
        local,
        mesh=mesh,
        in_specs=(
            P("dp", "mp"),
            P(),
            P(),
            P("dp", None),
            P(),
            P("mp"),
            P(),
            P(),
            P("dp", "mp"),
            P("dp", "mp"),
            P("dp", "mp"),
            P("mp", "dp"),
            P("mp", None),
            P("dp", None, "mp"),
            P("dp", None, "mp"),
            P("dp", "mp", None),
        ),
        out_specs=P("dp", "mp"),
        check_vma=False,
    )
```

```python
import jax
import jax.numpy as jnp
import numpy as np
from jax import lax
from jax.experimental import pallas as pl
from jax.experimental.pallas import tpu as pltpu
from jax.sharding import PartitionSpec as P

D = 2048
HEAD_DIM = 128
FF = 1024
EXPERTS = 64
TOPK = 8
CAP = 32


EPS = 1e-06
ROPE_BASE = 10000.0
NEG = -1e30


def rope_tables(position):
    halves = HEAD_DIM // 2
    exponent = jnp.arange(halves, dtype=jnp.float32) * (2.0 / HEAD_DIM)
    frequency = jnp.power(jnp.float32(ROPE_BASE), -exponent)
    angle = position.astype(jnp.float32)[:, None] * frequency[None, :]
    cos_table = jnp.cos(angle)
    sin_table = jnp.sin(angle)
    return (jnp.concatenate([cos_table, cos_table], 1), jnp.concatenate([sin_table, sin_table], 1))


def head_prep(projected, head_gain, cos_table, sin_table):
    row_count = projected.shape[0]
    per_head = projected.reshape(row_count, -1, HEAD_DIM)
    normed = (
        per_head * lax.rsqrt(jnp.mean(per_head * per_head, axis=2, keepdims=True) + EPS) * head_gain
    )
    halves = HEAD_DIM // 2
    rotated = jnp.concatenate([-normed[:, :, halves:], normed[:, :, :halves]], 2)
    turned = normed * cos_table[:, None, :] + rotated * sin_table[:, None, :]
    return turned.reshape(row_count, -1).astype(jnp.bfloat16)


def segment_info(lengths, global_row):
    count = jnp.arange(lengths.shape[0], dtype=jnp.int32)
    request_end = jnp.sum(jnp.where(count[None, :] <= count[:, None], lengths[None, :], 0), axis=1)
    request_start = request_end - lengths
    segment = jnp.sum((request_end[None, :] <= global_row[:, None]).astype(jnp.int32), axis=1)
    chosen = segment[:, None] == jnp.arange(lengths.shape[0], dtype=jnp.int32)[None, :]
    begin = jnp.sum(jnp.where(chosen, request_start[None, :], 0), axis=1)
    return (segment, global_row - begin)


MESH = pl.DeviceIdType.MESH


def greet_neighbours():
    index = lax.axis_index("dp")
    x = lax.axis_index("mp")
    layers = lax.axis_size("dp") // 4
    z, y = index // 4, (index // 2) % 2
    barrier = pltpu.get_barrier_semaphore()
    across_y, across_x = (index + 2 - 4 * y, x), (index, 1 - x)
    to_twin = (index + 1 - 2 * (index % 2), x)
    for peer in (across_y, across_x, to_twin):
        pl.semaphore_signal(barrier, inc=1, device_id=peer, device_id_type=MESH)
    has_up, has_down = z < layers - 1, z > 0

    @pl.when(has_up)
    def _():
        pl.semaphore_signal(barrier, inc=1, device_id=(index + 4, x), device_id_type=MESH)

    @pl.when(has_down)
    def _():
        pl.semaphore_signal(barrier, inc=1, device_id=(index - 4, x), device_id_type=MESH)

    pl.semaphore_wait(barrier, 3 + has_up.astype(jnp.int32) + has_down.astype(jnp.int32))


def gather_kernel(block_ref, out_ref, *sems):
    greet_neighbours()
    gather_steps(block_ref, out_ref, *sems)


def gather_steps(block_ref, out_ref, local_sem, a_sem, up_sem, down_sem, b_sem, twin_sem, recv_sem):
    index = lax.axis_index("dp")
    x = lax.axis_index("mp")
    layers = lax.axis_size("dp") // 4
    z, y, core = index // 4, (index // 2) % 2, index % 2
    rows, width = block_ref.shape
    to_a = (index + core * (2 - 4 * y), x + (1 - core) * (1 - 2 * x))
    to_b = (index + (1 - core) * (2 - 4 * y), x + core * (1 - 2 * x))
    to_twin = (index + 1 - 2 * core, x)
    to_up, to_down = (index + 4, x), (index - 4, x)

    def place(layer, da, db, which):
        dy = which * da + (1 - which) * db
        dx = (1 - which) * da + which * db
        yy, xx = y + dy * (1 - 2 * y), x + dx * (1 - 2 * x)
        return layer * 4 + yy * 2 + which, xx

    def view(spot):
        return out_ref.at[
            pl.ds(pl.multiple_of(spot[0] * rows, rows), rows),
            pl.ds(pl.multiple_of(spot[1] * width, width), width),
        ]

    def send(spot, sem, device, own=False):
        return pltpu.make_async_remote_copy(
            src_ref=block_ref if own else view(spot),
            dst_ref=view(spot),
            send_sem=sem,
            recv_sem=recv_sem.at[spot[0] * 2 + spot[1]],
            device_id=device,
            device_id_type=MESH,
        )

    def arrive(spot):
        send(spot, local_sem, to_twin).wait_recv()

    has_up, has_down = z < layers - 1, z > 0
    home = place(z, 0, 0, core)
    keep = pltpu.make_async_copy(block_ref, view(home), local_sem)
    first = send(home, a_sem, to_a, True)

    def spread(layer, da, own, act):
        spot = place(layer, da, 0, core)
        slot = layer * 2 + da

        @pl.when((layer <= z) & has_up)
        def _():
            act(send(spot, up_sem.at[slot], to_up, own))

        @pl.when((layer >= z) & has_down)
        def _():
            act(send(spot, down_sem.at[slot], to_down, own))

        act(send(spot, b_sem.at[slot], to_b, own))
        act(send(spot, twin_sem.at[slot * 2], to_twin, own))

    def hand_over(layer, da, act):
        spot = place(layer, da, 1, core)
        act(send(spot, twin_sem.at[(layer * 2 + da) * 2 + 1], to_twin))

    start = lambda copy: copy.start()
    finish = lambda copy: copy.wait_send()
    first.start()
    spread(z, 0, True, start)
    keep.start()
    arrive(place(z, 1, 0, core))
    spread(z, 1, False, start)

    def both(distance, run):
        for da in range(2):
            @pl.when(z >= distance)
            def _():
                run(z - distance, da)

            @pl.when(z + distance < layers)
            def _():
                run(z + distance, da)

    def onward(layer, da):
        arrive(place(layer, da, 0, core))
        spread(layer, da, False, start)

    def across(layer, da):
        arrive(place(layer, da, 1, core))
        hand_over(layer, da, start)

    for distance in range(1, layers):
        both(distance, onward)
        if distance == 1:
            for da in range(2):
                across(z, da)
        else:
            both(distance - 1, across)
    both(layers - 1, across)
    keep.wait()
    first.wait_send()
    for layer in range(layers):
        for da in range(2):
            spread(layer, da, False, finish)
            hand_over(layer, da, finish)
            for db in range(2):
                arrive(place(layer, da, db, 1 - core))


def gather_scratch(dp_count, mp_count, layers):
    dma = pltpu.SemaphoreType.DMA
    return [
        dma,
        dma,
        dma((layers * 2,)),
        dma((layers * 2,)),
        dma((layers * 2,)),
        dma((layers * 4,)),
        dma((dp_count * mp_count,)),
    ]


def gather_blocks(block):
    dp_count, mp_count = lax.axis_size("dp"), lax.axis_size("mp")
    rows, width = block.shape
    if mp_count != 2 or dp_count % 4:
        wide = lax.all_gather(block, "mp", axis=1, tiled=True)
        return lax.all_gather(wide, "dp", axis=0, tiled=True)
    layers = dp_count // 4
    return pl.pallas_call(
        gather_kernel,
        out_shape=jax.ShapeDtypeStruct((dp_count * rows, mp_count * width), block.dtype),
        in_specs=[pl.BlockSpec(memory_space=pl.ANY)],
        out_specs=pl.BlockSpec(memory_space=pl.ANY),
        scratch_shapes=gather_scratch(dp_count, mp_count, layers),
        compiler_params=pltpu.CompilerParams(collective_id=0, has_side_effects=True),
        name="gather_blocks",
    )(block)


def scatter_kernel(
    parts_ref,
    out_ref,
    mine,
    twin,
    cross,
    rise,
    fall,
    last,
    total,
    load_sem,
    twin_send,
    cross_send,
    z_send,
    last_send,
    twin_recv,
    cross_recv,
    rise_recv,
    fall_recv,
    last_recv,
):
    index = lax.axis_index("dp")
    x = lax.axis_index("mp")
    layers = lax.axis_size("dp") // 4
    z, y, core = index // 4, (index // 2) % 2, index % 2
    rows, width = out_ref.shape
    to_a = (index + core * (2 - 4 * y), x + (1 - core) * (1 - 2 * x))
    to_b = (index + (1 - core) * (2 - 4 * y), x + core * (1 - 2 * x))
    to_twin = (index + 1 - 2 * core, x)
    to_up, to_down = (index + 4, x), (index - 4, x)
    has_up, has_down = z < layers - 1, z > 0

    def view(layer, da, db, which):
        dy = which * da + (1 - which) * db
        dx = (1 - which) * da + which * db
        yy, xx = y + dy * (1 - 2 * y), x + dx * (1 - 2 * x)
        row = (layer * 4 + yy * 2 + which) * rows
        return parts_ref.at[
            pl.ds(pl.multiple_of(row, rows), rows),
            pl.ds(pl.multiple_of(xx * width, width), width),
        ]

    def remote(source, target, send_sem, recv_sem, device):
        return pltpu.make_async_remote_copy(
            src_ref=source,
            dst_ref=target,
            send_sem=send_sem,
            recv_sem=recv_sem,
            device_id=device,
            device_id_type=MESH,
        )

    barrier = pltpu.get_barrier_semaphore()
    for peer in (to_a, to_b, to_twin):
        pl.semaphore_signal(barrier, inc=1, device_id=peer, device_id_type=MESH)

    @pl.when(has_up)
    def _():
        pl.semaphore_signal(barrier, inc=1, device_id=to_up, device_id_type=MESH)

    @pl.when(has_down)
    def _():
        pl.semaphore_signal(barrier, inc=1, device_id=to_down, device_id_type=MESH)

    def outward(run):
        for distance in range(layers - 1, 0, -1):
            for da in range(2):
                @pl.when(z + distance < layers)
                def _():
                    run(z + distance, da, True)

                @pl.when(z >= distance)
                def _():
                    run(z - distance, da, False)

    def home(run):
        for da in (1, 0):
            run(z, da, None)

    def load(layer, da, db):
        slot = (layer * 2 + da) * 2 + db
        return pltpu.make_async_copy(view(layer, da, db, core), mine.at[slot], load_sem.at[slot])

    def to_other_core(layer, da, db):
        slot = (layer * 2 + da) * 2 + db
        return remote(
            view(layer, da, db, 1 - core),
            twin.at[slot],
            twin_send.at[slot],
            twin_recv.at[slot],
            to_twin,
        )

    def to_cross(layer, da):
        pair = layer * 2 + da
        return remote(
            mine.at[pair * 2 + 1], cross.at[pair], cross_send.at[pair], cross_recv.at[pair], to_b
        )

    def upward(layer, da):
        pair = layer * 2 + da
        return remote(mine.at[pair * 2], rise.at[pair], z_send.at[pair], rise_recv.at[pair], to_up)

    def downward(layer, da):
        pair = layer * 2 + da
        return remote(
            mine.at[pair * 2], fall.at[pair], z_send.at[pair], fall_recv.at[pair], to_down
        )

    def to_last():
        return remote(mine.at[(z * 2 + 1) * 2], last, last_send, last_recv, to_a)

    def add(target, *sources):
        step = 16

        def body(turn, carry):
            at = pl.ds(pl.multiple_of(turn * step, step), step)
            value = sources[0][at, :].astype(jnp.float32)
            for source in sources[1:]:
                value = value + source[at, :].astype(jnp.float32)
            target[at, :] = value.astype(target.dtype)
            return carry

        lax.fori_loop(0, rows // step, body, 0)

    for db in (1, 0):
        outward(lambda layer, da, up: load(layer, da, db).start())
        home(lambda layer, da, up: load(layer, da, db).start())
    pl.semaphore_wait(barrier, 3 + has_up.astype(jnp.int32) + has_down.astype(jnp.int32))
    for db in (1, 0):
        outward(lambda layer, da, up: to_other_core(layer, da, db).start())
        home(lambda layer, da, up: to_other_core(layer, da, db).start())

    def pair_up(layer, da, up):
        slot = (layer * 2 + da) * 2 + 1
        load(layer, da, 1).wait()
        to_other_core(layer, da, 1).wait_recv()
        add(mine.at[slot], mine.at[slot], twin.at[slot])
        to_cross(layer, da).start()

    outward(pair_up)
    home(pair_up)

    def collect(layer, da, target):
        pair = layer * 2 + da
        load(layer, da, 0).wait()
        to_other_core(layer, da, 0).wait_recv()
        to_cross(layer, da).wait_recv()
        add(target, mine.at[pair * 2], twin.at[pair * 2], cross.at[pair])

    def pass_on(layer, da, up):
        pair = layer * 2 + da
        collect(layer, da, total)
        if up:
            @pl.when(has_down)
            def _():
                upward(layer, da).wait_recv()
                add(total, total, rise.at[pair])
        else:
            @pl.when(has_up)
            def _():
                downward(layer, da).wait_recv()
                add(total, total, fall.at[pair])
        add(mine.at[pair * 2], total)
        (upward if up else downward)(layer, da).start()

    outward(pass_on)

    def settle(layer, da, up):
        pair = layer * 2 + da
        target = total if da else out_ref
        collect(layer, da, target)

        @pl.when(has_down)
        def _():
            upward(layer, da).wait_recv()
            add(target, target, rise.at[pair])

        @pl.when(has_up)
        def _():
            downward(layer, da).wait_recv()
            add(target, target, fall.at[pair])

        if da:
            add(mine.at[pair * 2], total)
            to_last().start()

    home(settle)
    to_last().wait_recv()
    add(out_ref, out_ref, last)

    def finish(layer, da, up):
        to_other_core(layer, da, 0).wait_send()
        to_other_core(layer, da, 1).wait_send()
        to_cross(layer, da).wait_send()
        if up is not None:
            (upward if up else downward)(layer, da).wait_send()

    outward(finish)
    home(finish)
    to_last().wait_send()


def scatter_sum(parts):
    dp_count, mp_count = lax.axis_size("dp"), lax.axis_size("mp")
    rows, width = parts.shape[0] // dp_count, parts.shape[1] // mp_count
    if mp_count != 2 or dp_count % 4:
        halves = lax.psum_scatter(parts, "mp", scatter_dimension=1, tiled=True)
        return lax.psum_scatter(halves, "dp", scatter_dimension=0, tiled=True)
    pairs = dp_count // 2
    dma = pltpu.SemaphoreType.DMA
    block = (rows, width)
    return pl.pallas_call(
        scatter_kernel,
        out_shape=jax.ShapeDtypeStruct(block, jnp.float32),
        in_specs=[pl.BlockSpec(memory_space=pl.ANY)],
        out_specs=pl.BlockSpec(memory_space=pltpu.VMEM),
        scratch_shapes=[
            pltpu.VMEM((2 * pairs,) + block, jnp.bfloat16),
            pltpu.VMEM((2 * pairs,) + block, jnp.bfloat16),
            pltpu.VMEM((pairs,) + block, jnp.bfloat16),
            pltpu.VMEM((pairs,) + block, jnp.bfloat16),
            pltpu.VMEM((pairs,) + block, jnp.bfloat16),
            pltpu.VMEM(block, jnp.bfloat16),
            pltpu.VMEM(block, jnp.float32),
            dma((2 * pairs,)),
            dma((2 * pairs,)),
            dma((pairs,)),
            dma((pairs,)),
            dma,
            dma((2 * pairs,)),
            dma((pairs,)),
            dma((pairs,)),
            dma((pairs,)),
            dma,
        ],
        compiler_params=pltpu.CompilerParams(
            collective_id=1, has_side_effects=True, vmem_limit_bytes=40 * 1024 * 1024
        ),
        name="scatter_sum",
    )(parts.astype(jnp.bfloat16))


def attention(queries, keys, values, query_seg, query_row, key_seg, key_row, keep_mask):
    scale = HEAD_DIM ** (-0.5)
    scores = (
        lax.dot_general(
            queries, keys, (((1,), (1,)), ((), ())), preferred_element_type=jnp.float32
        )
        * scale
    )
    visible = (query_seg[:, None] == key_seg[None, :]) & (
        (keep_mask[None, :] == 1) | (query_row[:, None] == key_row[None, :])
    )
    masked = jnp.where(visible, scores, NEG)
    top = jnp.max(masked, axis=1, keepdims=True)
    weights = jnp.where(visible, jnp.exp(masked - top), 0.0)
    totals = jnp.sum(weights, axis=1, keepdims=True)
    mixed = jnp.dot(weights.astype(jnp.bfloat16), values, preferred_element_type=jnp.float32)
    return (mixed / totals).astype(jnp.bfloat16)


def local_any(
    tokens,
    lengths,
    keep_mask,
    routes,
    attention_gain,
    mixture_gain,
    query_gain,
    key_gain,
    query_weight,
    key_weight,
    value_weight,
    output_weight,
    router_weight,
    expert_gate,
    expert_up,
    expert_down,
):
    tok_rows = tokens.shape[0]
    dp_count = lax.axis_size("dp")
    dp_index = lax.axis_index("dp")
    mp_index = lax.axis_index("mp")
    local_width = query_weight.shape[1]
    local_heads = local_width // HEAD_DIM
    share = dp_count // local_heads
    part = dp_index % share
    total_rows = tok_rows * dp_count

    weight_rows = query_weight.shape[0]
    packed = jnp.stack([query_weight, key_weight, value_weight]).reshape(
        3, weight_rows, local_heads, HEAD_DIM
    )
    packed = packed.transpose(2, 1, 0, 3).reshape(local_heads, weight_rows, 3 * HEAD_DIM)
    packed = jnp.repeat(packed, share, axis=0)
    head_weight = lax.all_to_all(packed, "dp", split_axis=0, concat_axis=0, tiled=True)
    head_weight = head_weight.reshape(dp_count * weight_rows, 3 * HEAD_DIM)

    all_tokens, head_weight, late_weight = lax.optimization_barrier(
        (gather_blocks(tokens), head_weight, output_weight)
    )
    all_output_weight = lax.all_gather(late_weight, "dp", axis=1, tiled=True)
    xfloat = all_tokens.astype(jnp.float32)
    all_in = (
        xfloat * lax.rsqrt(jnp.mean(xfloat * xfloat, axis=1, keepdims=True) + EPS) * attention_gain
    ).astype(jnp.bfloat16)
    all_routes = lax.all_gather(routes, "dp", axis=0, tiled=True)
    all_gain = lax.all_gather(mixture_gain, "mp", axis=0, tiled=True)
    all_router = lax.all_gather(router_weight, "mp", axis=0, tiled=True)

    key_row = jnp.arange(total_rows, dtype=jnp.int32)
    key_seg, key_pos = segment_info(lengths, key_row)
    cos_table, sin_table = rope_tables(key_pos)

    def own(array):
        split = array.reshape((local_heads, share, tok_rows) + array.shape[1:])
        taken = lax.dynamic_index_in_dim(split, part, 1, keepdims=False)
        return taken.reshape((local_heads * tok_rows,) + array.shape[1:])

    projected = jnp.dot(all_in, head_weight, preferred_element_type=jnp.float32)
    queries = head_prep(
        own(projected[:, :HEAD_DIM]), query_gain, own(cos_table), own(sin_table)
    )
    keys = head_prep(projected[:, HEAD_DIM : 2 * HEAD_DIM], key_gain, cos_table, sin_table)
    values = projected[:, 2 * HEAD_DIM :].astype(jnp.bfloat16)
    attended = attention(
        queries, keys, values, own(key_seg), own(key_row), key_seg, key_row, keep_mask
    )
    groups = [[head * share + p for head in range(local_heads)] for p in range(share)]
    attended = lax.all_to_all(
        attended.reshape(local_heads, tok_rows, HEAD_DIM),
        "dp",
        split_axis=0,
        concat_axis=0,
        tiled=True,
        axis_index_groups=groups,
    )
    attended = attended.transpose(1, 0, 2).reshape(tok_rows, local_width)
    partial_out = jnp.dot(attended, all_output_weight, preferred_element_type=jnp.float32)
    summed_out = lax.psum_scatter(partial_out, "mp", scatter_dimension=1, tiled=True)
    residual = (tokens.astype(jnp.float32) + summed_out).astype(jnp.bfloat16)
    all_residual = gather_blocks(residual)
    hfloat = all_residual.astype(jnp.float32)
    inverse = lax.rsqrt(jnp.mean(hfloat * hfloat, axis=1, keepdims=True) + EPS)
    mixed_in = (hfloat * all_gain * inverse).astype(jnp.bfloat16)

    own_rows = lax.dynamic_slice_in_dim(all_residual, dp_index * tok_rows, tok_rows, 0)
    own_float = own_rows.astype(jnp.float32)
    own_inverse = lax.rsqrt(jnp.mean(own_float * own_float, axis=1, keepdims=True) + EPS)
    logits = (
        jnp.dot(own_float * all_gain, all_router, precision=lax.Precision.HIGHEST) * own_inverse
    )

    ids = jnp.arange(tok_rows, dtype=jnp.int32)
    earlier = (ids[:, None] < ids[None, :]).astype(jnp.bfloat16)
    slots = jnp.arange(CAP, dtype=jnp.int32)

    def chosen_slots(named):
        before = jnp.dot(
            named.astype(jnp.bfloat16).reshape(-1, tok_rows),
            earlier,
            preferred_element_type=jnp.float32,
        ).reshape(named.shape)
        place = jnp.where(named, before.astype(jnp.int32), -1)
        return place[:, :, None, :] == slots[None, None, :, None]

    exp_local = EXPERTS // dp_count
    gate_local = expert_gate[0]
    up_local = expert_up[0]
    down_local = expert_down[0]
    unit_count = gate_local.shape[1]
    held = max(1, unit_count // FF)
    units = unit_count // held
    first_expert = (mp_index * unit_count) // FF

    own_experts = dp_index * exp_local + first_expert + jnp.arange(held, dtype=jnp.int32)
    block_routes = all_routes.reshape(dp_count, tok_rows, TOPK)
    here = jnp.any(block_routes[:, None] == own_experts[None, :, None, None], axis=3)
    chosen = chosen_slots(here)
    select = chosen.astype(jnp.bfloat16).reshape(dp_count, held * CAP, tok_rows)
    rows_in = lax.dot_general(
        select,
        mixed_in.reshape(dp_count, tok_rows, D),
        (((2,), (1,)), ((0,), (0,))),
        preferred_element_type=jnp.float32,
    ).astype(jnp.bfloat16)
    rows_in = rows_in.reshape(dp_count, held, CAP, D)
    experts = jnp.arange(EXPERTS, dtype=jnp.int32)
    named = jnp.any(routes[:, :, None] == experts[None, None, :], axis=1)
    sigmoid_vals = jax.nn.sigmoid(logits) * named.astype(jnp.float32)
    route_weight = sigmoid_vals / jnp.sum(sigmoid_vals, axis=1, keepdims=True)
    all_weights = lax.all_gather(route_weight, "dp", axis=0, tiled=True)
    outs = []
    for index in range(held):
        rows = rows_in[:, index].reshape(dp_count * CAP, D)
        low, high = index * units, (index + 1) * units
        gate_val = jnp.dot(rows, gate_local[:, low:high], preferred_element_type=jnp.float32)
        up_val = jnp.dot(rows, up_local[:, low:high], preferred_element_type=jnp.float32)
        hidden = (jax.nn.silu(gate_val) * up_val).astype(jnp.bfloat16)
        out = jnp.dot(hidden, down_local[low:high], preferred_element_type=jnp.float32)
        outs.append(out.astype(jnp.bfloat16).reshape(dp_count, CAP, D))
    first_own = dp_index * exp_local + first_expert
    own_weights = lax.dynamic_slice_in_dim(all_weights, first_own, held, 1)
    own_weights = own_weights.reshape(dp_count, tok_rows, held).transpose(0, 2, 1)
    spread = jnp.where(chosen, own_weights[:, :, None, :], 0.0)
    spread_high = spread.astype(jnp.bfloat16)
    spread_low = (spread - spread_high.astype(jnp.float32)).astype(jnp.bfloat16)
    contract = (((1,), (1,)), ((0,), (0,)))
    both = jnp.concatenate([spread_high, spread_low], 2).reshape(
        dp_count, held * 2 * CAP, tok_rows
    )
    out_rows = jnp.concatenate(sum([[out, out] for out in outs], []), axis=1)
    parts = lax.dot_general(both, out_rows, contract, preferred_element_type=jnp.float32)
    mixture = scatter_sum(parts.reshape(total_rows, D))
    return (residual.astype(jnp.float32) + mixture).astype(jnp.bfloat16)


def row_starts(lengths_ref):
    ends, starts, total = [], [], 0
    for index in range(lengths_ref.shape[0]):
        starts.append(total)
        total = total + lengths_ref[index]
        ends.append(total)
    return ends, starts


def segment_of(row, ends):
    segment = (row >= ends[0]).astype(jnp.int32)
    for end in ends[1:]:
        segment = segment + (row >= end).astype(jnp.int32)
    return segment


def front_kernel(
    lengths_ref,
    tokens_ref,
    query_ref,
    key_ref,
    value_ref,
    last_ref,
    gain_ref,
    query_gain_ref,
    key_gain_ref,
    keep_ref,
    frequency_ref,
    cos_ref,
    sin_ref,
    out_ref,
    all_last_ref,
    held,
    weight,
    normed,
    keys,
    values,
    queries,
    start_cos,
    start_sin,
    head_send,
    head_recv,
    head_hand_send,
    head_hand_recv,
    head_local,
    local_sem,
    a_sem,
    rise_sem,
    fall_sem,
    b_sem,
    hand_sem,
    block_recv,
    last_rise,
    last_fall,
    last_side,
    last_hand,
    last_recv,
):
    index = lax.axis_index("dp")
    x = lax.axis_index("mp")
    dp_count = lax.axis_size("dp")
    layers = dp_count // 4
    chips = dp_count // 2
    core, chip = index % 2, index // 2
    z, y = index // 4, chip % 2
    rows, half = tokens_ref.shape
    total = dp_count * rows
    chunk = 2 * rows
    to_a = (index + core * (2 - 4 * y), x + (1 - core) * (1 - 2 * x))
    to_b = (index + (1 - core) * (2 - 4 * y), x + core * (1 - 2 * x))
    to_twin = (index + 1 - 2 * core, x)
    to_side = (index + 2 - 4 * y, x)
    to_up, to_down = (index + 4, x), (index - 4, x)
    has_up, has_down = z < layers - 1, z > 0

    def remote(source, target, send_sem, recv_sem, device):
        return pltpu.make_async_remote_copy(
            src_ref=source,
            dst_ref=target,
            send_sem=send_sem,
            recv_sem=recv_sem,
            device_id=device,
            device_id_type=MESH,
        )

    def tiles(start, step, size):
        return pl.ds(pl.multiple_of(start + step * size, size), size)

    barrier = pltpu.get_barrier_semaphore()
    for step in range(1, chips):
        peer = lax.rem(chip + step, chips) * 2 + core
        pl.semaphore_signal(barrier, inc=1, device_id=(peer, x), device_id_type=MESH)
    for peer in (to_twin, (index, 1 - x)):
        pl.semaphore_signal(barrier, inc=1, device_id=peer, device_id_type=MESH)

    def place(layer, da, db, which):
        dy = which * da + (1 - which) * db
        dx = (1 - which) * da + which * db
        yy, xx = y + dy * (1 - 2 * y), x + dx * (1 - 2 * x)
        return layer * 4 + yy * 2 + which, xx

    def view(spot):
        return held.at[tiles(0, spot[0], rows), tiles(0, spot[1], half)]

    def send(spot, sem, device, own_block=False):
        return remote(
            tokens_ref if own_block else view(spot),
            view(spot),
            sem,
            block_recv.at[spot[0] * 2 + spot[1]],
            device,
        )

    def arrive(spot):
        send(spot, local_sem.at[0], to_twin).wait_recv()

    late = core == 0

    def spread_out(layer, da, own_block, act):
        spot = place(layer, da, 0, core)
        slot = layer * 2 + da
        along = jnp.logical_not(late) if da else jnp.bool_(True)

        @pl.when((layer <= z) & has_up & along)
        def _():
            act(send(spot, rise_sem.at[slot], to_up, own_block))

        @pl.when((layer >= z) & has_down & along)
        def _():
            act(send(spot, fall_sem.at[slot], to_down, own_block))

        if not da:
            @pl.when((layer == z) | late)
            def _():
                act(send(spot, a_sem.at[layer], to_a, own_block))

        act(send(spot, b_sem.at[slot], to_b, own_block))
        act(send(spot, hand_sem.at[slot * 2], to_twin, own_block))

    def hand_over(layer, da, act):
        spot = place(layer, da, 1, core)
        act(send(spot, hand_sem.at[(layer * 2 + da) * 2 + 1], to_twin))

    start = lambda copy: copy.start()
    finish = lambda copy: copy.wait_send()
    keep_block = pltpu.make_async_copy(tokens_ref, view(place(z, 0, 0, core)), local_sem.at[1])

    sources = (query_ref, key_ref, value_ref)

    def head_part(step, which):
        other = lax.rem(chip + step, chips)
        return remote(
            sources[which].at[:, tiles(0, other, HEAD_DIM)],
            weight.at[tiles(0, index, rows), which * HEAD_DIM : (which + 1) * HEAD_DIM],
            head_send.at[step * 3 + which],
            head_recv.at[step * 3 + which],
            (other * 2 + core, x),
        )

    def head_keep(which):
        return pltpu.make_async_copy(
            sources[which].at[:, tiles(0, chip, HEAD_DIM)],
            weight.at[tiles(0, index, rows), which * HEAD_DIM : (which + 1) * HEAD_DIM],
            head_local.at[which],
        )

    def head_hand(step):
        block = lax.rem(chip + step, chips) * 2 + core
        at = weight.at[tiles(0, block, rows), :]
        return remote(at, at, head_hand_send.at[step], head_hand_recv.at[step], to_twin)

    def last_view(layer, side, which):
        yy = y + side * (1 - 2 * y)
        return all_last_ref.at[:, tiles(0, layer * 4 + yy * 2 + which, rows)]

    def last_copy(layer, side, sem, device, own_block=False):
        target = last_view(layer, side, core)
        return remote(
            last_ref if own_block else target,
            target,
            sem,
            last_recv.at[(layer * 2 + side) * 2],
            device,
        )

    def last_to_side(layer, own_block=False):
        target = last_view(layer, 0, core)
        return remote(
            last_ref if own_block else target,
            target,
            last_side.at[layer],
            last_recv.at[(layer * 2 + 1) * 2],
            to_side,
        )

    def last_to_twin(layer, side, own_block=False):
        target = last_view(layer, side, core)
        return remote(
            last_ref if own_block else target,
            target,
            last_hand.at[layer * 2 + side],
            last_recv.at[(layer * 2 + side) * 2 + 1],
            to_twin,
        )

    last_keep = pltpu.make_async_copy(last_ref, last_view(z, 0, core), local_sem.at[2])

    def last_spread(layer, own_block, act):
        @pl.when((layer <= z) & has_up)
        def _():
            act(last_copy(layer, 0, last_rise.at[layer], to_up, own_block))

        @pl.when((layer >= z) & has_down)
        def _():
            act(last_copy(layer, 0, last_fall.at[layer], to_down, own_block))

        act(last_to_side(layer, own_block))
        act(last_to_twin(layer, 0, own_block))

    def last_onward(layer):
        last_copy(layer, 0, last_rise.at[layer], to_up).wait_recv()
        last_spread(layer, False, start)

    def last_over(layer):
        last_to_side(layer).wait_recv()
        last_to_twin(layer, 1).start()

    pl.semaphore_wait(barrier, chips + 1)
    spread_out(z, 0, True, start)
    for which in range(3):
        head_keep(which).start()
    for step in range(1, chips):
        for which in range(3):
            head_part(step, which).start()
    keep_block.start()
    last_keep.start()

    ends, starts = row_starts(lengths_ref)
    which_row = lax.broadcasted_iota(jnp.int32, (8, HEAD_DIM), 0)
    begin = jnp.zeros((8, HEAD_DIM), jnp.int32)
    for number, first_row in enumerate(starts):
        begin = jnp.where(which_row == number, first_row, begin)
    angle = begin.astype(jnp.float32) * frequency_ref[...]
    start_cos[...] = jnp.cos(angle)
    start_sin[...] = jnp.sin(angle)

    def turn(projected, head_gain, row, at):
        square = jnp.mean(projected * projected, axis=1, keepdims=True)
        value = projected * lax.rsqrt(square + EPS) * head_gain
        cos_s, sin_s = start_cos[0:1, :], start_sin[0:1, :]
        for number in range(1, len(starts)):
            past = row >= ends[number - 1]
            cos_s = jnp.where(past, start_cos[number : number + 1, :], cos_s)
            sin_s = jnp.where(past, start_sin[number : number + 1, :], sin_s)
        cos_g, sin_g = cos_ref[at, :], sin_ref[at, :]
        cos_t = cos_g * cos_s + sin_g * sin_s
        sin_t = sin_g * cos_s - cos_g * sin_s
        lane = lax.broadcasted_iota(jnp.int32, value.shape, 1)
        halves = pltpu.roll(value, HEAD_DIM // 2, 1)
        rotated = jnp.where(lane < HEAD_DIM // 2, -halves, halves)
        return (value * cos_t + rotated * sin_t).astype(jnp.bfloat16)

    def take(layer):
        for da in range(2):
            for db in range(2):
                arrive(place(layer, da, db, 1 - core))

        def project(step, carry):
            position = layer * 2 + step
            at = tiles(0, position, chunk)
            value = held[at, :].astype(jnp.float32)
            inverse = lax.rsqrt(jnp.mean(value * value, axis=1, keepdims=True) + EPS)
            normed[...] = (value * inverse * gain_ref[...]).astype(jnp.bfloat16)
            both_parts = jnp.dot(
                normed[...], weight[:, HEAD_DIM:], preferred_element_type=jnp.float32
            )
            row = lax.broadcasted_iota(jnp.int32, (chunk, HEAD_DIM), 0) + position * chunk
            keys[at, :] = turn(both_parts[:, :HEAD_DIM], key_gain_ref[...], row, at)
            values[at, :] = both_parts[:, HEAD_DIM:].astype(jnp.bfloat16)
            asked = jnp.dot(
                normed[tiles(0, core, rows), :],
                weight[:, :HEAD_DIM],
                preferred_element_type=jnp.float32,
            )
            own_at = tiles(0, position * 2 + core, rows)
            row = lax.broadcasted_iota(jnp.int32, (rows, HEAD_DIM), 0) + (
                (position * 2 + core) * rows
            )
            queries[tiles(0, position, rows), :] = turn(asked, query_gain_ref[...], row, own_at)
            return carry

        lax.fori_loop(0, 2, project, 0)

    def both(distance, run):
        @pl.when(z >= distance)
        def _():
            run(z - distance)

        @pl.when(z + distance < layers)
        def _():
            run(z + distance)

    def onward(layer):
        for da in range(2):
            arrive(place(layer, da, 0, core))
            spread_out(layer, da, False, start)

    def over(layer):
        for da in range(2):
            arrive(place(layer, da, 1, core))
            hand_over(layer, da, start)

    arrive(place(z, 1, 0, core))
    spread_out(z, 1, False, start)
    both(1, onward)
    over(z)
    for which in range(3):
        head_keep(which).wait()
    head_hand(0).start()
    for step in range(1, chips):
        for which in range(3):
            head_part(step, which).wait_recv()
    for step in range(1, chips):
        head_hand(step).start()
    both(2, onward)
    both(1, over)
    last_spread(z, True, start)
    keep_block.wait()
    for step in range(chips):
        head_hand(step).wait_recv()
    take(z)
    both(1, take)
    both(3, onward)
    both(1, last_onward)
    both(2, over)
    both(2, take)
    last_over(z)
    both(2, last_onward)
    both(3, over)
    both(3, take)
    both(1, last_over)
    both(3, last_onward)

    key_row = lax.broadcasted_iota(jnp.int32, (1, total), 1)
    key_seg = jnp.where(keep_ref[...] == 1, segment_of(key_row, ends), -1)
    scale = HEAD_DIM ** (-0.5) * 1.4426950408889634

    def attend(step, carry):
        at = tiles(0, step, chunk)
        scores = lax.dot_general(
            queries[at, :], keys[...], (((1,), (1,)), ((), ())), preferred_element_type=jnp.float32
        )
        local_row = lax.broadcasted_iota(jnp.int32, (chunk, 1), 0)
        second = (local_row >= rows).astype(jnp.int32)
        row = ((step * 2 + second) * 2 + core) * rows + local_row - second * rows
        visible = (segment_of(row, ends) == key_seg) | (row == key_row)
        masked = jnp.where(visible, scores, NEG)
        top = jnp.max(masked, axis=1, keepdims=True)
        weights = jnp.exp2((masked - top) * scale)
        totals = jnp.sum(weights, axis=1, keepdims=True)
        mixed = jnp.dot(
            weights.astype(jnp.bfloat16), values[...], preferred_element_type=jnp.float32
        )
        out_ref[at, :] = (mixed / totals).astype(jnp.bfloat16)
        return carry

    turns = total // 2 // chunk
    lax.fori_loop(0, turns // 2, attend, 0)
    both(2, last_over)
    lax.fori_loop(turns // 2, turns, attend, 0)
    both(3, last_over)

    last_keep.wait()

    def drain(layer, carry):
        for da in range(2):
            spread_out(layer, da, False, finish)
            hand_over(layer, da, finish)
            last_to_twin(layer, da).wait_recv()
        last_spread(layer, False, finish)
        last_to_twin(layer, 1).wait_send()
        return carry

    lax.fori_loop(0, layers, drain, 0)
    head_hand(0).wait_send()
    for step in range(1, chips):
        head_hand(step).wait_send()
        for which in range(3):
            head_part(step, which).wait_send()


def front_call(
    tokens,
    lengths,
    keep_mask,
    attention_gain,
    query_gain,
    key_gain,
    query_weight,
    key_weight,
    value_weight,
    output_weight,
):
    dp_count, mp_count = lax.axis_size("dp"), lax.axis_size("mp")
    rows, half = tokens.shape
    total, width = dp_count * rows, mp_count * half
    layers, chips = dp_count // 4, dp_count // 2
    halves = HEAD_DIM // 2
    exponent = np.arange(halves, dtype=np.float32) * np.float32(2.0 / HEAD_DIM)
    frequency = np.power(np.float32(ROPE_BASE), -exponent).astype(np.float32)
    frequency = np.concatenate([frequency, frequency])[None, :]
    angle = np.arange(total, dtype=np.float32)[:, None] * frequency
    cos_table = np.cos(angle.astype(np.float64)).astype(np.float32)
    sin_table = np.sin(angle.astype(np.float64)).astype(np.float32)
    smem = pl.BlockSpec(memory_space=pltpu.SMEM)
    vmem = pl.BlockSpec(memory_space=pltpu.VMEM)
    hbm = pl.BlockSpec(memory_space=pltpu.HBM)
    dma = pltpu.SemaphoreType.DMA
    narrow = jnp.bfloat16
    return pl.pallas_call(
        front_kernel,
        out_shape=(
            jax.ShapeDtypeStruct((total // 2, HEAD_DIM), narrow),
            jax.ShapeDtypeStruct((output_weight.shape[0], dp_count * rows), narrow),
        ),
        in_specs=[smem] + [hbm] * 5 + [vmem] * 7,
        out_specs=(vmem, hbm),
        scratch_shapes=[
            pltpu.VMEM((total, width), narrow),
            pltpu.VMEM((width, 3 * HEAD_DIM), narrow),
            pltpu.VMEM((2 * rows, width), narrow),
            pltpu.VMEM((total, HEAD_DIM), narrow),
            pltpu.VMEM((total, HEAD_DIM), narrow),
            pltpu.VMEM((total // 2, HEAD_DIM), narrow),
            pltpu.VMEM((8, HEAD_DIM), jnp.float32),
            pltpu.VMEM((8, HEAD_DIM), jnp.float32),
            dma((3 * chips,)),
            dma((3 * chips,)),
            dma((chips,)),
            dma((chips,)),
            dma((3,)),
            dma((3,)),
            dma((layers,)),
            dma((layers * 2,)),
            dma((layers * 2,)),
            dma((layers * 2,)),
            dma((layers * 4,)),
            dma((dp_count * mp_count,)),
            dma((layers,)),
            dma((layers,)),
            dma((layers,)),
            dma((layers * 2,)),
            dma((layers * 4,)),
        ],
        compiler_params=pltpu.CompilerParams(
            collective_id=3, has_side_effects=True, vmem_limit_bytes=40 * 1024 * 1024
        ),
        name="attention_layer",
    )(
        lengths,
        tokens,
        query_weight,
        key_weight,
        value_weight,
        output_weight,
        attention_gain[None, :],
        query_gain[None, :],
        key_gain[None, :],
        keep_mask[None, :],
        jnp.asarray(frequency),
        jnp.asarray(cos_table),
        jnp.asarray(sin_table),
    )


def layer_kernel(
    attended_ref,
    weight_ref,
    tokens_ref,
    routes_ref,
    router_ref,
    gain_ref,
    gate_ref,
    up_ref,
    down_ref,
    out_ref,
    gathered,
    sent_half,
    got_half,
    residual,
    all_routes,
    all_router,
    all_gain,
    held,
    mixed,
    gate,
    up,
    down,
    rows_in,
    hidden,
    wide,
    spread,
    twin,
    cross,
    rise,
    fall,
    last,
    swap_send,
    swap_recv,
    route_send,
    route_recv,
    pair_send,
    pair_recv,
    local_sem,
    gate_sem,
    up_sem,
    down_sem,
    first_sem,
    rise_sem,
    fall_sem,
    b_sem,
    hand_sem,
    block_recv,
    twin_send,
    cross_send,
    z_send,
    last_send,
    twin_recv,
    cross_recv,
    rise_recv,
    fall_recv,
    last_recv,
):
    index = lax.axis_index("dp")
    x = lax.axis_index("mp")
    dp_count = lax.axis_size("dp")
    layers = dp_count // 4
    heads = attended_ref.shape[0]
    core, chip = index % 2, index // 2
    z, y = index // 4, chip % 2
    rows, half = tokens_ref.shape
    width = 2 * half
    tile = 256
    held_count = rows_in.shape[0]
    units = hidden.shape[1]
    first_expert = index * (EXPERTS // dp_count) + x * held_count
    to_a = (index + core * (2 - 4 * y), x + (1 - core) * (1 - 2 * x))
    to_b = (index + (1 - core) * (2 - 4 * y), x + core * (1 - 2 * x))
    to_twin = (index + 1 - 2 * core, x)
    to_up, to_down = (index + 4, x), (index - 4, x)
    has_up, has_down = z < layers - 1, z > 0

    def remote(source, target, send_sem, recv_sem, device):
        return pltpu.make_async_remote_copy(
            src_ref=source,
            dst_ref=target,
            send_sem=send_sem,
            recv_sem=recv_sem,
            device_id=device,
            device_id_type=MESH,
        )

    def tiles(start, step, size):
        return pl.ds(pl.multiple_of(start + step * size, size), size)

    barrier = pltpu.get_barrier_semaphore()
    for step in range(1, dp_count):
        peer = lax.rem(index + step, dp_count)
        pl.semaphore_signal(barrier, inc=1, device_id=(peer, x), device_id_type=MESH)
    pl.semaphore_signal(barrier, inc=1, device_id=(index, 1 - x), device_id_type=MESH)

    load_wide = pltpu.make_async_copy(weight_ref, wide, local_sem.at[4])
    load_wide.start()

    def load_expert(expert):
        columns = tiles(0, expert, units)
        return (
            pltpu.make_async_copy(gate_ref.at[:, columns], gate.at[:, columns], gate_sem.at[expert]),
            pltpu.make_async_copy(up_ref.at[:, columns], up.at[:, columns], up_sem.at[expert]),
            pltpu.make_async_copy(down_ref.at[columns, :], down.at[columns, :], down_sem.at[expert]),
        )

    own_columns = tiles(0, chip, HEAD_DIM)
    own_half = tiles(0, x, half)

    def swap(step):
        other = lax.rem(chip + step, heads)
        return remote(
            attended_ref.at[other],
            gathered.at[:, own_columns],
            swap_send.at[step],
            swap_recv.at[step],
            (other * 2 + core, x),
        )

    def route(step):
        return remote(
            routes_ref,
            all_routes.at[index],
            route_send.at[step],
            route_recv.at[step],
            (lax.rem(index + step, dp_count), x),
        )

    across_x = (index, 1 - x)
    router_copy = remote(
        router_ref, all_router.at[own_half, :], pair_send.at[0], pair_recv.at[0], across_x
    )
    gain_copy = remote(
        gain_ref, all_gain.at[:, own_half], pair_send.at[1], pair_recv.at[1], across_x
    )

    def half_copy(turn):
        at = tiles(0, turn, tile)
        return remote(
            sent_half.at[:, at],
            got_half.at[:, at],
            pair_send.at[2 + turn],
            pair_recv.at[2 + turn],
            across_x,
        )

    keep = [
        pltpu.make_async_copy(
            attended_ref.at[chip], gathered.at[:, own_columns], local_sem.at[0]
        ),
        pltpu.make_async_copy(routes_ref, all_routes.at[index], local_sem.at[1]),
        pltpu.make_async_copy(router_ref, all_router.at[own_half, :], local_sem.at[2]),
        pltpu.make_async_copy(gain_ref, all_gain.at[:, own_half], local_sem.at[3]),
    ]
    for copy in keep:
        copy.start()
    pl.semaphore_wait(barrier, dp_count)
    for step in range(1, heads):
        swap(step).start()
    gain_copy.start()
    router_copy.start()
    for step in range(1, dp_count):
        route(step).start()
    for expert in range(held_count):
        for copy in load_expert(expert):
            copy.start()
    keep[0].wait()
    load_wide.wait()
    for step in range(1, heads):
        swap(step).wait_recv()

    def away(turn, carry):
        sent_half[:, tiles(0, turn, tile)] = jnp.dot(
            gathered[...],
            wide[:, tiles((1 - x) * half, turn, tile)],
            preferred_element_type=jnp.float32,
        )
        half_copy(turn).start()
        return carry

    lax.fori_loop(0, half // tile, away, 0)

    def stay(turn, carry):
        at = tiles(0, turn, tile)
        out_ref[:, at] = tokens_ref[:, at].astype(jnp.float32) + jnp.dot(
            gathered[...],
            wide[:, tiles(x * half, turn, tile)],
            preferred_element_type=jnp.float32,
        )
        return carry

    lax.fori_loop(0, half // tile, stay, 0)

    def settle_tile(turn, carry):
        at = tiles(0, turn, tile)
        half_copy(turn).wait_recv()
        residual[:, at] = (out_ref[:, at] + got_half[:, at]).astype(jnp.bfloat16)
        out_ref[:, at] = residual[:, at].astype(jnp.float32)
        return carry

    lax.fori_loop(0, half // tile, settle_tile, 0)

    def place(layer, da, db, which):
        dy = which * da + (1 - which) * db
        dx = (1 - which) * da + which * db
        yy, xx = y + dy * (1 - 2 * y), x + dx * (1 - 2 * x)
        return layer * 4 + yy * 2 + which, xx

    def view(spot):
        return held.at[tiles(0, spot[0], rows), tiles(0, spot[1], half)]

    def send(spot, sem, device, own_block=False):
        return remote(
            residual if own_block else view(spot),
            view(spot),
            sem,
            block_recv.at[spot[0] * 2 + spot[1]],
            device,
        )

    def arrive(spot):
        send(spot, first_sem.at[1], to_twin).wait_recv()

    home_spot = place(z, 0, 0, core)
    keep_block = pltpu.make_async_copy(residual, view(home_spot), first_sem.at[1])
    first = send(home_spot, first_sem.at[0], to_a, True)

    def spread_out(layer, da, own_block, act):
        spot = place(layer, da, 0, core)
        slot = layer * 2 + da

        @pl.when((layer <= z) & has_up)
        def _():
            act(send(spot, rise_sem.at[slot], to_up, own_block))

        @pl.when((layer >= z) & has_down)
        def _():
            act(send(spot, fall_sem.at[slot], to_down, own_block))

        act(send(spot, b_sem.at[slot], to_b, own_block))
        act(send(spot, hand_sem.at[slot * 2], to_twin, own_block))

    def hand_over(layer, da, act):
        spot = place(layer, da, 1, core)
        act(send(spot, hand_sem.at[(layer * 2 + da) * 2 + 1], to_twin))

    start = lambda copy: copy.start()
    finish = lambda copy: copy.wait_send()

    earlier = (
        lax.broadcasted_iota(jnp.int32, (rows, rows), 0)
        < lax.broadcasted_iota(jnp.int32, (rows, rows), 1)
    ).astype(jnp.bfloat16)
    expert_id = lax.broadcasted_iota(jnp.int32, (EXPERTS, rows), 0)
    slot_id = lax.broadcasted_iota(jnp.int32, (CAP, rows), 0)

    def block_slots(block, logits, inverse):
        named_ids = all_routes[block]
        named = named_ids[0:1, :] == expert_id
        for k in range(1, TOPK):
            named = named | (named_ids[k : k + 1, :] == expert_id)
        logits_t = jnp.transpose(logits * inverse)[:EXPERTS]
        sigmoid = jnp.where(named, 1.0 / (1.0 + jnp.exp(-logits_t)), 0.0)
        route = sigmoid / jnp.sum(sigmoid, axis=0, keepdims=True)
        named_f = named.astype(jnp.float32)
        here, weight = [], []
        for expert in range(held_count):
            own = expert_id == first_expert + expert
            here.append(jnp.sum(jnp.where(own, named_f, 0.0), axis=0, keepdims=True))
            weight.append(jnp.sum(jnp.where(own, route, 0.0), axis=0, keepdims=True))
        stacked = jnp.concatenate(here + [jnp.zeros((8 - held_count, rows), jnp.float32)], 0)
        before = jnp.dot(
            stacked.astype(jnp.bfloat16), earlier, preferred_element_type=jnp.float32
        )
        slot_of = jnp.where(stacked > 0.5, before.astype(jnp.int32), -1)
        chosen = jnp.concatenate(
            [slot_of[expert : expert + 1, :] == slot_id for expert in range(held_count)], 0
        )
        weights = jnp.concatenate(
            [jnp.broadcast_to(w, (CAP, rows)) for w in weight], 0
        )
        spread_w = jnp.where(chosen, weights, 0.0)
        high = spread_w.astype(jnp.bfloat16)
        low = (spread_w - high.astype(jnp.float32)).astype(jnp.bfloat16)
        return chosen.astype(jnp.float32).astype(jnp.bfloat16), high, low

    chunk = 2 * rows

    def take(layer):
        for da in range(2):
            for db in range(2):
                arrive(place(layer, da, db, 1 - core))

        def one(step, carry):
            position = layer * 2 + step
            at = tiles(0, position, chunk)
            h = held[at, :].astype(jnp.float32)
            inverse = lax.rsqrt(jnp.mean(h * h, axis=1, keepdims=True) + EPS)
            mixed[...] = (h * all_gain[0:1, :] * inverse).astype(jnp.bfloat16)
            logits = jnp.dot(held[at, :], all_router[...], preferred_element_type=jnp.float32)
            logits = logits[:, :128] + logits[:, 128:]
            logits = logits + pltpu.roll(logits, EXPERTS, 1)
            chosen, spreads = [], []
            for side in range(2):
                part = slice(side * rows, (side + 1) * rows)
                pick, high, low = block_slots(position * 2 + side, logits[part], inverse[part])
                chosen.append(pick)
                spreads += [(high, side), (low, side)]
            empty = jnp.zeros_like(chosen[0])
            select = jnp.concatenate(
                [
                    jnp.concatenate([chosen[0], empty], 1),
                    jnp.concatenate([empty, chosen[1]], 1),
                ],
                0,
            )
            taken = jnp.dot(select, mixed[...], preferred_element_type=jnp.float32).astype(
                jnp.bfloat16
            )
            for side in range(2):
                for expert in range(held_count):
                    source = (side * held_count + expert) * CAP
                    rows_in[expert, tiles(0, position * 2 + side, CAP), :] = taken[
                        source : source + CAP
                    ]
            spread[position] = jnp.concatenate(
                [
                    jnp.concatenate([value, empty] if side == 0 else [empty, value], 1)
                    for value, side in spreads
                ],
                0,
            )
            return carry

        lax.fori_loop(0, 2, one, 0)

    first.start()
    spread_out(z, 0, True, start)
    keep_block.start()
    arrive(place(z, 1, 0, core))
    spread_out(z, 1, False, start)

    def both(distance, run):
        @pl.when(z >= distance)
        def _():
            run(z - distance)

        @pl.when(z + distance < layers)
        def _():
            run(z + distance)

    def onward(layer):
        for da in range(2):
            arrive(place(layer, da, 0, core))
            spread_out(layer, da, False, start)

    def over(layer):
        for da in range(2):
            arrive(place(layer, da, 1, core))
            hand_over(layer, da, start)

    keep_block.wait()
    for copy in keep[1:]:
        copy.wait()
    gain_copy.wait_recv()
    router_copy.wait_recv()
    for step in range(1, dp_count):
        route(step).wait_recv()
    for distance in range(1, layers):
        both(distance, onward)
        if distance == 1:
            over(z)
            take(z)
        else:
            both(distance - 1, over)
            both(distance - 1, take)
    both(layers - 1, over)
    both(layers - 1, take)

    for expert in range(held_count):
        load_gate, load_up, load_down = load_expert(expert)
        load_gate.wait()
        load_up.wait()

        def widen(turn, carry):
            columns = tiles(expert * units, turn, tile)
            gate_val = jnp.dot(
                rows_in[expert], gate[:, columns], preferred_element_type=jnp.float32
            )
            up_val = jnp.dot(rows_in[expert], up[:, columns], preferred_element_type=jnp.float32)
            silu = gate_val / (1.0 + jnp.exp(-gate_val))
            hidden[:, tiles(0, turn, tile)] = (silu * up_val).astype(jnp.bfloat16)
            return carry

        lax.fori_loop(0, units // tile, widen, 0)
        load_down.wait()
        slots = hidden.shape[0]

        def narrow(turn, carry):
            at = tiles(0, turn, tile)
            wide[expert * slots : (expert + 1) * slots, at] = jnp.dot(
                hidden[...],
                down[expert * units : (expert + 1) * units, at],
                preferred_element_type=jnp.float32,
            ).astype(jnp.bfloat16)
            return carry

        lax.fori_loop(0, width // tile, narrow, 0)

    first.wait_send()
    for turn in range(half // tile):
        half_copy(turn).wait_send()
    total = sent_half

    def sent(layer, carry):
        for da in range(2):
            spread_out(layer, da, False, finish)
            hand_over(layer, da, finish)
        return carry

    lax.fori_loop(0, layers, sent, 0)

    def combine(position):
        pieces = []
        for side in range(2):
            block = position * 2 + side
            pieces += [
                wide[tiles(expert * dp_count * CAP, block, CAP), :] for expert in range(held_count)
            ] * 2
        held[tiles(0, position, chunk), :] = lax.dot_general(
            spread[position],
            jnp.concatenate(pieces, 0),
            (((0,), (0,)), ((), ())),
            preferred_element_type=jnp.float32,
        ).astype(jnp.bfloat16)

    def mine(layer, da, db):
        return view(place(layer, da, db, core))

    def to_other_core(layer, da, db):
        slot = (layer * 2 + da) * 2 + db
        other = 1 - core
        return remote(
            view(place(layer, da, db, other)),
            twin.at[slot],
            twin_send.at[slot],
            twin_recv.at[slot],
            to_twin,
        )

    def to_cross(layer, da):
        pair = layer * 2 + da
        return remote(
            mine(layer, da, 1), cross.at[pair], cross_send.at[pair], cross_recv.at[pair], to_b
        )

    def upward(layer, da):
        pair = layer * 2 + da
        return remote(
            mine(layer, da, 0), rise.at[pair], z_send.at[pair], rise_recv.at[pair], to_up
        )

    def downward(layer, da):
        pair = layer * 2 + da
        return remote(
            mine(layer, da, 0), fall.at[pair], z_send.at[pair], fall_recv.at[pair], to_down
        )

    def to_last():
        return remote(mine(z, 1, 0), last, last_send, last_recv, to_a)

    def add(target, *sources):
        step = 32

        def body(turn, carry):
            at = tiles(0, turn, step)
            value = sources[0][at, :].astype(jnp.float32)
            for source in sources[1:]:
                value = value + source[at, :].astype(jnp.float32)
            target[at, :] = value.astype(target.dtype)
            return carry

        lax.fori_loop(0, rows // step, body, 0)

    inner = ((z == 1) | (z == 2)).astype(jnp.int32)
    below = (z < layers // 2).astype(jnp.int32)

    def ordered(step):
        step = jnp.asarray(step, jnp.int32)
        turned = step + inner * ((step == 2).astype(jnp.int32) - (step == 3).astype(jnp.int32))
        return turned + below * (layers - 1 - 2 * turned)

    def make(step, carry):
        layer = ordered(step)

        def one(side, inner_carry):
            combine(layer * 2 + side)
            return inner_carry

        lax.fori_loop(0, 2, one, 0)
        for db in (1, 0):
            for da in (1, 0):
                to_other_core(layer, da, db).start()
        return carry

    def pair_up(step):
        layer = ordered(step)
        for da in range(2):
            slot = (layer * 2 + da) * 2 + 1
            to_other_core(layer, da, 1).wait_recv()
            add(mine(layer, da, 1), mine(layer, da, 1), twin.at[slot])
            to_cross(layer, da).start()

    def make_and_pair(step, carry):
        make(step, 0)
        pair_up(step - 1)
        return carry

    make(0, 0)
    lax.fori_loop(1, layers, make_and_pair, 0)
    pair_up(layers - 1)

    def collect(layer, da, target):
        pair = layer * 2 + da
        to_other_core(layer, da, 0).wait_recv()
        to_cross(layer, da).wait_recv()
        add(target, mine(layer, da, 0), twin.at[pair * 2], cross.at[pair])

    def pass_on(step, carry):
        layer = ordered(step)
        rising = layer > z
        for da in range(2):
            pair = layer * 2 + da
            collect(layer, da, total)

            @pl.when(rising & has_down)
            def _():
                upward(layer, da).wait_recv()
                add(total, total, rise.at[pair])

            @pl.when(jnp.logical_not(rising) & has_up)
            def _():
                downward(layer, da).wait_recv()
                add(total, total, fall.at[pair])

            add(mine(layer, da, 0), total)

            @pl.when(rising)
            def _():
                upward(layer, da).start()

            @pl.when(jnp.logical_not(rising))
            def _():
                downward(layer, da).start()

        return carry

    lax.fori_loop(0, layers - 1, pass_on, 0)

    for da in (1, 0):
        pair = z * 2 + da
        collect(z, da, total)

        @pl.when(has_down)
        def _():
            upward(z, da).wait_recv()
            add(total, total, rise.at[pair])

        @pl.when(has_up)
        def _():
            downward(z, da).wait_recv()
            add(total, total, fall.at[pair])

        if da:
            add(mine(z, 1, 0), total)
            to_last().start()
    to_last().wait_recv()
    add(out_ref, out_ref, total, last)

    def finish_layer(step, carry):
        layer = ordered(step)
        for da in range(2):
            to_other_core(layer, da, 0).wait_send()
            to_other_core(layer, da, 1).wait_send()
            to_cross(layer, da).wait_send()

            @pl.when(layer != z)
            def _():
                upward(layer, da).wait_send()

        return carry

    lax.fori_loop(0, layers, finish_layer, 0)
    to_last().wait_send()
    for step in range(1, heads):
        swap(step).wait_send()
    gain_copy.wait_send()
    router_copy.wait_send()
    for step in range(1, dp_count):
        route(step).wait_send()


def layer_call(attended, weight, tokens, routes, router, gain, gate, up, down):
    dp_count, mp_count = lax.axis_size("dp"), lax.axis_size("mp")
    rows, half = tokens.shape
    width = mp_count * half
    heads = attended.shape[0]
    layers = dp_count // 4
    pairs = dp_count // 2
    held_count = gate.shape[1] // FF
    dma = pltpu.SemaphoreType.DMA
    vmem = pl.BlockSpec(memory_space=pltpu.VMEM)
    hbm = pl.BlockSpec(memory_space=pltpu.HBM)
    block = (rows, half)
    narrow = jnp.bfloat16
    return pl.pallas_call(
        layer_kernel,
        out_shape=jax.ShapeDtypeStruct(block, jnp.float32),
        in_specs=[vmem, hbm, vmem, vmem, vmem, vmem, hbm, hbm, hbm],
        out_specs=vmem,
        scratch_shapes=[
            pltpu.VMEM((rows, heads * HEAD_DIM), narrow),
            pltpu.VMEM(block, jnp.float32),
            pltpu.VMEM(block, jnp.float32),
            pltpu.VMEM(block, narrow),
            pltpu.VMEM((dp_count,) + routes.shape, routes.dtype),
            pltpu.VMEM((width, router.shape[1]), narrow),
            pltpu.VMEM((gain.shape[0], width), jnp.float32),
            pltpu.VMEM((dp_count * rows, width), narrow),
            pltpu.VMEM((2 * rows, width), narrow),
            pltpu.VMEM(gate.shape, narrow),
            pltpu.VMEM(up.shape, narrow),
            pltpu.VMEM(down.shape, narrow),
            pltpu.VMEM((held_count, dp_count * CAP, width), narrow),
            pltpu.VMEM((dp_count * CAP, FF), narrow),
            pltpu.VMEM(weight.shape, narrow),
            pltpu.VMEM((dp_count // 2, 4 * held_count * CAP, 2 * rows), narrow),
            pltpu.VMEM((2 * pairs,) + block, narrow),
            pltpu.VMEM((pairs,) + block, narrow),
            pltpu.VMEM((pairs,) + block, narrow),
            pltpu.VMEM((pairs,) + block, narrow),
            pltpu.VMEM(block, narrow),
            dma((heads,)),
            dma((heads,)),
            dma((dp_count,)),
            dma((dp_count,)),
            dma((2 + half // 256,)),
            dma((2 + half // 256,)),
            dma((5,)),
            dma((held_count,)),
            dma((held_count,)),
            dma((held_count,)),
            dma((2,)),
            dma((layers * 2,)),
            dma((layers * 2,)),
            dma((layers * 2,)),
            dma((layers * 4,)),
            dma((dp_count * mp_count,)),
            dma((2 * pairs,)),
            dma((pairs,)),
            dma((pairs,)),
            dma,
            dma((2 * pairs,)),
            dma((pairs,)),
            dma((pairs,)),
            dma((pairs,)),
            dma,
        ],
        compiler_params=pltpu.CompilerParams(
            collective_id=2, has_side_effects=True, vmem_limit_bytes=60 * 1024 * 1024
        ),
        name="mixture_layer",
    )(attended, weight, tokens, routes, router, gain, gate, up, down)


def split_three(value):
    high = value.astype(jnp.bfloat16)
    rest = value - high.astype(jnp.float32)
    middle = rest.astype(jnp.bfloat16)
    low = (rest - middle.astype(jnp.float32)).astype(jnp.bfloat16)
    return high, middle, low


def local_paired(
    tokens,
    lengths,
    keep_mask,
    routes,
    attention_gain,
    mixture_gain,
    query_gain,
    key_gain,
    query_weight,
    key_weight,
    value_weight,
    output_weight,
    router_weight,
    expert_gate,
    expert_up,
    expert_down,
):
    tok_rows, half = tokens.shape
    local_heads = query_weight.shape[1] // HEAD_DIM
    attended, all_output_weight = front_call(
        tokens,
        lengths,
        keep_mask,
        attention_gain,
        query_gain,
        key_gain,
        query_weight,
        key_weight,
        value_weight,
        output_weight,
    )
    attended = attended.reshape(local_heads, tok_rows, HEAD_DIM)
    parts = split_three(mixture_gain[:, None] * router_weight)
    router = jnp.concatenate(parts + (jnp.zeros_like(parts[0]),), axis=1)
    routes_t = routes.T
    gain = jnp.broadcast_to(mixture_gain[None, :], (8, half))
    return layer_call(
        attended,
        all_output_weight,
        tokens,
        routes_t,
        router,
        gain,
        expert_gate[0],
        expert_up[0],
        expert_down[0],
    ).astype(jnp.bfloat16)


def local(*arrays):
    paired = lax.axis_size("mp") == 2 and lax.axis_size("dp") == 16
    return (local_paired if paired else local_any)(*arrays)


def solution(mesh):
    return jax.shard_map(
        local,
        mesh=mesh,
        in_specs=(
            P("dp", "mp"),
            P(),
            P(),
            P("dp", None),
            P(),
            P("mp"),
            P(),
            P(),
            P("dp", "mp"),
            P("dp", "mp"),
            P("dp", "mp"),
            P("mp", "dp"),
            P("mp", None),
            P("dp", None, "mp"),
            P("dp", None, "mp"),
            P("dp", "mp", None),
        ),
        out_specs=P("dp", "mp"),
        check_vma=False,
    )
```

```python
import jax
import jax.numpy as jnp
import numpy as np
from jax import lax
from jax.experimental import pallas as pl
from jax.experimental.pallas import tpu as pltpu
from jax.sharding import PartitionSpec as P

D = 2048
HEAD_DIM = 128
FF = 1024
EXPERTS = 64
TOPK = 8
CAP = 32


EPS = 1e-06
ROPE_BASE = 10000.0
NEG = -1e30


def rope_tables(position):
    halves = HEAD_DIM // 2
    exponent = jnp.arange(halves, dtype=jnp.float32) * (2.0 / HEAD_DIM)
    frequency = jnp.power(jnp.float32(ROPE_BASE), -exponent)
    angle = position.astype(jnp.float32)[:, None] * frequency[None, :]
    cos_table = jnp.cos(angle)
    sin_table = jnp.sin(angle)
    return (jnp.concatenate([cos_table, cos_table], 1), jnp.concatenate([sin_table, sin_table], 1))


def head_prep(projected, head_gain, cos_table, sin_table):
    row_count = projected.shape[0]
    per_head = projected.reshape(row_count, -1, HEAD_DIM)
    normed = (
        per_head * lax.rsqrt(jnp.mean(per_head * per_head, axis=2, keepdims=True) + EPS) * head_gain
    )
    halves = HEAD_DIM // 2
    rotated = jnp.concatenate([-normed[:, :, halves:], normed[:, :, :halves]], 2)
    turned = normed * cos_table[:, None, :] + rotated * sin_table[:, None, :]
    return turned.reshape(row_count, -1).astype(jnp.bfloat16)


def segment_info(lengths, global_row):
    count = jnp.arange(lengths.shape[0], dtype=jnp.int32)
    request_end = jnp.sum(jnp.where(count[None, :] <= count[:, None], lengths[None, :], 0), axis=1)
    request_start = request_end - lengths
    segment = jnp.sum((request_end[None, :] <= global_row[:, None]).astype(jnp.int32), axis=1)
    chosen = segment[:, None] == jnp.arange(lengths.shape[0], dtype=jnp.int32)[None, :]
    begin = jnp.sum(jnp.where(chosen, request_start[None, :], 0), axis=1)
    return (segment, global_row - begin)


MESH = pl.DeviceIdType.MESH


def greet_neighbours():
    index = lax.axis_index("dp")
    x = lax.axis_index("mp")
    layers = lax.axis_size("dp") // 4
    z, y = index // 4, (index // 2) % 2
    barrier = pltpu.get_barrier_semaphore()
    across_y, across_x = (index + 2 - 4 * y, x), (index, 1 - x)
    to_twin = (index + 1 - 2 * (index % 2), x)
    for peer in (across_y, across_x, to_twin):
        pl.semaphore_signal(barrier, inc=1, device_id=peer, device_id_type=MESH)
    has_up, has_down = z < layers - 1, z > 0

    @pl.when(has_up)
    def _():
        pl.semaphore_signal(barrier, inc=1, device_id=(index + 4, x), device_id_type=MESH)

    @pl.when(has_down)
    def _():
        pl.semaphore_signal(barrier, inc=1, device_id=(index - 4, x), device_id_type=MESH)

    pl.semaphore_wait(barrier, 3 + has_up.astype(jnp.int32) + has_down.astype(jnp.int32))


def gather_kernel(block_ref, out_ref, *sems):
    greet_neighbours()
    gather_steps(block_ref, out_ref, *sems)


def gather_steps(block_ref, out_ref, local_sem, a_sem, up_sem, down_sem, b_sem, twin_sem, recv_sem):
    index = lax.axis_index("dp")
    x = lax.axis_index("mp")
    layers = lax.axis_size("dp") // 4
    z, y, core = index // 4, (index // 2) % 2, index % 2
    rows, width = block_ref.shape
    to_a = (index + core * (2 - 4 * y), x + (1 - core) * (1 - 2 * x))
    to_b = (index + (1 - core) * (2 - 4 * y), x + core * (1 - 2 * x))
    to_twin = (index + 1 - 2 * core, x)
    to_up, to_down = (index + 4, x), (index - 4, x)

    def place(layer, da, db, which):
        dy = which * da + (1 - which) * db
        dx = (1 - which) * da + which * db
        yy, xx = y + dy * (1 - 2 * y), x + dx * (1 - 2 * x)
        return layer * 4 + yy * 2 + which, xx

    def view(spot):
        return out_ref.at[
            pl.ds(pl.multiple_of(spot[0] * rows, rows), rows),
            pl.ds(pl.multiple_of(spot[1] * width, width), width),
        ]

    def send(spot, sem, device, own=False):
        return pltpu.make_async_remote_copy(
            src_ref=block_ref if own else view(spot),
            dst_ref=view(spot),
            send_sem=sem,
            recv_sem=recv_sem.at[spot[0] * 2 + spot[1]],
            device_id=device,
            device_id_type=MESH,
        )

    def arrive(spot):
        send(spot, local_sem, to_twin).wait_recv()

    has_up, has_down = z < layers - 1, z > 0
    home = place(z, 0, 0, core)
    keep = pltpu.make_async_copy(block_ref, view(home), local_sem)
    first = send(home, a_sem, to_a, True)

    def spread(layer, da, own, act):
        spot = place(layer, da, 0, core)
        slot = layer * 2 + da

        @pl.when((layer <= z) & has_up)
        def _():
            act(send(spot, up_sem.at[slot], to_up, own))

        @pl.when((layer >= z) & has_down)
        def _():
            act(send(spot, down_sem.at[slot], to_down, own))

        act(send(spot, b_sem.at[slot], to_b, own))
        act(send(spot, twin_sem.at[slot * 2], to_twin, own))

    def hand_over(layer, da, act):
        spot = place(layer, da, 1, core)
        act(send(spot, twin_sem.at[(layer * 2 + da) * 2 + 1], to_twin))

    start = lambda copy: copy.start()
    finish = lambda copy: copy.wait_send()
    first.start()
    spread(z, 0, True, start)
    keep.start()
    arrive(place(z, 1, 0, core))
    spread(z, 1, False, start)

    def both(distance, run):
        for da in range(2):
            @pl.when(z >= distance)
            def _():
                run(z - distance, da)

            @pl.when(z + distance < layers)
            def _():
                run(z + distance, da)

    def onward(layer, da):
        arrive(place(layer, da, 0, core))
        spread(layer, da, False, start)

    def across(layer, da):
        arrive(place(layer, da, 1, core))
        hand_over(layer, da, start)

    for distance in range(1, layers):
        both(distance, onward)
        if distance == 1:
            for da in range(2):
                across(z, da)
        else:
            both(distance - 1, across)
    both(layers - 1, across)
    keep.wait()
    first.wait_send()
    for layer in range(layers):
        for da in range(2):
            spread(layer, da, False, finish)
            hand_over(layer, da, finish)
            for db in range(2):
                arrive(place(layer, da, db, 1 - core))


def gather_scratch(dp_count, mp_count, layers):
    dma = pltpu.SemaphoreType.DMA
    return [
        dma,
        dma,
        dma((layers * 2,)),
        dma((layers * 2,)),
        dma((layers * 2,)),
        dma((layers * 4,)),
        dma((dp_count * mp_count,)),
    ]


def gather_blocks(block):
    dp_count, mp_count = lax.axis_size("dp"), lax.axis_size("mp")
    rows, width = block.shape
    if mp_count != 2 or dp_count % 4:
        wide = lax.all_gather(block, "mp", axis=1, tiled=True)
        return lax.all_gather(wide, "dp", axis=0, tiled=True)
    layers = dp_count // 4
    return pl.pallas_call(
        gather_kernel,
        out_shape=jax.ShapeDtypeStruct((dp_count * rows, mp_count * width), block.dtype),
        in_specs=[pl.BlockSpec(memory_space=pl.ANY)],
        out_specs=pl.BlockSpec(memory_space=pl.ANY),
        scratch_shapes=gather_scratch(dp_count, mp_count, layers),
        compiler_params=pltpu.CompilerParams(collective_id=0, has_side_effects=True),
        name="gather_blocks",
    )(block)


def scatter_kernel(
    parts_ref,
    out_ref,
    mine,
    twin,
    cross,
    rise,
    fall,
    last,
    total,
    load_sem,
    twin_send,
    cross_send,
    z_send,
    last_send,
    twin_recv,
    cross_recv,
    rise_recv,
    fall_recv,
    last_recv,
):
    index = lax.axis_index("dp")
    x = lax.axis_index("mp")
    layers = lax.axis_size("dp") // 4
    z, y, core = index // 4, (index // 2) % 2, index % 2
    rows, width = out_ref.shape
    to_a = (index + core * (2 - 4 * y), x + (1 - core) * (1 - 2 * x))
    to_b = (index + (1 - core) * (2 - 4 * y), x + core * (1 - 2 * x))
    to_twin = (index + 1 - 2 * core, x)
    to_up, to_down = (index + 4, x), (index - 4, x)
    has_up, has_down = z < layers - 1, z > 0

    def view(layer, da, db, which):
        dy = which * da + (1 - which) * db
        dx = (1 - which) * da + which * db
        yy, xx = y + dy * (1 - 2 * y), x + dx * (1 - 2 * x)
        row = (layer * 4 + yy * 2 + which) * rows
        return parts_ref.at[
            pl.ds(pl.multiple_of(row, rows), rows),
            pl.ds(pl.multiple_of(xx * width, width), width),
        ]

    def remote(source, target, send_sem, recv_sem, device):
        return pltpu.make_async_remote_copy(
            src_ref=source,
            dst_ref=target,
            send_sem=send_sem,
            recv_sem=recv_sem,
            device_id=device,
            device_id_type=MESH,
        )

    barrier = pltpu.get_barrier_semaphore()
    for peer in (to_a, to_b, to_twin):
        pl.semaphore_signal(barrier, inc=1, device_id=peer, device_id_type=MESH)

    @pl.when(has_up)
    def _():
        pl.semaphore_signal(barrier, inc=1, device_id=to_up, device_id_type=MESH)

    @pl.when(has_down)
    def _():
        pl.semaphore_signal(barrier, inc=1, device_id=to_down, device_id_type=MESH)

    def outward(run):
        for distance in range(layers - 1, 0, -1):
            for da in range(2):
                @pl.when(z + distance < layers)
                def _():
                    run(z + distance, da, True)

                @pl.when(z >= distance)
                def _():
                    run(z - distance, da, False)

    def home(run):
        for da in (1, 0):
            run(z, da, None)

    def load(layer, da, db):
        slot = (layer * 2 + da) * 2 + db
        return pltpu.make_async_copy(view(layer, da, db, core), mine.at[slot], load_sem.at[slot])

    def to_other_core(layer, da, db):
        slot = (layer * 2 + da) * 2 + db
        return remote(
            view(layer, da, db, 1 - core),
            twin.at[slot],
            twin_send.at[slot],
            twin_recv.at[slot],
            to_twin,
        )

    def to_cross(layer, da):
        pair = layer * 2 + da
        return remote(
            mine.at[pair * 2 + 1], cross.at[pair], cross_send.at[pair], cross_recv.at[pair], to_b
        )

    def upward(layer, da):
        pair = layer * 2 + da
        return remote(mine.at[pair * 2], rise.at[pair], z_send.at[pair], rise_recv.at[pair], to_up)

    def downward(layer, da):
        pair = layer * 2 + da
        return remote(
            mine.at[pair * 2], fall.at[pair], z_send.at[pair], fall_recv.at[pair], to_down
        )

    def to_last():
        return remote(mine.at[(z * 2 + 1) * 2], last, last_send, last_recv, to_a)

    def add(target, *sources):
        step = 16

        def body(turn, carry):
            at = pl.ds(pl.multiple_of(turn * step, step), step)
            value = sources[0][at, :].astype(jnp.float32)
            for source in sources[1:]:
                value = value + source[at, :].astype(jnp.float32)
            target[at, :] = value.astype(target.dtype)
            return carry

        lax.fori_loop(0, rows // step, body, 0)

    for db in (1, 0):
        outward(lambda layer, da, up: load(layer, da, db).start())
        home(lambda layer, da, up: load(layer, da, db).start())
    pl.semaphore_wait(barrier, 3 + has_up.astype(jnp.int32) + has_down.astype(jnp.int32))
    for db in (1, 0):
        outward(lambda layer, da, up: to_other_core(layer, da, db).start())
        home(lambda layer, da, up: to_other_core(layer, da, db).start())

    def pair_up(layer, da, up):
        slot = (layer * 2 + da) * 2 + 1
        load(layer, da, 1).wait()
        to_other_core(layer, da, 1).wait_recv()
        add(mine.at[slot], mine.at[slot], twin.at[slot])
        to_cross(layer, da).start()

    outward(pair_up)
    home(pair_up)

    def collect(layer, da, target):
        pair = layer * 2 + da
        load(layer, da, 0).wait()
        to_other_core(layer, da, 0).wait_recv()
        to_cross(layer, da).wait_recv()
        add(target, mine.at[pair * 2], twin.at[pair * 2], cross.at[pair])

    def pass_on(layer, da, up):
        pair = layer * 2 + da
        collect(layer, da, total)
        if up:
            @pl.when(has_down)
            def _():
                upward(layer, da).wait_recv()
                add(total, total, rise.at[pair])
        else:
            @pl.when(has_up)
            def _():
                downward(layer, da).wait_recv()
                add(total, total, fall.at[pair])
        add(mine.at[pair * 2], total)
        (upward if up else downward)(layer, da).start()

    outward(pass_on)

    def settle(layer, da, up):
        pair = layer * 2 + da
        target = total if da else out_ref
        collect(layer, da, target)

        @pl.when(has_down)
        def _():
            upward(layer, da).wait_recv()
            add(target, target, rise.at[pair])

        @pl.when(has_up)
        def _():
            downward(layer, da).wait_recv()
            add(target, target, fall.at[pair])

        if da:
            add(mine.at[pair * 2], total)
            to_last().start()

    home(settle)
    to_last().wait_recv()
    add(out_ref, out_ref, last)

    def finish(layer, da, up):
        to_other_core(layer, da, 0).wait_send()
        to_other_core(layer, da, 1).wait_send()
        to_cross(layer, da).wait_send()
        if up is not None:
            (upward if up else downward)(layer, da).wait_send()

    outward(finish)
    home(finish)
    to_last().wait_send()


def scatter_sum(parts):
    dp_count, mp_count = lax.axis_size("dp"), lax.axis_size("mp")
    rows, width = parts.shape[0] // dp_count, parts.shape[1] // mp_count
    if mp_count != 2 or dp_count % 4:
        halves = lax.psum_scatter(parts, "mp", scatter_dimension=1, tiled=True)
        return lax.psum_scatter(halves, "dp", scatter_dimension=0, tiled=True)
    pairs = dp_count // 2
    dma = pltpu.SemaphoreType.DMA
    block = (rows, width)
    return pl.pallas_call(
        scatter_kernel,
        out_shape=jax.ShapeDtypeStruct(block, jnp.float32),
        in_specs=[pl.BlockSpec(memory_space=pl.ANY)],
        out_specs=pl.BlockSpec(memory_space=pltpu.VMEM),
        scratch_shapes=[
            pltpu.VMEM((2 * pairs,) + block, jnp.bfloat16),
            pltpu.VMEM((2 * pairs,) + block, jnp.bfloat16),
            pltpu.VMEM((pairs,) + block, jnp.bfloat16),
            pltpu.VMEM((pairs,) + block, jnp.bfloat16),
            pltpu.VMEM((pairs,) + block, jnp.bfloat16),
            pltpu.VMEM(block, jnp.bfloat16),
            pltpu.VMEM(block, jnp.float32),
            dma((2 * pairs,)),
            dma((2 * pairs,)),
            dma((pairs,)),
            dma((pairs,)),
            dma,
            dma((2 * pairs,)),
            dma((pairs,)),
            dma((pairs,)),
            dma((pairs,)),
            dma,
        ],
        compiler_params=pltpu.CompilerParams(
            collective_id=1, has_side_effects=True, vmem_limit_bytes=40 * 1024 * 1024
        ),
        name="scatter_sum",
    )(parts.astype(jnp.bfloat16))


def attention(queries, keys, values, query_seg, query_row, key_seg, key_row, keep_mask):
    scale = HEAD_DIM ** (-0.5)
    scores = (
        lax.dot_general(
            queries, keys, (((1,), (1,)), ((), ())), preferred_element_type=jnp.float32
        )
        * scale
    )
    visible = (query_seg[:, None] == key_seg[None, :]) & (
        (keep_mask[None, :] == 1) | (query_row[:, None] == key_row[None, :])
    )
    masked = jnp.where(visible, scores, NEG)
    top = jnp.max(masked, axis=1, keepdims=True)
    weights = jnp.where(visible, jnp.exp(masked - top), 0.0)
    totals = jnp.sum(weights, axis=1, keepdims=True)
    mixed = jnp.dot(weights.astype(jnp.bfloat16), values, preferred_element_type=jnp.float32)
    return (mixed / totals).astype(jnp.bfloat16)


def local_any(
    tokens,
    lengths,
    keep_mask,
    routes,
    attention_gain,
    mixture_gain,
    query_gain,
    key_gain,
    query_weight,
    key_weight,
    value_weight,
    output_weight,
    router_weight,
    expert_gate,
    expert_up,
    expert_down,
):
    tok_rows = tokens.shape[0]
    dp_count = lax.axis_size("dp")
    dp_index = lax.axis_index("dp")
    mp_index = lax.axis_index("mp")
    local_width = query_weight.shape[1]
    local_heads = local_width // HEAD_DIM
    share = dp_count // local_heads
    part = dp_index % share
    total_rows = tok_rows * dp_count

    weight_rows = query_weight.shape[0]
    packed = jnp.stack([query_weight, key_weight, value_weight]).reshape(
        3, weight_rows, local_heads, HEAD_DIM
    )
    packed = packed.transpose(2, 1, 0, 3).reshape(local_heads, weight_rows, 3 * HEAD_DIM)
    packed = jnp.repeat(packed, share, axis=0)
    head_weight = lax.all_to_all(packed, "dp", split_axis=0, concat_axis=0, tiled=True)
    head_weight = head_weight.reshape(dp_count * weight_rows, 3 * HEAD_DIM)

    all_tokens, head_weight, late_weight = lax.optimization_barrier(
        (gather_blocks(tokens), head_weight, output_weight)
    )
    all_output_weight = lax.all_gather(late_weight, "dp", axis=1, tiled=True)
    xfloat = all_tokens.astype(jnp.float32)
    all_in = (
        xfloat * lax.rsqrt(jnp.mean(xfloat * xfloat, axis=1, keepdims=True) + EPS) * attention_gain
    ).astype(jnp.bfloat16)
    all_routes = lax.all_gather(routes, "dp", axis=0, tiled=True)
    all_gain = lax.all_gather(mixture_gain, "mp", axis=0, tiled=True)
    all_router = lax.all_gather(router_weight, "mp", axis=0, tiled=True)

    key_row = jnp.arange(total_rows, dtype=jnp.int32)
    key_seg, key_pos = segment_info(lengths, key_row)
    cos_table, sin_table = rope_tables(key_pos)

    def own(array):
        split = array.reshape((local_heads, share, tok_rows) + array.shape[1:])
        taken = lax.dynamic_index_in_dim(split, part, 1, keepdims=False)
        return taken.reshape((local_heads * tok_rows,) + array.shape[1:])

    projected = jnp.dot(all_in, head_weight, preferred_element_type=jnp.float32)
    queries = head_prep(
        own(projected[:, :HEAD_DIM]), query_gain, own(cos_table), own(sin_table)
    )
    keys = head_prep(projected[:, HEAD_DIM : 2 * HEAD_DIM], key_gain, cos_table, sin_table)
    values = projected[:, 2 * HEAD_DIM :].astype(jnp.bfloat16)
    attended = attention(
        queries, keys, values, own(key_seg), own(key_row), key_seg, key_row, keep_mask
    )
    groups = [[head * share + p for head in range(local_heads)] for p in range(share)]
    attended = lax.all_to_all(
        attended.reshape(local_heads, tok_rows, HEAD_DIM),
        "dp",
        split_axis=0,
        concat_axis=0,
        tiled=True,
        axis_index_groups=groups,
    )
    attended = attended.transpose(1, 0, 2).reshape(tok_rows, local_width)
    partial_out = jnp.dot(attended, all_output_weight, preferred_element_type=jnp.float32)
    summed_out = lax.psum_scatter(partial_out, "mp", scatter_dimension=1, tiled=True)
    residual = (tokens.astype(jnp.float32) + summed_out).astype(jnp.bfloat16)
    all_residual = gather_blocks(residual)
    hfloat = all_residual.astype(jnp.float32)
    inverse = lax.rsqrt(jnp.mean(hfloat * hfloat, axis=1, keepdims=True) + EPS)
    mixed_in = (hfloat * all_gain * inverse).astype(jnp.bfloat16)

    own_rows = lax.dynamic_slice_in_dim(all_residual, dp_index * tok_rows, tok_rows, 0)
    own_float = own_rows.astype(jnp.float32)
    own_inverse = lax.rsqrt(jnp.mean(own_float * own_float, axis=1, keepdims=True) + EPS)
    logits = (
        jnp.dot(own_float * all_gain, all_router, precision=lax.Precision.HIGHEST) * own_inverse
    )

    ids = jnp.arange(tok_rows, dtype=jnp.int32)
    earlier = (ids[:, None] < ids[None, :]).astype(jnp.bfloat16)
    slots = jnp.arange(CAP, dtype=jnp.int32)

    def chosen_slots(named):
        before = jnp.dot(
            named.astype(jnp.bfloat16).reshape(-1, tok_rows),
            earlier,
            preferred_element_type=jnp.float32,
        ).reshape(named.shape)
        place = jnp.where(named, before.astype(jnp.int32), -1)
        return place[:, :, None, :] == slots[None, None, :, None]

    exp_local = EXPERTS // dp_count
    gate_local = expert_gate[0]
    up_local = expert_up[0]
    down_local = expert_down[0]
    unit_count = gate_local.shape[1]
    held = max(1, unit_count // FF)
    units = unit_count // held
    first_expert = (mp_index * unit_count) // FF

    own_experts = dp_index * exp_local + first_expert + jnp.arange(held, dtype=jnp.int32)
    block_routes = all_routes.reshape(dp_count, tok_rows, TOPK)
    here = jnp.any(block_routes[:, None] == own_experts[None, :, None, None], axis=3)
    chosen = chosen_slots(here)
    select = chosen.astype(jnp.bfloat16).reshape(dp_count, held * CAP, tok_rows)
    rows_in = lax.dot_general(
        select,
        mixed_in.reshape(dp_count, tok_rows, D),
        (((2,), (1,)), ((0,), (0,))),
        preferred_element_type=jnp.float32,
    ).astype(jnp.bfloat16)
    rows_in = rows_in.reshape(dp_count, held, CAP, D)
    experts = jnp.arange(EXPERTS, dtype=jnp.int32)
    named = jnp.any(routes[:, :, None] == experts[None, None, :], axis=1)
    sigmoid_vals = jax.nn.sigmoid(logits) * named.astype(jnp.float32)
    route_weight = sigmoid_vals / jnp.sum(sigmoid_vals, axis=1, keepdims=True)
    all_weights = lax.all_gather(route_weight, "dp", axis=0, tiled=True)
    outs = []
    for index in range(held):
        rows = rows_in[:, index].reshape(dp_count * CAP, D)
        low, high = index * units, (index + 1) * units
        gate_val = jnp.dot(rows, gate_local[:, low:high], preferred_element_type=jnp.float32)
        up_val = jnp.dot(rows, up_local[:, low:high], preferred_element_type=jnp.float32)
        hidden = (jax.nn.silu(gate_val) * up_val).astype(jnp.bfloat16)
        out = jnp.dot(hidden, down_local[low:high], preferred_element_type=jnp.float32)
        outs.append(out.astype(jnp.bfloat16).reshape(dp_count, CAP, D))
    first_own = dp_index * exp_local + first_expert
    own_weights = lax.dynamic_slice_in_dim(all_weights, first_own, held, 1)
    own_weights = own_weights.reshape(dp_count, tok_rows, held).transpose(0, 2, 1)
    spread = jnp.where(chosen, own_weights[:, :, None, :], 0.0)
    spread_high = spread.astype(jnp.bfloat16)
    spread_low = (spread - spread_high.astype(jnp.float32)).astype(jnp.bfloat16)
    contract = (((1,), (1,)), ((0,), (0,)))
    both = jnp.concatenate([spread_high, spread_low], 2).reshape(
        dp_count, held * 2 * CAP, tok_rows
    )
    out_rows = jnp.concatenate(sum([[out, out] for out in outs], []), axis=1)
    parts = lax.dot_general(both, out_rows, contract, preferred_element_type=jnp.float32)
    mixture = scatter_sum(parts.reshape(total_rows, D))
    return (residual.astype(jnp.float32) + mixture).astype(jnp.bfloat16)


def row_starts(lengths_ref):
    ends, starts, total = [], [], 0
    for index in range(lengths_ref.shape[0]):
        starts.append(total)
        total = total + lengths_ref[index]
        ends.append(total)
    return ends, starts


def segment_of(row, ends):
    segment = (row >= ends[0]).astype(jnp.int32)
    for end in ends[1:]:
        segment = segment + (row >= end).astype(jnp.int32)
    return segment


def front_kernel(
    lengths_ref,
    tokens_ref,
    query_ref,
    key_ref,
    value_ref,
    last_ref,
    gain_hbm,
    query_gain_hbm,
    key_gain_hbm,
    keep_hbm,
    frequency_hbm,
    cos_hbm,
    sin_hbm,
    out_ref,
    all_last_ref,
    gain_ref,
    query_gain_ref,
    key_gain_ref,
    keep_ref,
    frequency_ref,
    cos_ref,
    sin_ref,
    fetch_sem,
    held,
    mixed_rows,
    weight,
    normed,
    keys,
    values,
    queries,
    start_cos,
    start_sin,
    head_send,
    head_recv,
    head_hand_send,
    head_hand_recv,
    head_local,
    local_sem,
    a_sem,
    rise_sem,
    fall_sem,
    b_sem,
    hand_sem,
    block_recv,
    last_rise,
    last_fall,
    last_side,
    last_hand,
    last_recv,
    out_sem,
):
    index = lax.axis_index("dp")
    x = lax.axis_index("mp")
    dp_count = lax.axis_size("dp")
    layers = dp_count // 4
    chips = dp_count // 2
    core, chip = index % 2, index // 2
    z, y = index // 4, chip % 2
    rows, half = tokens_ref.shape
    total = dp_count * rows
    chunk = 2 * rows
    to_a = (index + core * (2 - 4 * y), x + (1 - core) * (1 - 2 * x))
    to_b = (index + (1 - core) * (2 - 4 * y), x + core * (1 - 2 * x))
    to_twin = (index + 1 - 2 * core, x)
    to_side = (index + 2 - 4 * y, x)
    to_up, to_down = (index + 4, x), (index - 4, x)
    has_up, has_down = z < layers - 1, z > 0

    def remote(source, target, send_sem, recv_sem, device):
        return pltpu.make_async_remote_copy(
            src_ref=source,
            dst_ref=target,
            send_sem=send_sem,
            recv_sem=recv_sem,
            device_id=device,
            device_id_type=MESH,
        )

    def tiles(start, step, size):
        return pl.ds(pl.multiple_of(start + step * size, size), size)

    barrier = pltpu.get_barrier_semaphore()
    for step in range(1, chips):
        peer = lax.rem(chip + step, chips) * 2 + core
        pl.semaphore_signal(barrier, inc=1, device_id=(peer, x), device_id_type=MESH)
    for peer in (to_twin, (index, 1 - x)):
        pl.semaphore_signal(barrier, inc=1, device_id=peer, device_id_type=MESH)

    fetches = [
        pltpu.make_async_copy(source, target, fetch_sem.at[number])
        for number, (source, target) in enumerate(
            (
                (frequency_hbm, frequency_ref),
                (gain_hbm, gain_ref),
                (query_gain_hbm, query_gain_ref),
                (key_gain_hbm, key_gain_ref),
                (keep_hbm, keep_ref),
                (cos_hbm, cos_ref),
                (sin_hbm, sin_ref),
            )
        )
    ]
    for fetch in fetches:
        fetch.start()

    def place(layer, da, db, which):
        dy = which * da + (1 - which) * db
        dx = (1 - which) * da + which * db
        yy, xx = y + dy * (1 - 2 * y), x + dx * (1 - 2 * x)
        return layer * 4 + yy * 2 + which, xx

    def view(spot):
        return held.at[tiles(0, spot[0], rows), tiles(0, spot[1], half)]

    def send(spot, sem, device, own_block=False):
        return remote(
            tokens_ref if own_block else view(spot),
            view(spot),
            sem,
            block_recv.at[spot[0] * 2 + spot[1]],
            device,
        )

    def arrive(spot):
        send(spot, local_sem.at[0], to_twin).wait_recv()

    late = core == 0

    def spread_out(layer, da, own_block, act):
        spot = place(layer, da, 0, core)
        slot = layer * 2 + da
        along = jnp.logical_not(late) if da else jnp.bool_(True)

        @pl.when((layer <= z) & has_up & along)
        def _():
            act(send(spot, rise_sem.at[slot], to_up, own_block))

        @pl.when((layer >= z) & has_down & along)
        def _():
            act(send(spot, fall_sem.at[slot], to_down, own_block))

        if not da:
            @pl.when((layer == z) | late)
            def _():
                act(send(spot, a_sem.at[layer], to_a, own_block))

        act(send(spot, b_sem.at[slot], to_b, own_block))
        act(send(spot, hand_sem.at[slot * 2], to_twin, own_block))

    def hand_over(layer, da, act):
        spot = place(layer, da, 1, core)
        act(send(spot, hand_sem.at[(layer * 2 + da) * 2 + 1], to_twin))

    start = lambda copy: copy.start()
    finish = lambda copy: copy.wait_send()
    keep_block = pltpu.make_async_copy(tokens_ref, view(place(z, 0, 0, core)), local_sem.at[1])

    sources = (query_ref, key_ref, value_ref)

    def head_part(step, which):
        other = lax.rem(chip + step, chips)
        return remote(
            sources[which].at[:, tiles(0, other, HEAD_DIM)],
            weight.at[tiles(0, index, rows), which * HEAD_DIM : (which + 1) * HEAD_DIM],
            head_send.at[step * 3 + which],
            head_recv.at[step * 3 + which],
            (other * 2 + core, x),
        )

    def head_keep(which):
        return pltpu.make_async_copy(
            sources[which].at[:, tiles(0, chip, HEAD_DIM)],
            weight.at[tiles(0, index, rows), which * HEAD_DIM : (which + 1) * HEAD_DIM],
            head_local.at[which],
        )

    def head_hand(step):
        block = lax.rem(chip + step, chips) * 2 + core
        at = weight.at[tiles(0, block, rows), :]
        return remote(at, at, head_hand_send.at[step], head_hand_recv.at[step], to_twin)

    def last_view(layer, side, which):
        yy = y + side * (1 - 2 * y)
        return all_last_ref.at[:, tiles(0, layer * 4 + yy * 2 + which, rows)]

    def last_copy(layer, side, sem, device, own_block=False):
        target = last_view(layer, side, core)
        return remote(
            last_ref if own_block else target,
            target,
            sem,
            last_recv.at[(layer * 2 + side) * 2],
            device,
        )

    def last_to_side(layer, own_block=False):
        target = last_view(layer, 0, core)
        return remote(
            last_ref if own_block else target,
            target,
            last_side.at[layer],
            last_recv.at[(layer * 2 + 1) * 2],
            to_side,
        )

    def last_to_twin(layer, side, own_block=False):
        target = last_view(layer, side, core)
        return remote(
            last_ref if own_block else target,
            target,
            last_hand.at[layer * 2 + side],
            last_recv.at[(layer * 2 + side) * 2 + 1],
            to_twin,
        )

    last_keep = pltpu.make_async_copy(last_ref, last_view(z, 0, core), local_sem.at[2])

    def last_spread(layer, own_block, act):
        @pl.when((layer <= z) & has_up)
        def _():
            act(last_copy(layer, 0, last_rise.at[layer], to_up, own_block))

        @pl.when((layer >= z) & has_down)
        def _():
            act(last_copy(layer, 0, last_fall.at[layer], to_down, own_block))

        act(last_to_side(layer, own_block))
        act(last_to_twin(layer, 0, own_block))

    def last_onward(layer):
        last_copy(layer, 0, last_rise.at[layer], to_up).wait_recv()
        last_spread(layer, False, start)

    def last_over(layer):
        last_to_side(layer).wait_recv()
        last_to_twin(layer, 1).start()

    pl.semaphore_wait(barrier, chips + 1)
    spread_out(z, 0, True, start)
    for which in range(3):
        head_keep(which).start()
    for step in range(1, chips):
        for which in range(3):
            head_part(step, which).start()
    keep_block.start()
    last_keep.start()

    fetches[0].wait()
    ends, starts = row_starts(lengths_ref)
    which_row = lax.broadcasted_iota(jnp.int32, (8, HEAD_DIM), 0)
    begin = jnp.zeros((8, HEAD_DIM), jnp.int32)
    for number, first_row in enumerate(starts):
        begin = jnp.where(which_row == number, first_row, begin)
    angle = begin.astype(jnp.float32) * frequency_ref[...]
    start_cos[...] = jnp.cos(angle)
    start_sin[...] = jnp.sin(angle)

    def turn(projected, head_gain, row, at):
        square = jnp.mean(projected * projected, axis=1, keepdims=True)
        value = projected * lax.rsqrt(square + EPS) * head_gain
        cos_s, sin_s = start_cos[0:1, :], start_sin[0:1, :]
        for number in range(1, len(starts)):
            past = row >= ends[number - 1]
            cos_s = jnp.where(past, start_cos[number : number + 1, :], cos_s)
            sin_s = jnp.where(past, start_sin[number : number + 1, :], sin_s)
        cos_g, sin_g = cos_ref[at, :], sin_ref[at, :]
        cos_t = cos_g * cos_s + sin_g * sin_s
        sin_t = sin_g * cos_s - cos_g * sin_s
        lane = lax.broadcasted_iota(jnp.int32, value.shape, 1)
        halves = pltpu.roll(value, HEAD_DIM // 2, 1)
        rotated = jnp.where(lane < HEAD_DIM // 2, -halves, halves)
        return (value * cos_t + rotated * sin_t).astype(jnp.bfloat16)

    def take(layer):
        for da in range(2):
            for db in range(2):
                arrive(place(layer, da, db, 1 - core))

        def project(step, carry):
            position = layer * 2 + step
            at = tiles(0, position, chunk)
            value = held[at, :].astype(jnp.float32)
            inverse = lax.rsqrt(jnp.mean(value * value, axis=1, keepdims=True) + EPS)
            normed[...] = (value * inverse * gain_ref[...]).astype(jnp.bfloat16)
            both_parts = jnp.dot(
                normed[...], weight[:, HEAD_DIM:], preferred_element_type=jnp.float32
            )
            row = lax.broadcasted_iota(jnp.int32, (chunk, HEAD_DIM), 0) + position * chunk
            keys[at, :] = turn(both_parts[:, :HEAD_DIM], key_gain_ref[...], row, at)
            values[at, :] = both_parts[:, HEAD_DIM:].astype(jnp.bfloat16)
            asked = jnp.dot(
                normed[tiles(0, core, rows), :],
                weight[:, :HEAD_DIM],
                preferred_element_type=jnp.float32,
            )
            own_at = tiles(0, position * 2 + core, rows)
            row = lax.broadcasted_iota(jnp.int32, (rows, HEAD_DIM), 0) + (
                (position * 2 + core) * rows
            )
            queries[tiles(0, position, rows), :] = turn(asked, query_gain_ref[...], row, own_at)
            return carry

        lax.fori_loop(0, 2, project, 0)

    def both(distance, run):
        @pl.when(z >= distance)
        def _():
            run(z - distance)

        @pl.when(z + distance < layers)
        def _():
            run(z + distance)

    def onward(layer):
        for da in range(2):
            arrive(place(layer, da, 0, core))
            spread_out(layer, da, False, start)

    def over(layer):
        for da in range(2):
            arrive(place(layer, da, 1, core))
            hand_over(layer, da, start)

    arrive(place(z, 1, 0, core))
    spread_out(z, 1, False, start)
    both(1, onward)
    over(z)
    for which in range(3):
        head_keep(which).wait()
    head_hand(0).start()
    for step in range(1, chips):
        for which in range(3):
            head_part(step, which).wait_recv()
    for step in range(1, chips):
        head_hand(step).start()
    both(2, onward)
    both(1, over)
    last_spread(z, True, start)
    keep_block.wait()
    for step in range(chips):
        head_hand(step).wait_recv()
    for fetch in fetches[1:]:
        fetch.wait()
    take(z)
    both(1, take)
    both(3, onward)
    both(1, last_onward)
    both(2, over)
    both(2, take)
    last_over(z)
    both(2, last_onward)
    both(3, over)
    both(3, take)
    both(1, last_over)
    both(3, last_onward)

    key_row = lax.broadcasted_iota(jnp.int32, (1, total), 1)
    key_seg = jnp.where(keep_ref[...] == 1, segment_of(key_row, ends), -1)
    scale = HEAD_DIM ** (-0.5) * 1.4426950408889634

    def put_out(step):
        at = tiles(0, step, chunk)
        return pltpu.make_async_copy(mixed_rows.at[at, :], out_ref.at[at, :], out_sem.at[step])

    def attend(step, carry):
        at = tiles(0, step, chunk)
        scores = lax.dot_general(
            queries[at, :], keys[...], (((1,), (1,)), ((), ())), preferred_element_type=jnp.float32
        )
        local_row = lax.broadcasted_iota(jnp.int32, (chunk, 1), 0)
        second = (local_row >= rows).astype(jnp.int32)
        row = ((step * 2 + second) * 2 + core) * rows + local_row - second * rows
        visible = (segment_of(row, ends) == key_seg) | (row == key_row)
        masked = jnp.where(visible, scores, NEG)
        top = jnp.max(masked, axis=1, keepdims=True)
        weights = jnp.exp2((masked - top) * scale)
        totals = jnp.sum(weights, axis=1, keepdims=True)
        mixed = jnp.dot(
            weights.astype(jnp.bfloat16), values[...], preferred_element_type=jnp.float32
        )
        mixed_rows[at, :] = (mixed / totals).astype(jnp.bfloat16)
        put_out(step).start()
        return carry

    turns = total // 2 // chunk
    lax.fori_loop(0, turns // 2, attend, 0)
    both(2, last_over)
    lax.fori_loop(turns // 2, turns, attend, 0)
    both(3, last_over)

    last_keep.wait()
    for step in range(turns):
        put_out(step).wait()

    def drain(layer, carry):
        for da in range(2):
            spread_out(layer, da, False, finish)
            hand_over(layer, da, finish)
            last_to_twin(layer, da).wait_recv()
        last_spread(layer, False, finish)
        last_to_twin(layer, 1).wait_send()
        return carry

    lax.fori_loop(0, layers, drain, 0)
    head_hand(0).wait_send()
    for step in range(1, chips):
        head_hand(step).wait_send()
        for which in range(3):
            head_part(step, which).wait_send()


def front_call(
    tokens,
    lengths,
    keep_mask,
    attention_gain,
    query_gain,
    key_gain,
    query_weight,
    key_weight,
    value_weight,
    output_weight,
):
    dp_count, mp_count = lax.axis_size("dp"), lax.axis_size("mp")
    rows, half = tokens.shape
    total, width = dp_count * rows, mp_count * half
    layers, chips = dp_count // 4, dp_count // 2
    halves = HEAD_DIM // 2
    exponent = np.arange(halves, dtype=np.float32) * np.float32(2.0 / HEAD_DIM)
    frequency = np.power(np.float32(ROPE_BASE), -exponent).astype(np.float32)
    frequency = np.concatenate([frequency, frequency])[None, :]
    angle = np.arange(total, dtype=np.float32)[:, None] * frequency
    cos_table = np.cos(angle.astype(np.float64)).astype(np.float32)
    sin_table = np.sin(angle.astype(np.float64)).astype(np.float32)
    smem = pl.BlockSpec(memory_space=pltpu.SMEM)
    hbm = pl.BlockSpec(memory_space=pltpu.HBM)
    dma = pltpu.SemaphoreType.DMA
    narrow = jnp.bfloat16
    return pl.pallas_call(
        front_kernel,
        out_shape=(
            jax.ShapeDtypeStruct((total // 2, HEAD_DIM), narrow),
            jax.ShapeDtypeStruct((output_weight.shape[0], dp_count * rows), narrow),
        ),
        in_specs=[smem] + [hbm] * 12,
        out_specs=(hbm, hbm),
        scratch_shapes=[
            pltpu.VMEM((1, width), jnp.float32),
            pltpu.VMEM((1, HEAD_DIM), jnp.float32),
            pltpu.VMEM((1, HEAD_DIM), jnp.float32),
            pltpu.VMEM((1, total), jnp.int32),
            pltpu.VMEM((1, HEAD_DIM), jnp.float32),
            pltpu.VMEM((total, HEAD_DIM), jnp.float32),
            pltpu.VMEM((total, HEAD_DIM), jnp.float32),
            dma((7,)),
            pltpu.VMEM((total, width), narrow),
            pltpu.VMEM((total // 2, HEAD_DIM), narrow),
            pltpu.VMEM((width, 3 * HEAD_DIM), narrow),
            pltpu.VMEM((2 * rows, width), narrow),
            pltpu.VMEM((total, HEAD_DIM), narrow),
            pltpu.VMEM((total, HEAD_DIM), narrow),
            pltpu.VMEM((total // 2, HEAD_DIM), narrow),
            pltpu.VMEM((8, HEAD_DIM), jnp.float32),
            pltpu.VMEM((8, HEAD_DIM), jnp.float32),
            dma((3 * chips,)),
            dma((3 * chips,)),
            dma((chips,)),
            dma((chips,)),
            dma((3,)),
            dma((3,)),
            dma((layers,)),
            dma((layers * 2,)),
            dma((layers * 2,)),
            dma((layers * 2,)),
            dma((layers * 4,)),
            dma((dp_count * mp_count,)),
            dma((layers,)),
            dma((layers,)),
            dma((layers,)),
            dma((layers * 2,)),
            dma((layers * 4,)),
            dma((chips // 2,)),
        ],
        compiler_params=pltpu.CompilerParams(
            collective_id=3, has_side_effects=True, vmem_limit_bytes=60 * 1024 * 1024
        ),
        name="attention_layer",
    )(
        lengths,
        tokens,
        query_weight,
        key_weight,
        value_weight,
        output_weight,
        attention_gain[None, :],
        query_gain[None, :],
        key_gain[None, :],
        keep_mask[None, :],
        jnp.asarray(frequency),
        jnp.asarray(cos_table),
        jnp.asarray(sin_table),
    )


def layer_kernel(
    attended_ref,
    weight_ref,
    tokens_ref,
    routes_ref,
    router_ref,
    gain_ref,
    gate_ref,
    up_ref,
    down_ref,
    out_ref,
    gathered,
    sent_half,
    got_half,
    residual,
    router_own,
    all_routes,
    all_router,
    all_gain,
    held,
    mixed,
    gate,
    up,
    down,
    rows_in,
    hidden,
    wide,
    spread,
    twin,
    cross,
    rise,
    fall,
    last,
    far,
    swap_send,
    swap_recv,
    route_send,
    route_recv,
    pair_send,
    pair_recv,
    local_sem,
    gate_sem,
    up_sem,
    down_sem,
    first_sem,
    rise_sem,
    fall_sem,
    b_sem,
    hand_sem,
    block_recv,
    far_sem,
    far_recv,
    twin_send,
    cross_send,
    z_send,
    last_send,
    twin_recv,
    cross_recv,
    rise_recv,
    fall_recv,
    last_recv,
):
    index = lax.axis_index("dp")
    x = lax.axis_index("mp")
    dp_count = lax.axis_size("dp")
    layers = dp_count // 4
    heads = attended_ref.shape[0]
    core, chip = index % 2, index // 2
    z, y = index // 4, chip % 2
    rows, half = tokens_ref.shape
    width = 2 * half
    tile = 256
    held_count = rows_in.shape[0]
    units = hidden.shape[1]
    first_expert = index * (EXPERTS // dp_count) + x * held_count
    to_a = (index + core * (2 - 4 * y), x + (1 - core) * (1 - 2 * x))
    to_b = (index + (1 - core) * (2 - 4 * y), x + core * (1 - 2 * x))
    to_twin = (index + 1 - 2 * core, x)
    to_up, to_down = (index + 4, x), (index - 4, x)
    has_up, has_down = z < layers - 1, z > 0

    def remote(source, target, send_sem, recv_sem, device):
        return pltpu.make_async_remote_copy(
            src_ref=source,
            dst_ref=target,
            send_sem=send_sem,
            recv_sem=recv_sem,
            device_id=device,
            device_id_type=MESH,
        )

    def tiles(start, step, size):
        return pl.ds(pl.multiple_of(start + step * size, size), size)

    barrier = pltpu.get_barrier_semaphore()
    for step in range(1, dp_count):
        peer = lax.rem(index + step, dp_count)
        pl.semaphore_signal(barrier, inc=1, device_id=(peer, x), device_id_type=MESH)
    pl.semaphore_signal(barrier, inc=1, device_id=(index, 1 - x), device_id_type=MESH)

    load_wide = pltpu.make_async_copy(weight_ref, wide, local_sem.at[4])
    load_wide.start()

    def load_expert(expert):
        columns = tiles(0, expert, units)
        return (
            pltpu.make_async_copy(gate_ref.at[:, columns], gate.at[:, columns], gate_sem.at[expert]),
            pltpu.make_async_copy(up_ref.at[:, columns], up.at[:, columns], up_sem.at[expert]),
            pltpu.make_async_copy(down_ref.at[columns, :], down.at[columns, :], down_sem.at[expert]),
        )

    own_columns = tiles(0, chip, HEAD_DIM)
    own_half = tiles(0, x, half)

    def swap(step):
        other = lax.rem(chip + step, heads)
        return remote(
            attended_ref.at[other],
            gathered.at[:, own_columns],
            swap_send.at[step],
            swap_recv.at[step],
            (other * 2 + core, x),
        )

    def route(step):
        return remote(
            routes_ref,
            all_routes.at[index],
            route_send.at[step],
            route_recv.at[step],
            (lax.rem(index + step, dp_count), x),
        )

    across_x = (index, 1 - x)
    router_half = all_router.at[:, own_half]
    router_copy = remote(router_half, router_half, pair_send.at[0], pair_recv.at[0], across_x)
    gain_copy = remote(gain_ref, all_gain.at[x], pair_send.at[1], pair_recv.at[1], across_x)

    def half_copy(turn):
        at = tiles(0, turn, tile)
        return remote(
            sent_half.at[:, at],
            got_half.at[:, at],
            pair_send.at[2 + turn],
            pair_recv.at[2 + turn],
            across_x,
        )

    keep = [
        pltpu.make_async_copy(
            attended_ref.at[chip], gathered.at[:, own_columns], local_sem.at[0]
        ),
        pltpu.make_async_copy(routes_ref, all_routes.at[index], local_sem.at[1]),
        pltpu.make_async_copy(router_ref, router_own, local_sem.at[2]),
        pltpu.make_async_copy(gain_ref, all_gain.at[x], local_sem.at[3]),
        pltpu.make_async_copy(tokens_ref, residual, local_sem.at[5]),
    ]
    for copy in keep:
        copy.start()
    pl.semaphore_wait(barrier, dp_count)
    for step in range(1, heads):
        swap(step).start()
    gain_copy.start()
    for step in range(1, dp_count):
        route(step).start()
    for expert in range(held_count):
        for copy in load_expert(expert):
            copy.start()
    for copy in keep[1:]:
        copy.wait()
    rest = router_own[...] * all_gain[x]
    for term in range(3):
        rounded = rest.astype(jnp.bfloat16)
        all_router[term * EXPERTS : (term + 1) * EXPERTS, own_half] = rounded
        rest = rest - rounded.astype(jnp.float32)
    all_router[3 * EXPERTS :, own_half] = jnp.zeros(rest.shape, jnp.bfloat16)
    router_copy.start()
    keep[0].wait()
    load_wide.wait()
    for step in range(1, heads):
        swap(step).wait_recv()

    def away(turn, carry):
        sent_half[:, tiles(0, turn, tile)] = jnp.dot(
            gathered[...],
            wide[:, tiles((1 - x) * half, turn, tile)],
            preferred_element_type=jnp.float32,
        )
        half_copy(turn).start()
        return carry

    lax.fori_loop(0, half // tile, away, 0)

    def stay(turn, carry):
        at = tiles(0, turn, tile)
        out_ref[:, at] = residual[:, at].astype(jnp.float32) + jnp.dot(
            gathered[...],
            wide[:, tiles(x * half, turn, tile)],
            preferred_element_type=jnp.float32,
        )
        return carry

    lax.fori_loop(0, half // tile, stay, 0)

    def settle_tile(turn, carry):
        at = tiles(0, turn, tile)
        half_copy(turn).wait_recv()
        residual[:, at] = (out_ref[:, at] + got_half[:, at]).astype(jnp.bfloat16)
        out_ref[:, at] = residual[:, at].astype(jnp.float32)
        return carry

    lax.fori_loop(0, half // tile, settle_tile, 0)

    def place(layer, da, db, which):
        dy = which * da + (1 - which) * db
        dx = (1 - which) * da + which * db
        yy, xx = y + dy * (1 - 2 * y), x + dx * (1 - 2 * x)
        return layer * 4 + yy * 2 + which, xx

    def view(spot):
        return held.at[tiles(0, spot[0], rows), tiles(0, spot[1], half)]

    def send(spot, sem, device, own_block=False):
        return remote(
            residual if own_block else view(spot),
            view(spot),
            sem,
            block_recv.at[spot[0] * 2 + spot[1]],
            device,
        )

    def arrive(spot):
        send(spot, first_sem.at[1], to_twin).wait_recv()

    home_spot = place(z, 0, 0, core)
    keep_block = pltpu.make_async_copy(residual, view(home_spot), first_sem.at[1])
    first = send(home_spot, first_sem.at[0], to_a, True)

    def spread_out(layer, da, own_block, act):
        spot = place(layer, da, 0, core)
        slot = layer * 2 + da
        up_too = (layer <= z) & has_up
        down_too = (layer >= z) & has_down
        if da:
            up_too = up_too & (z + 1 - layer < layers - 1)
            down_too = down_too & (layer - z + 1 < layers - 1)
        else:

            @pl.when((z - layer == layers - 1) | (layer - z == layers - 1))
            def _():
                act(send(spot, far_sem, to_a, own_block))

        @pl.when(up_too)
        def _():
            act(send(spot, rise_sem.at[slot], to_up, own_block))

        @pl.when(down_too)
        def _():
            act(send(spot, fall_sem.at[slot], to_down, own_block))

        act(send(spot, b_sem.at[slot], to_b, own_block))
        act(send(spot, hand_sem.at[slot * 2], to_twin, own_block))

    def hand_over(layer, da, act):
        spot = place(layer, da, 1, core)
        act(send(spot, hand_sem.at[(layer * 2 + da) * 2 + 1], to_twin))

    start = lambda copy: copy.start()
    finish = lambda copy: copy.wait_send()

    earlier = (
        lax.broadcasted_iota(jnp.int32, (rows, rows), 0)
        < lax.broadcasted_iota(jnp.int32, (rows, rows), 1)
    ).astype(jnp.bfloat16)
    expert_id = lax.broadcasted_iota(jnp.int32, (EXPERTS, rows), 0)
    slot_id = lax.broadcasted_iota(jnp.int32, (CAP, rows), 0)

    def block_slots(block, logits, inverse):
        named_ids = all_routes[block]
        named = named_ids[0:1, :] == expert_id
        for k in range(1, TOPK):
            named = named | (named_ids[k : k + 1, :] == expert_id)
        logits_t = jnp.transpose(logits * inverse)[:EXPERTS]
        sigmoid = jnp.where(named, 1.0 / (1.0 + jnp.exp(-logits_t)), 0.0)
        route = sigmoid / jnp.sum(sigmoid, axis=0, keepdims=True)
        named_f = named.astype(jnp.float32)
        here, weight = [], []
        for expert in range(held_count):
            own = expert_id == first_expert + expert
            here.append(jnp.sum(jnp.where(own, named_f, 0.0), axis=0, keepdims=True))
            weight.append(jnp.sum(jnp.where(own, route, 0.0), axis=0, keepdims=True))
        stacked = jnp.concatenate(here + [jnp.zeros((8 - held_count, rows), jnp.float32)], 0)
        before = jnp.dot(
            stacked.astype(jnp.bfloat16), earlier, preferred_element_type=jnp.float32
        )
        slot_of = jnp.where(stacked > 0.5, before.astype(jnp.int32), -1)
        chosen = jnp.concatenate(
            [slot_of[expert : expert + 1, :] == slot_id for expert in range(held_count)], 0
        )
        weights = jnp.concatenate(
            [jnp.broadcast_to(w, (CAP, rows)) for w in weight], 0
        )
        spread_w = jnp.where(chosen, weights, 0.0)
        high = spread_w.astype(jnp.bfloat16)
        low = (spread_w - high.astype(jnp.float32)).astype(jnp.bfloat16)
        return chosen.astype(jnp.float32).astype(jnp.bfloat16), high, low

    chunk = 2 * rows

    def take(layer):
        for da in range(2):
            for db in range(2):
                arrive(place(layer, da, db, 1 - core))

        def one(step, carry):
            position = layer * 2 + step
            at = tiles(0, position, chunk)
            h = held[at, :].astype(jnp.float32)
            inverse = lax.rsqrt(jnp.mean(h * h, axis=1, keepdims=True) + EPS)
            gain_row = jnp.concatenate([all_gain[0], all_gain[1]], 1)
            mixed[...] = (h * gain_row * inverse).astype(jnp.bfloat16)
            logits = lax.dot_general(
                held[at, :],
                all_router[...],
                (((1,), (1,)), ((), ())),
                preferred_element_type=jnp.float32,
            )
            logits = logits[:, :128] + logits[:, 128:]
            logits = logits + pltpu.roll(logits, EXPERTS, 1)
            chosen, spreads = [], []
            for side in range(2):
                part = slice(side * rows, (side + 1) * rows)
                pick, high, low = block_slots(position * 2 + side, logits[part], inverse[part])
                chosen.append(pick)
                spreads += [(high, side), (low, side)]
            empty = jnp.zeros_like(chosen[0])
            select = jnp.concatenate(
                [
                    jnp.concatenate([chosen[0], empty], 1),
                    jnp.concatenate([empty, chosen[1]], 1),
                ],
                0,
            )
            taken = jnp.dot(select, mixed[...], preferred_element_type=jnp.float32).astype(
                jnp.bfloat16
            )
            for side in range(2):
                for expert in range(held_count):
                    source = (side * held_count + expert) * CAP
                    rows_in[expert, tiles(0, position * 2 + side, CAP), :] = taken[
                        source : source + CAP
                    ]
            spread[position] = jnp.concatenate(
                [
                    jnp.concatenate([value, empty] if side == 0 else [empty, value], 1)
                    for value, side in spreads
                ],
                0,
            )
            return carry

        lax.fori_loop(0, 2, one, 0)

    first.start()
    spread_out(z, 0, True, start)
    keep_block.start()
    arrive(place(z, 1, 0, core))
    spread_out(z, 1, False, start)

    def both(distance, run):
        @pl.when(z >= distance)
        def _():
            run(z - distance)

        @pl.when(z + distance < layers)
        def _():
            run(z + distance)

    def onward(layer):
        for da in range(2):
            arrive(place(layer, da, 0, core))
            spread_out(layer, da, False, start)

    def over(layer):
        for da in range(2):
            arrive(place(layer, da, 1, core))
            hand_over(layer, da, start)

    keep_block.wait()
    gain_copy.wait_recv()
    router_copy.wait_recv()
    for step in range(1, dp_count):
        route(step).wait_recv()
    for distance in range(1, layers):
        both(distance, onward)
        if distance == 1:
            over(z)
            take(z)
        else:
            both(distance - 1, over)
            both(distance - 1, take)
    both(layers - 1, over)
    both(layers - 1, take)

    for expert in range(held_count):
        load_gate, load_up, load_down = load_expert(expert)
        load_gate.wait()
        load_up.wait()

        def widen(turn, carry):
            columns = tiles(expert * units, turn, tile)
            gate_val = jnp.dot(
                rows_in[expert], gate[:, columns], preferred_element_type=jnp.float32
            )
            up_val = jnp.dot(rows_in[expert], up[:, columns], preferred_element_type=jnp.float32)
            silu = gate_val / (1.0 + jnp.exp(-gate_val))
            hidden[:, tiles(0, turn, tile)] = (silu * up_val).astype(jnp.bfloat16)
            return carry

        lax.fori_loop(0, units // tile, widen, 0)
        load_down.wait()
        slots = hidden.shape[0]

        def narrow(turn, carry):
            at = tiles(0, turn, tile)
            wide[expert * slots : (expert + 1) * slots, at] = jnp.dot(
                hidden[...],
                down[expert * units : (expert + 1) * units, at],
                preferred_element_type=jnp.float32,
            ).astype(jnp.bfloat16)
            return carry

        lax.fori_loop(0, width // tile, narrow, 0)

    first.wait_send()
    for turn in range(half // tile):
        half_copy(turn).wait_send()

    def sent(layer, carry):
        for da in range(2):
            spread_out(layer, da, False, finish)
            hand_over(layer, da, finish)
        return carry

    lax.fori_loop(0, layers, sent, 0)

    def combine(position):
        pieces = []
        for side in range(2):
            block = position * 2 + side
            pieces += [
                wide[tiles(expert * dp_count * CAP, block, CAP), :] for expert in range(held_count)
            ] * 2
        held[tiles(0, position, chunk), :] = lax.dot_general(
            spread[position],
            jnp.concatenate(pieces, 0),
            (((0,), (0,)), ((), ())),
            preferred_element_type=jnp.float32,
        ).astype(jnp.bfloat16)

    def mine(layer, da, db):
        return view(place(layer, da, db, core))

    def to_other_core(layer, da, db):
        slot = (layer * 2 + da) * 2 + db
        other = 1 - core
        return remote(
            view(place(layer, da, db, other)),
            twin.at[slot],
            twin_send.at[slot],
            twin_recv.at[slot],
            to_twin,
        )

    def to_cross(layer, da):
        pair = layer * 2 + da
        return remote(
            mine(layer, da, 1), cross.at[pair], cross_send.at[pair], cross_recv.at[pair], to_b
        )

    def upward(layer, da):
        pair = layer * 2 + da
        return remote(
            mine(layer, da, 0), rise.at[pair], z_send.at[pair], rise_recv.at[pair], to_up
        )

    def downward(layer, da):
        pair = layer * 2 + da
        return remote(
            mine(layer, da, 0), fall.at[pair], z_send.at[pair], fall_recv.at[pair], to_down
        )

    def to_last():
        return remote(mine(z, 1, 0), last, last_send, last_recv, to_a)

    def add(target, *sources):
        step = 32

        def body(turn, carry):
            at = tiles(0, turn, step)
            value = sources[0][at, :].astype(jnp.float32)
            for source in sources[1:]:
                value = value + source[at, :].astype(jnp.float32)
            target[at, :] = value.astype(target.dtype)
            return carry

        lax.fori_loop(0, rows // step, body, 0)

    inner = ((z == 1) | (z == 2)).astype(jnp.int32)
    below = (z < layers // 2).astype(jnp.int32)

    def ordered(step):
        step = jnp.asarray(step, jnp.int32)
        turned = step + inner * ((step == 2).astype(jnp.int32) - (step == 3).astype(jnp.int32))
        return turned + below * (layers - 1 - 2 * turned)

    def make(step, carry):
        layer = ordered(step)

        def one(side, inner_carry):
            combine(layer * 2 + side)
            return inner_carry

        lax.fori_loop(0, 2, one, 0)
        for db in (1, 0):
            for da in (1, 0):
                to_other_core(layer, da, db).start()
        return carry

    def pair_up(step):
        layer = ordered(step)
        for da in range(2):
            slot = (layer * 2 + da) * 2 + 1
            to_other_core(layer, da, 1).wait_recv()
            add(mine(layer, da, 1), mine(layer, da, 1), twin.at[slot])
            to_cross(layer, da).start()

    def make_and_pair(step, carry):
        make(step, 0)
        pair_up(step - 1)
        return carry

    make(0, 0)
    lax.fori_loop(1, layers, make_and_pair, 0)
    pair_up(layers - 1)

    def far_copy(layer):
        return remote(mine(layer, 1, 0), far, far_sem, far_recv, to_a)

    def gather_sum(layer, da, target, *more):
        pair = layer * 2 + da
        to_other_core(layer, da, 0).wait_recv()
        to_cross(layer, da).wait_recv()
        terms = (mine(layer, da, 0), twin.at[pair * 2], cross.at[pair]) + more
        reach = layers - 2 if da else layers
        from_down = has_down & (layer >= z) & (layer - z < reach)
        from_up = has_up & (layer <= z) & (z - layer < reach)

        @pl.when(from_down)
        def _():
            upward(layer, da).wait_recv()

        @pl.when(from_up)
        def _():
            downward(layer, da).wait_recv()

        @pl.when(from_down & from_up)
        def _():
            add(target, *terms, rise.at[pair], fall.at[pair])

        @pl.when(from_down & jnp.logical_not(from_up))
        def _():
            add(target, *terms, rise.at[pair])

        @pl.when(from_up & jnp.logical_not(from_down))
        def _():
            add(target, *terms, fall.at[pair])

        @pl.when(jnp.logical_not(from_up | from_down))
        def _():
            add(target, *terms)

    def pass_on(step, carry):
        layer = ordered(step)
        rising = layer > z
        is_far = (layer - z == layers - 1) | (z - layer == layers - 1)
        near = jnp.logical_not(is_far)

        gather_sum(layer, 1, mine(layer, 1, 0))

        @pl.when(is_far)
        def _():
            far_copy(layer).start()

        @pl.when(near & rising)
        def _():
            upward(layer, 1).start()

        @pl.when(near & jnp.logical_not(rising))
        def _():
            downward(layer, 1).start()

        @pl.when(near)
        def _():
            gather_sum(layer, 0, mine(layer, 0, 0))

        @pl.when(is_far)
        def _():
            pair = layer * 2
            to_other_core(layer, 0, 0).wait_recv()
            to_cross(layer, 0).wait_recv()
            far_copy(layer).wait_recv()
            add(mine(layer, 0, 0), mine(layer, 0, 0), twin.at[pair * 2], cross.at[pair], far)

        @pl.when(rising)
        def _():
            upward(layer, 0).start()

        @pl.when(jnp.logical_not(rising))
        def _():
            downward(layer, 0).start()

        return carry

    lax.fori_loop(0, layers - 1, pass_on, 0)
    gather_sum(z, 1, mine(z, 1, 0))
    to_last().start()
    gather_sum(z, 0, out_ref, out_ref)
    to_last().wait_recv()
    add(out_ref, out_ref, last)

    def finish_layer(step, carry):
        layer = ordered(step)
        for da in range(2):
            to_other_core(layer, da, 0).wait_send()
            to_other_core(layer, da, 1).wait_send()
            to_cross(layer, da).wait_send()

            is_far = (layer - z == layers - 1) | (z - layer == layers - 1)
            along = (layer != z) & jnp.logical_not(is_far) if da else layer != z

            @pl.when(along)
            def _():
                upward(layer, da).wait_send()

            if da:

                @pl.when(is_far)
                def _():
                    far_copy(layer).wait_send()

        return carry

    lax.fori_loop(0, layers, finish_layer, 0)
    to_last().wait_send()
    for step in range(1, heads):
        swap(step).wait_send()
    gain_copy.wait_send()
    router_copy.wait_send()
    for step in range(1, dp_count):
        route(step).wait_send()


def layer_call(attended, weight, tokens, routes, router, gain, gate, up, down):
    dp_count, mp_count = lax.axis_size("dp"), lax.axis_size("mp")
    rows, half = tokens.shape
    width = mp_count * half
    heads = attended.shape[0]
    layers = dp_count // 4
    pairs = dp_count // 2
    held_count = gate.shape[1] // FF
    dma = pltpu.SemaphoreType.DMA
    vmem = pl.BlockSpec(memory_space=pltpu.VMEM)
    hbm = pl.BlockSpec(memory_space=pltpu.HBM)
    block = (rows, half)
    narrow = jnp.bfloat16
    return pl.pallas_call(
        layer_kernel,
        out_shape=jax.ShapeDtypeStruct(block, jnp.float32),
        in_specs=[hbm] * 9,
        out_specs=vmem,
        scratch_shapes=[
            pltpu.VMEM((rows, heads * HEAD_DIM), narrow),
            pltpu.VMEM(block, jnp.float32),
            pltpu.VMEM(block, jnp.float32),
            pltpu.VMEM(block, narrow),
            pltpu.VMEM(router.shape, jnp.float32),
            pltpu.VMEM((dp_count,) + routes.shape, routes.dtype),
            pltpu.VMEM((4 * EXPERTS, width), narrow),
            pltpu.VMEM((mp_count, 1, half), jnp.float32),
            pltpu.VMEM((dp_count * rows, width), narrow),
            pltpu.VMEM((2 * rows, width), narrow),
            pltpu.VMEM(gate.shape, narrow),
            pltpu.VMEM(up.shape, narrow),
            pltpu.VMEM(down.shape, narrow),
            pltpu.VMEM((held_count, dp_count * CAP, width), narrow),
            pltpu.VMEM((dp_count * CAP, FF), narrow),
            pltpu.VMEM(weight.shape, narrow),
            pltpu.VMEM((dp_count // 2, 4 * held_count * CAP, 2 * rows), narrow),
            pltpu.VMEM((2 * pairs,) + block, narrow),
            pltpu.VMEM((pairs,) + block, narrow),
            pltpu.VMEM((pairs,) + block, narrow),
            pltpu.VMEM((pairs,) + block, narrow),
            pltpu.VMEM(block, narrow),
            pltpu.VMEM(block, narrow),
            dma((heads,)),
            dma((heads,)),
            dma((dp_count,)),
            dma((dp_count,)),
            dma((2 + half // 256,)),
            dma((2 + half // 256,)),
            dma((6,)),
            dma((held_count,)),
            dma((held_count,)),
            dma((held_count,)),
            dma((2,)),
            dma((layers * 2,)),
            dma((layers * 2,)),
            dma((layers * 2,)),
            dma((layers * 4,)),
            dma((dp_count * mp_count,)),
            dma,
            dma,
            dma((2 * pairs,)),
            dma((pairs,)),
            dma((pairs,)),
            dma,
            dma((2 * pairs,)),
            dma((pairs,)),
            dma((pairs,)),
            dma((pairs,)),
            dma,
        ],
        compiler_params=pltpu.CompilerParams(
            collective_id=2, has_side_effects=True, vmem_limit_bytes=60 * 1024 * 1024
        ),
        name="mixture_layer",
    )(attended, weight, tokens, routes, router, gain, gate, up, down)


def local_paired(
    tokens,
    lengths,
    keep_mask,
    routes,
    attention_gain,
    mixture_gain,
    query_gain,
    key_gain,
    query_weight,
    key_weight,
    value_weight,
    output_weight,
    router_weight,
    expert_gate,
    expert_up,
    expert_down,
):
    tok_rows, half = tokens.shape
    local_heads = query_weight.shape[1] // HEAD_DIM
    attended, all_output_weight = front_call(
        tokens,
        lengths,
        keep_mask,
        attention_gain,
        query_gain,
        key_gain,
        query_weight,
        key_weight,
        value_weight,
        output_weight,
    )
    attended = attended.reshape(local_heads, tok_rows, HEAD_DIM)
    return layer_call(
        attended,
        all_output_weight,
        tokens,
        routes.T,
        router_weight.T,
        mixture_gain[None, :],
        expert_gate[0],
        expert_up[0],
        expert_down[0],
    ).astype(jnp.bfloat16)


def local(*arrays):
    paired = lax.axis_size("mp") == 2 and lax.axis_size("dp") == 16
    return (local_paired if paired else local_any)(*arrays)


def solution(mesh):
    return jax.shard_map(
        local,
        mesh=mesh,
        in_specs=(
            P("dp", "mp"),
            P(),
            P(),
            P("dp", None),
            P(),
            P("mp"),
            P(),
            P(),
            P("dp", "mp"),
            P("dp", "mp"),
            P("dp", "mp"),
            P("mp", "dp"),
            P("mp", None),
            P("dp", None, "mp"),
            P("dp", None, "mp"),
            P("dp", "mp", None),
        ),
        out_specs=P("dp", "mp"),
        check_vma=False,
    )
```

```python
import jax
import jax.numpy as jnp
import numpy as np
from jax import lax
from jax.experimental import pallas as pl
from jax.experimental.pallas import tpu as pltpu
from jax.sharding import PartitionSpec as P

D = 2048
HEAD_DIM = 128
FF = 1024
EXPERTS = 64
TOPK = 8
CAP = 32


EPS = 1e-06
ROPE_BASE = 10000.0
NEG = -1e30


def rope_tables(position):
    halves = HEAD_DIM // 2
    exponent = jnp.arange(halves, dtype=jnp.float32) * (2.0 / HEAD_DIM)
    frequency = jnp.power(jnp.float32(ROPE_BASE), -exponent)
    angle = position.astype(jnp.float32)[:, None] * frequency[None, :]
    cos_table = jnp.cos(angle)
    sin_table = jnp.sin(angle)
    return (jnp.concatenate([cos_table, cos_table], 1), jnp.concatenate([sin_table, sin_table], 1))


def head_prep(projected, head_gain, cos_table, sin_table):
    row_count = projected.shape[0]
    per_head = projected.reshape(row_count, -1, HEAD_DIM)
    normed = (
        per_head * lax.rsqrt(jnp.mean(per_head * per_head, axis=2, keepdims=True) + EPS) * head_gain
    )
    halves = HEAD_DIM // 2
    rotated = jnp.concatenate([-normed[:, :, halves:], normed[:, :, :halves]], 2)
    turned = normed * cos_table[:, None, :] + rotated * sin_table[:, None, :]
    return turned.reshape(row_count, -1).astype(jnp.bfloat16)


def segment_info(lengths, global_row):
    count = jnp.arange(lengths.shape[0], dtype=jnp.int32)
    request_end = jnp.sum(jnp.where(count[None, :] <= count[:, None], lengths[None, :], 0), axis=1)
    request_start = request_end - lengths
    segment = jnp.sum((request_end[None, :] <= global_row[:, None]).astype(jnp.int32), axis=1)
    chosen = segment[:, None] == jnp.arange(lengths.shape[0], dtype=jnp.int32)[None, :]
    begin = jnp.sum(jnp.where(chosen, request_start[None, :], 0), axis=1)
    return (segment, global_row - begin)


MESH = pl.DeviceIdType.MESH


def greet_neighbours():
    index = lax.axis_index("dp")
    x = lax.axis_index("mp")
    layers = lax.axis_size("dp") // 4
    z, y = index // 4, (index // 2) % 2
    barrier = pltpu.get_barrier_semaphore()
    across_y, across_x = (index + 2 - 4 * y, x), (index, 1 - x)
    to_twin = (index + 1 - 2 * (index % 2), x)
    for peer in (across_y, across_x, to_twin):
        pl.semaphore_signal(barrier, inc=1, device_id=peer, device_id_type=MESH)
    has_up, has_down = z < layers - 1, z > 0

    @pl.when(has_up)
    def _():
        pl.semaphore_signal(barrier, inc=1, device_id=(index + 4, x), device_id_type=MESH)

    @pl.when(has_down)
    def _():
        pl.semaphore_signal(barrier, inc=1, device_id=(index - 4, x), device_id_type=MESH)

    pl.semaphore_wait(barrier, 3 + has_up.astype(jnp.int32) + has_down.astype(jnp.int32))


def gather_kernel(block_ref, out_ref, *sems):
    greet_neighbours()
    gather_steps(block_ref, out_ref, *sems)


def gather_steps(block_ref, out_ref, local_sem, a_sem, up_sem, down_sem, b_sem, twin_sem, recv_sem):
    index = lax.axis_index("dp")
    x = lax.axis_index("mp")
    layers = lax.axis_size("dp") // 4
    z, y, core = index // 4, (index // 2) % 2, index % 2
    rows, width = block_ref.shape
    to_a = (index + core * (2 - 4 * y), x + (1 - core) * (1 - 2 * x))
    to_b = (index + (1 - core) * (2 - 4 * y), x + core * (1 - 2 * x))
    to_twin = (index + 1 - 2 * core, x)
    to_up, to_down = (index + 4, x), (index - 4, x)

    def place(layer, da, db, which):
        dy = which * da + (1 - which) * db
        dx = (1 - which) * da + which * db
        yy, xx = y + dy * (1 - 2 * y), x + dx * (1 - 2 * x)
        return layer * 4 + yy * 2 + which, xx

    def view(spot):
        return out_ref.at[
            pl.ds(pl.multiple_of(spot[0] * rows, rows), rows),
            pl.ds(pl.multiple_of(spot[1] * width, width), width),
        ]

    def send(spot, sem, device, own=False):
        return pltpu.make_async_remote_copy(
            src_ref=block_ref if own else view(spot),
            dst_ref=view(spot),
            send_sem=sem,
            recv_sem=recv_sem.at[spot[0] * 2 + spot[1]],
            device_id=device,
            device_id_type=MESH,
        )

    def arrive(spot):
        send(spot, local_sem, to_twin).wait_recv()

    has_up, has_down = z < layers - 1, z > 0
    home = place(z, 0, 0, core)
    keep = pltpu.make_async_copy(block_ref, view(home), local_sem)
    first = send(home, a_sem, to_a, True)

    def spread(layer, da, own, act):
        spot = place(layer, da, 0, core)
        slot = layer * 2 + da

        @pl.when((layer <= z) & has_up)
        def _():
            act(send(spot, up_sem.at[slot], to_up, own))

        @pl.when((layer >= z) & has_down)
        def _():
            act(send(spot, down_sem.at[slot], to_down, own))

        act(send(spot, b_sem.at[slot], to_b, own))
        act(send(spot, twin_sem.at[slot * 2], to_twin, own))

    def hand_over(layer, da, act):
        spot = place(layer, da, 1, core)
        act(send(spot, twin_sem.at[(layer * 2 + da) * 2 + 1], to_twin))

    start = lambda copy: copy.start()
    finish = lambda copy: copy.wait_send()
    first.start()
    spread(z, 0, True, start)
    keep.start()
    arrive(place(z, 1, 0, core))
    spread(z, 1, False, start)

    def both(distance, run):
        for da in range(2):
            @pl.when(z >= distance)
            def _():
                run(z - distance, da)

            @pl.when(z + distance < layers)
            def _():
                run(z + distance, da)

    def onward(layer, da):
        arrive(place(layer, da, 0, core))
        spread(layer, da, False, start)

    def across(layer, da):
        arrive(place(layer, da, 1, core))
        hand_over(layer, da, start)

    for distance in range(1, layers):
        both(distance, onward)
        if distance == 1:
            for da in range(2):
                across(z, da)
        else:
            both(distance - 1, across)
    both(layers - 1, across)
    keep.wait()
    first.wait_send()
    for layer in range(layers):
        for da in range(2):
            spread(layer, da, False, finish)
            hand_over(layer, da, finish)
            for db in range(2):
                arrive(place(layer, da, db, 1 - core))


def gather_scratch(dp_count, mp_count, layers):
    dma = pltpu.SemaphoreType.DMA
    return [
        dma,
        dma,
        dma((layers * 2,)),
        dma((layers * 2,)),
        dma((layers * 2,)),
        dma((layers * 4,)),
        dma((dp_count * mp_count,)),
    ]


def gather_blocks(block):
    dp_count, mp_count = lax.axis_size("dp"), lax.axis_size("mp")
    rows, width = block.shape
    if mp_count != 2 or dp_count % 4:
        wide = lax.all_gather(block, "mp", axis=1, tiled=True)
        return lax.all_gather(wide, "dp", axis=0, tiled=True)
    layers = dp_count // 4
    return pl.pallas_call(
        gather_kernel,
        out_shape=jax.ShapeDtypeStruct((dp_count * rows, mp_count * width), block.dtype),
        in_specs=[pl.BlockSpec(memory_space=pl.ANY)],
        out_specs=pl.BlockSpec(memory_space=pl.ANY),
        scratch_shapes=gather_scratch(dp_count, mp_count, layers),
        compiler_params=pltpu.CompilerParams(collective_id=0, has_side_effects=True),
        name="gather_blocks",
    )(block)


def scatter_kernel(
    parts_ref,
    out_ref,
    mine,
    twin,
    cross,
    rise,
    fall,
    last,
    total,
    load_sem,
    twin_send,
    cross_send,
    z_send,
    last_send,
    twin_recv,
    cross_recv,
    rise_recv,
    fall_recv,
    last_recv,
):
    index = lax.axis_index("dp")
    x = lax.axis_index("mp")
    layers = lax.axis_size("dp") // 4
    z, y, core = index // 4, (index // 2) % 2, index % 2
    rows, width = out_ref.shape
    to_a = (index + core * (2 - 4 * y), x + (1 - core) * (1 - 2 * x))
    to_b = (index + (1 - core) * (2 - 4 * y), x + core * (1 - 2 * x))
    to_twin = (index + 1 - 2 * core, x)
    to_up, to_down = (index + 4, x), (index - 4, x)
    has_up, has_down = z < layers - 1, z > 0

    def view(layer, da, db, which):
        dy = which * da + (1 - which) * db
        dx = (1 - which) * da + which * db
        yy, xx = y + dy * (1 - 2 * y), x + dx * (1 - 2 * x)
        row = (layer * 4 + yy * 2 + which) * rows
        return parts_ref.at[
            pl.ds(pl.multiple_of(row, rows), rows),
            pl.ds(pl.multiple_of(xx * width, width), width),
        ]

    def remote(source, target, send_sem, recv_sem, device):
        return pltpu.make_async_remote_copy(
            src_ref=source,
            dst_ref=target,
            send_sem=send_sem,
            recv_sem=recv_sem,
            device_id=device,
            device_id_type=MESH,
        )

    barrier = pltpu.get_barrier_semaphore()
    for peer in (to_a, to_b, to_twin):
        pl.semaphore_signal(barrier, inc=1, device_id=peer, device_id_type=MESH)

    @pl.when(has_up)
    def _():
        pl.semaphore_signal(barrier, inc=1, device_id=to_up, device_id_type=MESH)

    @pl.when(has_down)
    def _():
        pl.semaphore_signal(barrier, inc=1, device_id=to_down, device_id_type=MESH)

    def outward(run):
        for distance in range(layers - 1, 0, -1):
            for da in range(2):
                @pl.when(z + distance < layers)
                def _():
                    run(z + distance, da, True)

                @pl.when(z >= distance)
                def _():
                    run(z - distance, da, False)

    def home(run):
        for da in (1, 0):
            run(z, da, None)

    def load(layer, da, db):
        slot = (layer * 2 + da) * 2 + db
        return pltpu.make_async_copy(view(layer, da, db, core), mine.at[slot], load_sem.at[slot])

    def to_other_core(layer, da, db):
        slot = (layer * 2 + da) * 2 + db
        return remote(
            view(layer, da, db, 1 - core),
            twin.at[slot],
            twin_send.at[slot],
            twin_recv.at[slot],
            to_twin,
        )

    def to_cross(layer, da):
        pair = layer * 2 + da
        return remote(
            mine.at[pair * 2 + 1], cross.at[pair], cross_send.at[pair], cross_recv.at[pair], to_b
        )

    def upward(layer, da):
        pair = layer * 2 + da
        return remote(mine.at[pair * 2], rise.at[pair], z_send.at[pair], rise_recv.at[pair], to_up)

    def downward(layer, da):
        pair = layer * 2 + da
        return remote(
            mine.at[pair * 2], fall.at[pair], z_send.at[pair], fall_recv.at[pair], to_down
        )

    def to_last():
        return remote(mine.at[(z * 2 + 1) * 2], last, last_send, last_recv, to_a)

    def add(target, *sources):
        step = 16

        def body(turn, carry):
            at = pl.ds(pl.multiple_of(turn * step, step), step)
            value = sources[0][at, :].astype(jnp.float32)
            for source in sources[1:]:
                value = value + source[at, :].astype(jnp.float32)
            target[at, :] = value.astype(target.dtype)
            return carry

        lax.fori_loop(0, rows // step, body, 0)

    for db in (1, 0):
        outward(lambda layer, da, up: load(layer, da, db).start())
        home(lambda layer, da, up: load(layer, da, db).start())
    pl.semaphore_wait(barrier, 3 + has_up.astype(jnp.int32) + has_down.astype(jnp.int32))
    for db in (1, 0):
        outward(lambda layer, da, up: to_other_core(layer, da, db).start())
        home(lambda layer, da, up: to_other_core(layer, da, db).start())

    def pair_up(layer, da, up):
        slot = (layer * 2 + da) * 2 + 1
        load(layer, da, 1).wait()
        to_other_core(layer, da, 1).wait_recv()
        add(mine.at[slot], mine.at[slot], twin.at[slot])
        to_cross(layer, da).start()

    outward(pair_up)
    home(pair_up)

    def collect(layer, da, target):
        pair = layer * 2 + da
        load(layer, da, 0).wait()
        to_other_core(layer, da, 0).wait_recv()
        to_cross(layer, da).wait_recv()
        add(target, mine.at[pair * 2], twin.at[pair * 2], cross.at[pair])

    def pass_on(layer, da, up):
        pair = layer * 2 + da
        collect(layer, da, total)
        if up:
            @pl.when(has_down)
            def _():
                upward(layer, da).wait_recv()
                add(total, total, rise.at[pair])
        else:
            @pl.when(has_up)
            def _():
                downward(layer, da).wait_recv()
                add(total, total, fall.at[pair])
        add(mine.at[pair * 2], total)
        (upward if up else downward)(layer, da).start()

    outward(pass_on)

    def settle(layer, da, up):
        pair = layer * 2 + da
        target = total if da else out_ref
        collect(layer, da, target)

        @pl.when(has_down)
        def _():
            upward(layer, da).wait_recv()
            add(target, target, rise.at[pair])

        @pl.when(has_up)
        def _():
            downward(layer, da).wait_recv()
            add(target, target, fall.at[pair])

        if da:
            add(mine.at[pair * 2], total)
            to_last().start()

    home(settle)
    to_last().wait_recv()
    add(out_ref, out_ref, last)

    def finish(layer, da, up):
        to_other_core(layer, da, 0).wait_send()
        to_other_core(layer, da, 1).wait_send()
        to_cross(layer, da).wait_send()
        if up is not None:
            (upward if up else downward)(layer, da).wait_send()

    outward(finish)
    home(finish)
    to_last().wait_send()


def scatter_sum(parts):
    dp_count, mp_count = lax.axis_size("dp"), lax.axis_size("mp")
    rows, width = parts.shape[0] // dp_count, parts.shape[1] // mp_count
    if mp_count != 2 or dp_count % 4:
        halves = lax.psum_scatter(parts, "mp", scatter_dimension=1, tiled=True)
        return lax.psum_scatter(halves, "dp", scatter_dimension=0, tiled=True)
    pairs = dp_count // 2
    dma = pltpu.SemaphoreType.DMA
    block = (rows, width)
    return pl.pallas_call(
        scatter_kernel,
        out_shape=jax.ShapeDtypeStruct(block, jnp.float32),
        in_specs=[pl.BlockSpec(memory_space=pl.ANY)],
        out_specs=pl.BlockSpec(memory_space=pltpu.VMEM),
        scratch_shapes=[
            pltpu.VMEM((2 * pairs,) + block, jnp.bfloat16),
            pltpu.VMEM((2 * pairs,) + block, jnp.bfloat16),
            pltpu.VMEM((pairs,) + block, jnp.bfloat16),
            pltpu.VMEM((pairs,) + block, jnp.bfloat16),
            pltpu.VMEM((pairs,) + block, jnp.bfloat16),
            pltpu.VMEM(block, jnp.bfloat16),
            pltpu.VMEM(block, jnp.float32),
            dma((2 * pairs,)),
            dma((2 * pairs,)),
            dma((pairs,)),
            dma((pairs,)),
            dma,
            dma((2 * pairs,)),
            dma((pairs,)),
            dma((pairs,)),
            dma((pairs,)),
            dma,
        ],
        compiler_params=pltpu.CompilerParams(
            collective_id=1, has_side_effects=True, vmem_limit_bytes=40 * 1024 * 1024
        ),
        name="scatter_sum",
    )(parts.astype(jnp.bfloat16))


def attention(queries, keys, values, query_seg, query_row, key_seg, key_row, keep_mask):
    scale = HEAD_DIM ** (-0.5)
    scores = (
        lax.dot_general(
            queries, keys, (((1,), (1,)), ((), ())), preferred_element_type=jnp.float32
        )
        * scale
    )
    visible = (query_seg[:, None] == key_seg[None, :]) & (
        (keep_mask[None, :] == 1) | (query_row[:, None] == key_row[None, :])
    )
    masked = jnp.where(visible, scores, NEG)
    top = jnp.max(masked, axis=1, keepdims=True)
    weights = jnp.where(visible, jnp.exp(masked - top), 0.0)
    totals = jnp.sum(weights, axis=1, keepdims=True)
    mixed = jnp.dot(weights.astype(jnp.bfloat16), values, preferred_element_type=jnp.float32)
    return (mixed / totals).astype(jnp.bfloat16)


def local_any(
    tokens,
    lengths,
    keep_mask,
    routes,
    attention_gain,
    mixture_gain,
    query_gain,
    key_gain,
    query_weight,
    key_weight,
    value_weight,
    output_weight,
    router_weight,
    expert_gate,
    expert_up,
    expert_down,
):
    tok_rows = tokens.shape[0]
    dp_count = lax.axis_size("dp")
    dp_index = lax.axis_index("dp")
    mp_index = lax.axis_index("mp")
    local_width = query_weight.shape[1]
    local_heads = local_width // HEAD_DIM
    share = dp_count // local_heads
    part = dp_index % share
    total_rows = tok_rows * dp_count

    weight_rows = query_weight.shape[0]
    packed = jnp.stack([query_weight, key_weight, value_weight]).reshape(
        3, weight_rows, local_heads, HEAD_DIM
    )
    packed = packed.transpose(2, 1, 0, 3).reshape(local_heads, weight_rows, 3 * HEAD_DIM)
    packed = jnp.repeat(packed, share, axis=0)
    head_weight = lax.all_to_all(packed, "dp", split_axis=0, concat_axis=0, tiled=True)
    head_weight = head_weight.reshape(dp_count * weight_rows, 3 * HEAD_DIM)

    all_tokens, head_weight, late_weight = lax.optimization_barrier(
        (gather_blocks(tokens), head_weight, output_weight)
    )
    all_output_weight = lax.all_gather(late_weight, "dp", axis=1, tiled=True)
    xfloat = all_tokens.astype(jnp.float32)
    all_in = (
        xfloat * lax.rsqrt(jnp.mean(xfloat * xfloat, axis=1, keepdims=True) + EPS) * attention_gain
    ).astype(jnp.bfloat16)
    all_routes = lax.all_gather(routes, "dp", axis=0, tiled=True)
    all_gain = lax.all_gather(mixture_gain, "mp", axis=0, tiled=True)
    all_router = lax.all_gather(router_weight, "mp", axis=0, tiled=True)

    key_row = jnp.arange(total_rows, dtype=jnp.int32)
    key_seg, key_pos = segment_info(lengths, key_row)
    cos_table, sin_table = rope_tables(key_pos)

    def own(array):
        split = array.reshape((local_heads, share, tok_rows) + array.shape[1:])
        taken = lax.dynamic_index_in_dim(split, part, 1, keepdims=False)
        return taken.reshape((local_heads * tok_rows,) + array.shape[1:])

    projected = jnp.dot(all_in, head_weight, preferred_element_type=jnp.float32)
    queries = head_prep(
        own(projected[:, :HEAD_DIM]), query_gain, own(cos_table), own(sin_table)
    )
    keys = head_prep(projected[:, HEAD_DIM : 2 * HEAD_DIM], key_gain, cos_table, sin_table)
    values = projected[:, 2 * HEAD_DIM :].astype(jnp.bfloat16)
    attended = attention(
        queries, keys, values, own(key_seg), own(key_row), key_seg, key_row, keep_mask
    )
    groups = [[head * share + p for head in range(local_heads)] for p in range(share)]
    attended = lax.all_to_all(
        attended.reshape(local_heads, tok_rows, HEAD_DIM),
        "dp",
        split_axis=0,
        concat_axis=0,
        tiled=True,
        axis_index_groups=groups,
    )
    attended = attended.transpose(1, 0, 2).reshape(tok_rows, local_width)
    partial_out = jnp.dot(attended, all_output_weight, preferred_element_type=jnp.float32)
    summed_out = lax.psum_scatter(partial_out, "mp", scatter_dimension=1, tiled=True)
    residual = (tokens.astype(jnp.float32) + summed_out).astype(jnp.bfloat16)
    all_residual = gather_blocks(residual)
    hfloat = all_residual.astype(jnp.float32)
    inverse = lax.rsqrt(jnp.mean(hfloat * hfloat, axis=1, keepdims=True) + EPS)
    mixed_in = (hfloat * all_gain * inverse).astype(jnp.bfloat16)

    own_rows = lax.dynamic_slice_in_dim(all_residual, dp_index * tok_rows, tok_rows, 0)
    own_float = own_rows.astype(jnp.float32)
    own_inverse = lax.rsqrt(jnp.mean(own_float * own_float, axis=1, keepdims=True) + EPS)
    logits = (
        jnp.dot(own_float * all_gain, all_router, precision=lax.Precision.HIGHEST) * own_inverse
    )

    ids = jnp.arange(tok_rows, dtype=jnp.int32)
    earlier = (ids[:, None] < ids[None, :]).astype(jnp.bfloat16)
    slots = jnp.arange(CAP, dtype=jnp.int32)

    def chosen_slots(named):
        before = jnp.dot(
            named.astype(jnp.bfloat16).reshape(-1, tok_rows),
            earlier,
            preferred_element_type=jnp.float32,
        ).reshape(named.shape)
        place = jnp.where(named, before.astype(jnp.int32), -1)
        return place[:, :, None, :] == slots[None, None, :, None]

    exp_local = EXPERTS // dp_count
    gate_local = expert_gate[0]
    up_local = expert_up[0]
    down_local = expert_down[0]
    unit_count = gate_local.shape[1]
    held = max(1, unit_count // FF)
    units = unit_count // held
    first_expert = (mp_index * unit_count) // FF

    own_experts = dp_index * exp_local + first_expert + jnp.arange(held, dtype=jnp.int32)
    block_routes = all_routes.reshape(dp_count, tok_rows, TOPK)
    here = jnp.any(block_routes[:, None] == own_experts[None, :, None, None], axis=3)
    chosen = chosen_slots(here)
    select = chosen.astype(jnp.bfloat16).reshape(dp_count, held * CAP, tok_rows)
    rows_in = lax.dot_general(
        select,
        mixed_in.reshape(dp_count, tok_rows, D),
        (((2,), (1,)), ((0,), (0,))),
        preferred_element_type=jnp.float32,
    ).astype(jnp.bfloat16)
    rows_in = rows_in.reshape(dp_count, held, CAP, D)
    experts = jnp.arange(EXPERTS, dtype=jnp.int32)
    named = jnp.any(routes[:, :, None] == experts[None, None, :], axis=1)
    sigmoid_vals = jax.nn.sigmoid(logits) * named.astype(jnp.float32)
    route_weight = sigmoid_vals / jnp.sum(sigmoid_vals, axis=1, keepdims=True)
    all_weights = lax.all_gather(route_weight, "dp", axis=0, tiled=True)
    outs = []
    for index in range(held):
        rows = rows_in[:, index].reshape(dp_count * CAP, D)
        low, high = index * units, (index + 1) * units
        gate_val = jnp.dot(rows, gate_local[:, low:high], preferred_element_type=jnp.float32)
        up_val = jnp.dot(rows, up_local[:, low:high], preferred_element_type=jnp.float32)
        hidden = (jax.nn.silu(gate_val) * up_val).astype(jnp.bfloat16)
        out = jnp.dot(hidden, down_local[low:high], preferred_element_type=jnp.float32)
        outs.append(out.astype(jnp.bfloat16).reshape(dp_count, CAP, D))
    first_own = dp_index * exp_local + first_expert
    own_weights = lax.dynamic_slice_in_dim(all_weights, first_own, held, 1)
    own_weights = own_weights.reshape(dp_count, tok_rows, held).transpose(0, 2, 1)
    spread = jnp.where(chosen, own_weights[:, :, None, :], 0.0)
    spread_high = spread.astype(jnp.bfloat16)
    spread_low = (spread - spread_high.astype(jnp.float32)).astype(jnp.bfloat16)
    contract = (((1,), (1,)), ((0,), (0,)))
    both = jnp.concatenate([spread_high, spread_low], 2).reshape(
        dp_count, held * 2 * CAP, tok_rows
    )
    out_rows = jnp.concatenate(sum([[out, out] for out in outs], []), axis=1)
    parts = lax.dot_general(both, out_rows, contract, preferred_element_type=jnp.float32)
    mixture = scatter_sum(parts.reshape(total_rows, D))
    return (residual.astype(jnp.float32) + mixture).astype(jnp.bfloat16)


def row_starts(lengths_ref):
    ends, starts, total = [], [], 0
    for index in range(lengths_ref.shape[0]):
        starts.append(total)
        total = total + lengths_ref[index]
        ends.append(total)
    return ends, starts


def segment_of(row, ends):
    segment = (row >= ends[0]).astype(jnp.int32)
    for end in ends[1:]:
        segment = segment + (row >= end).astype(jnp.int32)
    return segment


def front_kernel(
    lengths_ref,
    tokens_ref,
    query_ref,
    key_ref,
    value_ref,
    last_ref,
    router_ref,
    mixture_ref,
    gain_hbm,
    query_gain_hbm,
    key_gain_hbm,
    keep_hbm,
    frequency_hbm,
    cos_hbm,
    sin_hbm,
    out_ref,
    all_last_ref,
    all_router_ref,
    all_mixture_ref,
    gain_ref,
    query_gain_ref,
    key_gain_ref,
    keep_ref,
    frequency_ref,
    cos_ref,
    sin_ref,
    fetch_sem,
    held,
    mixed_rows,
    packed,
    pack_sem,
    pair_send,
    pair_recv,
    pair_local,
    weight,
    normed,
    keys,
    values,
    queries,
    start_cos,
    start_sin,
    head_send,
    head_recv,
    head_hand_send,
    head_hand_recv,
    head_local,
    local_sem,
    a_sem,
    rise_sem,
    fall_sem,
    b_sem,
    hand_sem,
    block_recv,
    last_rise,
    last_fall,
    last_side,
    last_hand,
    last_recv,
    out_sem,
):
    index = lax.axis_index("dp")
    x = lax.axis_index("mp")
    dp_count = lax.axis_size("dp")
    layers = dp_count // 4
    chips = dp_count // 2
    core, chip = index % 2, index // 2
    z, y = index // 4, chip % 2
    rows, half = tokens_ref.shape
    total = dp_count * rows
    chunk = 2 * rows
    to_a = (index + core * (2 - 4 * y), x + (1 - core) * (1 - 2 * x))
    to_b = (index + (1 - core) * (2 - 4 * y), x + core * (1 - 2 * x))
    to_twin = (index + 1 - 2 * core, x)
    to_side = (index + 2 - 4 * y, x)
    to_up, to_down = (index + 4, x), (index - 4, x)
    has_up, has_down = z < layers - 1, z > 0

    def remote(source, target, send_sem, recv_sem, device):
        return pltpu.make_async_remote_copy(
            src_ref=source,
            dst_ref=target,
            send_sem=send_sem,
            recv_sem=recv_sem,
            device_id=device,
            device_id_type=MESH,
        )

    def tiles(start, step, size):
        return pl.ds(pl.multiple_of(start + step * size, size), size)

    barrier = pltpu.get_barrier_semaphore()
    for step in range(1, chips):
        peer = lax.rem(chip + step, chips) * 2 + core
        pl.semaphore_signal(barrier, inc=1, device_id=(peer, x), device_id_type=MESH)
    for peer in (to_twin, (index, 1 - x)):
        pl.semaphore_signal(barrier, inc=1, device_id=peer, device_id_type=MESH)

    fetches = [
        pltpu.make_async_copy(source, target, fetch_sem.at[number])
        for number, (source, target) in enumerate(
            (
                (frequency_hbm, frequency_ref),
                (gain_hbm, gain_ref),
                (query_gain_hbm, query_gain_ref),
                (key_gain_hbm, key_gain_ref),
                (keep_hbm, keep_ref),
                (cos_hbm, cos_ref),
                (sin_hbm, sin_ref),
            )
        )
    ]
    packs = []
    for number, source in enumerate((query_ref, key_ref, value_ref)):
        for head in range(chips):
            packs.append(
                pltpu.make_async_copy(
                    source.at[:, head * HEAD_DIM : (head + 1) * HEAD_DIM],
                    packed.at[head, :, number * HEAD_DIM : (number + 1) * HEAD_DIM],
                    pack_sem.at[number * chips + head],
                )
            )
    for pack in packs:
        pack.start()
    for fetch in fetches:
        fetch.start()

    def place(layer, da, db, which):
        dy = which * da + (1 - which) * db
        dx = (1 - which) * da + which * db
        yy, xx = y + dy * (1 - 2 * y), x + dx * (1 - 2 * x)
        return layer * 4 + yy * 2 + which, xx

    def view(spot):
        return held.at[tiles(0, spot[0], rows), tiles(0, spot[1], half)]

    def send(spot, sem, device, own_block=False):
        return remote(
            tokens_ref if own_block else view(spot),
            view(spot),
            sem,
            block_recv.at[spot[0] * 2 + spot[1]],
            device,
        )

    def arrive(spot):
        send(spot, local_sem.at[0], to_twin).wait_recv()

    late = core == 0

    def spread_out(layer, da, own_block, act):
        spot = place(layer, da, 0, core)
        slot = layer * 2 + da
        along = jnp.logical_not(late) if da else jnp.bool_(True)

        @pl.when((layer <= z) & has_up & along)
        def _():
            act(send(spot, rise_sem.at[slot], to_up, own_block))

        @pl.when((layer >= z) & has_down & along)
        def _():
            act(send(spot, fall_sem.at[slot], to_down, own_block))

        if not da:
            @pl.when((layer == z) | late)
            def _():
                act(send(spot, a_sem.at[layer], to_a, own_block))

        act(send(spot, b_sem.at[slot], to_b, own_block))
        act(send(spot, hand_sem.at[slot * 2], to_twin, own_block))

    def hand_over(layer, da, act):
        spot = place(layer, da, 1, core)
        act(send(spot, hand_sem.at[(layer * 2 + da) * 2 + 1], to_twin))

    start = lambda copy: copy.start()
    finish = lambda copy: copy.wait_send()
    keep_block = pltpu.make_async_copy(tokens_ref, view(place(z, 0, 0, core)), local_sem.at[1])

    sources = (query_ref, key_ref, value_ref)

    def head_part(step):
        other = lax.rem(chip + step, chips)
        return remote(
            packed.at[other],
            weight.at[tiles(0, index, rows), :],
            head_send.at[step],
            head_recv.at[step],
            (other * 2 + core, x),
        )

    def across_x(source, target, number):
        return remote(
            source, target.at[x], pair_send.at[number], pair_recv.at[number], (index, 1 - x)
        )

    router_copy = across_x(router_ref, all_router_ref, 0)
    mixture_copy = across_x(mixture_ref, all_mixture_ref, 1)
    pair_keep = [
        pltpu.make_async_copy(router_ref, all_router_ref.at[x], pair_local.at[0]),
        pltpu.make_async_copy(mixture_ref, all_mixture_ref.at[x], pair_local.at[1]),
    ]

    def head_keep(which):
        return pltpu.make_async_copy(
            sources[which].at[:, tiles(0, chip, HEAD_DIM)],
            weight.at[tiles(0, index, rows), which * HEAD_DIM : (which + 1) * HEAD_DIM],
            head_local.at[which],
        )

    def head_hand(step):
        block = lax.rem(chip + step, chips) * 2 + core
        at = weight.at[tiles(0, block, rows), :]
        return remote(at, at, head_hand_send.at[step], head_hand_recv.at[step], to_twin)

    def last_view(layer, side, which):
        yy = y + side * (1 - 2 * y)
        return all_last_ref.at[layer * 4 + yy * 2 + which]

    def last_copy(layer, side, sem, device, own_block=False):
        target = last_view(layer, side, core)
        return remote(
            last_ref if own_block else target,
            target,
            sem,
            last_recv.at[(layer * 2 + side) * 2],
            device,
        )

    def last_to_side(layer, own_block=False):
        target = last_view(layer, 0, core)
        return remote(
            last_ref if own_block else target,
            target,
            last_side.at[layer],
            last_recv.at[(layer * 2 + 1) * 2],
            to_side,
        )

    def last_to_twin(layer, side, own_block=False):
        target = last_view(layer, side, core)
        return remote(
            last_ref if own_block else target,
            target,
            last_hand.at[layer * 2 + side],
            last_recv.at[(layer * 2 + side) * 2 + 1],
            to_twin,
        )

    last_keep = pltpu.make_async_copy(last_ref, last_view(z, 0, core), local_sem.at[2])

    def last_spread(layer, own_block, act):
        @pl.when((layer <= z) & has_up)
        def _():
            act(last_copy(layer, 0, last_rise.at[layer], to_up, own_block))

        @pl.when((layer >= z) & has_down)
        def _():
            act(last_copy(layer, 0, last_fall.at[layer], to_down, own_block))

        act(last_to_side(layer, own_block))
        act(last_to_twin(layer, 0, own_block))

    def last_onward(layer):
        last_copy(layer, 0, last_rise.at[layer], to_up).wait_recv()
        last_spread(layer, False, start)

    def last_over(layer):
        last_to_side(layer).wait_recv()
        last_to_twin(layer, 1).start()

    pl.semaphore_wait(barrier, chips + 1)
    spread_out(z, 0, True, start)
    for which in range(3):
        head_keep(which).start()
    for pack in packs:
        pack.wait()
    for step in range(1, chips):
        head_part(step).start()
    keep_block.start()
    last_keep.start()
    for copy in pair_keep:
        copy.start()

    fetches[0].wait()
    ends, starts = row_starts(lengths_ref)
    which_row = lax.broadcasted_iota(jnp.int32, (8, HEAD_DIM), 0)
    begin = jnp.zeros((8, HEAD_DIM), jnp.int32)
    for number, first_row in enumerate(starts):
        begin = jnp.where(which_row == number, first_row, begin)
    angle = begin.astype(jnp.float32) * frequency_ref[...]
    start_cos[...] = jnp.cos(angle)
    start_sin[...] = jnp.sin(angle)

    def turn(projected, head_gain, row, at):
        square = jnp.mean(projected * projected, axis=1, keepdims=True)
        value = projected * lax.rsqrt(square + EPS) * head_gain
        cos_s, sin_s = start_cos[0:1, :], start_sin[0:1, :]
        for number in range(1, len(starts)):
            past = row >= ends[number - 1]
            cos_s = jnp.where(past, start_cos[number : number + 1, :], cos_s)
            sin_s = jnp.where(past, start_sin[number : number + 1, :], sin_s)
        cos_g, sin_g = cos_ref[at, :], sin_ref[at, :]
        cos_t = cos_g * cos_s + sin_g * sin_s
        sin_t = sin_g * cos_s - cos_g * sin_s
        lane = lax.broadcasted_iota(jnp.int32, value.shape, 1)
        halves = pltpu.roll(value, HEAD_DIM // 2, 1)
        rotated = jnp.where(lane < HEAD_DIM // 2, -halves, halves)
        return (value * cos_t + rotated * sin_t).astype(jnp.bfloat16)

    def take(layer):
        for da in range(2):
            for db in range(2):
                arrive(place(layer, da, db, 1 - core))

        def project(step, carry):
            position = layer * 2 + step
            at = tiles(0, position, chunk)
            value = held[at, :].astype(jnp.float32)
            inverse = lax.rsqrt(jnp.mean(value * value, axis=1, keepdims=True) + EPS)
            normed[...] = (value * inverse * gain_ref[...]).astype(jnp.bfloat16)
            both_parts = jnp.dot(
                normed[...], weight[:, HEAD_DIM:], preferred_element_type=jnp.float32
            )
            row = lax.broadcasted_iota(jnp.int32, (chunk, HEAD_DIM), 0) + position * chunk
            keys[at, :] = turn(both_parts[:, :HEAD_DIM], key_gain_ref[...], row, at)
            values[at, :] = both_parts[:, HEAD_DIM:].astype(jnp.bfloat16)
            asked = jnp.dot(
                normed[tiles(0, core, rows), :],
                weight[:, :HEAD_DIM],
                preferred_element_type=jnp.float32,
            )
            own_at = tiles(0, position * 2 + core, rows)
            row = lax.broadcasted_iota(jnp.int32, (rows, HEAD_DIM), 0) + (
                (position * 2 + core) * rows
            )
            queries[tiles(0, position, rows), :] = turn(asked, query_gain_ref[...], row, own_at)
            return carry

        lax.fori_loop(0, 2, project, 0)

    def both(distance, run):
        @pl.when(z >= distance)
        def _():
            run(z - distance)

        @pl.when(z + distance < layers)
        def _():
            run(z + distance)

    def onward(layer):
        for da in range(2):
            arrive(place(layer, da, 0, core))
            spread_out(layer, da, False, start)

    def over(layer):
        for da in range(2):
            arrive(place(layer, da, 1, core))
            hand_over(layer, da, start)

    arrive(place(z, 1, 0, core))
    spread_out(z, 1, False, start)
    both(1, onward)
    over(z)
    for which in range(3):
        head_keep(which).wait()
    head_hand(0).start()
    for step in range(1, chips):
        head_part(step).wait_recv()
    for step in range(1, chips):
        head_hand(step).start()
    both(2, onward)
    both(1, over)
    last_spread(z, True, start)
    mixture_copy.start()
    router_copy.start()
    keep_block.wait()
    for step in range(chips):
        head_hand(step).wait_recv()
    for fetch in fetches[1:]:
        fetch.wait()
    take(z)
    both(1, take)
    both(3, onward)
    both(1, last_onward)
    both(2, over)
    both(2, take)
    last_over(z)
    both(2, last_onward)
    both(3, over)
    both(3, take)
    both(1, last_over)
    both(3, last_onward)

    key_row = lax.broadcasted_iota(jnp.int32, (1, total), 1)
    key_seg = jnp.where(keep_ref[...] == 1, segment_of(key_row, ends), -1)
    scale = HEAD_DIM ** (-0.5) * 1.4426950408889634

    def put_out(step):
        at = tiles(0, step, chunk)
        return pltpu.make_async_copy(mixed_rows.at[at, :], out_ref.at[at, :], out_sem.at[step])

    def attend(step, carry):
        at = tiles(0, step, chunk)
        scores = lax.dot_general(
            queries[at, :], keys[...], (((1,), (1,)), ((), ())), preferred_element_type=jnp.float32
        )
        local_row = lax.broadcasted_iota(jnp.int32, (chunk, 1), 0)
        second = (local_row >= rows).astype(jnp.int32)
        row = ((step * 2 + second) * 2 + core) * rows + local_row - second * rows
        visible = (segment_of(row, ends) == key_seg) | (row == key_row)
        masked = jnp.where(visible, scores, NEG)
        top = jnp.max(masked, axis=1, keepdims=True)
        weights = jnp.exp2((masked - top) * scale)
        totals = jnp.sum(weights, axis=1, keepdims=True)
        mixed = jnp.dot(
            weights.astype(jnp.bfloat16), values[...], preferred_element_type=jnp.float32
        )
        mixed_rows[at, :] = (mixed / totals).astype(jnp.bfloat16)
        put_out(step).start()
        return carry

    turns = total // 2 // chunk
    lax.fori_loop(0, turns // 2, attend, 0)
    both(2, last_over)
    lax.fori_loop(turns // 2, turns, attend, 0)
    both(3, last_over)

    last_keep.wait()
    for step in range(turns):
        put_out(step).wait()

    def drain(layer, carry):
        for da in range(2):
            spread_out(layer, da, False, finish)
            hand_over(layer, da, finish)
            last_to_twin(layer, da).wait_recv()
        last_spread(layer, False, finish)
        last_to_twin(layer, 1).wait_send()
        return carry

    lax.fori_loop(0, layers, drain, 0)
    head_hand(0).wait_send()
    for step in range(1, chips):
        head_hand(step).wait_send()
        head_part(step).wait_send()
    for copy in pair_keep + [mixture_copy, router_copy]:
        copy.wait()


def front_call(
    tokens,
    lengths,
    keep_mask,
    attention_gain,
    query_gain,
    key_gain,
    query_weight,
    key_weight,
    value_weight,
    output_weight,
    router,
    mixture_gain,
):
    dp_count, mp_count = lax.axis_size("dp"), lax.axis_size("mp")
    rows, half = tokens.shape
    total, width = dp_count * rows, mp_count * half
    layers, chips = dp_count // 4, dp_count // 2
    halves = HEAD_DIM // 2
    exponent = np.arange(halves, dtype=np.float32) * np.float32(2.0 / HEAD_DIM)
    frequency = np.power(np.float32(ROPE_BASE), -exponent).astype(np.float32)
    frequency = np.concatenate([frequency, frequency])[None, :]
    angle = np.arange(total, dtype=np.float32)[:, None] * frequency
    cos_table = np.cos(angle.astype(np.float64)).astype(np.float32)
    sin_table = np.sin(angle.astype(np.float64)).astype(np.float32)
    smem = pl.BlockSpec(memory_space=pltpu.SMEM)
    hbm = pl.BlockSpec(memory_space=pltpu.HBM)
    dma = pltpu.SemaphoreType.DMA
    narrow = jnp.bfloat16
    return pl.pallas_call(
        front_kernel,
        out_shape=(
            jax.ShapeDtypeStruct((total // 2, HEAD_DIM), narrow),
            jax.ShapeDtypeStruct((dp_count,) + output_weight.shape, narrow),
            jax.ShapeDtypeStruct((mp_count,) + router.shape, router.dtype),
            jax.ShapeDtypeStruct((mp_count,) + mixture_gain.shape, mixture_gain.dtype),
        ),
        in_specs=[smem] + [hbm] * 14,
        out_specs=(hbm,) * 4,
        scratch_shapes=[
            pltpu.VMEM((1, width), jnp.float32),
            pltpu.VMEM((1, HEAD_DIM), jnp.float32),
            pltpu.VMEM((1, HEAD_DIM), jnp.float32),
            pltpu.VMEM((1, total), jnp.int32),
            pltpu.VMEM((1, HEAD_DIM), jnp.float32),
            pltpu.VMEM((total, HEAD_DIM), jnp.float32),
            pltpu.VMEM((total, HEAD_DIM), jnp.float32),
            dma((7,)),
            pltpu.VMEM((total, width), narrow),
            pltpu.VMEM((total // 2, HEAD_DIM), narrow),
            pltpu.VMEM((chips, rows, 3 * HEAD_DIM), narrow),
            dma((3 * chips,)),
            dma((2,)),
            dma((2,)),
            dma((2,)),
            pltpu.VMEM((width, 3 * HEAD_DIM), narrow),
            pltpu.VMEM((2 * rows, width), narrow),
            pltpu.VMEM((total, HEAD_DIM), narrow),
            pltpu.VMEM((total, HEAD_DIM), narrow),
            pltpu.VMEM((total // 2, HEAD_DIM), narrow),
            pltpu.VMEM((8, HEAD_DIM), jnp.float32),
            pltpu.VMEM((8, HEAD_DIM), jnp.float32),
            dma((chips,)),
            dma((chips,)),
            dma((chips,)),
            dma((chips,)),
            dma((3,)),
            dma((3,)),
            dma((layers,)),
            dma((layers * 2,)),
            dma((layers * 2,)),
            dma((layers * 2,)),
            dma((layers * 4,)),
            dma((dp_count * mp_count,)),
            dma((layers,)),
            dma((layers,)),
            dma((layers,)),
            dma((layers * 2,)),
            dma((layers * 4,)),
            dma((chips // 2,)),
        ],
        compiler_params=pltpu.CompilerParams(
            collective_id=3, has_side_effects=True, vmem_limit_bytes=60 * 1024 * 1024
        ),
        name="attention_layer",
    )(
        lengths,
        tokens,
        query_weight,
        key_weight,
        value_weight,
        output_weight,
        router,
        mixture_gain,
        attention_gain[None, :],
        query_gain[None, :],
        key_gain[None, :],
        keep_mask[None, :],
        jnp.asarray(frequency),
        jnp.asarray(cos_table),
        jnp.asarray(sin_table),
    )


def layer_kernel(
    attended_ref,
    weight_ref,
    tokens_ref,
    routes_ref,
    router_ref,
    gain_ref,
    gate_ref,
    up_ref,
    down_ref,
    out_ref,
    gathered,
    sent_half,
    got_half,
    residual,
    router_own,
    all_routes,
    all_router,
    all_gain,
    held,
    mixed,
    gate,
    up,
    down,
    rows_in,
    hidden,
    wide,
    spread,
    twin,
    cross,
    rise,
    fall,
    last,
    far,
    swap_send,
    swap_recv,
    route_send,
    route_recv,
    pair_send,
    pair_recv,
    local_sem,
    wide_sem,
    gate_sem,
    up_sem,
    down_sem,
    first_sem,
    rise_sem,
    fall_sem,
    b_sem,
    hand_sem,
    block_recv,
    far_sem,
    far_recv,
    twin_send,
    cross_send,
    z_send,
    last_send,
    twin_recv,
    cross_recv,
    rise_recv,
    fall_recv,
    last_recv,
):
    index = lax.axis_index("dp")
    x = lax.axis_index("mp")
    dp_count = lax.axis_size("dp")
    layers = dp_count // 4
    heads = attended_ref.shape[0]
    core, chip = index % 2, index // 2
    z, y = index // 4, chip % 2
    rows, half = tokens_ref.shape
    width = 2 * half
    tile = 256
    held_count = rows_in.shape[0]
    units = hidden.shape[1]
    first_expert = index * (EXPERTS // dp_count) + x * held_count
    to_a = (index + core * (2 - 4 * y), x + (1 - core) * (1 - 2 * x))
    to_b = (index + (1 - core) * (2 - 4 * y), x + core * (1 - 2 * x))
    to_twin = (index + 1 - 2 * core, x)
    to_up, to_down = (index + 4, x), (index - 4, x)
    has_up, has_down = z < layers - 1, z > 0

    def remote(source, target, send_sem, recv_sem, device):
        return pltpu.make_async_remote_copy(
            src_ref=source,
            dst_ref=target,
            send_sem=send_sem,
            recv_sem=recv_sem,
            device_id=device,
            device_id_type=MESH,
        )

    def tiles(start, step, size):
        return pl.ds(pl.multiple_of(start + step * size, size), size)

    barrier = pltpu.get_barrier_semaphore()
    for step in range(1, dp_count):
        peer = lax.rem(index + step, dp_count)
        pl.semaphore_signal(barrier, inc=1, device_id=(peer, x), device_id_type=MESH)
    pl.semaphore_signal(barrier, inc=1, device_id=(index, 1 - x), device_id_type=MESH)

    load_wide = [
        pltpu.make_async_copy(
            weight_ref.at[block], wide.at[:, block * rows : (block + 1) * rows], wide_sem.at[block]
        )
        for block in range(dp_count)
    ]
    for load in load_wide:
        load.start()

    def load_expert(expert):
        columns = tiles(0, expert, units)
        return (
            pltpu.make_async_copy(gate_ref.at[:, columns], gate.at[:, columns], gate_sem.at[expert]),
            pltpu.make_async_copy(up_ref.at[:, columns], up.at[:, columns], up_sem.at[expert]),
            pltpu.make_async_copy(down_ref.at[columns, :], down.at[columns, :], down_sem.at[expert]),
        )


    def swap(step):
        other = lax.rem(chip + step, heads)
        return remote(
            attended_ref.at[other],
            gathered.at[chip],
            swap_send.at[step],
            swap_recv.at[step],
            (other * 2 + core, x),
        )

    def route(step):
        return remote(
            routes_ref,
            all_routes.at[index],
            route_send.at[step],
            route_recv.at[step],
            (lax.rem(index + step, dp_count), x),
        )

    across_x = (index, 1 - x)
    def half_copy(turn):
        at = tiles(0, turn, tile)
        return remote(
            sent_half.at[:, at],
            got_half.at[:, at],
            pair_send.at[turn],
            pair_recv.at[turn],
            across_x,
        )

    keep = [
        pltpu.make_async_copy(attended_ref.at[chip], gathered.at[chip], local_sem.at[0]),
        pltpu.make_async_copy(routes_ref, all_routes.at[index], local_sem.at[1]),
        pltpu.make_async_copy(router_ref, router_own, local_sem.at[2]),
        pltpu.make_async_copy(gain_ref, all_gain, local_sem.at[3]),
        pltpu.make_async_copy(tokens_ref, residual, local_sem.at[5]),
    ]
    for copy in keep:
        copy.start()
    pl.semaphore_wait(barrier, dp_count)
    for step in range(1, heads):
        swap(step).start()
    for expert in range(held_count):
        for copy in load_expert(expert):
            copy.start()
    for copy in keep[1:]:
        copy.wait()
    for side in range(2):
        at = slice(side * half, (side + 1) * half)
        rest = router_own[side] * all_gain[side]
        for term in range(3):
            rounded = rest.astype(jnp.bfloat16)
            all_router[term * EXPERTS : (term + 1) * EXPERTS, at] = rounded
            rest = rest - rounded.astype(jnp.float32)
        all_router[3 * EXPERTS :, at] = jnp.zeros(rest.shape, jnp.bfloat16)
    keep[0].wait()
    for load in load_wide:
        load.wait()
    for step in range(1, heads):
        swap(step).wait_recv()

    def all_heads():
        return jnp.concatenate([gathered[head] for head in range(heads)], 1)

    def away(turn, carry):
        sent_half[:, tiles(0, turn, tile)] = jnp.dot(
            all_heads(),
            wide[:, tiles((1 - x) * half, turn, tile)],
            preferred_element_type=jnp.float32,
        )
        half_copy(turn).start()
        return carry

    lax.fori_loop(0, half // tile, away, 0)
    for step in range(1, dp_count):
        route(step).start()

    def stay(turn, carry):
        at = tiles(0, turn, tile)
        out_ref[:, at] = residual[:, at].astype(jnp.float32) + jnp.dot(
            all_heads(),
            wide[:, tiles(x * half, turn, tile)],
            preferred_element_type=jnp.float32,
        )
        return carry

    lax.fori_loop(0, half // tile, stay, 0)

    def settle_tile(turn, carry):
        at = tiles(0, turn, tile)
        half_copy(turn).wait_recv()
        residual[:, at] = (out_ref[:, at] + got_half[:, at]).astype(jnp.bfloat16)
        out_ref[:, at] = residual[:, at].astype(jnp.float32)
        return carry

    lax.fori_loop(0, half // tile, settle_tile, 0)

    def place(layer, da, db, which):
        dy = which * da + (1 - which) * db
        dx = (1 - which) * da + which * db
        yy, xx = y + dy * (1 - 2 * y), x + dx * (1 - 2 * x)
        return layer * 4 + yy * 2 + which, xx

    def view(spot):
        return held.at[tiles(0, spot[0], rows), tiles(0, spot[1], half)]

    def send(spot, sem, device, own_block=False):
        return remote(
            residual if own_block else view(spot),
            view(spot),
            sem,
            block_recv.at[spot[0] * 2 + spot[1]],
            device,
        )

    def arrive(spot):
        send(spot, first_sem.at[1], to_twin).wait_recv()

    home_spot = place(z, 0, 0, core)
    keep_block = pltpu.make_async_copy(residual, view(home_spot), first_sem.at[1])
    first = send(home_spot, first_sem.at[0], to_a, True)

    def spread_out(layer, da, own_block, act):
        spot = place(layer, da, 0, core)
        slot = layer * 2 + da
        up_too = (layer <= z) & has_up
        down_too = (layer >= z) & has_down
        if da:
            up_too = up_too & (z + 1 - layer < layers - 1)
            down_too = down_too & (layer - z + 1 < layers - 1)
        else:

            @pl.when((z - layer == layers - 1) | (layer - z == layers - 1))
            def _():
                act(send(spot, far_sem, to_a, own_block))

        @pl.when(up_too)
        def _():
            act(send(spot, rise_sem.at[slot], to_up, own_block))

        @pl.when(down_too)
        def _():
            act(send(spot, fall_sem.at[slot], to_down, own_block))

        act(send(spot, b_sem.at[slot], to_b, own_block))
        act(send(spot, hand_sem.at[slot * 2], to_twin, own_block))

    def hand_over(layer, da, act):
        spot = place(layer, da, 1, core)
        act(send(spot, hand_sem.at[(layer * 2 + da) * 2 + 1], to_twin))

    start = lambda copy: copy.start()
    finish = lambda copy: copy.wait_send()

    earlier = (
        lax.broadcasted_iota(jnp.int32, (rows, rows), 0)
        < lax.broadcasted_iota(jnp.int32, (rows, rows), 1)
    ).astype(jnp.bfloat16)
    expert_id = lax.broadcasted_iota(jnp.int32, (EXPERTS, rows), 0)
    slot_id = lax.broadcasted_iota(jnp.int32, (CAP, rows), 0)

    def block_slots(block, logits, inverse):
        named_ids = all_routes[block]
        named = named_ids[0:1, :] == expert_id
        for k in range(1, TOPK):
            named = named | (named_ids[k : k + 1, :] == expert_id)
        logits_t = jnp.transpose(logits * inverse)[:EXPERTS]
        sigmoid = jnp.where(named, 1.0 / (1.0 + jnp.exp(-logits_t)), 0.0)
        route = sigmoid / jnp.sum(sigmoid, axis=0, keepdims=True)
        named_f = named.astype(jnp.float32)
        here, weight = [], []
        for expert in range(held_count):
            own = expert_id == first_expert + expert
            here.append(jnp.sum(jnp.where(own, named_f, 0.0), axis=0, keepdims=True))
            weight.append(jnp.sum(jnp.where(own, route, 0.0), axis=0, keepdims=True))
        stacked = jnp.concatenate(here + [jnp.zeros((8 - held_count, rows), jnp.float32)], 0)
        before = jnp.dot(
            stacked.astype(jnp.bfloat16), earlier, preferred_element_type=jnp.float32
        )
        slot_of = jnp.where(stacked > 0.5, before.astype(jnp.int32), -1)
        chosen = jnp.concatenate(
            [slot_of[expert : expert + 1, :] == slot_id for expert in range(held_count)], 0
        )
        weights = jnp.concatenate(
            [jnp.broadcast_to(w, (CAP, rows)) for w in weight], 0
        )
        spread_w = jnp.where(chosen, weights, 0.0)
        high = spread_w.astype(jnp.bfloat16)
        low = (spread_w - high.astype(jnp.float32)).astype(jnp.bfloat16)
        return chosen.astype(jnp.float32).astype(jnp.bfloat16), high, low

    chunk = 2 * rows

    def take(layer):
        for da in range(2):
            for db in range(2):
                arrive(place(layer, da, db, 1 - core))

        def one(step, carry):
            position = layer * 2 + step
            at = tiles(0, position, chunk)
            h = held[at, :].astype(jnp.float32)
            inverse = lax.rsqrt(jnp.mean(h * h, axis=1, keepdims=True) + EPS)
            gain_row = jnp.concatenate([all_gain[0], all_gain[1]], 1)
            mixed[...] = (h * gain_row * inverse).astype(jnp.bfloat16)
            logits = lax.dot_general(
                held[at, :],
                all_router[...],
                (((1,), (1,)), ((), ())),
                preferred_element_type=jnp.float32,
            )
            logits = logits[:, :128] + logits[:, 128:]
            logits = logits + pltpu.roll(logits, EXPERTS, 1)
            chosen, spreads = [], []
            for side in range(2):
                part = slice(side * rows, (side + 1) * rows)
                pick, high, low = block_slots(position * 2 + side, logits[part], inverse[part])
                chosen.append(pick)
                spreads += [(high, side), (low, side)]
            empty = jnp.zeros_like(chosen[0])
            select = jnp.concatenate(
                [
                    jnp.concatenate([chosen[0], empty], 1),
                    jnp.concatenate([empty, chosen[1]], 1),
                ],
                0,
            )
            taken = jnp.dot(select, mixed[...], preferred_element_type=jnp.float32).astype(
                jnp.bfloat16
            )
            for side in range(2):
                for expert in range(held_count):
                    source = (side * held_count + expert) * CAP
                    rows_in[expert, tiles(0, position * 2 + side, CAP), :] = taken[
                        source : source + CAP
                    ]
            spread[position] = jnp.concatenate(
                [
                    jnp.concatenate([value, empty] if side == 0 else [empty, value], 1)
                    for value, side in spreads
                ],
                0,
            )
            return carry

        lax.fori_loop(0, 2, one, 0)

    first.start()
    spread_out(z, 0, True, start)
    keep_block.start()
    arrive(place(z, 1, 0, core))
    spread_out(z, 1, False, start)

    def both(distance, run):
        @pl.when(z >= distance)
        def _():
            run(z - distance)

        @pl.when(z + distance < layers)
        def _():
            run(z + distance)

    def onward(layer):
        for da in range(2):
            arrive(place(layer, da, 0, core))
            spread_out(layer, da, False, start)

    def over(layer):
        for da in range(2):
            arrive(place(layer, da, 1, core))
            hand_over(layer, da, start)

    keep_block.wait()
    for step in range(1, dp_count):
        route(step).wait_recv()
    slots = hidden.shape[0]

    def feed(expert, part):
        at_rows = tiles(0, part, slots)

        def widen(turn, carry):
            columns = tiles(expert * units, turn, tile)
            gate_val = jnp.dot(
                rows_in[expert, at_rows, :], gate[:, columns], preferred_element_type=jnp.float32
            )
            up_val = jnp.dot(
                rows_in[expert, at_rows, :], up[:, columns], preferred_element_type=jnp.float32
            )
            silu = gate_val / (1.0 + jnp.exp(-gate_val))
            hidden[:, tiles(0, turn, tile)] = (silu * up_val).astype(jnp.bfloat16)
            return carry

        lax.fori_loop(0, units // tile, widen, 0)

        def narrow(turn, carry):
            at = tiles(0, turn, tile)
            wide[tiles(expert * 2 * slots, part, slots), at] = jnp.dot(
                hidden[...],
                down[expert * units : (expert + 1) * units, at],
                preferred_element_type=jnp.float32,
            ).astype(jnp.bfloat16)
            return carry

        lax.fori_loop(0, width // tile, narrow, 0)

    near_half = (z >= layers // 2).astype(jnp.int32)
    both(1, onward)
    over(z)
    take(z)
    both(2, onward)
    both(1, over)
    both(1, take)
    for expert in range(held_count):
        for load in load_expert(expert):
            load.wait()
    feed(0, near_half)
    both(3, onward)
    both(2, over)
    both(2, take)
    feed(1, near_half)
    both(3, over)
    both(3, take)
    for expert in range(held_count):
        feed(expert, 1 - near_half)

    first.wait_send()
    for turn in range(half // tile):
        half_copy(turn).wait_send()

    def sent(layer, carry):
        for da in range(2):
            spread_out(layer, da, False, finish)
            hand_over(layer, da, finish)
        return carry

    lax.fori_loop(0, layers, sent, 0)

    def combine(position):
        pieces = []
        for side in range(2):
            block = position * 2 + side
            pieces += [
                wide[tiles(expert * dp_count * CAP, block, CAP), :] for expert in range(held_count)
            ] * 2
        held[tiles(0, position, chunk), :] = lax.dot_general(
            spread[position],
            jnp.concatenate(pieces, 0),
            (((0,), (0,)), ((), ())),
            preferred_element_type=jnp.float32,
        ).astype(jnp.bfloat16)

    def mine(layer, da, db):
        return view(place(layer, da, db, core))

    def to_other_core(layer, da, db):
        slot = (layer * 2 + da) * 2 + db
        other = 1 - core
        return remote(
            view(place(layer, da, db, other)),
            twin.at[slot],
            twin_send.at[slot],
            twin_recv.at[slot],
            to_twin,
        )

    def to_cross(layer, da):
        pair = layer * 2 + da
        return remote(
            mine(layer, da, 1), cross.at[pair], cross_send.at[pair], cross_recv.at[pair], to_b
        )

    def upward(layer, da):
        pair = layer * 2 + da
        return remote(
            mine(layer, da, 0), rise.at[pair], z_send.at[pair], rise_recv.at[pair], to_up
        )

    def downward(layer, da):
        pair = layer * 2 + da
        return remote(
            mine(layer, da, 0), fall.at[pair], z_send.at[pair], fall_recv.at[pair], to_down
        )

    def to_last():
        return remote(mine(z, 1, 0), last, last_send, last_recv, to_a)

    def add(target, *sources):
        step = 32

        def body(turn, carry):
            at = tiles(0, turn, step)
            value = sources[0][at, :].astype(jnp.float32)
            for source in sources[1:]:
                value = value + source[at, :].astype(jnp.float32)
            target[at, :] = value.astype(target.dtype)
            return carry

        lax.fori_loop(0, rows // step, body, 0)

    inner = ((z == 1) | (z == 2)).astype(jnp.int32)
    below = (z < layers // 2).astype(jnp.int32)

    def ordered(step):
        step = jnp.asarray(step, jnp.int32)
        turned = step + inner * ((step == 2).astype(jnp.int32) - (step == 3).astype(jnp.int32))
        return turned + below * (layers - 1 - 2 * turned)

    def make(step, carry):
        layer = ordered(step)

        def one(side, inner_carry):
            combine(layer * 2 + side)
            return inner_carry

        lax.fori_loop(0, 2, one, 0)
        for db in (1, 0):
            for da in (1, 0):
                to_other_core(layer, da, db).start()
        return carry

    def pair_up(step):
        layer = ordered(step)
        for da in range(2):
            slot = (layer * 2 + da) * 2 + 1
            to_other_core(layer, da, 1).wait_recv()
            add(mine(layer, da, 1), mine(layer, da, 1), twin.at[slot])
            to_cross(layer, da).start()

    def make_and_pair(step, carry):
        make(step, 0)
        pair_up(step - 1)
        return carry

    make(0, 0)
    lax.fori_loop(1, layers, make_and_pair, 0)
    pair_up(layers - 1)

    def far_copy(layer):
        return remote(mine(layer, 1, 0), far, far_sem, far_recv, to_a)

    def gather_sum(layer, da, target, *more):
        pair = layer * 2 + da
        to_other_core(layer, da, 0).wait_recv()
        to_cross(layer, da).wait_recv()
        terms = (mine(layer, da, 0), twin.at[pair * 2], cross.at[pair]) + more
        reach = layers - 2 if da else layers
        from_down = has_down & (layer >= z) & (layer - z < reach)
        from_up = has_up & (layer <= z) & (z - layer < reach)

        @pl.when(from_down)
        def _():
            upward(layer, da).wait_recv()

        @pl.when(from_up)
        def _():
            downward(layer, da).wait_recv()

        @pl.when(from_down & from_up)
        def _():
            add(target, *terms, rise.at[pair], fall.at[pair])

        @pl.when(from_down & jnp.logical_not(from_up))
        def _():
            add(target, *terms, rise.at[pair])

        @pl.when(from_up & jnp.logical_not(from_down))
        def _():
            add(target, *terms, fall.at[pair])

        @pl.when(jnp.logical_not(from_up | from_down))
        def _():
            add(target, *terms)

    def pass_on(step, carry):
        layer = ordered(step)
        rising = layer > z
        is_far = (layer - z == layers - 1) | (z - layer == layers - 1)
        near = jnp.logical_not(is_far)

        gather_sum(layer, 1, mine(layer, 1, 0))

        @pl.when(is_far)
        def _():
            far_copy(layer).start()

        @pl.when(near & rising)
        def _():
            upward(layer, 1).start()

        @pl.when(near & jnp.logical_not(rising))
        def _():
            downward(layer, 1).start()

        @pl.when(near)
        def _():
            gather_sum(layer, 0, mine(layer, 0, 0))

        @pl.when(is_far)
        def _():
            pair = layer * 2
            to_other_core(layer, 0, 0).wait_recv()
            to_cross(layer, 0).wait_recv()
            far_copy(layer).wait_recv()
            add(mine(layer, 0, 0), mine(layer, 0, 0), twin.at[pair * 2], cross.at[pair], far)

        @pl.when(rising)
        def _():
            upward(layer, 0).start()

        @pl.when(jnp.logical_not(rising))
        def _():
            downward(layer, 0).start()

        return carry

    lax.fori_loop(0, layers - 1, pass_on, 0)
    gather_sum(z, 1, mine(z, 1, 0))
    to_last().start()
    gather_sum(z, 0, out_ref, out_ref)
    to_last().wait_recv()
    add(out_ref, out_ref, last)

    def finish_layer(step, carry):
        layer = ordered(step)
        for da in range(2):
            to_other_core(layer, da, 0).wait_send()
            to_other_core(layer, da, 1).wait_send()
            to_cross(layer, da).wait_send()

            is_far = (layer - z == layers - 1) | (z - layer == layers - 1)
            along = (layer != z) & jnp.logical_not(is_far) if da else layer != z

            @pl.when(along)
            def _():
                upward(layer, da).wait_send()

            if da:

                @pl.when(is_far)
                def _():
                    far_copy(layer).wait_send()

        return carry

    lax.fori_loop(0, layers, finish_layer, 0)
    to_last().wait_send()
    for step in range(1, heads):
        swap(step).wait_send()
    for step in range(1, dp_count):
        route(step).wait_send()


def layer_call(attended, weight, tokens, routes, router, gain, gate, up, down):
    dp_count, mp_count = lax.axis_size("dp"), lax.axis_size("mp")
    rows, half = tokens.shape
    width = mp_count * half
    heads = attended.shape[0]
    layers = dp_count // 4
    pairs = dp_count // 2
    held_count = gate.shape[1] // FF
    dma = pltpu.SemaphoreType.DMA
    vmem = pl.BlockSpec(memory_space=pltpu.VMEM)
    hbm = pl.BlockSpec(memory_space=pltpu.HBM)
    block = (rows, half)
    narrow = jnp.bfloat16
    return pl.pallas_call(
        layer_kernel,
        out_shape=jax.ShapeDtypeStruct(block, jnp.float32),
        in_specs=[hbm] * 9,
        out_specs=vmem,
        scratch_shapes=[
            pltpu.VMEM(attended.shape, narrow),
            pltpu.VMEM(block, jnp.float32),
            pltpu.VMEM(block, jnp.float32),
            pltpu.VMEM(block, narrow),
            pltpu.VMEM(router.shape, jnp.float32),
            pltpu.VMEM((dp_count,) + routes.shape, routes.dtype),
            pltpu.VMEM((4 * EXPERTS, width), narrow),
            pltpu.VMEM((mp_count, 1, half), jnp.float32),
            pltpu.VMEM((dp_count * rows, width), narrow),
            pltpu.VMEM((2 * rows, width), narrow),
            pltpu.VMEM(gate.shape, narrow),
            pltpu.VMEM(up.shape, narrow),
            pltpu.VMEM(down.shape, narrow),
            pltpu.VMEM((held_count, dp_count * CAP, width), narrow),
            pltpu.VMEM((dp_count // 2 * CAP, FF), narrow),
            pltpu.VMEM((weight.shape[1], width), narrow),
            pltpu.VMEM((dp_count // 2, 4 * held_count * CAP, 2 * rows), narrow),
            pltpu.VMEM((2 * pairs,) + block, narrow),
            pltpu.VMEM((pairs,) + block, narrow),
            pltpu.VMEM((pairs,) + block, narrow),
            pltpu.VMEM((pairs,) + block, narrow),
            pltpu.VMEM(block, narrow),
            pltpu.VMEM(block, narrow),
            dma((heads,)),
            dma((heads,)),
            dma((dp_count,)),
            dma((dp_count,)),
            dma((half // 256,)),
            dma((half // 256,)),
            dma((6,)),
            dma((dp_count,)),
            dma((held_count,)),
            dma((held_count,)),
            dma((held_count,)),
            dma((2,)),
            dma((layers * 2,)),
            dma((layers * 2,)),
            dma((layers * 2,)),
            dma((layers * 4,)),
            dma((dp_count * mp_count,)),
            dma,
            dma,
            dma((2 * pairs,)),
            dma((pairs,)),
            dma((pairs,)),
            dma,
            dma((2 * pairs,)),
            dma((pairs,)),
            dma((pairs,)),
            dma((pairs,)),
            dma,
        ],
        compiler_params=pltpu.CompilerParams(
            collective_id=2, has_side_effects=True, vmem_limit_bytes=60 * 1024 * 1024
        ),
        name="mixture_layer",
    )(attended, weight, tokens, routes, router, gain, gate, up, down)


def local_paired(
    tokens,
    lengths,
    keep_mask,
    routes,
    attention_gain,
    mixture_gain,
    query_gain,
    key_gain,
    query_weight,
    key_weight,
    value_weight,
    output_weight,
    router_weight,
    expert_gate,
    expert_up,
    expert_down,
):
    tok_rows, half = tokens.shape
    local_heads = query_weight.shape[1] // HEAD_DIM
    attended, all_output_weight, all_router, all_gain = front_call(
        tokens,
        lengths,
        keep_mask,
        attention_gain,
        query_gain,
        key_gain,
        query_weight,
        key_weight,
        value_weight,
        output_weight,
        router_weight.T,
        mixture_gain[None, :],
    )
    attended = attended.reshape(local_heads, tok_rows, HEAD_DIM)
    return layer_call(
        attended,
        all_output_weight,
        tokens,
        routes.T,
        all_router,
        all_gain,
        expert_gate[0],
        expert_up[0],
        expert_down[0],
    ).astype(jnp.bfloat16)


def local(*arrays):
    paired = lax.axis_size("mp") == 2 and lax.axis_size("dp") == 16
    return (local_paired if paired else local_any)(*arrays)


def solution(mesh):
    return jax.shard_map(
        local,
        mesh=mesh,
        in_specs=(
            P("dp", "mp"),
            P(),
            P(),
            P("dp", None),
            P(),
            P("mp"),
            P(),
            P(),
            P("dp", "mp"),
            P("dp", "mp"),
            P("dp", "mp"),
            P("mp", "dp"),
            P("mp", None),
            P("dp", None, "mp"),
            P("dp", None, "mp"),
            P("dp", "mp", None),
        ),
        out_specs=P("dp", "mp"),
        check_vma=False,
    )
```

```python
import jax
import jax.numpy as jnp
import numpy as np
from jax import lax
from jax.experimental import pallas as pl
from jax.experimental.pallas import tpu as pltpu
from jax.sharding import PartitionSpec as P

D = 2048
HEAD_DIM = 128
FF = 1024
EXPERTS = 64
TOPK = 8
CAP = 32


EPS = 1e-06
ROPE_BASE = 10000.0
NEG = -1e30


def rope_tables(position):
    halves = HEAD_DIM // 2
    exponent = jnp.arange(halves, dtype=jnp.float32) * (2.0 / HEAD_DIM)
    frequency = jnp.power(jnp.float32(ROPE_BASE), -exponent)
    angle = position.astype(jnp.float32)[:, None] * frequency[None, :]
    cos_table = jnp.cos(angle)
    sin_table = jnp.sin(angle)
    return (jnp.concatenate([cos_table, cos_table], 1), jnp.concatenate([sin_table, sin_table], 1))


def head_prep(projected, head_gain, cos_table, sin_table):
    row_count = projected.shape[0]
    per_head = projected.reshape(row_count, -1, HEAD_DIM)
    normed = (
        per_head * lax.rsqrt(jnp.mean(per_head * per_head, axis=2, keepdims=True) + EPS) * head_gain
    )
    halves = HEAD_DIM // 2
    rotated = jnp.concatenate([-normed[:, :, halves:], normed[:, :, :halves]], 2)
    turned = normed * cos_table[:, None, :] + rotated * sin_table[:, None, :]
    return turned.reshape(row_count, -1).astype(jnp.bfloat16)


def segment_info(lengths, global_row):
    count = jnp.arange(lengths.shape[0], dtype=jnp.int32)
    request_end = jnp.sum(jnp.where(count[None, :] <= count[:, None], lengths[None, :], 0), axis=1)
    request_start = request_end - lengths
    segment = jnp.sum((request_end[None, :] <= global_row[:, None]).astype(jnp.int32), axis=1)
    chosen = segment[:, None] == jnp.arange(lengths.shape[0], dtype=jnp.int32)[None, :]
    begin = jnp.sum(jnp.where(chosen, request_start[None, :], 0), axis=1)
    return (segment, global_row - begin)


MESH = pl.DeviceIdType.MESH


def greet_neighbours():
    index = lax.axis_index("dp")
    x = lax.axis_index("mp")
    layers = lax.axis_size("dp") // 4
    z, y = index // 4, (index // 2) % 2
    barrier = pltpu.get_barrier_semaphore()
    across_y, across_x = (index + 2 - 4 * y, x), (index, 1 - x)
    to_twin = (index + 1 - 2 * (index % 2), x)
    for peer in (across_y, across_x, to_twin):
        pl.semaphore_signal(barrier, inc=1, device_id=peer, device_id_type=MESH)
    has_up, has_down = z < layers - 1, z > 0

    @pl.when(has_up)
    def _():
        pl.semaphore_signal(barrier, inc=1, device_id=(index + 4, x), device_id_type=MESH)

    @pl.when(has_down)
    def _():
        pl.semaphore_signal(barrier, inc=1, device_id=(index - 4, x), device_id_type=MESH)

    pl.semaphore_wait(barrier, 3 + has_up.astype(jnp.int32) + has_down.astype(jnp.int32))


def gather_kernel(block_ref, out_ref, *sems):
    greet_neighbours()
    gather_steps(block_ref, out_ref, *sems)


def gather_steps(block_ref, out_ref, local_sem, a_sem, up_sem, down_sem, b_sem, twin_sem, recv_sem):
    index = lax.axis_index("dp")
    x = lax.axis_index("mp")
    layers = lax.axis_size("dp") // 4
    z, y, core = index // 4, (index // 2) % 2, index % 2
    rows, width = block_ref.shape
    to_a = (index + core * (2 - 4 * y), x + (1 - core) * (1 - 2 * x))
    to_b = (index + (1 - core) * (2 - 4 * y), x + core * (1 - 2 * x))
    to_twin = (index + 1 - 2 * core, x)
    to_up, to_down = (index + 4, x), (index - 4, x)

    def place(layer, da, db, which):
        dy = which * da + (1 - which) * db
        dx = (1 - which) * da + which * db
        yy, xx = y + dy * (1 - 2 * y), x + dx * (1 - 2 * x)
        return layer * 4 + yy * 2 + which, xx

    def view(spot):
        return out_ref.at[
            pl.ds(pl.multiple_of(spot[0] * rows, rows), rows),
            pl.ds(pl.multiple_of(spot[1] * width, width), width),
        ]

    def send(spot, sem, device, own=False):
        return pltpu.make_async_remote_copy(
            src_ref=block_ref if own else view(spot),
            dst_ref=view(spot),
            send_sem=sem,
            recv_sem=recv_sem.at[spot[0] * 2 + spot[1]],
            device_id=device,
            device_id_type=MESH,
        )

    def arrive(spot):
        send(spot, local_sem, to_twin).wait_recv()

    has_up, has_down = z < layers - 1, z > 0
    home = place(z, 0, 0, core)
    keep = pltpu.make_async_copy(block_ref, view(home), local_sem)
    first = send(home, a_sem, to_a, True)

    def spread(layer, da, own, act):
        spot = place(layer, da, 0, core)
        slot = layer * 2 + da

        @pl.when((layer <= z) & has_up)
        def _():
            act(send(spot, up_sem.at[slot], to_up, own))

        @pl.when((layer >= z) & has_down)
        def _():
            act(send(spot, down_sem.at[slot], to_down, own))

        act(send(spot, b_sem.at[slot], to_b, own))
        act(send(spot, twin_sem.at[slot * 2], to_twin, own))

    def hand_over(layer, da, act):
        spot = place(layer, da, 1, core)
        act(send(spot, twin_sem.at[(layer * 2 + da) * 2 + 1], to_twin))

    start = lambda copy: copy.start()
    finish = lambda copy: copy.wait_send()
    first.start()
    spread(z, 0, True, start)
    keep.start()
    arrive(place(z, 1, 0, core))
    spread(z, 1, False, start)

    def both(distance, run):
        for da in range(2):
            @pl.when(z >= distance)
            def _():
                run(z - distance, da)

            @pl.when(z + distance < layers)
            def _():
                run(z + distance, da)

    def onward(layer, da):
        arrive(place(layer, da, 0, core))
        spread(layer, da, False, start)

    def across(layer, da):
        arrive(place(layer, da, 1, core))
        hand_over(layer, da, start)

    for distance in range(1, layers):
        both(distance, onward)
        if distance == 1:
            for da in range(2):
                across(z, da)
        else:
            both(distance - 1, across)
    both(layers - 1, across)
    keep.wait()
    first.wait_send()
    for layer in range(layers):
        for da in range(2):
            spread(layer, da, False, finish)
            hand_over(layer, da, finish)
            for db in range(2):
                arrive(place(layer, da, db, 1 - core))


def gather_scratch(dp_count, mp_count, layers):
    dma = pltpu.SemaphoreType.DMA
    return [
        dma,
        dma,
        dma((layers * 2,)),
        dma((layers * 2,)),
        dma((layers * 2,)),
        dma((layers * 4,)),
        dma((dp_count * mp_count,)),
    ]


def gather_blocks(block):
    dp_count, mp_count = lax.axis_size("dp"), lax.axis_size("mp")
    rows, width = block.shape
    if mp_count != 2 or dp_count % 4:
        wide = lax.all_gather(block, "mp", axis=1, tiled=True)
        return lax.all_gather(wide, "dp", axis=0, tiled=True)
    layers = dp_count // 4
    return pl.pallas_call(
        gather_kernel,
        out_shape=jax.ShapeDtypeStruct((dp_count * rows, mp_count * width), block.dtype),
        in_specs=[pl.BlockSpec(memory_space=pl.ANY)],
        out_specs=pl.BlockSpec(memory_space=pl.ANY),
        scratch_shapes=gather_scratch(dp_count, mp_count, layers),
        compiler_params=pltpu.CompilerParams(collective_id=0, has_side_effects=True),
        name="gather_blocks",
    )(block)


def scatter_kernel(
    parts_ref,
    out_ref,
    mine,
    twin,
    cross,
    rise,
    fall,
    last,
    total,
    load_sem,
    twin_send,
    cross_send,
    z_send,
    last_send,
    twin_recv,
    cross_recv,
    rise_recv,
    fall_recv,
    last_recv,
):
    index = lax.axis_index("dp")
    x = lax.axis_index("mp")
    layers = lax.axis_size("dp") // 4
    z, y, core = index // 4, (index // 2) % 2, index % 2
    rows, width = out_ref.shape
    to_a = (index + core * (2 - 4 * y), x + (1 - core) * (1 - 2 * x))
    to_b = (index + (1 - core) * (2 - 4 * y), x + core * (1 - 2 * x))
    to_twin = (index + 1 - 2 * core, x)
    to_up, to_down = (index + 4, x), (index - 4, x)
    has_up, has_down = z < layers - 1, z > 0

    def view(layer, da, db, which):
        dy = which * da + (1 - which) * db
        dx = (1 - which) * da + which * db
        yy, xx = y + dy * (1 - 2 * y), x + dx * (1 - 2 * x)
        row = (layer * 4 + yy * 2 + which) * rows
        return parts_ref.at[
            pl.ds(pl.multiple_of(row, rows), rows),
            pl.ds(pl.multiple_of(xx * width, width), width),
        ]

    def remote(source, target, send_sem, recv_sem, device):
        return pltpu.make_async_remote_copy(
            src_ref=source,
            dst_ref=target,
            send_sem=send_sem,
            recv_sem=recv_sem,
            device_id=device,
            device_id_type=MESH,
        )

    barrier = pltpu.get_barrier_semaphore()
    for peer in (to_a, to_b, to_twin):
        pl.semaphore_signal(barrier, inc=1, device_id=peer, device_id_type=MESH)

    @pl.when(has_up)
    def _():
        pl.semaphore_signal(barrier, inc=1, device_id=to_up, device_id_type=MESH)

    @pl.when(has_down)
    def _():
        pl.semaphore_signal(barrier, inc=1, device_id=to_down, device_id_type=MESH)

    def outward(run):
        for distance in range(layers - 1, 0, -1):
            for da in range(2):
                @pl.when(z + distance < layers)
                def _():
                    run(z + distance, da, True)

                @pl.when(z >= distance)
                def _():
                    run(z - distance, da, False)

    def home(run):
        for da in (1, 0):
            run(z, da, None)

    def load(layer, da, db):
        slot = (layer * 2 + da) * 2 + db
        return pltpu.make_async_copy(view(layer, da, db, core), mine.at[slot], load_sem.at[slot])

    def to_other_core(layer, da, db):
        slot = (layer * 2 + da) * 2 + db
        return remote(
            view(layer, da, db, 1 - core),
            twin.at[slot],
            twin_send.at[slot],
            twin_recv.at[slot],
            to_twin,
        )

    def to_cross(layer, da):
        pair = layer * 2 + da
        return remote(
            mine.at[pair * 2 + 1], cross.at[pair], cross_send.at[pair], cross_recv.at[pair], to_b
        )

    def upward(layer, da):
        pair = layer * 2 + da
        return remote(mine.at[pair * 2], rise.at[pair], z_send.at[pair], rise_recv.at[pair], to_up)

    def downward(layer, da):
        pair = layer * 2 + da
        return remote(
            mine.at[pair * 2], fall.at[pair], z_send.at[pair], fall_recv.at[pair], to_down
        )

    def to_last():
        return remote(mine.at[(z * 2 + 1) * 2], last, last_send, last_recv, to_a)

    def add(target, *sources):
        step = 16

        def body(turn, carry):
            at = pl.ds(pl.multiple_of(turn * step, step), step)
            value = sources[0][at, :].astype(jnp.float32)
            for source in sources[1:]:
                value = value + source[at, :].astype(jnp.float32)
            target[at, :] = value.astype(target.dtype)
            return carry

        lax.fori_loop(0, rows // step, body, 0)

    for db in (1, 0):
        outward(lambda layer, da, up: load(layer, da, db).start())
        home(lambda layer, da, up: load(layer, da, db).start())
    pl.semaphore_wait(barrier, 3 + has_up.astype(jnp.int32) + has_down.astype(jnp.int32))
    for db in (1, 0):
        outward(lambda layer, da, up: to_other_core(layer, da, db).start())
        home(lambda layer, da, up: to_other_core(layer, da, db).start())

    def pair_up(layer, da, up):
        slot = (layer * 2 + da) * 2 + 1
        load(layer, da, 1).wait()
        to_other_core(layer, da, 1).wait_recv()
        add(mine.at[slot], mine.at[slot], twin.at[slot])
        to_cross(layer, da).start()

    outward(pair_up)
    home(pair_up)

    def collect(layer, da, target):
        pair = layer * 2 + da
        load(layer, da, 0).wait()
        to_other_core(layer, da, 0).wait_recv()
        to_cross(layer, da).wait_recv()
        add(target, mine.at[pair * 2], twin.at[pair * 2], cross.at[pair])

    def pass_on(layer, da, up):
        pair = layer * 2 + da
        collect(layer, da, total)
        if up:
            @pl.when(has_down)
            def _():
                upward(layer, da).wait_recv()
                add(total, total, rise.at[pair])
        else:
            @pl.when(has_up)
            def _():
                downward(layer, da).wait_recv()
                add(total, total, fall.at[pair])
        add(mine.at[pair * 2], total)
        (upward if up else downward)(layer, da).start()

    outward(pass_on)

    def settle(layer, da, up):
        pair = layer * 2 + da
        target = total if da else out_ref
        collect(layer, da, target)

        @pl.when(has_down)
        def _():
            upward(layer, da).wait_recv()
            add(target, target, rise.at[pair])

        @pl.when(has_up)
        def _():
            downward(layer, da).wait_recv()
            add(target, target, fall.at[pair])

        if da:
            add(mine.at[pair * 2], total)
            to_last().start()

    home(settle)
    to_last().wait_recv()
    add(out_ref, out_ref, last)

    def finish(layer, da, up):
        to_other_core(layer, da, 0).wait_send()
        to_other_core(layer, da, 1).wait_send()
        to_cross(layer, da).wait_send()
        if up is not None:
            (upward if up else downward)(layer, da).wait_send()

    outward(finish)
    home(finish)
    to_last().wait_send()


def scatter_sum(parts):
    dp_count, mp_count = lax.axis_size("dp"), lax.axis_size("mp")
    rows, width = parts.shape[0] // dp_count, parts.shape[1] // mp_count
    if mp_count != 2 or dp_count % 4:
        halves = lax.psum_scatter(parts, "mp", scatter_dimension=1, tiled=True)
        return lax.psum_scatter(halves, "dp", scatter_dimension=0, tiled=True)
    pairs = dp_count // 2
    dma = pltpu.SemaphoreType.DMA
    block = (rows, width)
    return pl.pallas_call(
        scatter_kernel,
        out_shape=jax.ShapeDtypeStruct(block, jnp.float32),
        in_specs=[pl.BlockSpec(memory_space=pl.ANY)],
        out_specs=pl.BlockSpec(memory_space=pltpu.VMEM),
        scratch_shapes=[
            pltpu.VMEM((2 * pairs,) + block, jnp.bfloat16),
            pltpu.VMEM((2 * pairs,) + block, jnp.bfloat16),
            pltpu.VMEM((pairs,) + block, jnp.bfloat16),
            pltpu.VMEM((pairs,) + block, jnp.bfloat16),
            pltpu.VMEM((pairs,) + block, jnp.bfloat16),
            pltpu.VMEM(block, jnp.bfloat16),
            pltpu.VMEM(block, jnp.float32),
            dma((2 * pairs,)),
            dma((2 * pairs,)),
            dma((pairs,)),
            dma((pairs,)),
            dma,
            dma((2 * pairs,)),
            dma((pairs,)),
            dma((pairs,)),
            dma((pairs,)),
            dma,
        ],
        compiler_params=pltpu.CompilerParams(
            collective_id=1, has_side_effects=True, vmem_limit_bytes=40 * 1024 * 1024
        ),
        name="scatter_sum",
    )(parts.astype(jnp.bfloat16))


def attention(queries, keys, values, query_seg, query_row, key_seg, key_row, keep_mask):
    scale = HEAD_DIM ** (-0.5)
    scores = (
        lax.dot_general(
            queries, keys, (((1,), (1,)), ((), ())), preferred_element_type=jnp.float32
        )
        * scale
    )
    visible = (query_seg[:, None] == key_seg[None, :]) & (
        (keep_mask[None, :] == 1) | (query_row[:, None] == key_row[None, :])
    )
    masked = jnp.where(visible, scores, NEG)
    top = jnp.max(masked, axis=1, keepdims=True)
    weights = jnp.where(visible, jnp.exp(masked - top), 0.0)
    totals = jnp.sum(weights, axis=1, keepdims=True)
    mixed = jnp.dot(weights.astype(jnp.bfloat16), values, preferred_element_type=jnp.float32)
    return (mixed / totals).astype(jnp.bfloat16)


def local_any(
    tokens,
    lengths,
    keep_mask,
    routes,
    attention_gain,
    mixture_gain,
    query_gain,
    key_gain,
    query_weight,
    key_weight,
    value_weight,
    output_weight,
    router_weight,
    expert_gate,
    expert_up,
    expert_down,
):
    tok_rows = tokens.shape[0]
    dp_count = lax.axis_size("dp")
    dp_index = lax.axis_index("dp")
    mp_index = lax.axis_index("mp")
    local_width = query_weight.shape[1]
    local_heads = local_width // HEAD_DIM
    share = dp_count // local_heads
    part = dp_index % share
    total_rows = tok_rows * dp_count

    weight_rows = query_weight.shape[0]
    packed = jnp.stack([query_weight, key_weight, value_weight]).reshape(
        3, weight_rows, local_heads, HEAD_DIM
    )
    packed = packed.transpose(2, 1, 0, 3).reshape(local_heads, weight_rows, 3 * HEAD_DIM)
    packed = jnp.repeat(packed, share, axis=0)
    head_weight = lax.all_to_all(packed, "dp", split_axis=0, concat_axis=0, tiled=True)
    head_weight = head_weight.reshape(dp_count * weight_rows, 3 * HEAD_DIM)

    all_tokens, head_weight, late_weight = lax.optimization_barrier(
        (gather_blocks(tokens), head_weight, output_weight)
    )
    all_output_weight = lax.all_gather(late_weight, "dp", axis=1, tiled=True)
    xfloat = all_tokens.astype(jnp.float32)
    all_in = (
        xfloat * lax.rsqrt(jnp.mean(xfloat * xfloat, axis=1, keepdims=True) + EPS) * attention_gain
    ).astype(jnp.bfloat16)
    all_routes = lax.all_gather(routes, "dp", axis=0, tiled=True)
    all_gain = lax.all_gather(mixture_gain, "mp", axis=0, tiled=True)
    all_router = lax.all_gather(router_weight, "mp", axis=0, tiled=True)

    key_row = jnp.arange(total_rows, dtype=jnp.int32)
    key_seg, key_pos = segment_info(lengths, key_row)
    cos_table, sin_table = rope_tables(key_pos)

    def own(array):
        split = array.reshape((local_heads, share, tok_rows) + array.shape[1:])
        taken = lax.dynamic_index_in_dim(split, part, 1, keepdims=False)
        return taken.reshape((local_heads * tok_rows,) + array.shape[1:])

    projected = jnp.dot(all_in, head_weight, preferred_element_type=jnp.float32)
    queries = head_prep(
        own(projected[:, :HEAD_DIM]), query_gain, own(cos_table), own(sin_table)
    )
    keys = head_prep(projected[:, HEAD_DIM : 2 * HEAD_DIM], key_gain, cos_table, sin_table)
    values = projected[:, 2 * HEAD_DIM :].astype(jnp.bfloat16)
    attended = attention(
        queries, keys, values, own(key_seg), own(key_row), key_seg, key_row, keep_mask
    )
    groups = [[head * share + p for head in range(local_heads)] for p in range(share)]
    attended = lax.all_to_all(
        attended.reshape(local_heads, tok_rows, HEAD_DIM),
        "dp",
        split_axis=0,
        concat_axis=0,
        tiled=True,
        axis_index_groups=groups,
    )
    attended = attended.transpose(1, 0, 2).reshape(tok_rows, local_width)
    partial_out = jnp.dot(attended, all_output_weight, preferred_element_type=jnp.float32)
    summed_out = lax.psum_scatter(partial_out, "mp", scatter_dimension=1, tiled=True)
    residual = (tokens.astype(jnp.float32) + summed_out).astype(jnp.bfloat16)
    all_residual = gather_blocks(residual)
    hfloat = all_residual.astype(jnp.float32)
    inverse = lax.rsqrt(jnp.mean(hfloat * hfloat, axis=1, keepdims=True) + EPS)
    mixed_in = (hfloat * all_gain * inverse).astype(jnp.bfloat16)

    own_rows = lax.dynamic_slice_in_dim(all_residual, dp_index * tok_rows, tok_rows, 0)
    own_float = own_rows.astype(jnp.float32)
    own_inverse = lax.rsqrt(jnp.mean(own_float * own_float, axis=1, keepdims=True) + EPS)
    logits = (
        jnp.dot(own_float * all_gain, all_router, precision=lax.Precision.HIGHEST) * own_inverse
    )

    ids = jnp.arange(tok_rows, dtype=jnp.int32)
    earlier = (ids[:, None] < ids[None, :]).astype(jnp.bfloat16)
    slots = jnp.arange(CAP, dtype=jnp.int32)

    def chosen_slots(named):
        before = jnp.dot(
            named.astype(jnp.bfloat16).reshape(-1, tok_rows),
            earlier,
            preferred_element_type=jnp.float32,
        ).reshape(named.shape)
        place = jnp.where(named, before.astype(jnp.int32), -1)
        return place[:, :, None, :] == slots[None, None, :, None]

    exp_local = EXPERTS // dp_count
    gate_local = expert_gate[0]
    up_local = expert_up[0]
    down_local = expert_down[0]
    unit_count = gate_local.shape[1]
    held = max(1, unit_count // FF)
    units = unit_count // held
    first_expert = (mp_index * unit_count) // FF

    own_experts = dp_index * exp_local + first_expert + jnp.arange(held, dtype=jnp.int32)
    block_routes = all_routes.reshape(dp_count, tok_rows, TOPK)
    here = jnp.any(block_routes[:, None] == own_experts[None, :, None, None], axis=3)
    chosen = chosen_slots(here)
    select = chosen.astype(jnp.bfloat16).reshape(dp_count, held * CAP, tok_rows)
    rows_in = lax.dot_general(
        select,
        mixed_in.reshape(dp_count, tok_rows, D),
        (((2,), (1,)), ((0,), (0,))),
        preferred_element_type=jnp.float32,
    ).astype(jnp.bfloat16)
    rows_in = rows_in.reshape(dp_count, held, CAP, D)
    experts = jnp.arange(EXPERTS, dtype=jnp.int32)
    named = jnp.any(routes[:, :, None] == experts[None, None, :], axis=1)
    sigmoid_vals = jax.nn.sigmoid(logits) * named.astype(jnp.float32)
    route_weight = sigmoid_vals / jnp.sum(sigmoid_vals, axis=1, keepdims=True)
    all_weights = lax.all_gather(route_weight, "dp", axis=0, tiled=True)
    outs = []
    for index in range(held):
        rows = rows_in[:, index].reshape(dp_count * CAP, D)
        low, high = index * units, (index + 1) * units
        gate_val = jnp.dot(rows, gate_local[:, low:high], preferred_element_type=jnp.float32)
        up_val = jnp.dot(rows, up_local[:, low:high], preferred_element_type=jnp.float32)
        hidden = (jax.nn.silu(gate_val) * up_val).astype(jnp.bfloat16)
        out = jnp.dot(hidden, down_local[low:high], preferred_element_type=jnp.float32)
        outs.append(out.astype(jnp.bfloat16).reshape(dp_count, CAP, D))
    first_own = dp_index * exp_local + first_expert
    own_weights = lax.dynamic_slice_in_dim(all_weights, first_own, held, 1)
    own_weights = own_weights.reshape(dp_count, tok_rows, held).transpose(0, 2, 1)
    spread = jnp.where(chosen, own_weights[:, :, None, :], 0.0)
    spread_high = spread.astype(jnp.bfloat16)
    spread_low = (spread - spread_high.astype(jnp.float32)).astype(jnp.bfloat16)
    contract = (((1,), (1,)), ((0,), (0,)))
    both = jnp.concatenate([spread_high, spread_low], 2).reshape(
        dp_count, held * 2 * CAP, tok_rows
    )
    out_rows = jnp.concatenate(sum([[out, out] for out in outs], []), axis=1)
    parts = lax.dot_general(both, out_rows, contract, preferred_element_type=jnp.float32)
    mixture = scatter_sum(parts.reshape(total_rows, D))
    return (residual.astype(jnp.float32) + mixture).astype(jnp.bfloat16)


def row_starts(lengths_ref):
    ends, starts, total = [], [], 0
    for index in range(lengths_ref.shape[0]):
        starts.append(total)
        total = total + lengths_ref[index]
        ends.append(total)
    return ends, starts


def segment_of(row, ends):
    segment = (row >= ends[0]).astype(jnp.int32)
    for end in ends[1:]:
        segment = segment + (row >= end).astype(jnp.int32)
    return segment


def front_kernel(
    lengths_ref,
    tokens_ref,
    query_ref,
    key_ref,
    value_ref,
    last_ref,
    router_ref,
    mixture_ref,
    gain_hbm,
    query_gain_hbm,
    key_gain_hbm,
    keep_hbm,
    frequency_hbm,
    cos_hbm,
    sin_hbm,
    out_ref,
    all_last_ref,
    all_router_ref,
    all_mixture_ref,
    gain_ref,
    query_gain_ref,
    key_gain_ref,
    keep_ref,
    frequency_ref,
    cos_ref,
    sin_ref,
    fetch_sem,
    held,
    mixed_rows,
    packed,
    pack_sem,
    pair_send,
    pair_recv,
    pair_local,
    weight,
    normed,
    keys,
    values,
    queries,
    start_cos,
    start_sin,
    head_send,
    head_recv,
    head_hand_send,
    head_hand_recv,
    head_local,
    local_sem,
    a_sem,
    rise_sem,
    fall_sem,
    b_sem,
    hand_sem,
    block_recv,
    last_rise,
    last_fall,
    last_side,
    last_hand,
    last_recv,
    swap_send,
    swap_recv,
    out_sem,
):
    index = lax.axis_index("dp")
    x = lax.axis_index("mp")
    dp_count = lax.axis_size("dp")
    layers = dp_count // 4
    chips = dp_count // 2
    core, chip = index % 2, index // 2
    z, y = index // 4, chip % 2
    rows, half = tokens_ref.shape
    total = dp_count * rows
    chunk = 2 * rows
    to_a = (index + 2 - 4 * y, x)
    to_b = (index, 1 - x)
    to_twin = (index + 1 - 2 * core, x)
    to_side = (index + 2 - 4 * y, x)
    to_up, to_down = (index + 4, x), (index - 4, x)
    has_up, has_down = z < layers - 1, z > 0

    def remote(source, target, send_sem, recv_sem, device):
        return pltpu.make_async_remote_copy(
            src_ref=source,
            dst_ref=target,
            send_sem=send_sem,
            recv_sem=recv_sem,
            device_id=device,
            device_id_type=MESH,
        )

    def tiles(start, step, size):
        return pl.ds(pl.multiple_of(start + step * size, size), size)

    barrier = pltpu.get_barrier_semaphore()
    for step in range(1, chips):
        peer = lax.rem(chip + step, chips) * 2 + core
        pl.semaphore_signal(barrier, inc=1, device_id=(peer, x), device_id_type=MESH)
    for peer in (to_twin, (index, 1 - x)):
        pl.semaphore_signal(barrier, inc=1, device_id=peer, device_id_type=MESH)

    fetches = [
        pltpu.make_async_copy(source, target, fetch_sem.at[number])
        for number, (source, target) in enumerate(
            (
                (frequency_hbm, frequency_ref),
                (gain_hbm, gain_ref),
                (query_gain_hbm, query_gain_ref),
                (key_gain_hbm, key_gain_ref),
                (keep_hbm, keep_ref),
                (cos_hbm, cos_ref),
                (sin_hbm, sin_ref),
            )
        )
    ]
    packs = []
    for number, source in enumerate((query_ref, key_ref, value_ref)):
        for head in range(chips):
            packs.append(
                pltpu.make_async_copy(
                    source.at[:, head * HEAD_DIM : (head + 1) * HEAD_DIM],
                    packed.at[head, :, number * HEAD_DIM : (number + 1) * HEAD_DIM],
                    pack_sem.at[number * chips + head],
                )
            )
    for pack in packs:
        pack.start()
    for fetch in fetches:
        fetch.start()

    def place(layer, da, db, which):
        yy, xx = y + da * (1 - 2 * y), x + db * (1 - 2 * x)
        return layer * 4 + yy * 2 + which, xx

    def view(spot):
        return held.at[tiles(0, spot[0], rows), tiles(0, spot[1], half)]

    def send(spot, sem, device, own_block=False):
        return remote(
            tokens_ref if own_block else view(spot),
            view(spot),
            sem,
            block_recv.at[spot[0] * 2 + spot[1]],
            device,
        )

    def arrive(spot):
        send(spot, local_sem.at[0], to_twin).wait_recv()

    late = core < 2

    def spread_out(layer, da, own_block, act):
        spot = place(layer, da, 0, core)
        slot = layer * 2 + da
        along = jnp.logical_not(late) if da else jnp.bool_(True)

        @pl.when((layer <= z) & has_up & along)
        def _():
            act(send(spot, rise_sem.at[slot], to_up, own_block))

        @pl.when((layer >= z) & has_down & along)
        def _():
            act(send(spot, fall_sem.at[slot], to_down, own_block))

        if not da:
            @pl.when((layer == z) | late)
            def _():
                act(send(spot, a_sem.at[layer], to_a, own_block))

        act(send(spot, b_sem.at[slot], to_b, own_block))
        act(send(spot, hand_sem.at[slot * 2], to_twin, own_block))

    def hand_over(layer, da, act):
        spot = place(layer, da, 1, core)
        act(send(spot, hand_sem.at[(layer * 2 + da) * 2 + 1], to_twin))

    start = lambda copy: copy.start()
    finish = lambda copy: copy.wait_send()
    keep_block = pltpu.make_async_copy(tokens_ref, view(place(z, 0, 0, core)), local_sem.at[1])

    sources = (query_ref, key_ref, value_ref)

    def head_part(step):
        other = lax.rem(chip + step, chips)
        return remote(
            packed.at[other],
            weight.at[tiles(0, index, rows), :],
            head_send.at[step],
            head_recv.at[step],
            (other * 2 + core, x),
        )

    def across_x(source, target, number):
        return remote(
            source, target.at[x], pair_send.at[number], pair_recv.at[number], (index, 1 - x)
        )

    router_copy = across_x(router_ref, all_router_ref, 0)
    mixture_copy = across_x(mixture_ref, all_mixture_ref, 1)
    pair_keep = [
        pltpu.make_async_copy(router_ref, all_router_ref.at[x], pair_local.at[0]),
        pltpu.make_async_copy(mixture_ref, all_mixture_ref.at[x], pair_local.at[1]),
    ]

    def head_keep(which):
        return pltpu.make_async_copy(
            sources[which].at[:, tiles(0, chip, HEAD_DIM)],
            weight.at[tiles(0, index, rows), which * HEAD_DIM : (which + 1) * HEAD_DIM],
            head_local.at[which],
        )

    def head_hand(step):
        block = lax.rem(chip + step, chips) * 2 + core
        at = weight.at[tiles(0, block, rows), :]
        return remote(at, at, head_hand_send.at[step], head_hand_recv.at[step], to_twin)

    def last_view(layer, side, which):
        yy = y + side * (1 - 2 * y)
        return all_last_ref.at[layer * 4 + yy * 2 + which]

    def last_copy(layer, side, sem, device, own_block=False):
        target = last_view(layer, side, core)
        return remote(
            last_ref if own_block else target,
            target,
            sem,
            last_recv.at[(layer * 2 + side) * 2],
            device,
        )

    def last_to_side(layer, own_block=False):
        target = last_view(layer, 0, core)
        return remote(
            last_ref if own_block else target,
            target,
            last_side.at[layer],
            last_recv.at[(layer * 2 + 1) * 2],
            to_side,
        )

    def last_to_twin(layer, side, own_block=False):
        target = last_view(layer, side, core)
        return remote(
            last_ref if own_block else target,
            target,
            last_hand.at[layer * 2 + side],
            last_recv.at[(layer * 2 + side) * 2 + 1],
            to_twin,
        )

    last_keep = pltpu.make_async_copy(last_ref, last_view(z, 0, core), local_sem.at[2])

    def last_spread(layer, own_block, act):
        @pl.when((layer <= z) & has_up)
        def _():
            act(last_copy(layer, 0, last_rise.at[layer], to_up, own_block))

        @pl.when((layer >= z) & has_down)
        def _():
            act(last_copy(layer, 0, last_fall.at[layer], to_down, own_block))

        act(last_to_side(layer, own_block))
        act(last_to_twin(layer, 0, own_block))

    def last_onward(layer):
        last_copy(layer, 0, last_rise.at[layer], to_up).wait_recv()
        last_spread(layer, False, start)

    def last_over(layer):
        last_to_side(layer).wait_recv()
        last_to_twin(layer, 1).start()

    pl.semaphore_wait(barrier, chips + 1)
    spread_out(z, 0, True, start)
    for which in range(3):
        head_keep(which).start()
    for pack in packs:
        pack.wait()
    for step in range(1, chips):
        head_part(step).start()
    keep_block.start()
    last_keep.start()
    for copy in pair_keep:
        copy.start()

    fetches[0].wait()
    ends, starts = row_starts(lengths_ref)
    which_row = lax.broadcasted_iota(jnp.int32, (8, HEAD_DIM), 0)
    begin = jnp.zeros((8, HEAD_DIM), jnp.int32)
    for number, first_row in enumerate(starts):
        begin = jnp.where(which_row == number, first_row, begin)
    angle = begin.astype(jnp.float32) * frequency_ref[...]
    start_cos[...] = jnp.cos(angle)
    start_sin[...] = jnp.sin(angle)

    def turn(projected, head_gain, row, at):
        square = jnp.mean(projected * projected, axis=1, keepdims=True)
        value = projected * lax.rsqrt(square + EPS) * head_gain
        cos_s, sin_s = start_cos[0:1, :], start_sin[0:1, :]
        for number in range(1, len(starts)):
            past = row >= ends[number - 1]
            cos_s = jnp.where(past, start_cos[number : number + 1, :], cos_s)
            sin_s = jnp.where(past, start_sin[number : number + 1, :], sin_s)
        cos_g, sin_g = cos_ref[at, :], sin_ref[at, :]
        cos_t = cos_g * cos_s + sin_g * sin_s
        sin_t = sin_g * cos_s - cos_g * sin_s
        lane = lax.broadcasted_iota(jnp.int32, value.shape, 1)
        halves = pltpu.roll(value, HEAD_DIM // 2, 1)
        rotated = jnp.where(lane < HEAD_DIM // 2, -halves, halves)
        return (value * cos_t + rotated * sin_t).astype(jnp.bfloat16)

    def take(layer):
        for da in range(2):
            for db in range(2):
                arrive(place(layer, da, db, 1 - core))

        def project(step, carry):
            position = layer * 2 + step
            at = tiles(0, position, chunk)
            value = held[at, :].astype(jnp.float32)
            inverse = lax.rsqrt(jnp.mean(value * value, axis=1, keepdims=True) + EPS)
            normed[...] = (value * inverse * gain_ref[...]).astype(jnp.bfloat16)
            both_parts = jnp.dot(
                normed[...], weight[:, HEAD_DIM:], preferred_element_type=jnp.float32
            )
            row = lax.broadcasted_iota(jnp.int32, (chunk, HEAD_DIM), 0) + position * chunk
            keys[at, :] = turn(both_parts[:, :HEAD_DIM], key_gain_ref[...], row, at)
            values[at, :] = both_parts[:, HEAD_DIM:].astype(jnp.bfloat16)
            asked = jnp.dot(
                normed[tiles(0, core, rows), :],
                weight[:, :HEAD_DIM],
                preferred_element_type=jnp.float32,
            )
            own_at = tiles(0, position * 2 + core, rows)
            row = lax.broadcasted_iota(jnp.int32, (rows, HEAD_DIM), 0) + (
                (position * 2 + core) * rows
            )
            queries[tiles(0, position, rows), :] = turn(asked, query_gain_ref[...], row, own_at)
            return carry

        lax.fori_loop(0, 2, project, 0)

    def both(distance, run):
        @pl.when(z >= distance)
        def _():
            run(z - distance)

        @pl.when(z + distance < layers)
        def _():
            run(z + distance)

    def onward(layer):
        for da in range(2):
            arrive(place(layer, da, 0, core))
            spread_out(layer, da, False, start)

    def over(layer):
        for da in range(2):
            arrive(place(layer, da, 1, core))
            hand_over(layer, da, start)

    arrive(place(z, 1, 0, core))
    spread_out(z, 1, False, start)
    both(1, onward)
    over(z)
    for which in range(3):
        head_keep(which).wait()
    head_hand(0).start()
    for step in range(1, chips):
        head_part(step).wait_recv()
    for step in range(1, chips):
        head_hand(step).start()
    both(2, onward)
    both(1, over)
    last_spread(z, True, start)
    mixture_copy.start()
    router_copy.start()
    keep_block.wait()
    for step in range(chips):
        head_hand(step).wait_recv()
    for fetch in fetches[1:]:
        fetch.wait()
    take(z)
    both(1, take)
    both(3, onward)
    both(1, last_onward)
    both(2, over)
    both(2, take)
    last_over(z)
    both(2, last_onward)
    both(3, over)
    both(3, take)
    both(1, last_over)
    both(3, last_onward)

    key_row = lax.broadcasted_iota(jnp.int32, (1, total), 1)
    key_seg = jnp.where(keep_ref[...] == 1, segment_of(key_row, ends), -1)
    scale = HEAD_DIM ** (-0.5) * 1.4426950408889634

    def swap(block):
        return remote(
            mixed_rows.at[tiles(0, block, rows), :],
            out_ref.at[chip],
            swap_send.at[block],
            swap_recv.at[chip],
            (block * 2 + core, x),
        )

    def swapped(source):
        return remote(
            mixed_rows.at[0:rows, :],
            out_ref.at[source],
            swap_send.at[source],
            swap_recv.at[source],
            to_twin,
        )

    swap_keep = pltpu.make_async_copy(
        mixed_rows.at[tiles(0, chip, rows), :], out_ref.at[chip], out_sem
    )

    def attend(step, carry):
        at = tiles(0, step, chunk)
        scores = lax.dot_general(
            queries[at, :], keys[...], (((1,), (1,)), ((), ())), preferred_element_type=jnp.float32
        )
        local_row = lax.broadcasted_iota(jnp.int32, (chunk, 1), 0)
        second = (local_row >= rows).astype(jnp.int32)
        row = ((step * 2 + second) * 2 + core) * rows + local_row - second * rows
        visible = (segment_of(row, ends) == key_seg) | (row == key_row)
        masked = jnp.where(visible, scores, NEG)
        top = jnp.max(masked, axis=1, keepdims=True)
        weights = jnp.exp2((masked - top) * scale)
        totals = jnp.sum(weights, axis=1, keepdims=True)
        mixed = jnp.dot(
            weights.astype(jnp.bfloat16), values[...], preferred_element_type=jnp.float32
        )
        mixed_rows[at, :] = (mixed / totals).astype(jnp.bfloat16)
        for side in range(2):
            block = step * 2 + side

            @pl.when(block != chip)
            def _():
                swap(block).start()

            @pl.when(block == chip)
            def _():
                swap_keep.start()

        return carry

    turns = total // 2 // chunk
    lax.fori_loop(0, turns // 2, attend, 0)
    both(2, last_over)
    lax.fori_loop(turns // 2, turns, attend, 0)
    both(3, last_over)

    last_keep.wait()
    swap_keep.wait()

    def settle_swap(other, carry):
        @pl.when(other != chip)
        def _():
            swapped(other).wait_recv()
            swap(other).wait_send()

        return carry

    lax.fori_loop(0, chips, settle_swap, 0)

    def drain(layer, carry):
        for da in range(2):
            spread_out(layer, da, False, finish)
            hand_over(layer, da, finish)
            last_to_twin(layer, da).wait_recv()
        last_spread(layer, False, finish)
        last_to_twin(layer, 1).wait_send()
        return carry

    lax.fori_loop(0, layers, drain, 0)
    head_hand(0).wait_send()
    for step in range(1, chips):
        head_hand(step).wait_send()
        head_part(step).wait_send()
    for copy in pair_keep + [mixture_copy, router_copy]:
        copy.wait()


def front_call(
    tokens,
    lengths,
    keep_mask,
    attention_gain,
    query_gain,
    key_gain,
    query_weight,
    key_weight,
    value_weight,
    output_weight,
    router,
    mixture_gain,
):
    dp_count, mp_count = lax.axis_size("dp"), lax.axis_size("mp")
    rows, half = tokens.shape
    total, width = dp_count * rows, mp_count * half
    layers, chips = dp_count // 4, dp_count // 2
    halves = HEAD_DIM // 2
    exponent = np.arange(halves, dtype=np.float32) * np.float32(2.0 / HEAD_DIM)
    frequency = np.power(np.float32(ROPE_BASE), -exponent).astype(np.float32)
    frequency = np.concatenate([frequency, frequency])[None, :]
    angle = np.arange(total, dtype=np.float32)[:, None] * frequency
    cos_table = np.cos(angle.astype(np.float64)).astype(np.float32)
    sin_table = np.sin(angle.astype(np.float64)).astype(np.float32)
    smem = pl.BlockSpec(memory_space=pltpu.SMEM)
    hbm = pl.BlockSpec(memory_space=pltpu.HBM)
    dma = pltpu.SemaphoreType.DMA
    narrow = jnp.bfloat16
    return pl.pallas_call(
        front_kernel,
        out_shape=(
            jax.ShapeDtypeStruct((chips, rows, HEAD_DIM), narrow),
            jax.ShapeDtypeStruct((dp_count,) + output_weight.shape, narrow),
            jax.ShapeDtypeStruct((mp_count,) + router.shape, router.dtype),
            jax.ShapeDtypeStruct((mp_count,) + mixture_gain.shape, mixture_gain.dtype),
        ),
        in_specs=[smem] + [hbm] * 14,
        out_specs=(hbm,) * 4,
        scratch_shapes=[
            pltpu.VMEM((1, width), jnp.float32),
            pltpu.VMEM((1, HEAD_DIM), jnp.float32),
            pltpu.VMEM((1, HEAD_DIM), jnp.float32),
            pltpu.VMEM((1, total), jnp.int32),
            pltpu.VMEM((1, HEAD_DIM), jnp.float32),
            pltpu.VMEM((total, HEAD_DIM), jnp.float32),
            pltpu.VMEM((total, HEAD_DIM), jnp.float32),
            dma((7,)),
            pltpu.VMEM((total, width), narrow),
            pltpu.VMEM((total // 2, HEAD_DIM), narrow),
            pltpu.VMEM((chips, rows, 3 * HEAD_DIM), narrow),
            dma((3 * chips,)),
            dma((2,)),
            dma((2,)),
            dma((2,)),
            pltpu.VMEM((width, 3 * HEAD_DIM), narrow),
            pltpu.VMEM((2 * rows, width), narrow),
            pltpu.VMEM((total, HEAD_DIM), narrow),
            pltpu.VMEM((total, HEAD_DIM), narrow),
            pltpu.VMEM((total // 2, HEAD_DIM), narrow),
            pltpu.VMEM((8, HEAD_DIM), jnp.float32),
            pltpu.VMEM((8, HEAD_DIM), jnp.float32),
            dma((chips,)),
            dma((chips,)),
            dma((chips,)),
            dma((chips,)),
            dma((3,)),
            dma((3,)),
            dma((layers,)),
            dma((layers * 2,)),
            dma((layers * 2,)),
            dma((layers * 2,)),
            dma((layers * 4,)),
            dma((dp_count * mp_count,)),
            dma((layers,)),
            dma((layers,)),
            dma((layers,)),
            dma((layers * 2,)),
            dma((layers * 4,)),
            dma((chips,)),
            dma((chips,)),
            dma,
        ],
        compiler_params=pltpu.CompilerParams(
            collective_id=3, has_side_effects=True, vmem_limit_bytes=60 * 1024 * 1024
        ),
        name="attention_layer",
    )(
        lengths,
        tokens,
        query_weight,
        key_weight,
        value_weight,
        output_weight,
        router,
        mixture_gain,
        attention_gain[None, :],
        query_gain[None, :],
        key_gain[None, :],
        keep_mask[None, :],
        jnp.asarray(frequency),
        jnp.asarray(cos_table),
        jnp.asarray(sin_table),
    )


def layer_kernel(
    attended_ref,
    weight_ref,
    tokens_ref,
    routes_ref,
    router_ref,
    gain_ref,
    gate_ref,
    up_ref,
    down_ref,
    out_ref,
    gathered,
    sent_half,
    got_half,
    residual,
    router_own,
    all_routes,
    all_router,
    all_gain,
    held,
    mixed,
    gate,
    up,
    down,
    rows_in,
    hidden,
    wide,
    spread,
    twin,
    cross,
    rise,
    fall,
    last,
    far,
    route_send,
    route_recv,
    pair_send,
    pair_recv,
    local_sem,
    wide_sem,
    gate_sem,
    up_sem,
    down_sem,
    first_sem,
    rise_sem,
    fall_sem,
    b_sem,
    hand_sem,
    block_recv,
    far_sem,
    merge_send,
    far_recv,
    twin_send,
    cross_send,
    z_send,
    last_send,
    twin_recv,
    cross_recv,
    rise_recv,
    fall_recv,
    last_recv,
):
    index = lax.axis_index("dp")
    x = lax.axis_index("mp")
    dp_count = lax.axis_size("dp")
    layers = dp_count // 4
    heads = attended_ref.shape[0]
    core, chip = index % 2, index // 2
    z, y = index // 4, chip % 2
    rows, half = tokens_ref.shape
    width = 2 * half
    tile = 256
    held_count = rows_in.shape[0]
    units = hidden.shape[1]
    first_expert = index * (EXPERTS // dp_count) + x * held_count
    to_a = (index + core * (2 - 4 * y), x + (1 - core) * (1 - 2 * x))
    to_b = (index + (1 - core) * (2 - 4 * y), x + core * (1 - 2 * x))
    to_twin = (index + 1 - 2 * core, x)
    to_up, to_down = (index + 4, x), (index - 4, x)
    has_up, has_down = z < layers - 1, z > 0

    def remote(source, target, send_sem, recv_sem, device):
        return pltpu.make_async_remote_copy(
            src_ref=source,
            dst_ref=target,
            send_sem=send_sem,
            recv_sem=recv_sem,
            device_id=device,
            device_id_type=MESH,
        )

    def tiles(start, step, size):
        return pl.ds(pl.multiple_of(start + step * size, size), size)

    barrier = pltpu.get_barrier_semaphore()
    for step in range(1, dp_count):
        peer = lax.rem(index + step, dp_count)
        pl.semaphore_signal(barrier, inc=1, device_id=(peer, x), device_id_type=MESH)
    pl.semaphore_signal(barrier, inc=1, device_id=(index, 1 - x), device_id_type=MESH)

    load_wide = [
        pltpu.make_async_copy(
            weight_ref.at[block], wide.at[:, block * rows : (block + 1) * rows], wide_sem.at[block]
        )
        for block in range(dp_count)
    ]
    for load in load_wide:
        load.start()

    def load_expert(expert):
        columns = tiles(0, expert, units)
        return (
            pltpu.make_async_copy(gate_ref.at[:, columns], gate.at[:, columns], gate_sem.at[expert]),
            pltpu.make_async_copy(up_ref.at[:, columns], up.at[:, columns], up_sem.at[expert]),
            pltpu.make_async_copy(down_ref.at[columns, :], down.at[columns, :], down_sem.at[expert]),
        )


    def route(step):
        return remote(
            routes_ref,
            all_routes.at[index],
            route_send.at[step],
            route_recv.at[step],
            (lax.rem(index + step, dp_count), x),
        )

    across_x = (index, 1 - x)
    def half_copy(turn):
        at = tiles(0, turn, tile)
        return remote(
            sent_half.at[:, at],
            got_half.at[:, at],
            pair_send.at[turn],
            pair_recv.at[turn],
            across_x,
        )

    keep = [
        pltpu.make_async_copy(attended_ref, gathered, local_sem.at[0]),
        pltpu.make_async_copy(routes_ref, all_routes.at[index], local_sem.at[1]),
        pltpu.make_async_copy(router_ref, router_own, local_sem.at[2]),
        pltpu.make_async_copy(gain_ref, all_gain, local_sem.at[3]),
        pltpu.make_async_copy(tokens_ref, residual, local_sem.at[5]),
    ]
    for copy in keep:
        copy.start()
    pl.semaphore_wait(barrier, dp_count)
    for expert in range(held_count):
        for copy in load_expert(expert):
            copy.start()
    for copy in keep[1:]:
        copy.wait()
    for side in range(2):
        at = slice(side * half, (side + 1) * half)
        rest = router_own[side] * all_gain[side]
        for term in range(3):
            rounded = rest.astype(jnp.bfloat16)
            all_router[term * EXPERTS : (term + 1) * EXPERTS, at] = rounded
            rest = rest - rounded.astype(jnp.float32)
        all_router[3 * EXPERTS :, at] = jnp.zeros(rest.shape, jnp.bfloat16)
    keep[0].wait()
    for load in load_wide:
        load.wait()

    def all_heads():
        return jnp.concatenate([gathered[head] for head in range(heads)], 1)

    def away(turn, carry):
        sent_half[:, tiles(0, turn, tile)] = jnp.dot(
            all_heads(),
            wide[:, tiles((1 - x) * half, turn, tile)],
            preferred_element_type=jnp.float32,
        ).astype(jnp.bfloat16)
        half_copy(turn).start()
        return carry

    lax.fori_loop(0, half // tile, away, 0)
    for step in range(1, dp_count):
        route(step).start()

    def stay(turn, carry):
        at = tiles(0, turn, tile)
        out_ref[:, at] = residual[:, at].astype(jnp.float32) + jnp.dot(
            all_heads(),
            wide[:, tiles(x * half, turn, tile)],
            preferred_element_type=jnp.float32,
        )
        return carry

    lax.fori_loop(0, half // tile, stay, 0)

    def settle_tile(turn, carry):
        at = tiles(0, turn, tile)
        half_copy(turn).wait_recv()
        residual[:, at] = (out_ref[:, at] + got_half[:, at].astype(jnp.float32)).astype(
            jnp.bfloat16
        )
        out_ref[:, at] = residual[:, at].astype(jnp.float32)
        return carry

    lax.fori_loop(0, half // tile, settle_tile, 0)

    def place(layer, da, db, which):
        dy = which * da + (1 - which) * db
        dx = (1 - which) * da + which * db
        yy, xx = y + dy * (1 - 2 * y), x + dx * (1 - 2 * x)
        return layer * 4 + yy * 2 + which, xx

    def view(spot):
        return held.at[tiles(0, spot[0], rows), tiles(0, spot[1], half)]

    def send(spot, sem, device, own_block=False):
        return remote(
            residual if own_block else view(spot),
            view(spot),
            sem,
            block_recv.at[spot[0] * 2 + spot[1]],
            device,
        )

    def arrive(spot):
        send(spot, first_sem.at[1], to_twin).wait_recv()

    home_spot = place(z, 0, 0, core)
    keep_block = pltpu.make_async_copy(residual, view(home_spot), first_sem.at[1])
    first = send(home_spot, first_sem.at[0], to_a, True)

    def spread_out(layer, da, own_block, act):
        spot = place(layer, da, 0, core)
        slot = layer * 2 + da
        up_too = (layer <= z) & has_up
        down_too = (layer >= z) & has_down
        if da:
            up_too = up_too & (z + 1 - layer < layers - 1)
            down_too = down_too & (layer - z + 1 < layers - 1)
        else:

            @pl.when((z - layer == layers - 1) | (layer - z == layers - 1))
            def _():
                act(send(spot, far_sem, to_a, own_block))

        @pl.when(up_too)
        def _():
            act(send(spot, rise_sem.at[slot], to_up, own_block))

        @pl.when(down_too)
        def _():
            act(send(spot, fall_sem.at[slot], to_down, own_block))

        act(send(spot, b_sem.at[slot], to_b, own_block))
        act(send(spot, hand_sem.at[slot * 2], to_twin, own_block))

    def hand_over(layer, da, act):
        spot = place(layer, da, 1, core)
        act(send(spot, hand_sem.at[(layer * 2 + da) * 2 + 1], to_twin))

    start = lambda copy: copy.start()
    finish = lambda copy: copy.wait_send()

    earlier = (
        lax.broadcasted_iota(jnp.int32, (rows, rows), 0)
        < lax.broadcasted_iota(jnp.int32, (rows, rows), 1)
    ).astype(jnp.bfloat16)
    expert_id = lax.broadcasted_iota(jnp.int32, (EXPERTS, rows), 0)
    slot_id = lax.broadcasted_iota(jnp.int32, (CAP, rows), 0)

    def block_slots(block, logits, inverse):
        named_ids = all_routes[block]
        named = named_ids[0:1, :] == expert_id
        for k in range(1, TOPK):
            named = named | (named_ids[k : k + 1, :] == expert_id)
        logits_t = jnp.transpose(logits * inverse)[:EXPERTS]
        sigmoid = jnp.where(named, 1.0 / (1.0 + jnp.exp(-logits_t)), 0.0)
        route = sigmoid / jnp.sum(sigmoid, axis=0, keepdims=True)
        named_f = named.astype(jnp.float32)
        here, weight = [], []
        for expert in range(held_count):
            own = expert_id == first_expert + expert
            here.append(jnp.sum(jnp.where(own, named_f, 0.0), axis=0, keepdims=True))
            weight.append(jnp.sum(jnp.where(own, route, 0.0), axis=0, keepdims=True))
        stacked = jnp.concatenate(here + [jnp.zeros((8 - held_count, rows), jnp.float32)], 0)
        before = jnp.dot(
            stacked.astype(jnp.bfloat16), earlier, preferred_element_type=jnp.float32
        )
        slot_of = jnp.where(stacked > 0.5, before.astype(jnp.int32), -1)
        chosen = jnp.concatenate(
            [slot_of[expert : expert + 1, :] == slot_id for expert in range(held_count)], 0
        )
        weights = jnp.concatenate(
            [jnp.broadcast_to(w, (CAP, rows)) for w in weight], 0
        )
        spread_w = jnp.where(chosen, weights, 0.0)
        high = spread_w.astype(jnp.bfloat16)
        low = (spread_w - high.astype(jnp.float32)).astype(jnp.bfloat16)
        return chosen.astype(jnp.float32).astype(jnp.bfloat16), high, low

    chunk = 2 * rows

    def take(layer):
        for da in range(2):
            for db in range(2):
                arrive(place(layer, da, db, 1 - core))

        def one(step, carry):
            position = layer * 2 + step
            at = tiles(0, position, chunk)
            h = held[at, :].astype(jnp.float32)
            inverse = lax.rsqrt(jnp.mean(h * h, axis=1, keepdims=True) + EPS)
            gain_row = jnp.concatenate([all_gain[0], all_gain[1]], 1)
            mixed[...] = (h * gain_row * inverse).astype(jnp.bfloat16)
            logits = lax.dot_general(
                held[at, :],
                all_router[...],
                (((1,), (1,)), ((), ())),
                preferred_element_type=jnp.float32,
            )
            logits = logits[:, :128] + logits[:, 128:]
            logits = logits + pltpu.roll(logits, EXPERTS, 1)
            chosen, spreads = [], []
            for side in range(2):
                part = slice(side * rows, (side + 1) * rows)
                pick, high, low = block_slots(position * 2 + side, logits[part], inverse[part])
                chosen.append(pick)
                spreads += [(high, side), (low, side)]
            empty = jnp.zeros_like(chosen[0])
            select = jnp.concatenate(
                [
                    jnp.concatenate([chosen[0], empty], 1),
                    jnp.concatenate([empty, chosen[1]], 1),
                ],
                0,
            )
            taken = jnp.dot(select, mixed[...], preferred_element_type=jnp.float32).astype(
                jnp.bfloat16
            )
            for side in range(2):
                for expert in range(held_count):
                    source = (side * held_count + expert) * CAP
                    rows_in[expert, tiles(0, position * 2 + side, CAP), :] = taken[
                        source : source + CAP
                    ]
            spread[position] = jnp.concatenate(
                [
                    jnp.concatenate([value, empty] if side == 0 else [empty, value], 1)
                    for value, side in spreads
                ],
                0,
            )
            return carry

        lax.fori_loop(0, 2, one, 0)

    first.start()
    spread_out(z, 0, True, start)
    keep_block.start()
    arrive(place(z, 1, 0, core))
    spread_out(z, 1, False, start)

    def both(distance, run):
        @pl.when(z >= distance)
        def _():
            run(z - distance)

        @pl.when(z + distance < layers)
        def _():
            run(z + distance)

    def onward(layer):
        for da in range(2):
            arrive(place(layer, da, 0, core))
            spread_out(layer, da, False, start)

    def over(layer):
        for da in range(2):
            arrive(place(layer, da, 1, core))
            hand_over(layer, da, start)

    keep_block.wait()
    for step in range(1, dp_count):
        route(step).wait_recv()
    slots = hidden.shape[0]

    def feed(expert, part):
        at_rows = tiles(0, part, slots)

        def widen(turn, carry):
            columns = tiles(expert * units, turn, tile)
            gate_val = jnp.dot(
                rows_in[expert, at_rows, :], gate[:, columns], preferred_element_type=jnp.float32
            )
            up_val = jnp.dot(
                rows_in[expert, at_rows, :], up[:, columns], preferred_element_type=jnp.float32
            )
            silu = gate_val / (1.0 + jnp.exp(-gate_val))
            hidden[:, tiles(0, turn, tile)] = (silu * up_val).astype(jnp.bfloat16)
            return carry

        lax.fori_loop(0, units // tile, widen, 0)

        def narrow(turn, carry):
            at = tiles(0, turn, tile)
            wide[tiles(expert * 2 * slots, part, slots), at] = jnp.dot(
                hidden[...],
                down[expert * units : (expert + 1) * units, at],
                preferred_element_type=jnp.float32,
            ).astype(jnp.bfloat16)
            return carry

        lax.fori_loop(0, width // tile, narrow, 0)

    near_half = (z >= layers // 2).astype(jnp.int32)
    both(1, onward)
    over(z)
    take(z)
    both(2, onward)
    both(1, over)
    both(1, take)
    for expert in range(held_count):
        for load in load_expert(expert):
            load.wait()
    feed(0, near_half)
    both(3, onward)
    both(2, over)
    both(2, take)
    feed(1, near_half)
    both(3, over)
    both(3, take)
    for expert in range(held_count):
        feed(expert, 1 - near_half)

    first.wait_send()
    for turn in range(half // tile):
        half_copy(turn).wait_send()

    def sent(layer, carry):
        for da in range(2):
            spread_out(layer, da, False, finish)
            hand_over(layer, da, finish)
        return carry

    lax.fori_loop(0, layers, sent, 0)

    def combine(position):
        pieces = []
        for side in range(2):
            block = position * 2 + side
            pieces += [
                wide[tiles(expert * dp_count * CAP, block, CAP), :] for expert in range(held_count)
            ] * 2
        held[tiles(0, position, chunk), :] = lax.dot_general(
            spread[position],
            jnp.concatenate(pieces, 0),
            (((0,), (0,)), ((), ())),
            preferred_element_type=jnp.float32,
        ).astype(jnp.bfloat16)

    def mine(layer, da, db):
        return view(place(layer, da, db, core))

    def to_other_core(layer, da, db):
        slot = (layer * 2 + da) * 2 + db
        other = 1 - core
        return remote(
            view(place(layer, da, db, other)),
            twin.at[slot],
            twin_send.at[slot],
            twin_recv.at[slot],
            to_twin,
        )

    def to_cross(layer, da):
        pair = layer * 2 + da
        return remote(
            mine(layer, da, 1), cross.at[pair], cross_send.at[pair], cross_recv.at[pair], to_b
        )

    def upward(layer, da):
        pair = layer * 2 + da
        return remote(
            mine(layer, da, 0), rise.at[pair], z_send.at[pair], rise_recv.at[pair], to_up
        )

    def downward(layer, da):
        pair = layer * 2 + da
        return remote(
            mine(layer, da, 0), fall.at[pair], z_send.at[pair], fall_recv.at[pair], to_down
        )

    def to_last():
        return remote(mine(z, 1, 0), last, last_send, last_recv, to_a)

    def add(target, *sources):
        step = 32

        def body(turn, carry):
            at = tiles(0, turn, step)
            value = sources[0][at, :].astype(jnp.float32)
            for source in sources[1:]:
                value = value + source[at, :].astype(jnp.float32)
            target[at, :] = value.astype(target.dtype)
            return carry

        lax.fori_loop(0, rows // step, body, 0)

    inner = ((z == 1) | (z == 2)).astype(jnp.int32)
    below = (z < layers // 2).astype(jnp.int32)

    def ordered(step):
        step = jnp.asarray(step, jnp.int32)
        turned = step + inner * ((step == 2).astype(jnp.int32) - (step == 3).astype(jnp.int32))
        return turned + below * (layers - 1 - 2 * turned)

    def make(step, carry):
        layer = ordered(step)

        def one(side, inner_carry):
            combine(layer * 2 + side)
            return inner_carry

        lax.fori_loop(0, 2, one, 0)
        for db in (1, 0):
            for da in (1, 0):
                to_other_core(layer, da, db).start()
        return carry

    def pair_up(step):
        layer = ordered(step)
        for da in range(2):
            slot = (layer * 2 + da) * 2 + 1
            to_other_core(layer, da, 1).wait_recv()
            add(mine(layer, da, 1), mine(layer, da, 1), twin.at[slot])
            to_cross(layer, da).start()

    def make_and_pair(step, carry):
        make(step, 0)
        pair_up(step - 1)
        return carry

    make(0, 0)
    lax.fori_loop(1, layers, make_and_pair, 0)
    pair_up(layers - 1)

    def merges(layer):
        return ((z == 0) & (layer >= 2)) | ((z == layers - 1) & (layer <= layers - 3))

    def far_copy(layer):
        return remote(
            mine(layer, 1, 0), far.at[layer % 2], merge_send.at[layer % 2], far_recv.at[layer % 2], to_a
        )

    def gather_sum(layer, da, target, *more):
        pair = layer * 2 + da
        to_other_core(layer, da, 0).wait_recv()
        to_cross(layer, da).wait_recv()
        terms = (mine(layer, da, 0), twin.at[pair * 2], cross.at[pair]) + more
        from_down = has_down & (layer >= z)
        from_up = has_up & (layer <= z)
        if da:
            from_down = from_down & jnp.logical_not((z == 1) & (layer >= 2))
            from_up = from_up & jnp.logical_not((z == layers - 2) & (layer <= layers - 3))

        @pl.when(from_down)
        def _():
            upward(layer, da).wait_recv()

        @pl.when(from_up)
        def _():
            downward(layer, da).wait_recv()

        @pl.when(from_down & from_up)
        def _():
            add(target, *terms, rise.at[pair], fall.at[pair])

        @pl.when(from_down & jnp.logical_not(from_up))
        def _():
            add(target, *terms, rise.at[pair])

        @pl.when(from_up & jnp.logical_not(from_down))
        def _():
            add(target, *terms, fall.at[pair])

        @pl.when(jnp.logical_not(from_up | from_down))
        def _():
            add(target, *terms)

    def pass_on(step, carry):
        layer = ordered(step)
        rising = layer > z
        is_far = merges(layer)
        near = jnp.logical_not(is_far)

        gather_sum(layer, 1, mine(layer, 1, 0))

        @pl.when(is_far)
        def _():
            far_copy(layer).start()

        @pl.when(near & rising)
        def _():
            upward(layer, 1).start()

        @pl.when(near & jnp.logical_not(rising))
        def _():
            downward(layer, 1).start()

        @pl.when(near)
        def _():
            gather_sum(layer, 0, mine(layer, 0, 0))

        @pl.when(is_far)
        def _():
            pair = layer * 2
            to_other_core(layer, 0, 0).wait_recv()
            to_cross(layer, 0).wait_recv()
            far_copy(layer).wait_recv()
            add(
                mine(layer, 0, 0),
                mine(layer, 0, 0),
                twin.at[pair * 2],
                cross.at[pair],
                far.at[layer % 2],
            )

        @pl.when(rising)
        def _():
            upward(layer, 0).start()

        @pl.when(jnp.logical_not(rising))
        def _():
            downward(layer, 0).start()

        return carry

    lax.fori_loop(0, layers - 1, pass_on, 0)
    gather_sum(z, 1, mine(z, 1, 0))
    to_last().start()
    gather_sum(z, 0, out_ref, out_ref)
    to_last().wait_recv()
    add(out_ref, out_ref, last)

    def finish_layer(step, carry):
        layer = ordered(step)
        for da in range(2):
            to_other_core(layer, da, 0).wait_send()
            to_other_core(layer, da, 1).wait_send()
            to_cross(layer, da).wait_send()

            is_far = merges(layer)
            along = (layer != z) & jnp.logical_not(is_far) if da else layer != z

            @pl.when(along)
            def _():
                upward(layer, da).wait_send()

            if da:

                @pl.when(is_far)
                def _():
                    far_copy(layer).wait_send()

        return carry

    lax.fori_loop(0, layers, finish_layer, 0)
    to_last().wait_send()
    for step in range(1, dp_count):
        route(step).wait_send()


def layer_call(attended, weight, tokens, routes, router, gain, gate, up, down):
    dp_count, mp_count = lax.axis_size("dp"), lax.axis_size("mp")
    rows, half = tokens.shape
    width = mp_count * half
    layers = dp_count // 4
    pairs = dp_count // 2
    held_count = gate.shape[1] // FF
    dma = pltpu.SemaphoreType.DMA
    vmem = pl.BlockSpec(memory_space=pltpu.VMEM)
    hbm = pl.BlockSpec(memory_space=pltpu.HBM)
    block = (rows, half)
    narrow = jnp.bfloat16
    return pl.pallas_call(
        layer_kernel,
        out_shape=jax.ShapeDtypeStruct(block, jnp.float32),
        in_specs=[hbm] * 9,
        out_specs=vmem,
        scratch_shapes=[
            pltpu.VMEM(attended.shape, narrow),
            pltpu.VMEM(block, narrow),
            pltpu.VMEM(block, narrow),
            pltpu.VMEM(block, narrow),
            pltpu.VMEM(router.shape, jnp.float32),
            pltpu.VMEM((dp_count,) + routes.shape, routes.dtype),
            pltpu.VMEM((4 * EXPERTS, width), narrow),
            pltpu.VMEM((mp_count, 1, half), jnp.float32),
            pltpu.VMEM((dp_count * rows, width), narrow),
            pltpu.VMEM((2 * rows, width), narrow),
            pltpu.VMEM(gate.shape, narrow),
            pltpu.VMEM(up.shape, narrow),
            pltpu.VMEM(down.shape, narrow),
            pltpu.VMEM((held_count, dp_count * CAP, width), narrow),
            pltpu.VMEM((dp_count // 2 * CAP, FF), narrow),
            pltpu.VMEM((weight.shape[1], width), narrow),
            pltpu.VMEM((dp_count // 2, 4 * held_count * CAP, 2 * rows), narrow),
            pltpu.VMEM((2 * pairs,) + block, narrow),
            pltpu.VMEM((pairs,) + block, narrow),
            pltpu.VMEM((pairs,) + block, narrow),
            pltpu.VMEM((pairs,) + block, narrow),
            pltpu.VMEM(block, narrow),
            pltpu.VMEM((2,) + block, narrow),
            dma((dp_count,)),
            dma((dp_count,)),
            dma((half // 256,)),
            dma((half // 256,)),
            dma((6,)),
            dma((dp_count,)),
            dma((held_count,)),
            dma((held_count,)),
            dma((held_count,)),
            dma((2,)),
            dma((layers * 2,)),
            dma((layers * 2,)),
            dma((layers * 2,)),
            dma((layers * 4,)),
            dma((dp_count * mp_count,)),
            dma,
            dma((2,)),
            dma((2,)),
            dma((2 * pairs,)),
            dma((pairs,)),
            dma((pairs,)),
            dma,
            dma((2 * pairs,)),
            dma((pairs,)),
            dma((pairs,)),
            dma((pairs,)),
            dma,
        ],
        compiler_params=pltpu.CompilerParams(
            collective_id=2, has_side_effects=True, vmem_limit_bytes=60 * 1024 * 1024
        ),
        name="mixture_layer",
    )(attended, weight, tokens, routes, router, gain, gate, up, down)


def local_paired(
    tokens,
    lengths,
    keep_mask,
    routes,
    attention_gain,
    mixture_gain,
    query_gain,
    key_gain,
    query_weight,
    key_weight,
    value_weight,
    output_weight,
    router_weight,
    expert_gate,
    expert_up,
    expert_down,
):
    tok_rows, half = tokens.shape
    local_heads = query_weight.shape[1] // HEAD_DIM
    attended, all_output_weight, all_router, all_gain = front_call(
        tokens,
        lengths,
        keep_mask,
        attention_gain,
        query_gain,
        key_gain,
        query_weight,
        key_weight,
        value_weight,
        output_weight,
        router_weight.T,
        mixture_gain[None, :],
    )
    return layer_call(
        attended,
        all_output_weight,
        tokens,
        routes.T,
        all_router,
        all_gain,
        expert_gate[0],
        expert_up[0],
        expert_down[0],
    ).astype(jnp.bfloat16)


def local(*arrays):
    paired = lax.axis_size("mp") == 2 and lax.axis_size("dp") == 16
    return (local_paired if paired else local_any)(*arrays)


def solution(mesh):
    return jax.shard_map(
        local,
        mesh=mesh,
        in_specs=(
            P("dp", "mp"),
            P(),
            P(),
            P("dp", None),
            P(),
            P("mp"),
            P(),
            P(),
            P("dp", "mp"),
            P("dp", "mp"),
            P("dp", "mp"),
            P("mp", "dp"),
            P("mp", None),
            P("dp", None, "mp"),
            P("dp", None, "mp"),
            P("dp", "mp", None),
        ),
        out_specs=P("dp", "mp"),
        check_vma=False,
    )
```

```python
import jax
import jax.numpy as jnp
import numpy as np
from jax import lax
from jax.experimental import pallas as pl
from jax.experimental.pallas import tpu as pltpu
from jax.sharding import PartitionSpec as P

D = 2048
HEAD_DIM = 128
FF = 1024
EXPERTS = 64
TOPK = 8
CAP = 32


EPS = 1e-06
ROPE_BASE = 10000.0
NEG = -1e30


def rope_tables(position):
    halves = HEAD_DIM // 2
    exponent = jnp.arange(halves, dtype=jnp.float32) * (2.0 / HEAD_DIM)
    frequency = jnp.power(jnp.float32(ROPE_BASE), -exponent)
    angle = position.astype(jnp.float32)[:, None] * frequency[None, :]
    cos_table = jnp.cos(angle)
    sin_table = jnp.sin(angle)
    return (jnp.concatenate([cos_table, cos_table], 1), jnp.concatenate([sin_table, sin_table], 1))


def head_prep(projected, head_gain, cos_table, sin_table):
    row_count = projected.shape[0]
    per_head = projected.reshape(row_count, -1, HEAD_DIM)
    normed = (
        per_head * lax.rsqrt(jnp.mean(per_head * per_head, axis=2, keepdims=True) + EPS) * head_gain
    )
    halves = HEAD_DIM // 2
    rotated = jnp.concatenate([-normed[:, :, halves:], normed[:, :, :halves]], 2)
    turned = normed * cos_table[:, None, :] + rotated * sin_table[:, None, :]
    return turned.reshape(row_count, -1).astype(jnp.bfloat16)


def segment_info(lengths, global_row):
    count = jnp.arange(lengths.shape[0], dtype=jnp.int32)
    request_end = jnp.sum(jnp.where(count[None, :] <= count[:, None], lengths[None, :], 0), axis=1)
    request_start = request_end - lengths
    segment = jnp.sum((request_end[None, :] <= global_row[:, None]).astype(jnp.int32), axis=1)
    chosen = segment[:, None] == jnp.arange(lengths.shape[0], dtype=jnp.int32)[None, :]
    begin = jnp.sum(jnp.where(chosen, request_start[None, :], 0), axis=1)
    return (segment, global_row - begin)


MESH = pl.DeviceIdType.MESH


def greet_neighbours():
    index = lax.axis_index("dp")
    x = lax.axis_index("mp")
    layers = lax.axis_size("dp") // 4
    z, y = index // 4, (index // 2) % 2
    barrier = pltpu.get_barrier_semaphore()
    across_y, across_x = (index + 2 - 4 * y, x), (index, 1 - x)
    to_twin = (index + 1 - 2 * (index % 2), x)
    for peer in (across_y, across_x, to_twin):
        pl.semaphore_signal(barrier, inc=1, device_id=peer, device_id_type=MESH)
    has_up, has_down = z < layers - 1, z > 0

    @pl.when(has_up)
    def _():
        pl.semaphore_signal(barrier, inc=1, device_id=(index + 4, x), device_id_type=MESH)

    @pl.when(has_down)
    def _():
        pl.semaphore_signal(barrier, inc=1, device_id=(index - 4, x), device_id_type=MESH)

    pl.semaphore_wait(barrier, 3 + has_up.astype(jnp.int32) + has_down.astype(jnp.int32))


def gather_kernel(block_ref, out_ref, *sems):
    greet_neighbours()
    gather_steps(block_ref, out_ref, *sems)


def gather_steps(block_ref, out_ref, local_sem, a_sem, up_sem, down_sem, b_sem, twin_sem, recv_sem):
    index = lax.axis_index("dp")
    x = lax.axis_index("mp")
    layers = lax.axis_size("dp") // 4
    z, y, core = index // 4, (index // 2) % 2, index % 2
    rows, width = block_ref.shape
    to_a = (index + core * (2 - 4 * y), x + (1 - core) * (1 - 2 * x))
    to_b = (index + (1 - core) * (2 - 4 * y), x + core * (1 - 2 * x))
    to_twin = (index + 1 - 2 * core, x)
    to_up, to_down = (index + 4, x), (index - 4, x)

    def place(layer, da, db, which):
        dy = which * da + (1 - which) * db
        dx = (1 - which) * da + which * db
        yy, xx = y + dy * (1 - 2 * y), x + dx * (1 - 2 * x)
        return layer * 4 + yy * 2 + which, xx

    def view(spot):
        return out_ref.at[
            pl.ds(pl.multiple_of(spot[0] * rows, rows), rows),
            pl.ds(pl.multiple_of(spot[1] * width, width), width),
        ]

    def send(spot, sem, device, own=False):
        return pltpu.make_async_remote_copy(
            src_ref=block_ref if own else view(spot),
            dst_ref=view(spot),
            send_sem=sem,
            recv_sem=recv_sem.at[spot[0] * 2 + spot[1]],
            device_id=device,
            device_id_type=MESH,
        )

    def arrive(spot):
        send(spot, local_sem, to_twin).wait_recv()

    has_up, has_down = z < layers - 1, z > 0
    home = place(z, 0, 0, core)
    keep = pltpu.make_async_copy(block_ref, view(home), local_sem)
    first = send(home, a_sem, to_a, True)

    def spread(layer, da, own, act):
        spot = place(layer, da, 0, core)
        slot = layer * 2 + da

        @pl.when((layer <= z) & has_up)
        def _():
            act(send(spot, up_sem.at[slot], to_up, own))

        @pl.when((layer >= z) & has_down)
        def _():
            act(send(spot, down_sem.at[slot], to_down, own))

        act(send(spot, b_sem.at[slot], to_b, own))
        act(send(spot, twin_sem.at[slot * 2], to_twin, own))

    def hand_over(layer, da, act):
        spot = place(layer, da, 1, core)
        act(send(spot, twin_sem.at[(layer * 2 + da) * 2 + 1], to_twin))

    start = lambda copy: copy.start()
    finish = lambda copy: copy.wait_send()
    first.start()
    spread(z, 0, True, start)
    keep.start()
    arrive(place(z, 1, 0, core))
    spread(z, 1, False, start)

    def both(distance, run):
        for da in range(2):
            @pl.when(z >= distance)
            def _():
                run(z - distance, da)

            @pl.when(z + distance < layers)
            def _():
                run(z + distance, da)

    def onward(layer, da):
        arrive(place(layer, da, 0, core))
        spread(layer, da, False, start)

    def across(layer, da):
        arrive(place(layer, da, 1, core))
        hand_over(layer, da, start)

    for distance in range(1, layers):
        both(distance, onward)
        if distance == 1:
            for da in range(2):
                across(z, da)
        else:
            both(distance - 1, across)
    both(layers - 1, across)
    keep.wait()
    first.wait_send()
    for layer in range(layers):
        for da in range(2):
            spread(layer, da, False, finish)
            hand_over(layer, da, finish)
            for db in range(2):
                arrive(place(layer, da, db, 1 - core))


def gather_scratch(dp_count, mp_count, layers):
    dma = pltpu.SemaphoreType.DMA
    return [
        dma,
        dma,
        dma((layers * 2,)),
        dma((layers * 2,)),
        dma((layers * 2,)),
        dma((layers * 4,)),
        dma((dp_count * mp_count,)),
    ]


def gather_blocks(block):
    dp_count, mp_count = lax.axis_size("dp"), lax.axis_size("mp")
    rows, width = block.shape
    if mp_count != 2 or dp_count % 4:
        wide = lax.all_gather(block, "mp", axis=1, tiled=True)
        return lax.all_gather(wide, "dp", axis=0, tiled=True)
    layers = dp_count // 4
    return pl.pallas_call(
        gather_kernel,
        out_shape=jax.ShapeDtypeStruct((dp_count * rows, mp_count * width), block.dtype),
        in_specs=[pl.BlockSpec(memory_space=pl.ANY)],
        out_specs=pl.BlockSpec(memory_space=pl.ANY),
        scratch_shapes=gather_scratch(dp_count, mp_count, layers),
        compiler_params=pltpu.CompilerParams(collective_id=0, has_side_effects=True),
        name="gather_blocks",
    )(block)


def scatter_kernel(
    parts_ref,
    out_ref,
    mine,
    twin,
    cross,
    rise,
    fall,
    last,
    total,
    load_sem,
    twin_send,
    cross_send,
    z_send,
    last_send,
    twin_recv,
    cross_recv,
    rise_recv,
    fall_recv,
    last_recv,
):
    index = lax.axis_index("dp")
    x = lax.axis_index("mp")
    layers = lax.axis_size("dp") // 4
    z, y, core = index // 4, (index // 2) % 2, index % 2
    rows, width = out_ref.shape
    to_a = (index + core * (2 - 4 * y), x + (1 - core) * (1 - 2 * x))
    to_b = (index + (1 - core) * (2 - 4 * y), x + core * (1 - 2 * x))
    to_twin = (index + 1 - 2 * core, x)
    to_up, to_down = (index + 4, x), (index - 4, x)
    has_up, has_down = z < layers - 1, z > 0

    def view(layer, da, db, which):
        dy = which * da + (1 - which) * db
        dx = (1 - which) * da + which * db
        yy, xx = y + dy * (1 - 2 * y), x + dx * (1 - 2 * x)
        row = (layer * 4 + yy * 2 + which) * rows
        return parts_ref.at[
            pl.ds(pl.multiple_of(row, rows), rows),
            pl.ds(pl.multiple_of(xx * width, width), width),
        ]

    def remote(source, target, send_sem, recv_sem, device):
        return pltpu.make_async_remote_copy(
            src_ref=source,
            dst_ref=target,
            send_sem=send_sem,
            recv_sem=recv_sem,
            device_id=device,
            device_id_type=MESH,
        )

    barrier = pltpu.get_barrier_semaphore()
    for peer in (to_a, to_b, to_twin):
        pl.semaphore_signal(barrier, inc=1, device_id=peer, device_id_type=MESH)

    @pl.when(has_up)
    def _():
        pl.semaphore_signal(barrier, inc=1, device_id=to_up, device_id_type=MESH)

    @pl.when(has_down)
    def _():
        pl.semaphore_signal(barrier, inc=1, device_id=to_down, device_id_type=MESH)

    def outward(run):
        for distance in range(layers - 1, 0, -1):
            for da in range(2):
                @pl.when(z + distance < layers)
                def _():
                    run(z + distance, da, True)

                @pl.when(z >= distance)
                def _():
                    run(z - distance, da, False)

    def home(run):
        for da in (1, 0):
            run(z, da, None)

    def load(layer, da, db):
        slot = (layer * 2 + da) * 2 + db
        return pltpu.make_async_copy(view(layer, da, db, core), mine.at[slot], load_sem.at[slot])

    def to_other_core(layer, da, db):
        slot = (layer * 2 + da) * 2 + db
        return remote(
            view(layer, da, db, 1 - core),
            twin.at[slot],
            twin_send.at[slot],
            twin_recv.at[slot],
            to_twin,
        )

    def to_cross(layer, da):
        pair = layer * 2 + da
        return remote(
            mine.at[pair * 2 + 1], cross.at[pair], cross_send.at[pair], cross_recv.at[pair], to_b
        )

    def upward(layer, da):
        pair = layer * 2 + da
        return remote(mine.at[pair * 2], rise.at[pair], z_send.at[pair], rise_recv.at[pair], to_up)

    def downward(layer, da):
        pair = layer * 2 + da
        return remote(
            mine.at[pair * 2], fall.at[pair], z_send.at[pair], fall_recv.at[pair], to_down
        )

    def to_last():
        return remote(mine.at[(z * 2 + 1) * 2], last, last_send, last_recv, to_a)

    def add(target, *sources):
        step = 16

        def body(turn, carry):
            at = pl.ds(pl.multiple_of(turn * step, step), step)
            value = sources[0][at, :].astype(jnp.float32)
            for source in sources[1:]:
                value = value + source[at, :].astype(jnp.float32)
            target[at, :] = value.astype(target.dtype)
            return carry

        lax.fori_loop(0, rows // step, body, 0)

    for db in (1, 0):
        outward(lambda layer, da, up: load(layer, da, db).start())
        home(lambda layer, da, up: load(layer, da, db).start())
    pl.semaphore_wait(barrier, 3 + has_up.astype(jnp.int32) + has_down.astype(jnp.int32))
    for db in (1, 0):
        outward(lambda layer, da, up: to_other_core(layer, da, db).start())
        home(lambda layer, da, up: to_other_core(layer, da, db).start())

    def pair_up(layer, da, up):
        slot = (layer * 2 + da) * 2 + 1
        load(layer, da, 1).wait()
        to_other_core(layer, da, 1).wait_recv()
        add(mine.at[slot], mine.at[slot], twin.at[slot])
        to_cross(layer, da).start()

    outward(pair_up)
    home(pair_up)

    def collect(layer, da, target):
        pair = layer * 2 + da
        load(layer, da, 0).wait()
        to_other_core(layer, da, 0).wait_recv()
        to_cross(layer, da).wait_recv()
        add(target, mine.at[pair * 2], twin.at[pair * 2], cross.at[pair])

    def pass_on(layer, da, up):
        pair = layer * 2 + da
        collect(layer, da, total)
        if up:
            @pl.when(has_down)
            def _():
                upward(layer, da).wait_recv()
                add(total, total, rise.at[pair])
        else:
            @pl.when(has_up)
            def _():
                downward(layer, da).wait_recv()
                add(total, total, fall.at[pair])
        add(mine.at[pair * 2], total)
        (upward if up else downward)(layer, da).start()

    outward(pass_on)

    def settle(layer, da, up):
        pair = layer * 2 + da
        target = total if da else out_ref
        collect(layer, da, target)

        @pl.when(has_down)
        def _():
            upward(layer, da).wait_recv()
            add(target, target, rise.at[pair])

        @pl.when(has_up)
        def _():
            downward(layer, da).wait_recv()
            add(target, target, fall.at[pair])

        if da:
            add(mine.at[pair * 2], total)
            to_last().start()

    home(settle)
    to_last().wait_recv()
    add(out_ref, out_ref, last)

    def finish(layer, da, up):
        to_other_core(layer, da, 0).wait_send()
        to_other_core(layer, da, 1).wait_send()
        to_cross(layer, da).wait_send()
        if up is not None:
            (upward if up else downward)(layer, da).wait_send()

    outward(finish)
    home(finish)
    to_last().wait_send()


def scatter_sum(parts):
    dp_count, mp_count = lax.axis_size("dp"), lax.axis_size("mp")
    rows, width = parts.shape[0] // dp_count, parts.shape[1] // mp_count
    if mp_count != 2 or dp_count % 4:
        halves = lax.psum_scatter(parts, "mp", scatter_dimension=1, tiled=True)
        return lax.psum_scatter(halves, "dp", scatter_dimension=0, tiled=True)
    pairs = dp_count // 2
    dma = pltpu.SemaphoreType.DMA
    block = (rows, width)
    return pl.pallas_call(
        scatter_kernel,
        out_shape=jax.ShapeDtypeStruct(block, jnp.float32),
        in_specs=[pl.BlockSpec(memory_space=pl.ANY)],
        out_specs=pl.BlockSpec(memory_space=pltpu.VMEM),
        scratch_shapes=[
            pltpu.VMEM((2 * pairs,) + block, jnp.bfloat16),
            pltpu.VMEM((2 * pairs,) + block, jnp.bfloat16),
            pltpu.VMEM((pairs,) + block, jnp.bfloat16),
            pltpu.VMEM((pairs,) + block, jnp.bfloat16),
            pltpu.VMEM((pairs,) + block, jnp.bfloat16),
            pltpu.VMEM(block, jnp.bfloat16),
            pltpu.VMEM(block, jnp.float32),
            dma((2 * pairs,)),
            dma((2 * pairs,)),
            dma((pairs,)),
            dma((pairs,)),
            dma,
            dma((2 * pairs,)),
            dma((pairs,)),
            dma((pairs,)),
            dma((pairs,)),
            dma,
        ],
        compiler_params=pltpu.CompilerParams(
            collective_id=1, has_side_effects=True, vmem_limit_bytes=40 * 1024 * 1024
        ),
        name="scatter_sum",
    )(parts.astype(jnp.bfloat16))


def attention(queries, keys, values, query_seg, query_row, key_seg, key_row, keep_mask):
    scale = HEAD_DIM ** (-0.5)
    scores = (
        lax.dot_general(
            queries, keys, (((1,), (1,)), ((), ())), preferred_element_type=jnp.float32
        )
        * scale
    )
    visible = (query_seg[:, None] == key_seg[None, :]) & (
        (keep_mask[None, :] == 1) | (query_row[:, None] == key_row[None, :])
    )
    masked = jnp.where(visible, scores, NEG)
    top = jnp.max(masked, axis=1, keepdims=True)
    weights = jnp.where(visible, jnp.exp(masked - top), 0.0)
    totals = jnp.sum(weights, axis=1, keepdims=True)
    mixed = jnp.dot(weights.astype(jnp.bfloat16), values, preferred_element_type=jnp.float32)
    return (mixed / totals).astype(jnp.bfloat16)


def local_any(
    tokens,
    lengths,
    keep_mask,
    routes,
    attention_gain,
    mixture_gain,
    query_gain,
    key_gain,
    query_weight,
    key_weight,
    value_weight,
    output_weight,
    router_weight,
    expert_gate,
    expert_up,
    expert_down,
):
    tok_rows = tokens.shape[0]
    dp_count = lax.axis_size("dp")
    dp_index = lax.axis_index("dp")
    mp_index = lax.axis_index("mp")
    local_width = query_weight.shape[1]
    local_heads = local_width // HEAD_DIM
    share = dp_count // local_heads
    part = dp_index % share
    total_rows = tok_rows * dp_count

    weight_rows = query_weight.shape[0]
    packed = jnp.stack([query_weight, key_weight, value_weight]).reshape(
        3, weight_rows, local_heads, HEAD_DIM
    )
    packed = packed.transpose(2, 1, 0, 3).reshape(local_heads, weight_rows, 3 * HEAD_DIM)
    packed = jnp.repeat(packed, share, axis=0)
    head_weight = lax.all_to_all(packed, "dp", split_axis=0, concat_axis=0, tiled=True)
    head_weight = head_weight.reshape(dp_count * weight_rows, 3 * HEAD_DIM)

    all_tokens, head_weight, late_weight = lax.optimization_barrier(
        (gather_blocks(tokens), head_weight, output_weight)
    )
    all_output_weight = lax.all_gather(late_weight, "dp", axis=1, tiled=True)
    xfloat = all_tokens.astype(jnp.float32)
    all_in = (
        xfloat * lax.rsqrt(jnp.mean(xfloat * xfloat, axis=1, keepdims=True) + EPS) * attention_gain
    ).astype(jnp.bfloat16)
    all_routes = lax.all_gather(routes, "dp", axis=0, tiled=True)
    all_gain = lax.all_gather(mixture_gain, "mp", axis=0, tiled=True)
    all_router = lax.all_gather(router_weight, "mp", axis=0, tiled=True)

    key_row = jnp.arange(total_rows, dtype=jnp.int32)
    key_seg, key_pos = segment_info(lengths, key_row)
    cos_table, sin_table = rope_tables(key_pos)

    def own(array):
        split = array.reshape((local_heads, share, tok_rows) + array.shape[1:])
        taken = lax.dynamic_index_in_dim(split, part, 1, keepdims=False)
        return taken.reshape((local_heads * tok_rows,) + array.shape[1:])

    projected = jnp.dot(all_in, head_weight, preferred_element_type=jnp.float32)
    queries = head_prep(
        own(projected[:, :HEAD_DIM]), query_gain, own(cos_table), own(sin_table)
    )
    keys = head_prep(projected[:, HEAD_DIM : 2 * HEAD_DIM], key_gain, cos_table, sin_table)
    values = projected[:, 2 * HEAD_DIM :].astype(jnp.bfloat16)
    attended = attention(
        queries, keys, values, own(key_seg), own(key_row), key_seg, key_row, keep_mask
    )
    groups = [[head * share + p for head in range(local_heads)] for p in range(share)]
    attended = lax.all_to_all(
        attended.reshape(local_heads, tok_rows, HEAD_DIM),
        "dp",
        split_axis=0,
        concat_axis=0,
        tiled=True,
        axis_index_groups=groups,
    )
    attended = attended.transpose(1, 0, 2).reshape(tok_rows, local_width)
    partial_out = jnp.dot(attended, all_output_weight, preferred_element_type=jnp.float32)
    summed_out = lax.psum_scatter(partial_out, "mp", scatter_dimension=1, tiled=True)
    residual = (tokens.astype(jnp.float32) + summed_out).astype(jnp.bfloat16)
    all_residual = gather_blocks(residual)
    hfloat = all_residual.astype(jnp.float32)
    inverse = lax.rsqrt(jnp.mean(hfloat * hfloat, axis=1, keepdims=True) + EPS)
    mixed_in = (hfloat * all_gain * inverse).astype(jnp.bfloat16)

    own_rows = lax.dynamic_slice_in_dim(all_residual, dp_index * tok_rows, tok_rows, 0)
    own_float = own_rows.astype(jnp.float32)
    own_inverse = lax.rsqrt(jnp.mean(own_float * own_float, axis=1, keepdims=True) + EPS)
    logits = (
        jnp.dot(own_float * all_gain, all_router, precision=lax.Precision.HIGHEST) * own_inverse
    )

    ids = jnp.arange(tok_rows, dtype=jnp.int32)
    earlier = (ids[:, None] < ids[None, :]).astype(jnp.bfloat16)
    slots = jnp.arange(CAP, dtype=jnp.int32)

    def chosen_slots(named):
        before = jnp.dot(
            named.astype(jnp.bfloat16).reshape(-1, tok_rows),
            earlier,
            preferred_element_type=jnp.float32,
        ).reshape(named.shape)
        place = jnp.where(named, before.astype(jnp.int32), -1)
        return place[:, :, None, :] == slots[None, None, :, None]

    exp_local = EXPERTS // dp_count
    gate_local = expert_gate[0]
    up_local = expert_up[0]
    down_local = expert_down[0]
    unit_count = gate_local.shape[1]
    held = max(1, unit_count // FF)
    units = unit_count // held
    first_expert = (mp_index * unit_count) // FF

    own_experts = dp_index * exp_local + first_expert + jnp.arange(held, dtype=jnp.int32)
    block_routes = all_routes.reshape(dp_count, tok_rows, TOPK)
    here = jnp.any(block_routes[:, None] == own_experts[None, :, None, None], axis=3)
    chosen = chosen_slots(here)
    select = chosen.astype(jnp.bfloat16).reshape(dp_count, held * CAP, tok_rows)
    rows_in = lax.dot_general(
        select,
        mixed_in.reshape(dp_count, tok_rows, D),
        (((2,), (1,)), ((0,), (0,))),
        preferred_element_type=jnp.float32,
    ).astype(jnp.bfloat16)
    rows_in = rows_in.reshape(dp_count, held, CAP, D)
    experts = jnp.arange(EXPERTS, dtype=jnp.int32)
    named = jnp.any(routes[:, :, None] == experts[None, None, :], axis=1)
    sigmoid_vals = jax.nn.sigmoid(logits) * named.astype(jnp.float32)
    route_weight = sigmoid_vals / jnp.sum(sigmoid_vals, axis=1, keepdims=True)
    all_weights = lax.all_gather(route_weight, "dp", axis=0, tiled=True)
    outs = []
    for index in range(held):
        rows = rows_in[:, index].reshape(dp_count * CAP, D)
        low, high = index * units, (index + 1) * units
        gate_val = jnp.dot(rows, gate_local[:, low:high], preferred_element_type=jnp.float32)
        up_val = jnp.dot(rows, up_local[:, low:high], preferred_element_type=jnp.float32)
        hidden = (jax.nn.silu(gate_val) * up_val).astype(jnp.bfloat16)
        out = jnp.dot(hidden, down_local[low:high], preferred_element_type=jnp.float32)
        outs.append(out.astype(jnp.bfloat16).reshape(dp_count, CAP, D))
    first_own = dp_index * exp_local + first_expert
    own_weights = lax.dynamic_slice_in_dim(all_weights, first_own, held, 1)
    own_weights = own_weights.reshape(dp_count, tok_rows, held).transpose(0, 2, 1)
    spread = jnp.where(chosen, own_weights[:, :, None, :], 0.0)
    spread_high = spread.astype(jnp.bfloat16)
    spread_low = (spread - spread_high.astype(jnp.float32)).astype(jnp.bfloat16)
    contract = (((1,), (1,)), ((0,), (0,)))
    both = jnp.concatenate([spread_high, spread_low], 2).reshape(
        dp_count, held * 2 * CAP, tok_rows
    )
    out_rows = jnp.concatenate(sum([[out, out] for out in outs], []), axis=1)
    parts = lax.dot_general(both, out_rows, contract, preferred_element_type=jnp.float32)
    mixture = scatter_sum(parts.reshape(total_rows, D))
    return (residual.astype(jnp.float32) + mixture).astype(jnp.bfloat16)


def row_starts(lengths_ref):
    ends, starts, total = [], [], 0
    for index in range(lengths_ref.shape[0]):
        starts.append(total)
        total = total + lengths_ref[index]
        ends.append(total)
    return ends, starts


def segment_of(row, ends):
    segment = (row >= ends[0]).astype(jnp.int32)
    for end in ends[1:]:
        segment = segment + (row >= end).astype(jnp.int32)
    return segment


def front_kernel(
    lengths_ref,
    tokens_ref,
    query_ref,
    key_ref,
    value_ref,
    last_ref,
    router_ref,
    mixture_ref,
    gain_hbm,
    query_gain_hbm,
    key_gain_hbm,
    keep_hbm,
    frequency_hbm,
    cos_hbm,
    sin_hbm,
    out_ref,
    all_last_ref,
    all_router_ref,
    all_mixture_ref,
    gain_ref,
    query_gain_ref,
    key_gain_ref,
    keep_ref,
    frequency_ref,
    cos_ref,
    sin_ref,
    fetch_sem,
    held,
    mixed_rows,
    packed,
    pack_sem,
    pair_send,
    pair_recv,
    pair_local,
    weight,
    normed,
    keys,
    values,
    queries,
    start_cos,
    start_sin,
    head_send,
    head_recv,
    head_hand_send,
    head_hand_recv,
    head_local,
    local_sem,
    a_sem,
    rise_sem,
    fall_sem,
    b_sem,
    hand_sem,
    block_recv,
    last_rise,
    last_fall,
    last_side,
    last_hand,
    last_recv,
    swap_send,
    swap_recv,
    out_sem,
):
    index = lax.axis_index("dp")
    x = lax.axis_index("mp")
    dp_count = lax.axis_size("dp")
    layers = dp_count // 4
    chips = dp_count // 2
    core, chip = index % 2, index // 2
    z, y = index // 4, chip % 2
    rows, half = tokens_ref.shape
    total = dp_count * rows
    chunk = 2 * rows
    to_a = (index + 2 - 4 * y, x)
    to_b = (index, 1 - x)
    to_twin = (index + 1 - 2 * core, x)
    to_side = (index + 2 - 4 * y, x)
    to_up, to_down = (index + 4, x), (index - 4, x)
    has_up, has_down = z < layers - 1, z > 0

    def remote(source, target, send_sem, recv_sem, device):
        return pltpu.make_async_remote_copy(
            src_ref=source,
            dst_ref=target,
            send_sem=send_sem,
            recv_sem=recv_sem,
            device_id=device,
            device_id_type=MESH,
        )

    def tiles(start, step, size):
        return pl.ds(pl.multiple_of(start + step * size, size), size)

    barrier = pltpu.get_barrier_semaphore()
    for step in range(1, chips):
        peer = lax.rem(chip + step, chips) * 2 + core
        pl.semaphore_signal(barrier, inc=1, device_id=(peer, x), device_id_type=MESH)
    for peer in (to_twin, (index, 1 - x)):
        pl.semaphore_signal(barrier, inc=1, device_id=peer, device_id_type=MESH)

    fetches = [
        pltpu.make_async_copy(source, target, fetch_sem.at[number])
        for number, (source, target) in enumerate(
            (
                (frequency_hbm, frequency_ref),
                (gain_hbm, gain_ref),
                (query_gain_hbm, query_gain_ref),
                (key_gain_hbm, key_gain_ref),
                (keep_hbm, keep_ref),
                (cos_hbm, cos_ref),
                (sin_hbm, sin_ref),
            )
        )
    ]
    packs = []
    for number, source in enumerate((query_ref, key_ref, value_ref)):
        for head in range(chips):
            packs.append(
                pltpu.make_async_copy(
                    source.at[:, head * HEAD_DIM : (head + 1) * HEAD_DIM],
                    packed.at[head, :, number * HEAD_DIM : (number + 1) * HEAD_DIM],
                    pack_sem.at[number * chips + head],
                )
            )
    for pack in packs:
        pack.start()
    for fetch in fetches:
        fetch.start()

    def place(layer, da, db, which):
        yy, xx = y + da * (1 - 2 * y), x + db * (1 - 2 * x)
        return layer * 4 + yy * 2 + which, xx

    def view(spot):
        return held.at[tiles(0, spot[0], rows), tiles(0, spot[1], half)]

    def send(spot, sem, device, own_block=False):
        return remote(
            tokens_ref if own_block else view(spot),
            view(spot),
            sem,
            block_recv.at[spot[0] * 2 + spot[1]],
            device,
        )

    def arrive(spot):
        send(spot, local_sem.at[0], to_twin).wait_recv()

    late = core < 2

    def spread_out(layer, da, own_block, act):
        spot = place(layer, da, 0, core)
        slot = layer * 2 + da
        along = jnp.logical_not(late) if da else jnp.bool_(True)

        @pl.when((layer <= z) & has_up & along)
        def _():
            act(send(spot, rise_sem.at[slot], to_up, own_block))

        @pl.when((layer >= z) & has_down & along)
        def _():
            act(send(spot, fall_sem.at[slot], to_down, own_block))

        if not da:
            @pl.when((layer == z) | late)
            def _():
                act(send(spot, a_sem.at[layer], to_a, own_block))

        act(send(spot, b_sem.at[slot], to_b, own_block))
        act(send(spot, hand_sem.at[slot * 2], to_twin, own_block))

    def hand_over(layer, da, act):
        spot = place(layer, da, 1, core)
        act(send(spot, hand_sem.at[(layer * 2 + da) * 2 + 1], to_twin))

    start = lambda copy: copy.start()
    finish = lambda copy: copy.wait_send()
    keep_block = pltpu.make_async_copy(tokens_ref, view(place(z, 0, 0, core)), local_sem.at[1])

    sources = (query_ref, key_ref, value_ref)

    def head_part(step):
        other = lax.rem(chip + step, chips)
        return remote(
            packed.at[other],
            weight.at[tiles(0, index, rows), :],
            head_send.at[step],
            head_recv.at[step],
            (other * 2 + core, x),
        )

    def across_x(source, target, number):
        return remote(
            source, target.at[x], pair_send.at[number], pair_recv.at[number], (index, 1 - x)
        )

    router_copy = across_x(router_ref, all_router_ref, 0)
    mixture_copy = across_x(mixture_ref, all_mixture_ref, 1)
    pair_keep = [
        pltpu.make_async_copy(router_ref, all_router_ref.at[x], pair_local.at[0]),
        pltpu.make_async_copy(mixture_ref, all_mixture_ref.at[x], pair_local.at[1]),
    ]

    def head_keep(which):
        return pltpu.make_async_copy(
            sources[which].at[:, tiles(0, chip, HEAD_DIM)],
            weight.at[tiles(0, index, rows), which * HEAD_DIM : (which + 1) * HEAD_DIM],
            head_local.at[which],
        )

    def head_hand(step):
        block = lax.rem(chip + step, chips) * 2 + core
        at = weight.at[tiles(0, block, rows), :]
        return remote(at, at, head_hand_send.at[step], head_hand_recv.at[step], to_twin)

    def last_view(layer, side, which):
        yy = y + side * (1 - 2 * y)
        return all_last_ref.at[layer * 4 + yy * 2 + which]

    def last_copy(layer, side, sem, device, own_block=False):
        target = last_view(layer, side, core)
        return remote(
            last_ref if own_block else target,
            target,
            sem,
            last_recv.at[(layer * 2 + side) * 2],
            device,
        )

    def last_to_side(layer, own_block=False):
        target = last_view(layer, 0, core)
        return remote(
            last_ref if own_block else target,
            target,
            last_side.at[layer],
            last_recv.at[(layer * 2 + 1) * 2],
            to_side,
        )

    def last_to_twin(layer, side, own_block=False):
        target = last_view(layer, side, core)
        return remote(
            last_ref if own_block else target,
            target,
            last_hand.at[layer * 2 + side],
            last_recv.at[(layer * 2 + side) * 2 + 1],
            to_twin,
        )

    last_keep = pltpu.make_async_copy(last_ref, last_view(z, 0, core), local_sem.at[2])

    def last_spread(layer, own_block, act):
        @pl.when((layer <= z) & has_up)
        def _():
            act(last_copy(layer, 0, last_rise.at[layer], to_up, own_block))

        @pl.when((layer >= z) & has_down)
        def _():
            act(last_copy(layer, 0, last_fall.at[layer], to_down, own_block))

        act(last_to_side(layer, own_block))
        act(last_to_twin(layer, 0, own_block))

    def last_onward(layer):
        last_copy(layer, 0, last_rise.at[layer], to_up).wait_recv()
        last_spread(layer, False, start)

    def last_over(layer):
        last_to_side(layer).wait_recv()
        last_to_twin(layer, 1).start()

    pl.semaphore_wait(barrier, chips + 1)
    spread_out(z, 0, True, start)
    for which in range(3):
        head_keep(which).start()
    for pack in packs:
        pack.wait()
    for step in range(1, chips):
        head_part(step).start()
    keep_block.start()
    last_keep.start()
    for copy in pair_keep:
        copy.start()

    fetches[0].wait()
    ends, starts = row_starts(lengths_ref)
    which_row = lax.broadcasted_iota(jnp.int32, (8, HEAD_DIM), 0)
    begin = jnp.zeros((8, HEAD_DIM), jnp.int32)
    for number, first_row in enumerate(starts):
        begin = jnp.where(which_row == number, first_row, begin)
    angle = begin.astype(jnp.float32) * frequency_ref[...]
    start_cos[...] = jnp.cos(angle)
    start_sin[...] = jnp.sin(angle)

    def turn(projected, head_gain, row, at):
        square = jnp.mean(projected * projected, axis=1, keepdims=True)
        value = projected * lax.rsqrt(square + EPS) * head_gain
        cos_s, sin_s = start_cos[0:1, :], start_sin[0:1, :]
        for number in range(1, len(starts)):
            past = row >= ends[number - 1]
            cos_s = jnp.where(past, start_cos[number : number + 1, :], cos_s)
            sin_s = jnp.where(past, start_sin[number : number + 1, :], sin_s)
        cos_g, sin_g = cos_ref[at, :], sin_ref[at, :]
        cos_t = cos_g * cos_s + sin_g * sin_s
        sin_t = sin_g * cos_s - cos_g * sin_s
        lane = lax.broadcasted_iota(jnp.int32, value.shape, 1)
        halves = pltpu.roll(value, HEAD_DIM // 2, 1)
        rotated = jnp.where(lane < HEAD_DIM // 2, -halves, halves)
        return (value * cos_t + rotated * sin_t).astype(jnp.bfloat16)

    def take(layer):
        for da in range(2):
            for db in range(2):
                arrive(place(layer, da, db, 1 - core))

        def project(step, carry):
            position = layer * 2 + step
            at = tiles(0, position, chunk)
            value = held[at, :].astype(jnp.float32)
            inverse = lax.rsqrt(jnp.mean(value * value, axis=1, keepdims=True) + EPS)
            normed[...] = (value * inverse * gain_ref[...]).astype(jnp.bfloat16)
            both_parts = jnp.dot(
                normed[...], weight[:, HEAD_DIM:], preferred_element_type=jnp.float32
            )
            row = lax.broadcasted_iota(jnp.int32, (chunk, HEAD_DIM), 0) + position * chunk
            keys[at, :] = turn(both_parts[:, :HEAD_DIM], key_gain_ref[...], row, at)
            values[at, :] = both_parts[:, HEAD_DIM:].astype(jnp.bfloat16)
            asked = jnp.dot(
                normed[tiles(0, core, rows), :],
                weight[:, :HEAD_DIM],
                preferred_element_type=jnp.float32,
            )
            own_at = tiles(0, position * 2 + core, rows)
            row = lax.broadcasted_iota(jnp.int32, (rows, HEAD_DIM), 0) + (
                (position * 2 + core) * rows
            )
            queries[tiles(0, position, rows), :] = turn(asked, query_gain_ref[...], row, own_at)
            return carry

        lax.fori_loop(0, 2, project, 0)

    def both(distance, run):
        @pl.when(z >= distance)
        def _():
            run(z - distance)

        @pl.when(z + distance < layers)
        def _():
            run(z + distance)

    def onward(layer):
        for da in range(2):
            arrive(place(layer, da, 0, core))
            spread_out(layer, da, False, start)

    def over(layer):
        for da in range(2):
            arrive(place(layer, da, 1, core))
            hand_over(layer, da, start)

    arrive(place(z, 1, 0, core))
    spread_out(z, 1, False, start)
    both(1, onward)
    over(z)
    for which in range(3):
        head_keep(which).wait()
    head_hand(0).start()
    for step in range(1, chips):
        head_part(step).wait_recv()
    for step in range(1, chips):
        head_hand(step).start()
    both(2, onward)
    both(1, over)
    last_spread(z, True, start)
    mixture_copy.start()
    router_copy.start()
    keep_block.wait()
    for step in range(chips):
        head_hand(step).wait_recv()
    for fetch in fetches[1:]:
        fetch.wait()
    take(z)
    both(1, take)
    both(3, onward)
    both(1, last_onward)
    both(2, over)
    both(2, take)
    last_over(z)
    both(2, last_onward)
    both(3, over)
    both(3, take)
    both(1, last_over)
    both(3, last_onward)

    key_row = lax.broadcasted_iota(jnp.int32, (1, total), 1)
    key_seg = jnp.where(keep_ref[...] == 1, segment_of(key_row, ends), -1)
    scale = HEAD_DIM ** (-0.5) * 1.4426950408889634

    def swap(block):
        return remote(
            mixed_rows.at[tiles(0, block, rows), :],
            out_ref.at[chip],
            swap_send.at[block],
            swap_recv.at[chip],
            (block * 2 + core, x),
        )

    def swapped(source):
        return remote(
            mixed_rows.at[0:rows, :],
            out_ref.at[source],
            swap_send.at[source],
            swap_recv.at[source],
            to_twin,
        )

    swap_keep = pltpu.make_async_copy(
        mixed_rows.at[tiles(0, chip, rows), :], out_ref.at[chip], out_sem
    )

    def attend(step, carry):
        at = tiles(0, step, chunk)
        scores = lax.dot_general(
            queries[at, :], keys[...], (((1,), (1,)), ((), ())), preferred_element_type=jnp.float32
        )
        local_row = lax.broadcasted_iota(jnp.int32, (chunk, 1), 0)
        second = (local_row >= rows).astype(jnp.int32)
        row = ((step * 2 + second) * 2 + core) * rows + local_row - second * rows
        visible = (segment_of(row, ends) == key_seg) | (row == key_row)
        masked = jnp.where(visible, scores, NEG)
        top = jnp.max(masked, axis=1, keepdims=True)
        weights = jnp.exp2((masked - top) * scale)
        totals = jnp.sum(weights, axis=1, keepdims=True)
        mixed = jnp.dot(
            weights.astype(jnp.bfloat16), values[...], preferred_element_type=jnp.float32
        )
        mixed_rows[at, :] = (mixed / totals).astype(jnp.bfloat16)
        for side in range(2):
            block = step * 2 + side

            @pl.when(block != chip)
            def _():
                swap(block).start()

            @pl.when(block == chip)
            def _():
                swap_keep.start()

        return carry

    turns = total // 2 // chunk
    lax.fori_loop(0, turns // 2, attend, 0)
    both(2, last_over)
    lax.fori_loop(turns // 2, turns, attend, 0)
    both(3, last_over)

    last_keep.wait()
    swap_keep.wait()

    def settle_swap(other, carry):
        @pl.when(other != chip)
        def _():
            swapped(other).wait_recv()
            swap(other).wait_send()

        return carry

    lax.fori_loop(0, chips, settle_swap, 0)

    def drain(layer, carry):
        for da in range(2):
            spread_out(layer, da, False, finish)
            hand_over(layer, da, finish)
            last_to_twin(layer, da).wait_recv()
        last_spread(layer, False, finish)
        last_to_twin(layer, 1).wait_send()
        return carry

    lax.fori_loop(0, layers, drain, 0)
    head_hand(0).wait_send()
    for step in range(1, chips):
        head_hand(step).wait_send()
        head_part(step).wait_send()
    for copy in pair_keep + [mixture_copy, router_copy]:
        copy.wait()


def front_call(
    tokens,
    lengths,
    keep_mask,
    attention_gain,
    query_gain,
    key_gain,
    query_weight,
    key_weight,
    value_weight,
    output_weight,
    router,
    mixture_gain,
):
    dp_count, mp_count = lax.axis_size("dp"), lax.axis_size("mp")
    rows, half = tokens.shape
    total, width = dp_count * rows, mp_count * half
    layers, chips = dp_count // 4, dp_count // 2
    halves = HEAD_DIM // 2
    exponent = np.arange(halves, dtype=np.float32) * np.float32(2.0 / HEAD_DIM)
    frequency = np.power(np.float32(ROPE_BASE), -exponent).astype(np.float32)
    frequency = np.concatenate([frequency, frequency])[None, :]
    angle = np.arange(total, dtype=np.float32)[:, None] * frequency
    cos_table = np.cos(angle.astype(np.float64)).astype(np.float32)
    sin_table = np.sin(angle.astype(np.float64)).astype(np.float32)
    smem = pl.BlockSpec(memory_space=pltpu.SMEM)
    hbm = pl.BlockSpec(memory_space=pltpu.HBM)
    dma = pltpu.SemaphoreType.DMA
    narrow = jnp.bfloat16
    return pl.pallas_call(
        front_kernel,
        out_shape=(
            jax.ShapeDtypeStruct((chips, rows, HEAD_DIM), narrow),
            jax.ShapeDtypeStruct((dp_count,) + output_weight.shape, narrow),
            jax.ShapeDtypeStruct((mp_count,) + router.shape, router.dtype),
            jax.ShapeDtypeStruct((mp_count,) + mixture_gain.shape, mixture_gain.dtype),
        ),
        in_specs=[smem] + [hbm] * 14,
        out_specs=(hbm,) * 4,
        scratch_shapes=[
            pltpu.VMEM((1, width), jnp.float32),
            pltpu.VMEM((1, HEAD_DIM), jnp.float32),
            pltpu.VMEM((1, HEAD_DIM), jnp.float32),
            pltpu.VMEM((1, total), jnp.int32),
            pltpu.VMEM((1, HEAD_DIM), jnp.float32),
            pltpu.VMEM((total, HEAD_DIM), jnp.float32),
            pltpu.VMEM((total, HEAD_DIM), jnp.float32),
            dma((7,)),
            pltpu.VMEM((total, width), narrow),
            pltpu.VMEM((total // 2, HEAD_DIM), narrow),
            pltpu.VMEM((chips, rows, 3 * HEAD_DIM), narrow),
            dma((3 * chips,)),
            dma((2,)),
            dma((2,)),
            dma((2,)),
            pltpu.VMEM((width, 3 * HEAD_DIM), narrow),
            pltpu.VMEM((2 * rows, width), narrow),
            pltpu.VMEM((total, HEAD_DIM), narrow),
            pltpu.VMEM((total, HEAD_DIM), narrow),
            pltpu.VMEM((total // 2, HEAD_DIM), narrow),
            pltpu.VMEM((8, HEAD_DIM), jnp.float32),
            pltpu.VMEM((8, HEAD_DIM), jnp.float32),
            dma((chips,)),
            dma((chips,)),
            dma((chips,)),
            dma((chips,)),
            dma((3,)),
            dma((3,)),
            dma((layers,)),
            dma((layers * 2,)),
            dma((layers * 2,)),
            dma((layers * 2,)),
            dma((layers * 4,)),
            dma((dp_count * mp_count,)),
            dma((layers,)),
            dma((layers,)),
            dma((layers,)),
            dma((layers * 2,)),
            dma((layers * 4,)),
            dma((chips,)),
            dma((chips,)),
            dma,
        ],
        compiler_params=pltpu.CompilerParams(
            collective_id=3, has_side_effects=True, vmem_limit_bytes=60 * 1024 * 1024
        ),
        name="attention_layer",
    )(
        lengths,
        tokens,
        query_weight,
        key_weight,
        value_weight,
        output_weight,
        router,
        mixture_gain,
        attention_gain[None, :],
        query_gain[None, :],
        key_gain[None, :],
        keep_mask[None, :],
        jnp.asarray(frequency),
        jnp.asarray(cos_table),
        jnp.asarray(sin_table),
    )


def layer_kernel(
    attended_ref,
    weight_ref,
    tokens_ref,
    routes_ref,
    router_ref,
    gain_ref,
    gate_ref,
    up_ref,
    down_ref,
    out_ref,
    gathered,
    sent_half,
    got_half,
    residual,
    router_own,
    all_routes,
    all_router,
    all_gain,
    held,
    mixed,
    gate,
    up,
    down,
    rows_in,
    hidden,
    wide,
    spread,
    twin,
    cross,
    rise,
    fall,
    last,
    far,
    route_send,
    route_recv,
    pair_send,
    pair_recv,
    local_sem,
    wide_sem,
    gate_sem,
    up_sem,
    down_sem,
    first_sem,
    rise_sem,
    fall_sem,
    b_sem,
    hand_sem,
    block_recv,
    far_sem,
    merge_send,
    far_recv,
    twin_send,
    cross_send,
    z_send,
    last_send,
    twin_recv,
    cross_recv,
    rise_recv,
    fall_recv,
    last_recv,
):
    index = lax.axis_index("dp")
    x = lax.axis_index("mp")
    dp_count = lax.axis_size("dp")
    layers = dp_count // 4
    heads = attended_ref.shape[0]
    core, chip = index % 2, index // 2
    z, y = index // 4, chip % 2
    rows, half = tokens_ref.shape
    width = 2 * half
    tile = 256
    held_count = rows_in.shape[0]
    units = hidden.shape[1]
    first_expert = index * (EXPERTS // dp_count) + x * held_count
    to_a = (index + core * (2 - 4 * y), x + (1 - core) * (1 - 2 * x))
    to_b = (index + (1 - core) * (2 - 4 * y), x + core * (1 - 2 * x))
    to_twin = (index + 1 - 2 * core, x)
    to_up, to_down = (index + 4, x), (index - 4, x)
    has_up, has_down = z < layers - 1, z > 0

    def remote(source, target, send_sem, recv_sem, device):
        return pltpu.make_async_remote_copy(
            src_ref=source,
            dst_ref=target,
            send_sem=send_sem,
            recv_sem=recv_sem,
            device_id=device,
            device_id_type=MESH,
        )

    def tiles(start, step, size):
        return pl.ds(pl.multiple_of(start + step * size, size), size)

    barrier = pltpu.get_barrier_semaphore()
    for step in range(1, dp_count):
        peer = lax.rem(index + step, dp_count)
        pl.semaphore_signal(barrier, inc=1, device_id=(peer, x), device_id_type=MESH)
    pl.semaphore_signal(barrier, inc=1, device_id=(index, 1 - x), device_id_type=MESH)

    load_wide = [
        pltpu.make_async_copy(
            weight_ref.at[block], wide.at[:, block * rows : (block + 1) * rows], wide_sem.at[block]
        )
        for block in range(dp_count)
    ]
    for load in load_wide:
        load.start()

    def load_expert(expert):
        columns = tiles(0, expert, units)
        return (
            pltpu.make_async_copy(gate_ref.at[:, columns], gate.at[:, columns], gate_sem.at[expert]),
            pltpu.make_async_copy(up_ref.at[:, columns], up.at[:, columns], up_sem.at[expert]),
            pltpu.make_async_copy(down_ref.at[columns, :], down.at[columns, :], down_sem.at[expert]),
        )


    def route(step):
        return remote(
            routes_ref,
            all_routes.at[index],
            route_send.at[step],
            route_recv.at[step],
            (lax.rem(index + step, dp_count), x),
        )

    across_x = (index, 1 - x)
    def half_copy(turn):
        at = tiles(0, turn, tile)
        return remote(
            sent_half.at[:, at],
            got_half.at[:, at],
            pair_send.at[turn],
            pair_recv.at[turn],
            across_x,
        )

    keep = [
        pltpu.make_async_copy(attended_ref, gathered, local_sem.at[0]),
        pltpu.make_async_copy(routes_ref, all_routes.at[index], local_sem.at[1]),
        pltpu.make_async_copy(router_ref, router_own, local_sem.at[2]),
        pltpu.make_async_copy(gain_ref, all_gain, local_sem.at[3]),
        pltpu.make_async_copy(tokens_ref, residual, local_sem.at[5]),
    ]
    for copy in keep:
        copy.start()
    pl.semaphore_wait(barrier, dp_count)
    for expert in range(held_count):
        for copy in load_expert(expert):
            copy.start()
    for copy in keep[1:]:
        copy.wait()
    for side in range(2):
        at = slice(side * half, (side + 1) * half)
        rest = router_own[side] * all_gain[side]
        for term in range(3):
            rounded = rest.astype(jnp.bfloat16)
            all_router[term * EXPERTS : (term + 1) * EXPERTS, at] = rounded
            rest = rest - rounded.astype(jnp.float32)
        all_router[3 * EXPERTS :, at] = jnp.zeros(rest.shape, jnp.bfloat16)
    keep[0].wait()
    for load in load_wide:
        load.wait()

    def all_heads():
        return jnp.concatenate([gathered[head] for head in range(heads)], 1)

    def away(turn, carry):
        sent_half[:, tiles(0, turn, tile)] = jnp.dot(
            all_heads(),
            wide[:, tiles((1 - x) * half, turn, tile)],
            preferred_element_type=jnp.float32,
        ).astype(jnp.bfloat16)
        half_copy(turn).start()
        return carry

    lax.fori_loop(0, half // tile, away, 0)
    for step in range(1, dp_count):
        route(step).start()

    def stay(turn, carry):
        at = tiles(0, turn, tile)
        out_ref[:, at] = residual[:, at].astype(jnp.float32) + jnp.dot(
            all_heads(),
            wide[:, tiles(x * half, turn, tile)],
            preferred_element_type=jnp.float32,
        )
        return carry

    lax.fori_loop(0, half // tile, stay, 0)

    def settle_tile(turn, carry):
        at = tiles(0, turn, tile)
        half_copy(turn).wait_recv()
        residual[:, at] = (out_ref[:, at] + got_half[:, at].astype(jnp.float32)).astype(
            jnp.bfloat16
        )
        out_ref[:, at] = residual[:, at].astype(jnp.float32)
        return carry

    lax.fori_loop(0, half // tile, settle_tile, 0)

    def place(layer, da, db, which):
        dy = which * da + (1 - which) * db
        dx = (1 - which) * da + which * db
        yy, xx = y + dy * (1 - 2 * y), x + dx * (1 - 2 * x)
        return layer * 4 + yy * 2 + which, xx

    def view(spot):
        return held.at[tiles(0, spot[0], rows), tiles(0, spot[1], half)]

    def send(spot, sem, device, own_block=False):
        return remote(
            residual if own_block else view(spot),
            view(spot),
            sem,
            block_recv.at[spot[0] * 2 + spot[1]],
            device,
        )

    def arrive(spot):
        send(spot, first_sem.at[1], to_twin).wait_recv()

    home_spot = place(z, 0, 0, core)
    keep_block = pltpu.make_async_copy(residual, view(home_spot), first_sem.at[1])
    first = send(home_spot, first_sem.at[0], to_a, True)

    def spread_out(layer, da, own_block, act):
        spot = place(layer, da, 0, core)
        slot = layer * 2 + da
        up_too = (layer <= z) & has_up
        down_too = (layer >= z) & has_down
        if da:
            up_too = up_too & (z + 1 - layer < layers - 1)
            down_too = down_too & (layer - z + 1 < layers - 1)
        else:

            @pl.when((z - layer == layers - 1) | (layer - z == layers - 1))
            def _():
                act(send(spot, far_sem, to_a, own_block))

        @pl.when(up_too)
        def _():
            act(send(spot, rise_sem.at[slot], to_up, own_block))

        @pl.when(down_too)
        def _():
            act(send(spot, fall_sem.at[slot], to_down, own_block))

        act(send(spot, b_sem.at[slot], to_b, own_block))
        act(send(spot, hand_sem.at[slot * 2], to_twin, own_block))

    def hand_over(layer, da, act):
        spot = place(layer, da, 1, core)
        act(send(spot, hand_sem.at[(layer * 2 + da) * 2 + 1], to_twin))

    start = lambda copy: copy.start()
    finish = lambda copy: copy.wait_send()

    earlier = (
        lax.broadcasted_iota(jnp.int32, (rows, rows), 0)
        < lax.broadcasted_iota(jnp.int32, (rows, rows), 1)
    ).astype(jnp.bfloat16)
    expert_id = lax.broadcasted_iota(jnp.int32, (EXPERTS, rows), 0)
    slot_id = lax.broadcasted_iota(jnp.int32, (CAP, rows), 0)

    def block_slots(block, logits, inverse):
        named_ids = all_routes[block]
        named = named_ids[0:1, :] == expert_id
        for k in range(1, TOPK):
            named = named | (named_ids[k : k + 1, :] == expert_id)
        logits_t = jnp.transpose(logits * inverse)[:EXPERTS]
        sigmoid = jnp.where(named, 1.0 / (1.0 + jnp.exp(-logits_t)), 0.0)
        route = sigmoid / jnp.sum(sigmoid, axis=0, keepdims=True)
        named_f = named.astype(jnp.float32)
        here, weight = [], []
        for expert in range(held_count):
            own = expert_id == first_expert + expert
            here.append(jnp.sum(jnp.where(own, named_f, 0.0), axis=0, keepdims=True))
            weight.append(jnp.sum(jnp.where(own, route, 0.0), axis=0, keepdims=True))
        stacked = jnp.concatenate(here + [jnp.zeros((8 - held_count, rows), jnp.float32)], 0)
        before = jnp.dot(
            stacked.astype(jnp.bfloat16), earlier, preferred_element_type=jnp.float32
        )
        slot_of = jnp.where(stacked > 0.5, before.astype(jnp.int32), -1)
        chosen = jnp.concatenate(
            [slot_of[expert : expert + 1, :] == slot_id for expert in range(held_count)], 0
        )
        weights = jnp.concatenate(
            [jnp.broadcast_to(w, (CAP, rows)) for w in weight], 0
        )
        spread_w = jnp.where(chosen, weights, 0.0)
        high = spread_w.astype(jnp.bfloat16)
        low = (spread_w - high.astype(jnp.float32)).astype(jnp.bfloat16)
        return chosen.astype(jnp.float32).astype(jnp.bfloat16), high, low

    chunk = 2 * rows

    def take(layer):
        for da in range(2):
            for db in range(2):
                arrive(place(layer, da, db, 1 - core))

        def one(step, carry):
            position = layer * 2 + step
            at = tiles(0, position, chunk)
            h = held[at, :].astype(jnp.float32)
            inverse = lax.rsqrt(jnp.mean(h * h, axis=1, keepdims=True) + EPS)
            gain_row = jnp.concatenate([all_gain[0], all_gain[1]], 1)
            mixed[...] = (h * gain_row * inverse).astype(jnp.bfloat16)
            logits = lax.dot_general(
                held[at, :],
                all_router[...],
                (((1,), (1,)), ((), ())),
                preferred_element_type=jnp.float32,
            )
            logits = logits[:, :128] + logits[:, 128:]
            logits = logits + pltpu.roll(logits, EXPERTS, 1)
            chosen, spreads = [], []
            for side in range(2):
                part = slice(side * rows, (side + 1) * rows)
                pick, high, low = block_slots(position * 2 + side, logits[part], inverse[part])
                chosen.append(pick)
                spreads += [(high, side), (low, side)]
            empty = jnp.zeros_like(chosen[0])
            select = jnp.concatenate(
                [
                    jnp.concatenate([chosen[0], empty], 1),
                    jnp.concatenate([empty, chosen[1]], 1),
                ],
                0,
            )
            taken = jnp.dot(select, mixed[...], preferred_element_type=jnp.float32).astype(
                jnp.bfloat16
            )
            for side in range(2):
                for expert in range(held_count):
                    source = (side * held_count + expert) * CAP
                    rows_in[expert, tiles(0, position * 2 + side, CAP), :] = taken[
                        source : source + CAP
                    ]
            spread[position] = jnp.concatenate(
                [
                    jnp.concatenate([value, empty] if side == 0 else [empty, value], 1)
                    for value, side in spreads
                ],
                0,
            )
            return carry

        lax.fori_loop(0, 2, one, 0)

    first.start()
    spread_out(z, 0, True, start)
    keep_block.start()
    arrive(place(z, 1, 0, core))
    spread_out(z, 1, False, start)

    def both(distance, run):
        @pl.when(z >= distance)
        def _():
            run(z - distance)

        @pl.when(z + distance < layers)
        def _():
            run(z + distance)

    def onward(layer):
        for da in range(2):
            arrive(place(layer, da, 0, core))
            spread_out(layer, da, False, start)

    def over(layer):
        for da in range(2):
            arrive(place(layer, da, 1, core))
            hand_over(layer, da, start)

    keep_block.wait()
    for step in range(1, dp_count):
        route(step).wait_recv()
    slots = hidden.shape[0]

    def feed(expert, part):
        at_rows = tiles(0, part, slots)

        def widen(turn, carry):
            columns = tiles(expert * units, turn, tile)
            gate_val = jnp.dot(
                rows_in[expert, at_rows, :], gate[:, columns], preferred_element_type=jnp.float32
            )
            up_val = jnp.dot(
                rows_in[expert, at_rows, :], up[:, columns], preferred_element_type=jnp.float32
            )
            silu = gate_val / (1.0 + jnp.exp(-gate_val))
            hidden[:, tiles(0, turn, tile)] = (silu * up_val).astype(jnp.bfloat16)
            return carry

        lax.fori_loop(0, units // tile, widen, 0)

        def narrow(turn, carry):
            at = tiles(0, turn, tile)
            wide[tiles(expert * 2 * slots, part, slots), at] = jnp.dot(
                hidden[...],
                down[expert * units : (expert + 1) * units, at],
                preferred_element_type=jnp.float32,
            ).astype(jnp.bfloat16)
            return carry

        lax.fori_loop(0, width // tile, narrow, 0)

    near_half = (z >= layers // 2).astype(jnp.int32)
    both(1, onward)
    over(z)
    take(z)
    both(2, onward)
    both(1, over)
    both(1, take)
    for expert in range(held_count):
        for load in load_expert(expert):
            load.wait()
    feed(0, near_half)
    both(3, onward)
    both(2, over)
    both(2, take)
    feed(1, near_half)
    both(3, over)
    both(3, take)
    for expert in range(held_count):
        feed(expert, 1 - near_half)

    first.wait_send()
    for turn in range(half // tile):
        half_copy(turn).wait_send()

    def sent(layer, carry):
        for da in range(2):
            spread_out(layer, da, False, finish)
            hand_over(layer, da, finish)
        return carry

    lax.fori_loop(0, layers, sent, 0)

    def combine(position):
        pieces = []
        for side in range(2):
            block = position * 2 + side
            pieces += [
                wide[tiles(expert * dp_count * CAP, block, CAP), :] for expert in range(held_count)
            ] * 2
        held[tiles(0, position, chunk), :] = lax.dot_general(
            spread[position],
            jnp.concatenate(pieces, 0),
            (((0,), (0,)), ((), ())),
            preferred_element_type=jnp.float32,
        ).astype(jnp.bfloat16)

    def mine(layer, da, db):
        return view(place(layer, da, db, core))

    def to_other_core(layer, da, db):
        slot = (layer * 2 + da) * 2 + db
        other = 1 - core
        return remote(
            view(place(layer, da, db, other)),
            twin.at[slot],
            twin_send.at[slot],
            twin_recv.at[slot],
            to_twin,
        )

    def to_cross(layer, da):
        pair = layer * 2 + da
        return remote(
            mine(layer, da, 1), cross.at[pair], cross_send.at[pair], cross_recv.at[pair], to_b
        )

    def upward(layer, da):
        pair = layer * 2 + da
        return remote(
            mine(layer, da, 0), rise.at[pair], z_send.at[pair], rise_recv.at[pair], to_up
        )

    def downward(layer, da):
        pair = layer * 2 + da
        return remote(
            mine(layer, da, 0), fall.at[pair], z_send.at[pair], fall_recv.at[pair], to_down
        )

    def to_last():
        return remote(mine(z, 1, 0), last, last_send, last_recv, to_a)

    def add(target, *sources):
        step = 32

        def body(turn, carry):
            at = tiles(0, turn, step)
            value = sources[0][at, :].astype(jnp.float32)
            for source in sources[1:]:
                value = value + source[at, :].astype(jnp.float32)
            target[at, :] = value.astype(target.dtype)
            return carry

        lax.fori_loop(0, rows // step, body, 0)

    inner = ((z == 1) | (z == 2)).astype(jnp.int32)
    below = (z < layers // 2).astype(jnp.int32)

    def ordered(step):
        step = jnp.asarray(step, jnp.int32)
        turned = step + inner * ((step == 2).astype(jnp.int32) - (step == 3).astype(jnp.int32))
        return turned + below * (layers - 1 - 2 * turned)

    def make(step, carry):
        layer = ordered(step)

        def one(side, inner_carry):
            combine(layer * 2 + side)
            return inner_carry

        lax.fori_loop(0, 2, one, 0)
        for db in (1, 0):
            for da in (1, 0):
                to_other_core(layer, da, db).start()
        return carry

    def pair_up(step):
        layer = ordered(step)
        for da in range(2):
            slot = (layer * 2 + da) * 2 + 1
            to_other_core(layer, da, 1).wait_recv()
            add(mine(layer, da, 1), mine(layer, da, 1), twin.at[slot])
            to_cross(layer, da).start()

    def make_and_pair(step, carry):
        make(step, 0)
        pair_up(step - 1)
        return carry

    make(0, 0)
    lax.fori_loop(1, layers, make_and_pair, 0)
    pair_up(layers - 1)

    def merges(layer):
        return ((z == 0) & (layer > z)) | ((z == layers - 1) & (layer < z))

    def far_copy(layer):
        return remote(
            mine(layer, 1, 0), far.at[layer % 3], merge_send.at[layer % 3], far_recv.at[layer % 3], to_a
        )

    def gather_sum(layer, da, target, *more):
        pair = layer * 2 + da
        to_other_core(layer, da, 0).wait_recv()
        to_cross(layer, da).wait_recv()
        terms = (mine(layer, da, 0), twin.at[pair * 2], cross.at[pair]) + more
        from_down = has_down & (layer >= z)
        from_up = has_up & (layer <= z)
        if da:
            from_down = from_down & (z != 1)
            from_up = from_up & (z != layers - 2)

        @pl.when(from_down)
        def _():
            upward(layer, da).wait_recv()

        @pl.when(from_up)
        def _():
            downward(layer, da).wait_recv()

        @pl.when(from_down & from_up)
        def _():
            add(target, *terms, rise.at[pair], fall.at[pair])

        @pl.when(from_down & jnp.logical_not(from_up))
        def _():
            add(target, *terms, rise.at[pair])

        @pl.when(from_up & jnp.logical_not(from_down))
        def _():
            add(target, *terms, fall.at[pair])

        @pl.when(jnp.logical_not(from_up | from_down))
        def _():
            add(target, *terms)

    def pass_on(step, carry):
        layer = ordered(step)
        rising = layer > z
        is_far = merges(layer)
        near = jnp.logical_not(is_far)

        gather_sum(layer, 1, mine(layer, 1, 0))

        @pl.when(is_far)
        def _():
            far_copy(layer).start()

        @pl.when(near & rising)
        def _():
            upward(layer, 1).start()

        @pl.when(near & jnp.logical_not(rising))
        def _():
            downward(layer, 1).start()

        @pl.when(near)
        def _():
            gather_sum(layer, 0, mine(layer, 0, 0))

        @pl.when(is_far)
        def _():
            pair = layer * 2
            to_other_core(layer, 0, 0).wait_recv()
            to_cross(layer, 0).wait_recv()
            far_copy(layer).wait_recv()
            add(
                mine(layer, 0, 0),
                mine(layer, 0, 0),
                twin.at[pair * 2],
                cross.at[pair],
                far.at[layer % 3],
            )

        @pl.when(rising)
        def _():
            upward(layer, 0).start()

        @pl.when(jnp.logical_not(rising))
        def _():
            downward(layer, 0).start()

        return carry

    lax.fori_loop(0, layers - 1, pass_on, 0)
    gather_sum(z, 1, mine(z, 1, 0))
    to_last().start()
    gather_sum(z, 0, out_ref, out_ref)
    to_last().wait_recv()
    add(out_ref, out_ref, last)

    def finish_layer(step, carry):
        layer = ordered(step)
        for da in range(2):
            to_other_core(layer, da, 0).wait_send()
            to_other_core(layer, da, 1).wait_send()
            to_cross(layer, da).wait_send()

            is_far = merges(layer)
            along = (layer != z) & jnp.logical_not(is_far) if da else layer != z

            @pl.when(along)
            def _():
                upward(layer, da).wait_send()

            if da:

                @pl.when(is_far)
                def _():
                    far_copy(layer).wait_send()

        return carry

    lax.fori_loop(0, layers, finish_layer, 0)
    to_last().wait_send()
    for step in range(1, dp_count):
        route(step).wait_send()


def layer_call(attended, weight, tokens, routes, router, gain, gate, up, down):
    dp_count, mp_count = lax.axis_size("dp"), lax.axis_size("mp")
    rows, half = tokens.shape
    width = mp_count * half
    layers = dp_count // 4
    pairs = dp_count // 2
    held_count = gate.shape[1] // FF
    dma = pltpu.SemaphoreType.DMA
    vmem = pl.BlockSpec(memory_space=pltpu.VMEM)
    hbm = pl.BlockSpec(memory_space=pltpu.HBM)
    block = (rows, half)
    narrow = jnp.bfloat16
    return pl.pallas_call(
        layer_kernel,
        out_shape=jax.ShapeDtypeStruct(block, jnp.float32),
        in_specs=[hbm] * 9,
        out_specs=vmem,
        scratch_shapes=[
            pltpu.VMEM(attended.shape, narrow),
            pltpu.VMEM(block, narrow),
            pltpu.VMEM(block, narrow),
            pltpu.VMEM(block, narrow),
            pltpu.VMEM(router.shape, jnp.float32),
            pltpu.VMEM((dp_count,) + routes.shape, routes.dtype),
            pltpu.VMEM((4 * EXPERTS, width), narrow),
            pltpu.VMEM((mp_count, 1, half), jnp.float32),
            pltpu.VMEM((dp_count * rows, width), narrow),
            pltpu.VMEM((2 * rows, width), narrow),
            pltpu.VMEM(gate.shape, narrow),
            pltpu.VMEM(up.shape, narrow),
            pltpu.VMEM(down.shape, narrow),
            pltpu.VMEM((held_count, dp_count * CAP, width), narrow),
            pltpu.VMEM((dp_count // 2 * CAP, FF), narrow),
            pltpu.VMEM((weight.shape[1], width), narrow),
            pltpu.VMEM((dp_count // 2, 4 * held_count * CAP, 2 * rows), narrow),
            pltpu.VMEM((2 * pairs,) + block, narrow),
            pltpu.VMEM((pairs,) + block, narrow),
            pltpu.VMEM((pairs,) + block, narrow),
            pltpu.VMEM((pairs,) + block, narrow),
            pltpu.VMEM(block, narrow),
            pltpu.VMEM((3,) + block, narrow),
            dma((dp_count,)),
            dma((dp_count,)),
            dma((half // 256,)),
            dma((half // 256,)),
            dma((6,)),
            dma((dp_count,)),
            dma((held_count,)),
            dma((held_count,)),
            dma((held_count,)),
            dma((2,)),
            dma((layers * 2,)),
            dma((layers * 2,)),
            dma((layers * 2,)),
            dma((layers * 4,)),
            dma((dp_count * mp_count,)),
            dma,
            dma((3,)),
            dma((3,)),
            dma((2 * pairs,)),
            dma((pairs,)),
            dma((pairs,)),
            dma,
            dma((2 * pairs,)),
            dma((pairs,)),
            dma((pairs,)),
            dma((pairs,)),
            dma,
        ],
        compiler_params=pltpu.CompilerParams(
            collective_id=2, has_side_effects=True, vmem_limit_bytes=60 * 1024 * 1024
        ),
        name="mixture_layer",
    )(attended, weight, tokens, routes, router, gain, gate, up, down)


def local_paired(
    tokens,
    lengths,
    keep_mask,
    routes,
    attention_gain,
    mixture_gain,
    query_gain,
    key_gain,
    query_weight,
    key_weight,
    value_weight,
    output_weight,
    router_weight,
    expert_gate,
    expert_up,
    expert_down,
):
    tok_rows, half = tokens.shape
    local_heads = query_weight.shape[1] // HEAD_DIM
    attended, all_output_weight, all_router, all_gain = front_call(
        tokens,
        lengths,
        keep_mask,
        attention_gain,
        query_gain,
        key_gain,
        query_weight,
        key_weight,
        value_weight,
        output_weight,
        router_weight.T,
        mixture_gain[None, :],
    )
    return layer_call(
        attended,
        all_output_weight,
        tokens,
        routes.T,
        all_router,
        all_gain,
        expert_gate[0],
        expert_up[0],
        expert_down[0],
    ).astype(jnp.bfloat16)


def local(*arrays):
    paired = lax.axis_size("mp") == 2 and lax.axis_size("dp") == 16
    return (local_paired if paired else local_any)(*arrays)


def solution(mesh):
    return jax.shard_map(
        local,
        mesh=mesh,
        in_specs=(
            P("dp", "mp"),
            P(),
            P(),
            P("dp", None),
            P(),
            P("mp"),
            P(),
            P(),
            P("dp", "mp"),
            P("dp", "mp"),
            P("dp", "mp"),
            P("mp", "dp"),
            P("mp", None),
            P("dp", None, "mp"),
            P("dp", None, "mp"),
            P("dp", "mp", None),
        ),
        out_specs=P("dp", "mp"),
        check_vma=False,
    )
```

```python
import jax
import jax.numpy as jnp
import numpy as np
from jax import lax
from jax.experimental import pallas as pl
from jax.experimental.pallas import tpu as pltpu
from jax.sharding import PartitionSpec as P

D = 2048
HEAD_DIM = 128
FF = 1024
EXPERTS = 64
TOPK = 8
CAP = 32


EPS = 1e-06
ROPE_BASE = 10000.0
NEG = -1e30


def rope_tables(position):
    halves = HEAD_DIM // 2
    exponent = jnp.arange(halves, dtype=jnp.float32) * (2.0 / HEAD_DIM)
    frequency = jnp.power(jnp.float32(ROPE_BASE), -exponent)
    angle = position.astype(jnp.float32)[:, None] * frequency[None, :]
    cos_table = jnp.cos(angle)
    sin_table = jnp.sin(angle)
    return (jnp.concatenate([cos_table, cos_table], 1), jnp.concatenate([sin_table, sin_table], 1))


def head_prep(projected, head_gain, cos_table, sin_table):
    row_count = projected.shape[0]
    per_head = projected.reshape(row_count, -1, HEAD_DIM)
    normed = (
        per_head * lax.rsqrt(jnp.mean(per_head * per_head, axis=2, keepdims=True) + EPS) * head_gain
    )
    halves = HEAD_DIM // 2
    rotated = jnp.concatenate([-normed[:, :, halves:], normed[:, :, :halves]], 2)
    turned = normed * cos_table[:, None, :] + rotated * sin_table[:, None, :]
    return turned.reshape(row_count, -1).astype(jnp.bfloat16)


def segment_info(lengths, global_row):
    count = jnp.arange(lengths.shape[0], dtype=jnp.int32)
    request_end = jnp.sum(jnp.where(count[None, :] <= count[:, None], lengths[None, :], 0), axis=1)
    request_start = request_end - lengths
    segment = jnp.sum((request_end[None, :] <= global_row[:, None]).astype(jnp.int32), axis=1)
    chosen = segment[:, None] == jnp.arange(lengths.shape[0], dtype=jnp.int32)[None, :]
    begin = jnp.sum(jnp.where(chosen, request_start[None, :], 0), axis=1)
    return (segment, global_row - begin)


MESH = pl.DeviceIdType.MESH


def greet_neighbours():
    index = lax.axis_index("dp")
    x = lax.axis_index("mp")
    layers = lax.axis_size("dp") // 4
    z, y = index // 4, (index // 2) % 2
    barrier = pltpu.get_barrier_semaphore()
    across_y, across_x = (index + 2 - 4 * y, x), (index, 1 - x)
    to_twin = (index + 1 - 2 * (index % 2), x)
    for peer in (across_y, across_x, to_twin):
        pl.semaphore_signal(barrier, inc=1, device_id=peer, device_id_type=MESH)
    has_up, has_down = z < layers - 1, z > 0

    @pl.when(has_up)
    def _():
        pl.semaphore_signal(barrier, inc=1, device_id=(index + 4, x), device_id_type=MESH)

    @pl.when(has_down)
    def _():
        pl.semaphore_signal(barrier, inc=1, device_id=(index - 4, x), device_id_type=MESH)

    pl.semaphore_wait(barrier, 3 + has_up.astype(jnp.int32) + has_down.astype(jnp.int32))


def gather_kernel(block_ref, out_ref, *sems):
    greet_neighbours()
    gather_steps(block_ref, out_ref, *sems)


def gather_steps(block_ref, out_ref, local_sem, a_sem, up_sem, down_sem, b_sem, twin_sem, recv_sem):
    index = lax.axis_index("dp")
    x = lax.axis_index("mp")
    layers = lax.axis_size("dp") // 4
    z, y, core = index // 4, (index // 2) % 2, index % 2
    rows, width = block_ref.shape
    to_a = (index + core * (2 - 4 * y), x + (1 - core) * (1 - 2 * x))
    to_b = (index + (1 - core) * (2 - 4 * y), x + core * (1 - 2 * x))
    to_twin = (index + 1 - 2 * core, x)
    to_up, to_down = (index + 4, x), (index - 4, x)

    def place(layer, da, db, which):
        dy = which * da + (1 - which) * db
        dx = (1 - which) * da + which * db
        yy, xx = y + dy * (1 - 2 * y), x + dx * (1 - 2 * x)
        return layer * 4 + yy * 2 + which, xx

    def view(spot):
        return out_ref.at[
            pl.ds(pl.multiple_of(spot[0] * rows, rows), rows),
            pl.ds(pl.multiple_of(spot[1] * width, width), width),
        ]

    def send(spot, sem, device, own=False):
        return pltpu.make_async_remote_copy(
            src_ref=block_ref if own else view(spot),
            dst_ref=view(spot),
            send_sem=sem,
            recv_sem=recv_sem.at[spot[0] * 2 + spot[1]],
            device_id=device,
            device_id_type=MESH,
        )

    def arrive(spot):
        send(spot, local_sem, to_twin).wait_recv()

    has_up, has_down = z < layers - 1, z > 0
    home = place(z, 0, 0, core)
    keep = pltpu.make_async_copy(block_ref, view(home), local_sem)
    first = send(home, a_sem, to_a, True)

    def spread(layer, da, own, act):
        spot = place(layer, da, 0, core)
        slot = layer * 2 + da

        @pl.when((layer <= z) & has_up)
        def _():
            act(send(spot, up_sem.at[slot], to_up, own))

        @pl.when((layer >= z) & has_down)
        def _():
            act(send(spot, down_sem.at[slot], to_down, own))

        act(send(spot, b_sem.at[slot], to_b, own))
        act(send(spot, twin_sem.at[slot * 2], to_twin, own))

    def hand_over(layer, da, act):
        spot = place(layer, da, 1, core)
        act(send(spot, twin_sem.at[(layer * 2 + da) * 2 + 1], to_twin))

    start = lambda copy: copy.start()
    finish = lambda copy: copy.wait_send()
    first.start()
    spread(z, 0, True, start)
    keep.start()
    arrive(place(z, 1, 0, core))
    spread(z, 1, False, start)

    def both(distance, run):
        for da in range(2):
            @pl.when(z >= distance)
            def _():
                run(z - distance, da)

            @pl.when(z + distance < layers)
            def _():
                run(z + distance, da)

    def onward(layer, da):
        arrive(place(layer, da, 0, core))
        spread(layer, da, False, start)

    def across(layer, da):
        arrive(place(layer, da, 1, core))
        hand_over(layer, da, start)

    for distance in range(1, layers):
        both(distance, onward)
        if distance == 1:
            for da in range(2):
                across(z, da)
        else:
            both(distance - 1, across)
    both(layers - 1, across)
    keep.wait()
    first.wait_send()
    for layer in range(layers):
        for da in range(2):
            spread(layer, da, False, finish)
            hand_over(layer, da, finish)
            for db in range(2):
                arrive(place(layer, da, db, 1 - core))


def gather_scratch(dp_count, mp_count, layers):
    dma = pltpu.SemaphoreType.DMA
    return [
        dma,
        dma,
        dma((layers * 2,)),
        dma((layers * 2,)),
        dma((layers * 2,)),
        dma((layers * 4,)),
        dma((dp_count * mp_count,)),
    ]


def gather_blocks(block):
    dp_count, mp_count = lax.axis_size("dp"), lax.axis_size("mp")
    rows, width = block.shape
    if mp_count != 2 or dp_count % 4:
        wide = lax.all_gather(block, "mp", axis=1, tiled=True)
        return lax.all_gather(wide, "dp", axis=0, tiled=True)
    layers = dp_count // 4
    return pl.pallas_call(
        gather_kernel,
        out_shape=jax.ShapeDtypeStruct((dp_count * rows, mp_count * width), block.dtype),
        in_specs=[pl.BlockSpec(memory_space=pl.ANY)],
        out_specs=pl.BlockSpec(memory_space=pl.ANY),
        scratch_shapes=gather_scratch(dp_count, mp_count, layers),
        compiler_params=pltpu.CompilerParams(collective_id=0, has_side_effects=True),
        name="gather_blocks",
    )(block)


def scatter_kernel(
    parts_ref,
    out_ref,
    mine,
    twin,
    cross,
    rise,
    fall,
    last,
    total,
    load_sem,
    twin_send,
    cross_send,
    z_send,
    last_send,
    twin_recv,
    cross_recv,
    rise_recv,
    fall_recv,
    last_recv,
):
    index = lax.axis_index("dp")
    x = lax.axis_index("mp")
    layers = lax.axis_size("dp") // 4
    z, y, core = index // 4, (index // 2) % 2, index % 2
    rows, width = out_ref.shape
    to_a = (index + core * (2 - 4 * y), x + (1 - core) * (1 - 2 * x))
    to_b = (index + (1 - core) * (2 - 4 * y), x + core * (1 - 2 * x))
    to_twin = (index + 1 - 2 * core, x)
    to_up, to_down = (index + 4, x), (index - 4, x)
    has_up, has_down = z < layers - 1, z > 0

    def view(layer, da, db, which):
        dy = which * da + (1 - which) * db
        dx = (1 - which) * da + which * db
        yy, xx = y + dy * (1 - 2 * y), x + dx * (1 - 2 * x)
        row = (layer * 4 + yy * 2 + which) * rows
        return parts_ref.at[
            pl.ds(pl.multiple_of(row, rows), rows),
            pl.ds(pl.multiple_of(xx * width, width), width),
        ]

    def remote(source, target, send_sem, recv_sem, device):
        return pltpu.make_async_remote_copy(
            src_ref=source,
            dst_ref=target,
            send_sem=send_sem,
            recv_sem=recv_sem,
            device_id=device,
            device_id_type=MESH,
        )

    barrier = pltpu.get_barrier_semaphore()
    for peer in (to_a, to_b, to_twin):
        pl.semaphore_signal(barrier, inc=1, device_id=peer, device_id_type=MESH)

    @pl.when(has_up)
    def _():
        pl.semaphore_signal(barrier, inc=1, device_id=to_up, device_id_type=MESH)

    @pl.when(has_down)
    def _():
        pl.semaphore_signal(barrier, inc=1, device_id=to_down, device_id_type=MESH)

    def outward(run):
        for distance in range(layers - 1, 0, -1):
            for da in range(2):
                @pl.when(z + distance < layers)
                def _():
                    run(z + distance, da, True)

                @pl.when(z >= distance)
                def _():
                    run(z - distance, da, False)

    def home(run):
        for da in (1, 0):
            run(z, da, None)

    def load(layer, da, db):
        slot = (layer * 2 + da) * 2 + db
        return pltpu.make_async_copy(view(layer, da, db, core), mine.at[slot], load_sem.at[slot])

    def to_other_core(layer, da, db):
        slot = (layer * 2 + da) * 2 + db
        return remote(
            view(layer, da, db, 1 - core),
            twin.at[slot],
            twin_send.at[slot],
            twin_recv.at[slot],
            to_twin,
        )

    def to_cross(layer, da):
        pair = layer * 2 + da
        return remote(
            mine.at[pair * 2 + 1], cross.at[pair], cross_send.at[pair], cross_recv.at[pair], to_b
        )

    def upward(layer, da):
        pair = layer * 2 + da
        return remote(mine.at[pair * 2], rise.at[pair], z_send.at[pair], rise_recv.at[pair], to_up)

    def downward(layer, da):
        pair = layer * 2 + da
        return remote(
            mine.at[pair * 2], fall.at[pair], z_send.at[pair], fall_recv.at[pair], to_down
        )

    def to_last():
        return remote(mine.at[(z * 2 + 1) * 2], last, last_send, last_recv, to_a)

    def add(target, *sources):
        step = 16

        def body(turn, carry):
            at = pl.ds(pl.multiple_of(turn * step, step), step)
            value = sources[0][at, :].astype(jnp.float32)
            for source in sources[1:]:
                value = value + source[at, :].astype(jnp.float32)
            target[at, :] = value.astype(target.dtype)
            return carry

        lax.fori_loop(0, rows // step, body, 0)

    for db in (1, 0):
        outward(lambda layer, da, up: load(layer, da, db).start())
        home(lambda layer, da, up: load(layer, da, db).start())
    pl.semaphore_wait(barrier, 3 + has_up.astype(jnp.int32) + has_down.astype(jnp.int32))
    for db in (1, 0):
        outward(lambda layer, da, up: to_other_core(layer, da, db).start())
        home(lambda layer, da, up: to_other_core(layer, da, db).start())

    def pair_up(layer, da, up):
        slot = (layer * 2 + da) * 2 + 1
        load(layer, da, 1).wait()
        to_other_core(layer, da, 1).wait_recv()
        add(mine.at[slot], mine.at[slot], twin.at[slot])
        to_cross(layer, da).start()

    outward(pair_up)
    home(pair_up)

    def collect(layer, da, target):
        pair = layer * 2 + da
        load(layer, da, 0).wait()
        to_other_core(layer, da, 0).wait_recv()
        to_cross(layer, da).wait_recv()
        add(target, mine.at[pair * 2], twin.at[pair * 2], cross.at[pair])

    def pass_on(layer, da, up):
        pair = layer * 2 + da
        collect(layer, da, total)
        if up:
            @pl.when(has_down)
            def _():
                upward(layer, da).wait_recv()
                add(total, total, rise.at[pair])
        else:
            @pl.when(has_up)
            def _():
                downward(layer, da).wait_recv()
                add(total, total, fall.at[pair])
        add(mine.at[pair * 2], total)
        (upward if up else downward)(layer, da).start()

    outward(pass_on)

    def settle(layer, da, up):
        pair = layer * 2 + da
        target = total if da else out_ref
        collect(layer, da, target)

        @pl.when(has_down)
        def _():
            upward(layer, da).wait_recv()
            add(target, target, rise.at[pair])

        @pl.when(has_up)
        def _():
            downward(layer, da).wait_recv()
            add(target, target, fall.at[pair])

        if da:
            add(mine.at[pair * 2], total)
            to_last().start()

    home(settle)
    to_last().wait_recv()
    add(out_ref, out_ref, last)

    def finish(layer, da, up):
        to_other_core(layer, da, 0).wait_send()
        to_other_core(layer, da, 1).wait_send()
        to_cross(layer, da).wait_send()
        if up is not None:
            (upward if up else downward)(layer, da).wait_send()

    outward(finish)
    home(finish)
    to_last().wait_send()


def scatter_sum(parts):
    dp_count, mp_count = lax.axis_size("dp"), lax.axis_size("mp")
    rows, width = parts.shape[0] // dp_count, parts.shape[1] // mp_count
    if mp_count != 2 or dp_count % 4:
        halves = lax.psum_scatter(parts, "mp", scatter_dimension=1, tiled=True)
        return lax.psum_scatter(halves, "dp", scatter_dimension=0, tiled=True)
    pairs = dp_count // 2
    dma = pltpu.SemaphoreType.DMA
    block = (rows, width)
    return pl.pallas_call(
        scatter_kernel,
        out_shape=jax.ShapeDtypeStruct(block, jnp.float32),
        in_specs=[pl.BlockSpec(memory_space=pl.ANY)],
        out_specs=pl.BlockSpec(memory_space=pltpu.VMEM),
        scratch_shapes=[
            pltpu.VMEM((2 * pairs,) + block, jnp.bfloat16),
            pltpu.VMEM((2 * pairs,) + block, jnp.bfloat16),
            pltpu.VMEM((pairs,) + block, jnp.bfloat16),
            pltpu.VMEM((pairs,) + block, jnp.bfloat16),
            pltpu.VMEM((pairs,) + block, jnp.bfloat16),
            pltpu.VMEM(block, jnp.bfloat16),
            pltpu.VMEM(block, jnp.float32),
            dma((2 * pairs,)),
            dma((2 * pairs,)),
            dma((pairs,)),
            dma((pairs,)),
            dma,
            dma((2 * pairs,)),
            dma((pairs,)),
            dma((pairs,)),
            dma((pairs,)),
            dma,
        ],
        compiler_params=pltpu.CompilerParams(
            collective_id=1, has_side_effects=True, vmem_limit_bytes=40 * 1024 * 1024
        ),
        name="scatter_sum",
    )(parts.astype(jnp.bfloat16))


def attention(queries, keys, values, query_seg, query_row, key_seg, key_row, keep_mask):
    scale = HEAD_DIM ** (-0.5)
    scores = (
        lax.dot_general(
            queries, keys, (((1,), (1,)), ((), ())), preferred_element_type=jnp.float32
        )
        * scale
    )
    visible = (query_seg[:, None] == key_seg[None, :]) & (
        (keep_mask[None, :] == 1) | (query_row[:, None] == key_row[None, :])
    )
    masked = jnp.where(visible, scores, NEG)
    top = jnp.max(masked, axis=1, keepdims=True)
    weights = jnp.where(visible, jnp.exp(masked - top), 0.0)
    totals = jnp.sum(weights, axis=1, keepdims=True)
    mixed = jnp.dot(weights.astype(jnp.bfloat16), values, preferred_element_type=jnp.float32)
    return (mixed / totals).astype(jnp.bfloat16)


def local_any(
    tokens,
    lengths,
    keep_mask,
    routes,
    attention_gain,
    mixture_gain,
    query_gain,
    key_gain,
    query_weight,
    key_weight,
    value_weight,
    output_weight,
    router_weight,
    expert_gate,
    expert_up,
    expert_down,
):
    tok_rows = tokens.shape[0]
    dp_count = lax.axis_size("dp")
    dp_index = lax.axis_index("dp")
    mp_index = lax.axis_index("mp")
    local_width = query_weight.shape[1]
    local_heads = local_width // HEAD_DIM
    share = dp_count // local_heads
    part = dp_index % share
    total_rows = tok_rows * dp_count

    weight_rows = query_weight.shape[0]
    packed = jnp.stack([query_weight, key_weight, value_weight]).reshape(
        3, weight_rows, local_heads, HEAD_DIM
    )
    packed = packed.transpose(2, 1, 0, 3).reshape(local_heads, weight_rows, 3 * HEAD_DIM)
    packed = jnp.repeat(packed, share, axis=0)
    head_weight = lax.all_to_all(packed, "dp", split_axis=0, concat_axis=0, tiled=True)
    head_weight = head_weight.reshape(dp_count * weight_rows, 3 * HEAD_DIM)

    all_tokens, head_weight, late_weight = lax.optimization_barrier(
        (gather_blocks(tokens), head_weight, output_weight)
    )
    all_output_weight = lax.all_gather(late_weight, "dp", axis=1, tiled=True)
    xfloat = all_tokens.astype(jnp.float32)
    all_in = (
        xfloat * lax.rsqrt(jnp.mean(xfloat * xfloat, axis=1, keepdims=True) + EPS) * attention_gain
    ).astype(jnp.bfloat16)
    all_routes = lax.all_gather(routes, "dp", axis=0, tiled=True)
    all_gain = lax.all_gather(mixture_gain, "mp", axis=0, tiled=True)
    all_router = lax.all_gather(router_weight, "mp", axis=0, tiled=True)

    key_row = jnp.arange(total_rows, dtype=jnp.int32)
    key_seg, key_pos = segment_info(lengths, key_row)
    cos_table, sin_table = rope_tables(key_pos)

    def own(array):
        split = array.reshape((local_heads, share, tok_rows) + array.shape[1:])
        taken = lax.dynamic_index_in_dim(split, part, 1, keepdims=False)
        return taken.reshape((local_heads * tok_rows,) + array.shape[1:])

    projected = jnp.dot(all_in, head_weight, preferred_element_type=jnp.float32)
    queries = head_prep(
        own(projected[:, :HEAD_DIM]), query_gain, own(cos_table), own(sin_table)
    )
    keys = head_prep(projected[:, HEAD_DIM : 2 * HEAD_DIM], key_gain, cos_table, sin_table)
    values = projected[:, 2 * HEAD_DIM :].astype(jnp.bfloat16)
    attended = attention(
        queries, keys, values, own(key_seg), own(key_row), key_seg, key_row, keep_mask
    )
    groups = [[head * share + p for head in range(local_heads)] for p in range(share)]
    attended = lax.all_to_all(
        attended.reshape(local_heads, tok_rows, HEAD_DIM),
        "dp",
        split_axis=0,
        concat_axis=0,
        tiled=True,
        axis_index_groups=groups,
    )
    attended = attended.transpose(1, 0, 2).reshape(tok_rows, local_width)
    partial_out = jnp.dot(attended, all_output_weight, preferred_element_type=jnp.float32)
    summed_out = lax.psum_scatter(partial_out, "mp", scatter_dimension=1, tiled=True)
    residual = (tokens.astype(jnp.float32) + summed_out).astype(jnp.bfloat16)
    all_residual = gather_blocks(residual)
    hfloat = all_residual.astype(jnp.float32)
    inverse = lax.rsqrt(jnp.mean(hfloat * hfloat, axis=1, keepdims=True) + EPS)
    mixed_in = (hfloat * all_gain * inverse).astype(jnp.bfloat16)

    own_rows = lax.dynamic_slice_in_dim(all_residual, dp_index * tok_rows, tok_rows, 0)
    own_float = own_rows.astype(jnp.float32)
    own_inverse = lax.rsqrt(jnp.mean(own_float * own_float, axis=1, keepdims=True) + EPS)
    logits = (
        jnp.dot(own_float * all_gain, all_router, precision=lax.Precision.HIGHEST) * own_inverse
    )

    ids = jnp.arange(tok_rows, dtype=jnp.int32)
    earlier = (ids[:, None] < ids[None, :]).astype(jnp.bfloat16)
    slots = jnp.arange(CAP, dtype=jnp.int32)

    def chosen_slots(named):
        before = jnp.dot(
            named.astype(jnp.bfloat16).reshape(-1, tok_rows),
            earlier,
            preferred_element_type=jnp.float32,
        ).reshape(named.shape)
        place = jnp.where(named, before.astype(jnp.int32), -1)
        return place[:, :, None, :] == slots[None, None, :, None]

    exp_local = EXPERTS // dp_count
    gate_local = expert_gate[0]
    up_local = expert_up[0]
    down_local = expert_down[0]
    unit_count = gate_local.shape[1]
    held = max(1, unit_count // FF)
    units = unit_count // held
    first_expert = (mp_index * unit_count) // FF

    own_experts = dp_index * exp_local + first_expert + jnp.arange(held, dtype=jnp.int32)
    block_routes = all_routes.reshape(dp_count, tok_rows, TOPK)
    here = jnp.any(block_routes[:, None] == own_experts[None, :, None, None], axis=3)
    chosen = chosen_slots(here)
    select = chosen.astype(jnp.bfloat16).reshape(dp_count, held * CAP, tok_rows)
    rows_in = lax.dot_general(
        select,
        mixed_in.reshape(dp_count, tok_rows, D),
        (((2,), (1,)), ((0,), (0,))),
        preferred_element_type=jnp.float32,
    ).astype(jnp.bfloat16)
    rows_in = rows_in.reshape(dp_count, held, CAP, D)
    experts = jnp.arange(EXPERTS, dtype=jnp.int32)
    named = jnp.any(routes[:, :, None] == experts[None, None, :], axis=1)
    sigmoid_vals = jax.nn.sigmoid(logits) * named.astype(jnp.float32)
    route_weight = sigmoid_vals / jnp.sum(sigmoid_vals, axis=1, keepdims=True)
    all_weights = lax.all_gather(route_weight, "dp", axis=0, tiled=True)
    outs = []
    for index in range(held):
        rows = rows_in[:, index].reshape(dp_count * CAP, D)
        low, high = index * units, (index + 1) * units
        gate_val = jnp.dot(rows, gate_local[:, low:high], preferred_element_type=jnp.float32)
        up_val = jnp.dot(rows, up_local[:, low:high], preferred_element_type=jnp.float32)
        hidden = (jax.nn.silu(gate_val) * up_val).astype(jnp.bfloat16)
        out = jnp.dot(hidden, down_local[low:high], preferred_element_type=jnp.float32)
        outs.append(out.astype(jnp.bfloat16).reshape(dp_count, CAP, D))
    first_own = dp_index * exp_local + first_expert
    own_weights = lax.dynamic_slice_in_dim(all_weights, first_own, held, 1)
    own_weights = own_weights.reshape(dp_count, tok_rows, held).transpose(0, 2, 1)
    spread = jnp.where(chosen, own_weights[:, :, None, :], 0.0)
    spread_high = spread.astype(jnp.bfloat16)
    spread_low = (spread - spread_high.astype(jnp.float32)).astype(jnp.bfloat16)
    contract = (((1,), (1,)), ((0,), (0,)))
    both = jnp.concatenate([spread_high, spread_low], 2).reshape(
        dp_count, held * 2 * CAP, tok_rows
    )
    out_rows = jnp.concatenate(sum([[out, out] for out in outs], []), axis=1)
    parts = lax.dot_general(both, out_rows, contract, preferred_element_type=jnp.float32)
    mixture = scatter_sum(parts.reshape(total_rows, D))
    return (residual.astype(jnp.float32) + mixture).astype(jnp.bfloat16)


def row_starts(lengths_ref):
    ends, starts, total = [], [], 0
    for index in range(lengths_ref.shape[0]):
        starts.append(total)
        total = total + lengths_ref[index]
        ends.append(total)
    return ends, starts


def segment_of(row, ends):
    segment = (row >= ends[0]).astype(jnp.int32)
    for end in ends[1:]:
        segment = segment + (row >= end).astype(jnp.int32)
    return segment


def front_kernel(
    lengths_ref,
    tokens_ref,
    query_ref,
    key_ref,
    value_ref,
    last_ref,
    router_ref,
    mixture_ref,
    gain_hbm,
    query_gain_hbm,
    key_gain_hbm,
    keep_hbm,
    frequency_hbm,
    cos_hbm,
    sin_hbm,
    out_ref,
    all_last_ref,
    all_router_ref,
    all_mixture_ref,
    gain_ref,
    query_gain_ref,
    key_gain_ref,
    keep_ref,
    frequency_ref,
    cos_ref,
    sin_ref,
    fetch_sem,
    held,
    mixed_rows,
    packed,
    pack_sem,
    pair_send,
    pair_recv,
    pair_local,
    weight,
    normed,
    keys,
    values,
    queries,
    start_cos,
    start_sin,
    head_send,
    head_recv,
    head_hand_send,
    head_hand_recv,
    head_local,
    local_sem,
    a_sem,
    rise_sem,
    fall_sem,
    b_sem,
    hand_sem,
    block_recv,
    last_rise,
    last_fall,
    last_side,
    last_hand,
    last_recv,
    swap_send,
    swap_recv,
    out_sem,
):
    index = lax.axis_index("dp")
    x = lax.axis_index("mp")
    dp_count = lax.axis_size("dp")
    layers = dp_count // 4
    chips = dp_count // 2
    core, chip = index % 2, index // 2
    z, y = index // 4, chip % 2
    rows, half = tokens_ref.shape
    total = dp_count * rows
    chunk = 2 * rows
    to_a = (index + 2 - 4 * y, x)
    to_b = (index, 1 - x)
    to_twin = (index + 1 - 2 * core, x)
    to_side = (index + 2 - 4 * y, x)
    to_up, to_down = (index + 4, x), (index - 4, x)
    has_up, has_down = z < layers - 1, z > 0

    def remote(source, target, send_sem, recv_sem, device):
        return pltpu.make_async_remote_copy(
            src_ref=source,
            dst_ref=target,
            send_sem=send_sem,
            recv_sem=recv_sem,
            device_id=device,
            device_id_type=MESH,
        )

    def tiles(start, step, size):
        return pl.ds(pl.multiple_of(start + step * size, size), size)

    barrier = pltpu.get_barrier_semaphore()
    for step in range(1, chips):
        peer = lax.rem(chip + step, chips) * 2 + core
        pl.semaphore_signal(barrier, inc=1, device_id=(peer, x), device_id_type=MESH)
    for peer in (to_twin, (index, 1 - x)):
        pl.semaphore_signal(barrier, inc=1, device_id=peer, device_id_type=MESH)

    fetches = [
        pltpu.make_async_copy(source, target, fetch_sem.at[number])
        for number, (source, target) in enumerate(
            (
                (frequency_hbm, frequency_ref),
                (gain_hbm, gain_ref),
                (query_gain_hbm, query_gain_ref),
                (key_gain_hbm, key_gain_ref),
                (keep_hbm, keep_ref),
                (cos_hbm, cos_ref),
                (sin_hbm, sin_ref),
            )
        )
    ]
    packs = []
    for number, source in enumerate((query_ref, key_ref, value_ref)):
        for head in range(chips):
            packs.append(
                pltpu.make_async_copy(
                    source.at[:, head * HEAD_DIM : (head + 1) * HEAD_DIM],
                    packed.at[head, :, number * HEAD_DIM : (number + 1) * HEAD_DIM],
                    pack_sem.at[number * chips + head],
                )
            )
    for pack in packs:
        pack.start()
    for fetch in fetches:
        fetch.start()

    def place(layer, da, db, which):
        yy, xx = y + da * (1 - 2 * y), x + db * (1 - 2 * x)
        return layer * 4 + yy * 2 + which, xx

    def view(spot):
        return held.at[tiles(0, spot[0], rows), tiles(0, spot[1], half)]

    def send(spot, sem, device, own_block=False):
        return remote(
            tokens_ref if own_block else view(spot),
            view(spot),
            sem,
            block_recv.at[spot[0] * 2 + spot[1]],
            device,
        )

    def arrive(spot):
        send(spot, local_sem.at[0], to_twin).wait_recv()

    late = core < 2

    def spread_out(layer, da, own_block, act):
        spot = place(layer, da, 0, core)
        slot = layer * 2 + da
        along = jnp.logical_not(late) if da else jnp.bool_(True)

        @pl.when((layer <= z) & has_up & along)
        def _():
            act(send(spot, rise_sem.at[slot], to_up, own_block))

        @pl.when((layer >= z) & has_down & along)
        def _():
            act(send(spot, fall_sem.at[slot], to_down, own_block))

        if not da:
            @pl.when((layer == z) | late)
            def _():
                act(send(spot, a_sem.at[layer], to_a, own_block))

        act(send(spot, b_sem.at[slot], to_b, own_block))
        act(send(spot, hand_sem.at[slot * 2], to_twin, own_block))

    def hand_over(layer, da, act):
        spot = place(layer, da, 1, core)
        act(send(spot, hand_sem.at[(layer * 2 + da) * 2 + 1], to_twin))

    start = lambda copy: copy.start()
    finish = lambda copy: copy.wait_send()
    keep_block = pltpu.make_async_copy(tokens_ref, view(place(z, 0, 0, core)), local_sem.at[1])

    sources = (query_ref, key_ref, value_ref)

    def head_part(step):
        other = lax.rem(chip + step, chips)
        return remote(
            packed.at[other],
            weight.at[tiles(0, index, rows), :],
            head_send.at[step],
            head_recv.at[step],
            (other * 2 + core, x),
        )

    def across_x(source, target, number):
        return remote(
            source, target.at[x], pair_send.at[number], pair_recv.at[number], (index, 1 - x)
        )

    router_copy = across_x(router_ref, all_router_ref, 0)
    mixture_copy = across_x(mixture_ref, all_mixture_ref, 1)
    pair_keep = [
        pltpu.make_async_copy(router_ref, all_router_ref.at[x], pair_local.at[0]),
        pltpu.make_async_copy(mixture_ref, all_mixture_ref.at[x], pair_local.at[1]),
    ]

    def head_keep(which):
        return pltpu.make_async_copy(
            sources[which].at[:, tiles(0, chip, HEAD_DIM)],
            weight.at[tiles(0, index, rows), which * HEAD_DIM : (which + 1) * HEAD_DIM],
            head_local.at[which],
        )

    def head_hand(step):
        block = lax.rem(chip + step, chips) * 2 + core
        at = weight.at[tiles(0, block, rows), :]
        return remote(at, at, head_hand_send.at[step], head_hand_recv.at[step], to_twin)

    def last_view(layer, side, which):
        yy = y + side * (1 - 2 * y)
        return all_last_ref.at[layer * 4 + yy * 2 + which]

    def last_copy(layer, side, sem, device, own_block=False):
        target = last_view(layer, side, core)
        return remote(
            last_ref if own_block else target,
            target,
            sem,
            last_recv.at[(layer * 2 + side) * 2],
            device,
        )

    def last_to_side(layer, own_block=False):
        target = last_view(layer, 0, core)
        return remote(
            last_ref if own_block else target,
            target,
            last_side.at[layer],
            last_recv.at[(layer * 2 + 1) * 2],
            to_side,
        )

    def last_to_twin(layer, side, own_block=False):
        target = last_view(layer, side, core)
        return remote(
            last_ref if own_block else target,
            target,
            last_hand.at[layer * 2 + side],
            last_recv.at[(layer * 2 + side) * 2 + 1],
            to_twin,
        )

    last_keep = pltpu.make_async_copy(last_ref, last_view(z, 0, core), local_sem.at[2])

    def last_spread(layer, own_block, act):
        @pl.when((layer <= z) & has_up)
        def _():
            act(last_copy(layer, 0, last_rise.at[layer], to_up, own_block))

        @pl.when((layer >= z) & has_down)
        def _():
            act(last_copy(layer, 0, last_fall.at[layer], to_down, own_block))

        act(last_to_side(layer, own_block))
        act(last_to_twin(layer, 0, own_block))

    def last_onward(layer):
        last_copy(layer, 0, last_rise.at[layer], to_up).wait_recv()
        last_spread(layer, False, start)

    def last_over(layer):
        last_to_side(layer).wait_recv()
        last_to_twin(layer, 1).start()

    pl.semaphore_wait(barrier, chips + 1)
    spread_out(z, 0, True, start)
    for which in range(3):
        head_keep(which).start()
    for pack in packs:
        pack.wait()
    for step in range(1, chips):
        head_part(step).start()
    keep_block.start()
    last_keep.start()
    for copy in pair_keep:
        copy.start()

    fetches[0].wait()
    ends, starts = row_starts(lengths_ref)
    which_row = lax.broadcasted_iota(jnp.int32, (8, HEAD_DIM), 0)
    begin = jnp.zeros((8, HEAD_DIM), jnp.int32)
    for number, first_row in enumerate(starts):
        begin = jnp.where(which_row == number, first_row, begin)
    angle = begin.astype(jnp.float32) * frequency_ref[...]
    start_cos[...] = jnp.cos(angle)
    start_sin[...] = jnp.sin(angle)

    def turn(projected, head_gain, row, at):
        square = jnp.mean(projected * projected, axis=1, keepdims=True)
        value = projected * lax.rsqrt(square + EPS) * head_gain
        cos_s, sin_s = start_cos[0:1, :], start_sin[0:1, :]
        for number in range(1, len(starts)):
            past = row >= ends[number - 1]
            cos_s = jnp.where(past, start_cos[number : number + 1, :], cos_s)
            sin_s = jnp.where(past, start_sin[number : number + 1, :], sin_s)
        cos_g, sin_g = cos_ref[at, :], sin_ref[at, :]
        cos_t = cos_g * cos_s + sin_g * sin_s
        sin_t = sin_g * cos_s - cos_g * sin_s
        lane = lax.broadcasted_iota(jnp.int32, value.shape, 1)
        halves = pltpu.roll(value, HEAD_DIM // 2, 1)
        rotated = jnp.where(lane < HEAD_DIM // 2, -halves, halves)
        return (value * cos_t + rotated * sin_t).astype(jnp.bfloat16)

    def take(layer):
        for da in range(2):
            for db in range(2):
                arrive(place(layer, da, db, 1 - core))

        def project(step, carry):
            position = layer * 2 + step
            at = tiles(0, position, chunk)
            value = held[at, :].astype(jnp.float32)
            inverse = lax.rsqrt(jnp.mean(value * value, axis=1, keepdims=True) + EPS)
            normed[...] = (value * inverse * gain_ref[...]).astype(jnp.bfloat16)
            both_parts = jnp.dot(
                normed[...], weight[:, HEAD_DIM:], preferred_element_type=jnp.float32
            )
            row = lax.broadcasted_iota(jnp.int32, (chunk, HEAD_DIM), 0) + position * chunk
            keys[at, :] = turn(both_parts[:, :HEAD_DIM], key_gain_ref[...], row, at)
            values[at, :] = both_parts[:, HEAD_DIM:].astype(jnp.bfloat16)
            asked = jnp.dot(
                normed[tiles(0, core, rows), :],
                weight[:, :HEAD_DIM],
                preferred_element_type=jnp.float32,
            )
            own_at = tiles(0, position * 2 + core, rows)
            row = lax.broadcasted_iota(jnp.int32, (rows, HEAD_DIM), 0) + (
                (position * 2 + core) * rows
            )
            queries[tiles(0, position, rows), :] = turn(asked, query_gain_ref[...], row, own_at)
            return carry

        lax.fori_loop(0, 2, project, 0)

    def both(distance, run):
        @pl.when(z >= distance)
        def _():
            run(z - distance)

        @pl.when(z + distance < layers)
        def _():
            run(z + distance)

    def onward(layer):
        for da in range(2):
            arrive(place(layer, da, 0, core))
            spread_out(layer, da, False, start)

    def over(layer):
        for da in range(2):
            arrive(place(layer, da, 1, core))
            hand_over(layer, da, start)

    arrive(place(z, 1, 0, core))
    spread_out(z, 1, False, start)
    both(1, onward)
    over(z)
    for which in range(3):
        head_keep(which).wait()
    head_hand(0).start()
    for step in range(1, chips):
        head_part(step).wait_recv()
    for step in range(1, chips):
        head_hand(step).start()
    both(2, onward)
    both(1, over)
    last_spread(z, True, start)
    mixture_copy.start()
    router_copy.start()
    keep_block.wait()
    for step in range(chips):
        head_hand(step).wait_recv()
    for fetch in fetches[1:]:
        fetch.wait()
    take(z)
    both(1, take)
    both(3, onward)
    both(1, last_onward)
    both(2, over)
    both(2, take)
    last_over(z)
    both(2, last_onward)
    both(3, over)
    both(3, take)
    both(1, last_over)
    both(3, last_onward)

    key_row = lax.broadcasted_iota(jnp.int32, (1, total), 1)
    key_seg = jnp.where(keep_ref[...] == 1, segment_of(key_row, ends), -1)
    scale = HEAD_DIM ** (-0.5) * 1.4426950408889634

    def swap(block):
        return remote(
            mixed_rows.at[tiles(0, block, rows), :],
            out_ref.at[chip],
            swap_send.at[block],
            swap_recv.at[chip],
            (block * 2 + core, x),
        )

    def swapped(source):
        return remote(
            mixed_rows.at[0:rows, :],
            out_ref.at[source],
            swap_send.at[source],
            swap_recv.at[source],
            to_twin,
        )

    swap_keep = pltpu.make_async_copy(
        mixed_rows.at[tiles(0, chip, rows), :], out_ref.at[chip], out_sem
    )

    def attend(step, carry):
        at = tiles(0, step, chunk)
        scores = lax.dot_general(
            queries[at, :], keys[...], (((1,), (1,)), ((), ())), preferred_element_type=jnp.float32
        )
        local_row = lax.broadcasted_iota(jnp.int32, (chunk, 1), 0)
        second = (local_row >= rows).astype(jnp.int32)
        row = ((step * 2 + second) * 2 + core) * rows + local_row - second * rows
        visible = (segment_of(row, ends) == key_seg) | (row == key_row)
        masked = jnp.where(visible, scores, NEG)
        top = jnp.max(masked, axis=1, keepdims=True)
        weights = jnp.exp2((masked - top) * scale)
        totals = jnp.sum(weights, axis=1, keepdims=True)
        mixed = jnp.dot(
            weights.astype(jnp.bfloat16), values[...], preferred_element_type=jnp.float32
        )
        mixed_rows[at, :] = (mixed / totals).astype(jnp.bfloat16)
        for side in range(2):
            block = step * 2 + side

            @pl.when(block != chip)
            def _():
                swap(block).start()

            @pl.when(block == chip)
            def _():
                swap_keep.start()

        return carry

    turns = total // 2 // chunk
    lax.fori_loop(0, turns // 2, attend, 0)
    both(2, last_over)
    lax.fori_loop(turns // 2, turns, attend, 0)
    both(3, last_over)

    last_keep.wait()
    swap_keep.wait()

    def settle_swap(other, carry):
        @pl.when(other != chip)
        def _():
            swapped(other).wait_recv()
            swap(other).wait_send()

        return carry

    lax.fori_loop(0, chips, settle_swap, 0)

    def drain(layer, carry):
        for da in range(2):
            spread_out(layer, da, False, finish)
            hand_over(layer, da, finish)
            last_to_twin(layer, da).wait_recv()
        last_spread(layer, False, finish)
        last_to_twin(layer, 1).wait_send()
        return carry

    lax.fori_loop(0, layers, drain, 0)
    head_hand(0).wait_send()
    for step in range(1, chips):
        head_hand(step).wait_send()
        head_part(step).wait_send()
    for copy in pair_keep + [mixture_copy, router_copy]:
        copy.wait()


def front_call(
    tokens,
    lengths,
    keep_mask,
    attention_gain,
    query_gain,
    key_gain,
    query_weight,
    key_weight,
    value_weight,
    output_weight,
    router,
    mixture_gain,
):
    dp_count, mp_count = lax.axis_size("dp"), lax.axis_size("mp")
    rows, half = tokens.shape
    total, width = dp_count * rows, mp_count * half
    layers, chips = dp_count // 4, dp_count // 2
    halves = HEAD_DIM // 2
    exponent = np.arange(halves, dtype=np.float32) * np.float32(2.0 / HEAD_DIM)
    frequency = np.power(np.float32(ROPE_BASE), -exponent).astype(np.float32)
    frequency = np.concatenate([frequency, frequency])[None, :]
    angle = np.arange(total, dtype=np.float32)[:, None] * frequency
    cos_table = np.cos(angle.astype(np.float64)).astype(np.float32)
    sin_table = np.sin(angle.astype(np.float64)).astype(np.float32)
    smem = pl.BlockSpec(memory_space=pltpu.SMEM)
    hbm = pl.BlockSpec(memory_space=pltpu.HBM)
    dma = pltpu.SemaphoreType.DMA
    narrow = jnp.bfloat16
    return pl.pallas_call(
        front_kernel,
        out_shape=(
            jax.ShapeDtypeStruct((chips, rows, HEAD_DIM), narrow),
            jax.ShapeDtypeStruct((dp_count,) + output_weight.shape, narrow),
            jax.ShapeDtypeStruct((mp_count,) + router.shape, router.dtype),
            jax.ShapeDtypeStruct((mp_count,) + mixture_gain.shape, mixture_gain.dtype),
        ),
        in_specs=[smem] + [hbm] * 14,
        out_specs=(hbm,) * 4,
        scratch_shapes=[
            pltpu.VMEM((1, width), jnp.float32),
            pltpu.VMEM((1, HEAD_DIM), jnp.float32),
            pltpu.VMEM((1, HEAD_DIM), jnp.float32),
            pltpu.VMEM((1, total), jnp.int32),
            pltpu.VMEM((1, HEAD_DIM), jnp.float32),
            pltpu.VMEM((total, HEAD_DIM), jnp.float32),
            pltpu.VMEM((total, HEAD_DIM), jnp.float32),
            dma((7,)),
            pltpu.VMEM((total, width), narrow),
            pltpu.VMEM((total // 2, HEAD_DIM), narrow),
            pltpu.VMEM((chips, rows, 3 * HEAD_DIM), narrow),
            dma((3 * chips,)),
            dma((2,)),
            dma((2,)),
            dma((2,)),
            pltpu.VMEM((width, 3 * HEAD_DIM), narrow),
            pltpu.VMEM((2 * rows, width), narrow),
            pltpu.VMEM((total, HEAD_DIM), narrow),
            pltpu.VMEM((total, HEAD_DIM), narrow),
            pltpu.VMEM((total // 2, HEAD_DIM), narrow),
            pltpu.VMEM((8, HEAD_DIM), jnp.float32),
            pltpu.VMEM((8, HEAD_DIM), jnp.float32),
            dma((chips,)),
            dma((chips,)),
            dma((chips,)),
            dma((chips,)),
            dma((3,)),
            dma((3,)),
            dma((layers,)),
            dma((layers * 2,)),
            dma((layers * 2,)),
            dma((layers * 2,)),
            dma((layers * 4,)),
            dma((dp_count * mp_count,)),
            dma((layers,)),
            dma((layers,)),
            dma((layers,)),
            dma((layers * 2,)),
            dma((layers * 4,)),
            dma((chips,)),
            dma((chips,)),
            dma,
        ],
        compiler_params=pltpu.CompilerParams(
            collective_id=3, has_side_effects=True, vmem_limit_bytes=60 * 1024 * 1024
        ),
        name="attention_layer",
    )(
        lengths,
        tokens,
        query_weight,
        key_weight,
        value_weight,
        output_weight,
        router,
        mixture_gain,
        attention_gain[None, :],
        query_gain[None, :],
        key_gain[None, :],
        keep_mask[None, :],
        jnp.asarray(frequency),
        jnp.asarray(cos_table),
        jnp.asarray(sin_table),
    )


def layer_kernel(
    attended_ref,
    weight_ref,
    tokens_ref,
    routes_ref,
    router_ref,
    gain_ref,
    gate_ref,
    up_ref,
    down_ref,
    out_ref,
    gathered,
    sent_half,
    got_half,
    residual,
    router_own,
    all_routes,
    all_router,
    all_gain,
    held,
    mixed,
    gate,
    up,
    down,
    rows_in,
    hidden,
    wide,
    spread,
    twin,
    cross,
    rise,
    fall,
    last,
    far,
    route_send,
    route_recv,
    pair_send,
    pair_recv,
    local_sem,
    wide_sem,
    gate_sem,
    up_sem,
    down_sem,
    first_sem,
    rise_sem,
    fall_sem,
    b_sem,
    hand_sem,
    block_recv,
    far_sem,
    merge_send,
    far_recv,
    twin_send,
    cross_send,
    z_send,
    last_send,
    twin_recv,
    cross_recv,
    rise_recv,
    fall_recv,
    last_recv,
):
    index = lax.axis_index("dp")
    x = lax.axis_index("mp")
    dp_count = lax.axis_size("dp")
    layers = dp_count // 4
    heads = attended_ref.shape[0]
    core, chip = index % 2, index // 2
    z, y = index // 4, chip % 2
    rows, half = tokens_ref.shape
    width = 2 * half
    tile = 256
    held_count = rows_in.shape[0]
    units = hidden.shape[1]
    first_expert = index * (EXPERTS // dp_count) + x * held_count
    to_a = (index + core * (2 - 4 * y), x + (1 - core) * (1 - 2 * x))
    to_b = (index + (1 - core) * (2 - 4 * y), x + core * (1 - 2 * x))
    to_twin = (index + 1 - 2 * core, x)
    to_up, to_down = (index + 4, x), (index - 4, x)
    has_up, has_down = z < layers - 1, z > 0

    def remote(source, target, send_sem, recv_sem, device):
        return pltpu.make_async_remote_copy(
            src_ref=source,
            dst_ref=target,
            send_sem=send_sem,
            recv_sem=recv_sem,
            device_id=device,
            device_id_type=MESH,
        )

    def tiles(start, step, size):
        return pl.ds(pl.multiple_of(start + step * size, size), size)

    barrier = pltpu.get_barrier_semaphore()
    for step in range(1, dp_count):
        peer = lax.rem(index + step, dp_count)
        pl.semaphore_signal(barrier, inc=1, device_id=(peer, x), device_id_type=MESH)
    pl.semaphore_signal(barrier, inc=1, device_id=(index, 1 - x), device_id_type=MESH)

    load_wide = [
        pltpu.make_async_copy(
            weight_ref.at[block], wide.at[:, block * rows : (block + 1) * rows], wide_sem.at[block]
        )
        for block in range(dp_count)
    ]
    for load in load_wide:
        load.start()

    def load_expert(expert):
        columns = tiles(0, expert, units)
        return (
            pltpu.make_async_copy(gate_ref.at[:, columns], gate.at[:, columns], gate_sem.at[expert]),
            pltpu.make_async_copy(up_ref.at[:, columns], up.at[:, columns], up_sem.at[expert]),
            pltpu.make_async_copy(down_ref.at[columns, :], down.at[columns, :], down_sem.at[expert]),
        )


    def route(step):
        return remote(
            routes_ref,
            all_routes.at[index],
            route_send.at[step],
            route_recv.at[step],
            (lax.rem(index + step, dp_count), x),
        )

    across_x = (index, 1 - x)
    def half_copy(turn):
        at = tiles(0, turn, tile)
        return remote(
            sent_half.at[:, at],
            got_half.at[:, at],
            pair_send.at[turn],
            pair_recv.at[turn],
            across_x,
        )

    keep = [
        pltpu.make_async_copy(attended_ref, gathered, local_sem.at[0]),
        pltpu.make_async_copy(routes_ref, all_routes.at[index], local_sem.at[1]),
        pltpu.make_async_copy(router_ref, router_own, local_sem.at[2]),
        pltpu.make_async_copy(gain_ref, all_gain, local_sem.at[3]),
        pltpu.make_async_copy(tokens_ref, residual, local_sem.at[5]),
    ]
    for copy in keep:
        copy.start()
    pl.semaphore_wait(barrier, dp_count)
    for expert in range(held_count):
        for copy in load_expert(expert):
            copy.start()
    for copy in keep[1:]:
        copy.wait()
    for side in range(2):
        at = slice(side * half, (side + 1) * half)
        rest = router_own[side] * all_gain[side]
        for term in range(3):
            rounded = rest.astype(jnp.bfloat16)
            all_router[term * EXPERTS : (term + 1) * EXPERTS, at] = rounded
            rest = rest - rounded.astype(jnp.float32)
        all_router[3 * EXPERTS :, at] = jnp.zeros(rest.shape, jnp.bfloat16)
    keep[0].wait()
    for load in load_wide:
        load.wait()

    def all_heads():
        return jnp.concatenate([gathered[head] for head in range(heads)], 1)

    def away(turn, carry):
        sent_half[:, tiles(0, turn, tile)] = jnp.dot(
            all_heads(),
            wide[:, tiles((1 - x) * half, turn, tile)],
            preferred_element_type=jnp.float32,
        ).astype(jnp.bfloat16)
        half_copy(turn).start()
        return carry

    lax.fori_loop(0, half // tile, away, 0)
    for step in range(1, dp_count):
        route(step).start()

    def stay(turn, carry):
        at = tiles(0, turn, tile)
        out_ref[:, at] = residual[:, at].astype(jnp.float32) + jnp.dot(
            all_heads(),
            wide[:, tiles(x * half, turn, tile)],
            preferred_element_type=jnp.float32,
        )
        return carry

    lax.fori_loop(0, half // tile, stay, 0)

    def settle_tile(turn, carry):
        at = tiles(0, turn, tile)
        half_copy(turn).wait_recv()
        residual[:, at] = (out_ref[:, at] + got_half[:, at].astype(jnp.float32)).astype(
            jnp.bfloat16
        )
        out_ref[:, at] = residual[:, at].astype(jnp.float32)
        return carry

    lax.fori_loop(0, half // tile, settle_tile, 0)

    def place(layer, da, db, which):
        dy = which * da + (1 - which) * db
        dx = (1 - which) * da + which * db
        yy, xx = y + dy * (1 - 2 * y), x + dx * (1 - 2 * x)
        return layer * 4 + yy * 2 + which, xx

    def view(spot):
        return held.at[tiles(0, spot[0], rows), tiles(0, spot[1], half)]

    def send(spot, sem, device, own_block=False):
        return remote(
            residual if own_block else view(spot),
            view(spot),
            sem,
            block_recv.at[spot[0] * 2 + spot[1]],
            device,
        )

    def arrive(spot):
        send(spot, first_sem.at[1], to_twin).wait_recv()

    home_spot = place(z, 0, 0, core)
    keep_block = pltpu.make_async_copy(residual, view(home_spot), first_sem.at[1])
    first = send(home_spot, first_sem.at[0], to_a, True)

    def spread_out(layer, da, own_block, act):
        spot = place(layer, da, 0, core)
        slot = layer * 2 + da
        up_too = (layer <= z) & has_up
        down_too = (layer >= z) & has_down
        if da:
            up_too = up_too & (z + 1 - layer < layers - 1)
            down_too = down_too & (layer - z + 1 < layers - 1)
        else:

            @pl.when((z - layer == layers - 1) | (layer - z == layers - 1))
            def _():
                act(send(spot, far_sem, to_a, own_block))

        @pl.when(up_too)
        def _():
            act(send(spot, rise_sem.at[slot], to_up, own_block))

        @pl.when(down_too)
        def _():
            act(send(spot, fall_sem.at[slot], to_down, own_block))

        act(send(spot, b_sem.at[slot], to_b, own_block))
        act(send(spot, hand_sem.at[slot * 2], to_twin, own_block))

    def hand_over(layer, da, act):
        spot = place(layer, da, 1, core)
        act(send(spot, hand_sem.at[(layer * 2 + da) * 2 + 1], to_twin))

    start = lambda copy: copy.start()
    finish = lambda copy: copy.wait_send()

    earlier = (
        lax.broadcasted_iota(jnp.int32, (rows, rows), 0)
        < lax.broadcasted_iota(jnp.int32, (rows, rows), 1)
    ).astype(jnp.bfloat16)
    expert_id = lax.broadcasted_iota(jnp.int32, (EXPERTS, rows), 0)
    slot_id = lax.broadcasted_iota(jnp.int32, (CAP, rows), 0)

    def block_slots(block, logits, inverse):
        named_ids = all_routes[block]
        named = named_ids[0:1, :] == expert_id
        for k in range(1, TOPK):
            named = named | (named_ids[k : k + 1, :] == expert_id)
        logits_t = jnp.transpose(logits * inverse)[:EXPERTS]
        sigmoid = jnp.where(named, 1.0 / (1.0 + jnp.exp(-logits_t)), 0.0)
        route = sigmoid / jnp.sum(sigmoid, axis=0, keepdims=True)
        named_f = named.astype(jnp.float32)
        here, weight = [], []
        for expert in range(held_count):
            own = expert_id == first_expert + expert
            here.append(jnp.sum(jnp.where(own, named_f, 0.0), axis=0, keepdims=True))
            weight.append(jnp.sum(jnp.where(own, route, 0.0), axis=0, keepdims=True))
        stacked = jnp.concatenate(here + [jnp.zeros((8 - held_count, rows), jnp.float32)], 0)
        before = jnp.dot(
            stacked.astype(jnp.bfloat16), earlier, preferred_element_type=jnp.float32
        )
        slot_of = jnp.where(stacked > 0.5, before.astype(jnp.int32), -1)
        chosen = jnp.concatenate(
            [slot_of[expert : expert + 1, :] == slot_id for expert in range(held_count)], 0
        )
        weights = jnp.concatenate(
            [jnp.broadcast_to(w, (CAP, rows)) for w in weight], 0
        )
        spread_w = jnp.where(chosen, weights, 0.0)
        high = spread_w.astype(jnp.bfloat16)
        low = (spread_w - high.astype(jnp.float32)).astype(jnp.bfloat16)
        return chosen.astype(jnp.float32).astype(jnp.bfloat16), high, low

    chunk = 2 * rows

    def take(layer):
        for da in range(2):
            for db in range(2):
                arrive(place(layer, da, db, 1 - core))

        def one(step, carry):
            position = layer * 2 + step
            at = tiles(0, position, chunk)
            h = held[at, :].astype(jnp.float32)
            inverse = lax.rsqrt(jnp.mean(h * h, axis=1, keepdims=True) + EPS)
            gain_row = jnp.concatenate([all_gain[0], all_gain[1]], 1)
            mixed[...] = (h * gain_row * inverse).astype(jnp.bfloat16)
            logits = lax.dot_general(
                held[at, :],
                all_router[...],
                (((1,), (1,)), ((), ())),
                preferred_element_type=jnp.float32,
            )
            logits = logits[:, :128] + logits[:, 128:]
            logits = logits + pltpu.roll(logits, EXPERTS, 1)
            chosen, spreads = [], []
            for side in range(2):
                part = slice(side * rows, (side + 1) * rows)
                pick, high, low = block_slots(position * 2 + side, logits[part], inverse[part])
                chosen.append(pick)
                spreads += [(high, side), (low, side)]
            empty = jnp.zeros_like(chosen[0])
            select = jnp.concatenate(
                [
                    jnp.concatenate([chosen[0], empty], 1),
                    jnp.concatenate([empty, chosen[1]], 1),
                ],
                0,
            )
            taken = jnp.dot(select, mixed[...], preferred_element_type=jnp.float32).astype(
                jnp.bfloat16
            )
            for side in range(2):
                for expert in range(held_count):
                    source = (side * held_count + expert) * CAP
                    rows_in[expert, tiles(0, position * 2 + side, CAP), :] = taken[
                        source : source + CAP
                    ]
            spread[position] = jnp.concatenate(
                [
                    jnp.concatenate([value, empty] if side == 0 else [empty, value], 1)
                    for value, side in spreads
                ],
                0,
            )
            return carry

        lax.fori_loop(0, 2, one, 0)

    first.start()
    spread_out(z, 0, True, start)
    keep_block.start()
    arrive(place(z, 1, 0, core))
    spread_out(z, 1, False, start)

    def both(distance, run):
        @pl.when(z >= distance)
        def _():
            run(z - distance)

        @pl.when(z + distance < layers)
        def _():
            run(z + distance)

    def onward(layer):
        for da in range(2):
            arrive(place(layer, da, 0, core))
            spread_out(layer, da, False, start)

    def over(layer):
        for da in range(2):
            arrive(place(layer, da, 1, core))
            hand_over(layer, da, start)

    keep_block.wait()
    for step in range(1, dp_count):
        route(step).wait_recv()
    slots = hidden.shape[0]

    broad = 2 * tile

    def feed(expert, part):
        at_rows = tiles(0, part, slots)

        def widen(turn, carry):
            columns = tiles(expert * units, turn, broad)
            gate_val = jnp.dot(
                rows_in[expert, at_rows, :], gate[:, columns], preferred_element_type=jnp.float32
            )
            up_val = jnp.dot(
                rows_in[expert, at_rows, :], up[:, columns], preferred_element_type=jnp.float32
            )
            silu = gate_val / (1.0 + jnp.exp(-gate_val))
            hidden[:, tiles(0, turn, broad)] = (silu * up_val).astype(jnp.bfloat16)
            return carry

        lax.fori_loop(0, units // broad, widen, 0)

        def narrow(turn, carry):
            at = tiles(0, turn, broad)
            wide[tiles(expert * 2 * slots, part, slots), at] = jnp.dot(
                hidden[...],
                down[expert * units : (expert + 1) * units, at],
                preferred_element_type=jnp.float32,
            ).astype(jnp.bfloat16)
            return carry

        lax.fori_loop(0, width // broad, narrow, 0)

    near_half = (z >= layers // 2).astype(jnp.int32)
    both(1, onward)
    over(z)
    take(z)
    both(2, onward)
    both(1, over)
    both(1, take)
    for expert in range(held_count):
        for load in load_expert(expert):
            load.wait()
    feed(0, near_half)
    both(3, onward)
    both(2, over)
    both(2, take)
    feed(1, near_half)
    both(3, over)
    both(3, take)
    for expert in range(held_count):
        feed(expert, 1 - near_half)

    first.wait_send()
    for turn in range(half // tile):
        half_copy(turn).wait_send()

    def sent(layer, carry):
        for da in range(2):
            spread_out(layer, da, False, finish)
            hand_over(layer, da, finish)
        return carry

    lax.fori_loop(0, layers, sent, 0)

    def combine(position):
        pieces = []
        for side in range(2):
            block = position * 2 + side
            pieces += [
                wide[tiles(expert * dp_count * CAP, block, CAP), :] for expert in range(held_count)
            ] * 2
        held[tiles(0, position, chunk), :] = lax.dot_general(
            spread[position],
            jnp.concatenate(pieces, 0),
            (((0,), (0,)), ((), ())),
            preferred_element_type=jnp.float32,
        ).astype(jnp.bfloat16)

    def mine(layer, da, db):
        return view(place(layer, da, db, core))

    def to_other_core(layer, da, db):
        slot = (layer * 2 + da) * 2 + db
        other = 1 - core
        return remote(
            view(place(layer, da, db, other)),
            twin.at[slot],
            twin_send.at[slot],
            twin_recv.at[slot],
            to_twin,
        )

    def to_cross(layer, da):
        pair = layer * 2 + da
        return remote(
            mine(layer, da, 1), cross.at[pair], cross_send.at[pair], cross_recv.at[pair], to_b
        )

    def upward(layer, da):
        pair = layer * 2 + da
        return remote(
            mine(layer, da, 0), rise.at[pair], z_send.at[pair], rise_recv.at[pair], to_up
        )

    def downward(layer, da):
        pair = layer * 2 + da
        return remote(
            mine(layer, da, 0), fall.at[pair], z_send.at[pair], fall_recv.at[pair], to_down
        )

    def to_last():
        return remote(mine(z, 1, 0), last, last_send, last_recv, to_a)

    def add(target, *sources):
        step = 32

        def body(turn, carry):
            at = tiles(0, turn, step)
            value = sources[0][at, :].astype(jnp.float32)
            for source in sources[1:]:
                value = value + source[at, :].astype(jnp.float32)
            target[at, :] = value.astype(target.dtype)
            return carry

        lax.fori_loop(0, rows // step, body, 0)

    inner = ((z == 1) | (z == 2)).astype(jnp.int32)
    below = (z < layers // 2).astype(jnp.int32)

    def ordered(step):
        step = jnp.asarray(step, jnp.int32)
        turned = step + inner * ((step == 2).astype(jnp.int32) - (step == 3).astype(jnp.int32))
        return turned + below * (layers - 1 - 2 * turned)

    def make(step, carry):
        layer = ordered(step)

        def one(side, inner_carry):
            combine(layer * 2 + side)
            return inner_carry

        lax.fori_loop(0, 2, one, 0)
        for db in (1, 0):
            for da in (1, 0):
                to_other_core(layer, da, db).start()
        return carry

    def pair_up(step):
        layer = ordered(step)
        for da in range(2):
            slot = (layer * 2 + da) * 2 + 1
            to_other_core(layer, da, 1).wait_recv()
            add(mine(layer, da, 1), mine(layer, da, 1), twin.at[slot])
            to_cross(layer, da).start()

    def make_and_pair(step, carry):
        make(step, 0)
        pair_up(step - 1)
        return carry

    make(0, 0)
    lax.fori_loop(1, layers, make_and_pair, 0)
    pair_up(layers - 1)

    def merges(layer):
        return ((z == 0) & (layer > z)) | ((z == layers - 1) & (layer < z))

    def far_copy(layer):
        return remote(
            mine(layer, 1, 0), far.at[layer % 3], merge_send.at[layer % 3], far_recv.at[layer % 3], to_a
        )

    def gather_sum(layer, da, target, *more):
        pair = layer * 2 + da
        to_other_core(layer, da, 0).wait_recv()
        to_cross(layer, da).wait_recv()
        terms = (mine(layer, da, 0), twin.at[pair * 2], cross.at[pair]) + more
        from_down = has_down & (layer >= z)
        from_up = has_up & (layer <= z)
        if da:
            from_down = from_down & (z != 1)
            from_up = from_up & (z != layers - 2)

        @pl.when(from_down)
        def _():
            upward(layer, da).wait_recv()

        @pl.when(from_up)
        def _():
            downward(layer, da).wait_recv()

        @pl.when(from_down & from_up)
        def _():
            add(target, *terms, rise.at[pair], fall.at[pair])

        @pl.when(from_down & jnp.logical_not(from_up))
        def _():
            add(target, *terms, rise.at[pair])

        @pl.when(from_up & jnp.logical_not(from_down))
        def _():
            add(target, *terms, fall.at[pair])

        @pl.when(jnp.logical_not(from_up | from_down))
        def _():
            add(target, *terms)

    def pass_on(step, carry):
        layer = ordered(step)
        rising = layer > z
        is_far = merges(layer)
        near = jnp.logical_not(is_far)

        gather_sum(layer, 1, mine(layer, 1, 0))

        @pl.when(is_far)
        def _():
            far_copy(layer).start()

        @pl.when(near & rising)
        def _():
            upward(layer, 1).start()

        @pl.when(near & jnp.logical_not(rising))
        def _():
            downward(layer, 1).start()

        @pl.when(near)
        def _():
            gather_sum(layer, 0, mine(layer, 0, 0))

        @pl.when(is_far)
        def _():
            pair = layer * 2
            to_other_core(layer, 0, 0).wait_recv()
            to_cross(layer, 0).wait_recv()
            far_copy(layer).wait_recv()
            add(
                mine(layer, 0, 0),
                mine(layer, 0, 0),
                twin.at[pair * 2],
                cross.at[pair],
                far.at[layer % 3],
            )

        @pl.when(rising)
        def _():
            upward(layer, 0).start()

        @pl.when(jnp.logical_not(rising))
        def _():
            downward(layer, 0).start()

        return carry

    lax.fori_loop(0, layers - 1, pass_on, 0)
    gather_sum(z, 1, mine(z, 1, 0))
    to_last().start()
    gather_sum(z, 0, out_ref, out_ref)
    to_last().wait_recv()
    add(out_ref, out_ref, last)

    def finish_layer(step, carry):
        layer = ordered(step)
        for da in range(2):
            to_other_core(layer, da, 0).wait_send()
            to_other_core(layer, da, 1).wait_send()
            to_cross(layer, da).wait_send()

            is_far = merges(layer)
            along = (layer != z) & jnp.logical_not(is_far) if da else layer != z

            @pl.when(along)
            def _():
                upward(layer, da).wait_send()

            if da:

                @pl.when(is_far)
                def _():
                    far_copy(layer).wait_send()

        return carry

    lax.fori_loop(0, layers, finish_layer, 0)
    to_last().wait_send()
    for step in range(1, dp_count):
        route(step).wait_send()


def layer_call(attended, weight, tokens, routes, router, gain, gate, up, down):
    dp_count, mp_count = lax.axis_size("dp"), lax.axis_size("mp")
    rows, half = tokens.shape
    width = mp_count * half
    layers = dp_count // 4
    pairs = dp_count // 2
    held_count = gate.shape[1] // FF
    dma = pltpu.SemaphoreType.DMA
    vmem = pl.BlockSpec(memory_space=pltpu.VMEM)
    hbm = pl.BlockSpec(memory_space=pltpu.HBM)
    block = (rows, half)
    narrow = jnp.bfloat16
    return pl.pallas_call(
        layer_kernel,
        out_shape=jax.ShapeDtypeStruct(block, jnp.float32),
        in_specs=[hbm] * 9,
        out_specs=vmem,
        scratch_shapes=[
            pltpu.VMEM(attended.shape, narrow),
            pltpu.VMEM(block, narrow),
            pltpu.VMEM(block, narrow),
            pltpu.VMEM(block, narrow),
            pltpu.VMEM(router.shape, jnp.float32),
            pltpu.VMEM((dp_count,) + routes.shape, routes.dtype),
            pltpu.VMEM((4 * EXPERTS, width), narrow),
            pltpu.VMEM((mp_count, 1, half), jnp.float32),
            pltpu.VMEM((dp_count * rows, width), narrow),
            pltpu.VMEM((2 * rows, width), narrow),
            pltpu.VMEM(gate.shape, narrow),
            pltpu.VMEM(up.shape, narrow),
            pltpu.VMEM(down.shape, narrow),
            pltpu.VMEM((held_count, dp_count * CAP, width), narrow),
            pltpu.VMEM((dp_count // 2 * CAP, FF), narrow),
            pltpu.VMEM((weight.shape[1], width), narrow),
            pltpu.VMEM((dp_count // 2, 4 * held_count * CAP, 2 * rows), narrow),
            pltpu.VMEM((2 * pairs,) + block, narrow),
            pltpu.VMEM((pairs,) + block, narrow),
            pltpu.VMEM((pairs,) + block, narrow),
            pltpu.VMEM((pairs,) + block, narrow),
            pltpu.VMEM(block, narrow),
            pltpu.VMEM((3,) + block, narrow),
            dma((dp_count,)),
            dma((dp_count,)),
            dma((half // 256,)),
            dma((half // 256,)),
            dma((6,)),
            dma((dp_count,)),
            dma((held_count,)),
            dma((held_count,)),
            dma((held_count,)),
            dma((2,)),
            dma((layers * 2,)),
            dma((layers * 2,)),
            dma((layers * 2,)),
            dma((layers * 4,)),
            dma((dp_count * mp_count,)),
            dma,
            dma((3,)),
            dma((3,)),
            dma((2 * pairs,)),
            dma((pairs,)),
            dma((pairs,)),
            dma,
            dma((2 * pairs,)),
            dma((pairs,)),
            dma((pairs,)),
            dma((pairs,)),
            dma,
        ],
        compiler_params=pltpu.CompilerParams(
            collective_id=2, has_side_effects=True, vmem_limit_bytes=60 * 1024 * 1024
        ),
        name="mixture_layer",
    )(attended, weight, tokens, routes, router, gain, gate, up, down)


def local_paired(
    tokens,
    lengths,
    keep_mask,
    routes,
    attention_gain,
    mixture_gain,
    query_gain,
    key_gain,
    query_weight,
    key_weight,
    value_weight,
    output_weight,
    router_weight,
    expert_gate,
    expert_up,
    expert_down,
):
    tok_rows, half = tokens.shape
    local_heads = query_weight.shape[1] // HEAD_DIM
    attended, all_output_weight, all_router, all_gain = front_call(
        tokens,
        lengths,
        keep_mask,
        attention_gain,
        query_gain,
        key_gain,
        query_weight,
        key_weight,
        value_weight,
        output_weight,
        router_weight.T,
        mixture_gain[None, :],
    )
    return layer_call(
        attended,
        all_output_weight,
        tokens,
        routes.T,
        all_router,
        all_gain,
        expert_gate[0],
        expert_up[0],
        expert_down[0],
    ).astype(jnp.bfloat16)


def local(*arrays):
    paired = lax.axis_size("mp") == 2 and lax.axis_size("dp") == 16
    return (local_paired if paired else local_any)(*arrays)


def solution(mesh):
    return jax.shard_map(
        local,
        mesh=mesh,
        in_specs=(
            P("dp", "mp"),
            P(),
            P(),
            P("dp", None),
            P(),
            P("mp"),
            P(),
            P(),
            P("dp", "mp"),
            P("dp", "mp"),
            P("dp", "mp"),
            P("mp", "dp"),
            P("mp", None),
            P("dp", None, "mp"),
            P("dp", None, "mp"),
            P("dp", "mp", None),
        ),
        out_specs=P("dp", "mp"),
        check_vma=False,
    )
```
